32 devices in a mesh: seq: 8 (over z, y), head: 4 (over x, core).
Axes of the slice: x: 2, y: 2, z: 4, core: 2. Of those that a mesh axis runs over, the one named last changes fastest.
Arguments:
- inputs: bfloat16 [2048, 768], P('seq', 'head'), may hold values from -6 to 6
- pre_gain: float32 [768], replicated, may hold values from 0.5 to 1.5
- w_query: bfloat16 [768, 768], P(None, 'head'), may hold values from -0.21875 to 0.21875
- w_key: bfloat16 [768, 768], P(None, 'head'), may hold values from -0.21875 to 0.21875
- w_value: bfloat16 [768, 768], P(None, 'head'), may hold values from -0.21875 to 0.21875
- mix_gate: bfloat16 [768, 768], P(None, 'head'), may hold values from -0.21875 to 0.21875
- w_rate: bfloat16 [768, 12], P(None, 'head'), may hold values from -0.21875 to 0.21875
- rate_bias: float32 [12], P('head'), may hold values from -1.5 to 1.5
- inner_gain: float32 [12, 64], P('head'), may hold values from 0.5 to 1.5
- inner_bias: float32 [12, 64], P('head'), may hold values from -1.8 to 1.8
- init_w_one: float32 [12, 64, 256], P('head'), may hold values from -0.75 to 0.75
- init_b_one: float32 [12, 256], P('head'), may hold values from -1.8 to 1.8
- init_w_two: float32 [12, 256, 64], P('head'), may hold values from -0.375 to 0.375
- init_b_two: float32 [12, 64], P('head'), may hold values from -3 to 3
- post_gain: float32 [768], P('head'), may hold values from 0.5 to 1.5
- post_bias: float32 [768], P('head'), may hold values from -3 to 3
- w_out: bfloat16 [768, 768], P('head'), may hold values from -0.21875 to 0.21875
- ffn_gain: float32 [768], replicated, may hold values from 0.5 to 1.5
- w_gate: bfloat16 [768, 2048], P(None, 'head'), may hold values from -0.21875 to 0.21875
- w_up: bfloat16 [768, 2048], P(None, 'head'), may hold values from -0.21875 to 0.21875
- w_down: bfloat16 [2048, 768], P('head'), may hold values from -0.125 to 0.125
- cotangent: bfloat16 [2048, 768], P('seq', 'head'), may hold values from -6 to 6
Outputs:
- outputs: float32 [2048, 768], P('seq', 'head')
- grad_inputs: float32 [2048, 768], P('seq', 'head')
- grad_pre_gain: float32 [768], P('head')
- grad_w_query: float32 [768, 768], P('seq', 'head')
- grad_w_key: float32 [768, 768], P('seq', 'head')
- grad_w_value: float32 [768, 768], P('seq', 'head')
- grad_mix_gate: float32 [768, 768], P('seq', 'head')
- grad_w_rate: float32 [768, 12], P(None, 'head')
- grad_rate_bias: float32 [12], P('head')
- grad_inner_gain: float32 [12, 64], P('head')
- grad_inner_bias: float32 [12, 64], P('head')
- grad_init_w_one: float32 [12, 64, 256], P('head')
- grad_init_b_one: float32 [12, 256], P('head')
- grad_init_w_two: float32 [12, 256, 64], P('head')
- grad_init_b_two: float32 [12, 64], P('head')
- grad_post_gain: float32 [768], P('head')
- grad_post_bias: float32 [768], P('head')
- grad_w_out: float32 [768, 768], P('head', 'seq')
- grad_ffn_gain: float32 [768], replicated
- grad_w_gate: float32 [768, 2048], P('seq', 'head')
- grad_w_up: float32 [768, 2048], P('seq', 'head')
- grad_w_down: float32 [2048, 768], P('head', 'seq')
The draws below stay inside these ranges and needn't reach their ends.
All inputs are finite; a program needn't handle non-finite values.
Results may differ from the reference program's by a relative error of at most 0.028.
Values may be sent and summed in bfloat16 or wider, within the bound.
A program may use at most 128 MiB of HBM per device.

```python
import jax
import jax.numpy as jnp
from jax import lax

D = 768
HEADS = 12
FF = 2048
HDIM = 64
INNER = 256
MINI = 16
TOKENS = 2048
SEQ_LEN = 2048
STRETCHES = 1


def shard_levels(key, shape, split, smallest, high):
    loudness = 1.0
    for axis_at, parts in split:
        steps = jax.random.uniform(jax.random.fold_in(jax.random.fold_in(key, 6), axis_at), (parts,), jnp.float32, smallest / len(split), high / len(split))
        loudness = loudness * jnp.repeat(jnp.exp(steps), shape[axis_at] // parts).reshape((-1,) + (1,) * (len(shape) - 1 - axis_at))
    return loudness


def scatter_about(key, dims, width, most, pieces=(), dtype=jnp.bfloat16):
    gain = shard_levels(key, dims, pieces, -0.22, 0.18) if pieces else 1.0
    array = jax.random.normal(key, dims, jnp.float32) * width * gain
    return jnp.minimum(jnp.maximum(array, -most), most).astype(dtype)


def setup_inputs(seed: int = 0) -> dict:
    keys = jax.random.split(jax.random.key(seed), 23)
    return {
        "inputs": scatter_about(keys[0], (TOKENS, D), 1.0, 6.0, ((0, 8), (1, 4))),
        "pre_gain": jnp.clip(1.0 + 0.1 * jax.random.normal(keys[1], (D,), jnp.float32), 0.5, 1.5),
        "w_query": scatter_about(keys[2], (D, D), D ** -0.5, 0.21875, ((1, 4),)),
        "w_key": scatter_about(keys[3], (D, D), D ** -0.5, 0.21875, ((1, 4),)),
        "w_value": scatter_about(keys[4], (D, D), D ** -0.5, 0.21875, ((1, 4),)),
        "mix_gate": scatter_about(keys[5], (D, D), D ** -0.5, 0.21875, ((1, 4),)),
        "w_rate": scatter_about(keys[6], (D, HEADS), D ** -0.5, 0.21875, ((1, 4),)),
        "rate_bias": jnp.clip(jax.random.uniform(keys[7], (HEADS,), jnp.float32, -1.5, 1.5) * shard_levels(keys[7], (HEADS,), ((0, 4),), -0.4, 0.0), -1.5, 1.5),
        "inner_gain": jnp.clip(1.0 + 0.1 * jax.random.normal(keys[8], (HEADS, HDIM), jnp.float32), 0.5, 1.5),
        "inner_bias": scatter_about(keys[9], (HEADS, HDIM), 0.3, 1.8, ((0, 4),), jnp.float32),
        "init_w_one": scatter_about(keys[10], (HEADS, HDIM, INNER), HDIM ** -0.5, 0.75, ((0, 4),), jnp.float32),
        "init_b_one": scatter_about(keys[11], (HEADS, INNER), 0.3, 1.8, ((0, 4),), jnp.float32),
        "init_w_two": scatter_about(keys[12], (HEADS, INNER, HDIM), INNER ** -0.5, 0.375, ((0, 4),), jnp.float32),
        "init_b_two": scatter_about(keys[13], (HEADS, HDIM), 0.5, 3.0, ((0, 4),), jnp.float32),
        "post_gain": jnp.clip(1.0 + 0.1 * jax.random.normal(keys[14], (D,), jnp.float32), 0.5, 1.5),
        "post_bias": scatter_about(keys[15], (D,), 0.5, 3.0, ((0, 4),), jnp.float32),
        "w_out": scatter_about(keys[16], (D, D), D ** -0.5, 0.21875, ((0, 4),)),
        "ffn_gain": jnp.clip(1.0 + 0.1 * jax.random.normal(keys[17], (D,), jnp.float32), 0.5, 1.5),
        "w_gate": scatter_about(keys[18], (D, FF), D ** -0.5, 0.21875, ((1, 4),)),
        "w_up": scatter_about(keys[19], (D, FF), D ** -0.5, 0.21875, ((1, 4),)),
        "w_down": scatter_about(keys[20], (FF, D), FF ** -0.5, 0.125, ((0, 4),)),
        "cotangent": scatter_about(keys[21], (TOKENS, D), 1.0, 6.0, ((0, 8), (1, 4))),
    }


eps_norm = 1e-06
gelu_scale = 0.7978845608028654
highest = lax.Precision.HIGHEST

@jax.custom_vjp
def low(v):
    return lax.optimization_barrier(v.astype(jnp.bfloat16)).astype(jnp.float32)

@jax.custom_vjp
def low_back(v):
    return v

def low_keep(v):
    return (low(v), None)

def low_pass(kept, grad):
    return (grad,)

def back_keep(v):
    return (v, None)

def back_low(kept, grad):
    return (low(grad),)
low.defvjp(low_keep, low_pass)
low_back.defvjp(back_keep, back_low)

def gelu_tanh(arg_value):
    cubic = arg_value + 0.044715 * arg_value * arg_value * arg_value
    return 0.5 * arg_value * (1.0 + jnp.tanh(gelu_scale * cubic))

def gelu_derivative(arg_value):
    tangent = jnp.tanh(gelu_scale * (arg_value + 0.044715 * arg_value * arg_value * arg_value))
    return 0.5 * (1.0 + tangent) + 0.5 * arg_value * (1.0 - tangent * tangent) * gelu_scale * (1.0 + 0.134145 * arg_value * arg_value)

def head_norm(values_in, gain_vec, bias_vec):
    centre = lax.optimization_barrier(jnp.mean(values_in, axis=-1, keepdims=True))
    centred = values_in - centre
    inv_scale = lax.rsqrt(lax.optimization_barrier(jnp.mean(centred * centred, axis=-1, keepdims=True)) + eps_norm)
    normed = centred * inv_scale
    return (normed, inv_scale, normed * gain_vec + bias_vec)

def mixing_contraction(form, left, right):
    return jnp.einsum(form, left, right, precision=highest)

def inner_update(state_now, mini_batch, gain_vec, bias_vec):
    first_weight, first_bias, second_weight, second_bias = state_now
    query_mb, key_minibatch, value_mb, rate_mb = mini_batch
    first_preactivation = mixing_contraction('uwf,ufo->uwo', key_minibatch, first_weight) + first_bias[:, None, :]
    hidden_activation = gelu_tanh(first_preactivation)
    second_preactivation = mixing_contraction('aeq,aqj->aej', hidden_activation, second_weight) + second_bias[:, None, :]
    normed, inv_scale, predicted = head_norm(second_preactivation, gain_vec[:, None, :], bias_vec[:, None, :])
    recon_err = predicted - (value_mb - key_minibatch)
    grad_normed = recon_err * gain_vec[:, None, :]
    second_gradient = inv_scale * (grad_normed - lax.optimization_barrier(jnp.mean(grad_normed, axis=-1, keepdims=True)) - normed * lax.optimization_barrier(jnp.mean(grad_normed * normed, axis=-1, keepdims=True)))
    first_gradient = mixing_contraction('tfu,tvu->tfv', second_gradient, second_weight) * gelu_derivative(first_preactivation)
    first_update_step = rate_mb[:, :, None] * first_gradient
    second_update_step = rate_mb[:, :, None] * second_gradient
    updated_state = (first_weight - mixing_contraction('pgw,pgy->pwy', key_minibatch, first_update_step), first_bias - lax.optimization_barrier(jnp.sum(first_update_step, axis=1)), second_weight - mixing_contraction('voj,von->vjn', hidden_activation, second_update_step), second_bias - lax.optimization_barrier(jnp.sum(second_update_step, axis=1)))
    return (updated_state, hidden_activation, first_update_step, second_update_step)

def inner_step(state_now, mini_batch, gain_vec, bias_vec):
    updated_state, hidden_activation, first_update_step, second_update_step = inner_update(state_now, mini_batch, gain_vec, bias_vec)
    first_weight, first_bias, second_weight, second_bias = state_now
    query_mb = mini_batch[0]
    key_minibatch = mini_batch[1]
    rows_mini = query_mb.shape[1]
    causal = jnp.tril(jnp.ones((rows_mini, rows_mini), jnp.float32))
    attend_one = mixing_contraction('htd,hsd->hts', query_mb, key_minibatch) * causal + causal
    bar_one = mixing_contraction('htd,hdi->hti', query_mb, first_weight) + first_bias[:, None, :] - mixing_contraction('hts,hsi->hti', attend_one, first_update_step)
    hidden_bar = gelu_tanh(bar_one)
    attend_two = mixing_contraction('hti,hsi->hts', hidden_bar, hidden_activation) * causal + causal
    bar_two = mixing_contraction('hti,hid->htd', hidden_bar, second_weight) + second_bias[:, None, :] - mixing_contraction('hts,hsd->htd', attend_two, second_update_step)
    shaped = head_norm(bar_two, gain_vec[:, None, :], bias_vec[:, None, :])[2]
    return (updated_state, query_mb + shaped)

def split_blocks(row_data, mini, head_count):
    total_rows = row_data.shape[0]
    return row_data.reshape(total_rows // mini, mini, head_count, -1).transpose(0, 2, 1, 3)

def prepare_blocks(query_rows, key_rows, value_rows, logit_rows, mini):
    total_rows, head_count = logit_rows.shape
    head_dim = query_rows.shape[1] // head_count
    rate_rows = jax.nn.sigmoid(logit_rows) / head_dim
    rate_blocks = rate_rows.reshape(total_rows // mini, mini, head_count).transpose(0, 2, 1)
    return (split_blocks(query_rows, mini, head_count), split_blocks(key_rows, mini, head_count), split_blocks(value_rows, mini, head_count), rate_blocks)

def run_block(query_rows, key_rows, value_rows, logit_rows, state_now, gain_vec, bias_vec, mini):
    blocks = prepare_blocks(query_rows, key_rows, value_rows, logit_rows, mini)

    def advance(carry, mini_batch):
        return inner_step(carry, mini_batch, gain_vec, bias_vec)
    final_state, block_out = lax.scan(jax.checkpoint(advance), state_now, blocks)
    merged = block_out.transpose(0, 2, 1, 3).reshape(query_rows.shape)
    return (merged, final_state)

def matmul_high(left, right):
    return jnp.dot(left, right, precision=highest, preferred_element_type=jnp.float32)

def forward_all(inputs, pre_gain, w_query, w_key, w_value, mix_gate, w_rate, rate_bias, inner_gain, inner_bias, init_w_one, init_b_one, init_w_two, init_b_two, post_gain, post_bias, w_out, ffn_gain, w_gate, w_up, w_down):

    def one_stretch(stretch):
        rms_one = lax.rsqrt(lax.optimization_barrier(jnp.mean(stretch * stretch, axis=-1, keepdims=True)) + eps_norm)
        normed_one = low(stretch * rms_one * pre_gain)
        queries = low_back(low(matmul_high(normed_one, w_query)))
        keys_in = low_back(low(matmul_high(normed_one, w_key)))
        values_in = low_back(low(matmul_high(normed_one, w_value)))
        gate_pre = low_back(matmul_high(normed_one, mix_gate))
        logits = low_back(matmul_high(normed_one, w_rate)) + rate_bias
        mixed, _ = run_block(queries, keys_in, values_in, logits, (init_w_one, init_b_one, init_w_two, init_b_two), inner_gain, inner_bias, MINI)
        mean_z = lax.optimization_barrier(jnp.mean(mixed, axis=-1, keepdims=True))
        var_z = lax.optimization_barrier(jnp.mean(mixed * mixed, axis=-1, keepdims=True)) - mean_z * mean_z
        post_out = (mixed - mean_z) * lax.rsqrt(var_z + eps_norm) * post_gain + post_bias
        gated = low(post_out * gelu_tanh(gate_pre))
        resid = stretch + low_back(matmul_high(gated, w_out))
        rms_two = lax.rsqrt(lax.optimization_barrier(jnp.mean(resid * resid, axis=-1, keepdims=True)) + eps_norm)
        normed_two = low(resid * rms_two * ffn_gain)
        gate_val = low_back(matmul_high(normed_two, w_gate))
        up_val = low_back(matmul_high(normed_two, w_up))
        hidden_ffn = low(jax.nn.silu(gate_val) * up_val)
        return resid + matmul_high(hidden_ffn, w_down)
    checked = jax.checkpoint(one_stretch)

    def scan_body(carry, stretch):
        return (carry, checked(stretch))
    stretches = inputs.reshape(STRETCHES, SEQ_LEN, D)
    _, results = lax.scan(scan_body, jnp.zeros((), jnp.float32), stretches)
    return results.reshape(TOKENS, D)

def reference(inputs, pre_gain, w_query, w_key, w_value, mix_gate, w_rate, rate_bias, inner_gain, inner_bias, init_w_one, init_b_one, init_w_two, init_b_two, post_gain, post_bias, w_out, ffn_gain, w_gate, w_up, w_down, cotangent):
    floats = [arg_item.astype(jnp.float32) for arg_item in (inputs, pre_gain, w_query, w_key, w_value, mix_gate, w_rate, rate_bias, inner_gain, inner_bias, init_w_one, init_b_one, init_w_two, init_b_two, post_gain, post_bias, w_out, ffn_gain, w_gate, w_up, w_down)]
    outputs, pullback = jax.vjp(forward_all, *floats)
    grads = pullback(cotangent.astype(jnp.float32))
    return (outputs, grads[0], grads[1], grads[2], grads[3], grads[4], grads[5], grads[6], grads[7], grads[8], grads[9], grads[10], grads[11], grads[12], grads[13], grads[14], grads[15], grads[16], grads[17], grads[18], grads[19], grads[20])
```

```python
import functools

import jax
import jax.numpy as jnp
from jax import lax
from jax.experimental import pallas as pl
from jax.experimental.pallas import tpu as pltpu
from jax.sharding import PartitionSpec as P

MINI = 16
CHAIN = 8
FIRST = 2
AUG = 80
eps_norm = 1e-06
gelu_scale = 0.7978845608028654
f32 = jnp.float32
bf16 = jnp.bfloat16


def dot_nn(a, b):
    return lax.dot_general(a, b, (((1,), (0,)), ((), ())), preferred_element_type=f32)


def dot_nt(a, b):
    return lax.dot_general(a, b, (((1,), (1,)), ((), ())), preferred_element_type=f32)


def dot_tn(a, b):
    return lax.dot_general(a, b, (((0,), (0,)), ((), ())), preferred_element_type=f32)


def mean_row(x):
    return jnp.sum(x, axis=1, keepdims=True) * (1.0 / x.shape[1])


def gelu_first(z):
    sq = z * z
    th = jnp.tanh(gelu_scale * z * (1.0 + 0.044715 * sq))
    half = 0.5 * (1.0 + th)
    act = z * half
    der = half + (0.5 * gelu_scale) * z * (1.0 - th * th) * (1.0 + 0.134145 * sq)
    return act, der


def gelu_second(z):
    sq = z * z
    th = jnp.tanh(gelu_scale * z * (1.0 + 0.044715 * sq))
    half = 0.5 * (1.0 + th)
    act = z * half
    slope = gelu_scale * (1.0 + 0.134145 * sq)
    sech = 1.0 - th * th
    der = half + 0.5 * z * sech * slope
    curve = sech * (slope + z * (0.5 * gelu_scale * 0.26829 * z) - z * th * slope * slope)
    return act, der, curve


def tri_mask():
    rows = lax.broadcasted_iota(jnp.int32, (MINI, MINI), 0)
    cols = lax.broadcasted_iota(jnp.int32, (MINI, MINI), 1)
    return jnp.where(rows >= cols, 1.0, 0.0).astype(f32)


def inner_target_grad(z, base, gain_sq, rate):
    mz = mean_row(z)
    m_zz = mean_row(z * z)
    zg = z * gain_sq
    m_zg = mean_row(zg)
    m_zzg = mean_row(zg * z)
    m_zb = mean_row(z * base)
    m_b = mean_row(base)
    m_sq = mean_row(gain_sq)
    inv = lax.rsqrt(m_zz - mz * mz + eps_norm)
    c_zg = m_zg - mz * m_sq
    c_zzg = m_zzg - mz * (m_zg + c_zg)
    c_zb = m_zb - mz * m_b
    m_g = inv * c_zg + m_b
    m_gn = inv * (inv * c_zzg + c_zb)
    zc = z - mz
    n = zc * inv
    grad = inv * (n * (gain_sq - m_gn) + (base - m_g))
    return rate * grad, zc


def forward_step(state, z1, key_aug, key_next, query_aug, base, rate, gain, gain_sq, bias, tri):
    w1, w2t, b2 = state
    act, der = gelu_first(z1)
    act_h = act.astype(bf16)
    w1_h = w1.astype(bf16)
    w2_h = w2t.astype(bf16)
    s2, zc = inner_target_grad(dot_nt(act_h, w2_h) + b2, base, gain_sq, rate)
    s2_h = s2.astype(bf16)
    upd = dot_nn(s2_h, w2_h)
    s1_h = (upd * der).astype(bf16)
    both = jnp.concatenate([key_next, query_aug], axis=0)
    coef = dot_nt(both, key_aug)
    coef = jnp.concatenate([coef[:MINI], coef[MINI:] * tri], axis=0)
    zz = dot_nn(both, w1_h) - dot_nn(coef.astype(bf16), s1_h)
    z1_next = zz[:MINI]
    z1b = zz[MINI:]
    new_w1 = w1 - dot_tn(key_aug, s1_h)
    new_w2t = w2t - dot_tn(s2_h, act_h)
    new_b2 = b2 - jnp.sum(s2, axis=0, keepdims=True)
    actb, _ = gelu_first(z1b)
    actb_h = actb.astype(bf16)
    att = (dot_nt(actb_h, act_h) + 1.0) * tri
    z2b = dot_nt(actb_h, w2_h) + b2 - dot_nn(att.astype(bf16), s2_h)
    z2b = z2b - mean_row(z2b)
    invb = lax.rsqrt(mean_row(z2b * z2b) + eps_norm)
    out = z2b * invb * gain + bias
    return (new_w1, new_w2t, new_b2), z1_next, out, (w1_h, w2_h, upd, zc, s2, z1b, z2b)


def backward_step(carry, saved, d_out, key_aug, query_aug, target, rate, keep, gain, gain_sq, bias, tri):
    p1, p2t, p2 = carry
    w1_h, w2_h, z1, upd, zc, s2, z1b, z2b = saved
    act, der, curve = gelu_second(z1)
    act_h = act.astype(bf16)
    actb, derb = gelu_first(z1b)
    actb_h = actb.astype(bf16)
    s2_h = s2.astype(bf16)
    s1_h = (upd * der).astype(bf16)
    p1_h = p1.astype(bf16)
    p2_h = p2t.astype(bf16)
    invb = lax.rsqrt(mean_row(z2b * z2b) + eps_norm)
    nb = z2b * invb
    dn = d_out * gain
    d_z2b = invb * (dn - mean_row(dn) - nb * mean_row(dn * nb))
    d_z2b_h = d_z2b.astype(bf16)
    d_att2 = (-dot_nt(d_z2b_h, s2_h) * tri).astype(bf16)
    d_actb = dot_nn(d_z2b_h, w2_h) + dot_nn(d_att2, act_h)
    d_z1b_h = (d_actb * derb).astype(bf16)
    att2 = ((dot_nt(actb_h, act_h) + 1.0) * tri).astype(bf16)
    att1 = (dot_nt(query_aug, key_aug) * tri).astype(bf16)
    c2 = dot_tn(att2, d_z2b_h)
    c3 = dot_tn(d_att2, actb_h)
    c1 = dot_tn(att1, d_z1b_h)
    d_att1 = (-dot_nt(d_z1b_h, s1_h) * tri).astype(bf16)
    d_query = dot_nt(d_z1b_h, w1_h) + dot_nn(d_att1, key_aug)
    d_key = dot_tn(d_att1, query_aug)
    d_s1 = -c1 - dot_nn(key_aug, p1_h)
    d_upd = d_s1 * der
    d_upd_h = d_upd.astype(bf16)
    d_s2 = dot_nt(d_upd_h, w2_h) - c2 - dot_nt(act_h, p2_h) - p2
    h = rate * d_s2
    inv = lax.rsqrt(mean_row(zc * zc) + eps_norm)
    n = zc * inv
    base = (bias - target) * gain
    big_g = n * gain_sq + base
    m_g = mean_row(big_g)
    m_gn = mean_row(big_g * n)
    m_sq = mean_row(gain_sq)
    ng = n * gain_sq
    m_ng = mean_row(ng)
    m_nng = mean_row(n * ng)
    g = inv * (big_g - m_g - n * m_gn)
    a1 = mean_row(h)
    a2 = mean_row(h * n)
    a3 = mean_row(h * gain_sq)
    a4 = mean_row(h * ng)
    a5 = mean_row(h * g)
    proj = h - a1 - n * a2
    d_g = inv * proj
    dnn = inv * (proj * gain_sq - h * m_gn - big_g * a2)
    m_dn = inv * (a3 - a1 * (m_sq + m_gn) - a2 * (m_ng + m_g))
    m_dnn = inv * (a4 - a1 * m_ng - a2 * (m_nng + 2.0 * m_gn))
    d_zc = inv * (dnn - m_dn - n * (m_dnn + a5))
    d_zc_h = d_zc.astype(bf16)
    d_act = dot_nn(d_zc_h, w2_h) + c3 - dot_nn(s2_h, p2_h)
    d_z1 = d_act * der + d_s1 * upd * curve
    d_z1_h = d_z1.astype(bf16)
    d_gg = d_g * gain
    d_key = d_key + dot_nt(d_z1_h, w1_h) - dot_nt(s1_h, p1_h)
    d_key = d_key[:, : gain.shape[1]] + d_gg
    d_query = d_query[:, : gain.shape[1]] + d_out
    d_value = -d_gg
    d_logit = keep * jnp.sum(d_s2 * s2, axis=1, keepdims=True)
    new_p1 = p1 + dot_tn(
        jnp.concatenate([key_aug, query_aug], axis=0), jnp.concatenate([d_z1_h, d_z1b_h], axis=0)
    )
    new_p2t = p2t + dot_tn(
        jnp.concatenate([s2_h, d_zc_h, d_z2b_h], axis=0),
        jnp.concatenate([d_upd_h, act_h, actb_h], axis=0),
    )
    new_p2 = p2 + jnp.sum(d_zc + d_z2b, axis=0, keepdims=True)
    d_bias = jnp.sum(d_out + d_gg, axis=0, keepdims=True)
    d_gain = jnp.sum(d_out * nb + d_g * (2.0 * n * gain + bias - target), axis=0, keepdims=True)
    return (new_p1, new_p2t, new_p2), (d_query, d_key, d_value, d_logit), d_gain, d_bias


def fwd_kernel(block, unroll, q_ref, k_ref, base_ref, rate_ref, w1_in, w2t_in, b2_in, gain_ref, bias_ref,
               out_ref, w1s_ref, w2s_ref, z1s_ref, upd_ref, zc_ref, s2_ref, z1b_ref, z2b_ref,
               w1, w2t, b2, z1):
    blk = pl.program_id(0)
    gain = gain_ref[...]
    bias = bias_ref[...]
    gain_sq = gain * gain
    tri = tri_mask()
    width = gain.shape[1]

    @pl.when(blk == 0)
    def _():
        w1[...] = w1_in[...]
        w2t[...] = w2t_in[...]
        b2[...] = b2_in[...]
        z1[...] = dot_nn(k_ref[0:MINI, :], w1_in[...].astype(bf16))

    def group(it, _):
        for u in range(unroll):
            loc = it * unroll + u
            row = pl.multiple_of(blk * block + loc * MINI, MINI)
            lrow = pl.multiple_of(loc * MINI, MINI)
            rows = pl.ds(row, MINI)
            lrows = pl.ds(lrow, MINI)
            q_aug = q_ref[rows, :]
            z1_now = z1[...]
            state, z1_next, out, saved = forward_step(
                (w1[...], w2t[...], b2[...]), z1_now, k_ref[rows, :], k_ref[pl.ds(row + MINI, MINI), :], q_aug,
                base_ref[rows, :], rate_ref[rows, :], gain, gain_sq, bias, tri)
            w1[...], w2t[...], b2[...] = state
            z1[...] = z1_next
            out_ref[lrows, :] = out + q_aug[:, :width].astype(f32)
            w1_h, w2_h, upd, zc, s2, z1b, z2b = saved
            w1s_ref[loc] = w1_h
            w2s_ref[loc] = w2_h
            z1s_ref[lrows, :] = z1_now
            upd_ref[lrows, :] = upd
            zc_ref[lrows, :] = zc
            s2_ref[lrows, :] = s2
            z1b_ref[lrows, :] = z1b
            z2b_ref[lrows, :] = z2b
        return 0

    lax.fori_loop(0, block // MINI // unroll, group, 0)


def chain_forward(q_aug, k_aug, base, rate, w1, w2t, b2, gain, bias, block=128, unroll=8):
    tokens = q_aug.shape[0]
    hidden = w1.shape[1]
    width = gain.shape[1]
    steps = tokens // MINI
    whole = lambda a: pl.BlockSpec(a.shape, lambda i: (0,) * a.ndim, pipeline_mode=pl.Buffered(1))
    rowblk = lambda w: pl.BlockSpec((block, w), lambda i: (i, 0))
    nb = block // MINI
    ins = (q_aug, k_aug, base, rate, w1, w2t, b2, gain, bias)
    return pl.pallas_call(
        functools.partial(fwd_kernel, block, unroll),
        grid=(tokens // block,),
        in_specs=[whole(a) for a in ins],
        out_specs=[rowblk(width),
                   pl.BlockSpec((nb, AUG, hidden), lambda i: (i, 0, 0)),
                   pl.BlockSpec((nb, width, hidden), lambda i: (i, 0, 0)),
                   rowblk(hidden), rowblk(hidden), rowblk(width), rowblk(width), rowblk(hidden), rowblk(width)],
        out_shape=[jax.ShapeDtypeStruct((tokens, width), f32),
                   jax.ShapeDtypeStruct((steps, AUG, hidden), bf16),
                   jax.ShapeDtypeStruct((steps, width, hidden), bf16),
                   jax.ShapeDtypeStruct((tokens, hidden), f32),
                   jax.ShapeDtypeStruct((tokens, hidden), f32),
                   jax.ShapeDtypeStruct((tokens, width), f32),
                   jax.ShapeDtypeStruct((tokens, width), f32),
                   jax.ShapeDtypeStruct((tokens, hidden), f32),
                   jax.ShapeDtypeStruct((tokens, width), f32)],
        scratch_shapes=[pltpu.VMEM((AUG, hidden), f32), pltpu.VMEM((width, hidden), f32),
                        pltpu.VMEM((1, width), f32), pltpu.VMEM((MINI, hidden), f32)],
        name="inner_forward",
    )(*ins)


def bwd_kernel(block, unroll, dout_ref, q_ref, k_ref, target_ref, rate_ref, keep_ref, gain_ref, bias_ref,
               w1s_ref, w2s_ref, z1s_ref, upd_ref, zc_ref, s2_ref, z1b_ref, z2b_ref,
               dq_ref, dk_ref, dv_ref, dl_ref, p1_out, p2t_out, p2_out, dg_out, db_out,
               p1, p2t, p2, dg, db):
    pid = pl.program_id(0)
    blk = pl.num_programs(0) - 1 - pid
    gain = gain_ref[...]
    bias = bias_ref[...]
    gain_sq = gain * gain
    tri = tri_mask()

    @pl.when(pid == 0)
    def _():
        for r in (p1, p2t, p2, dg, db):
            r[...] = jnp.zeros_like(r)

    count = block // MINI

    def group(it, _):
        for u in range(unroll):
            loc = count - 1 - (it * unroll + u)
            row = pl.multiple_of(blk * block + loc * MINI, MINI)
            lrow = pl.multiple_of(loc * MINI, MINI)
            rows = pl.ds(row, MINI)
            lr = pl.ds(lrow, MINI)
            saved = (w1s_ref[loc], w2s_ref[loc], z1s_ref[lr, :], upd_ref[lr, :], zc_ref[lr, :], s2_ref[lr, :],
                     z1b_ref[lr, :], z2b_ref[lr, :])
            carry, outs, dgn, dbn = backward_step(
                (p1[...], p2t[...], p2[...]), saved, dout_ref[rows, :].astype(f32), k_ref[rows, :], q_ref[rows, :],
                target_ref[rows, :], rate_ref[rows, :], keep_ref[rows, :], gain, gain_sq, bias, tri)
            p1[...], p2t[...], p2[...] = carry
            dg[...] += dgn
            db[...] += dbn
            dq_ref[lr, :], dk_ref[lr, :], dv_ref[lr, :] = (o.astype(bf16) for o in outs[:3])
            dl_ref[lr, :] = outs[3]
        return 0

    lax.fori_loop(0, count // unroll, group, 0)

    @pl.when(pid == pl.num_programs(0) - 1)
    def _():
        for o, r in zip((p1_out, p2t_out, p2_out, dg_out, db_out), (p1, p2t, p2, dg, db)):
            o[...] = r[...]


def chain_backward(dout, q_aug, k_aug, target, rate, keep, gain, bias, saved, block=128, unroll=4):
    tokens = q_aug.shape[0]
    width = gain.shape[1]
    hidden = saved[2].shape[1]
    steps = tokens // MINI
    nblk = tokens // block
    whole = lambda a: pl.BlockSpec(a.shape, lambda i: (0,) * a.ndim, pipeline_mode=pl.Buffered(1))
    rowblk = lambda w: pl.BlockSpec((block, w), lambda i: (nblk - 1 - i, 0))
    nb = block // MINI
    ins = (dout, q_aug, k_aug, target, rate, keep, gain, bias)
    acc = [(AUG, hidden), (width, hidden), (1, width), (1, width), (1, width)]
    return pl.pallas_call(
        functools.partial(bwd_kernel, block, unroll),
        grid=(nblk,),
        in_specs=[whole(a) for a in ins]
        + [pl.BlockSpec((nb, AUG, hidden), lambda i: (nblk - 1 - i, 0, 0)),
           pl.BlockSpec((nb, width, hidden), lambda i: (nblk - 1 - i, 0, 0)),
           rowblk(hidden), rowblk(hidden), rowblk(width), rowblk(width), rowblk(hidden), rowblk(width)],
        out_specs=[rowblk(width), rowblk(width), rowblk(width), rowblk(1)]
        + [pl.BlockSpec(s, lambda i: (0, 0)) for s in acc],
        out_shape=[jax.ShapeDtypeStruct((tokens, width), bf16)] * 3 + [jax.ShapeDtypeStruct((tokens, 1), f32)]
        + [jax.ShapeDtypeStruct(s, f32) for s in acc],
        scratch_shapes=[pltpu.VMEM(s, f32) for s in acc],
        name="inner_backward",
    )(*ins, *saved)


def groups_of(axis):
    count = lax.axis_size(axis)
    if count == CHAIN:
        return None
    return [list(range(start, start + CHAIN)) for start in range(0, count, CHAIN)]


def gelu_tanh(arg_value):
    cubic = arg_value + 0.044715 * arg_value * arg_value * arg_value
    return 0.5 * arg_value * (1.0 + jnp.tanh(gelu_scale * cubic))


def gelu_derivative(arg_value):
    tangent = jnp.tanh(gelu_scale * (arg_value + 0.044715 * arg_value * arg_value * arg_value))
    return 0.5 * (1.0 + tangent) + 0.5 * arg_value * (1.0 - tangent * tangent) * gelu_scale * (
        1.0 + 0.134145 * arg_value * arg_value
    )


def bf_product(form, left, right):
    return jnp.einsum(form, left, right, preferred_element_type=f32)


def to_owners(parts):
    heads, rows, width = parts.shape
    padded = jnp.pad(parts, ((FIRST, CHAIN - FIRST - heads), (0, 0), (0, 0)))
    got = lax.all_to_all(padded, "seq", 0, 0, axis_index_groups=groups_of("seq"), tiled=True)
    return got.reshape(CHAIN * rows, width)


def from_owners(rows_of_head, heads):
    total, width = rows_of_head.shape
    got = lax.all_to_all(
        rows_of_head.reshape(CHAIN, total // CHAIN, width), "seq", 0, 0,
        axis_index_groups=groups_of("seq"), tiled=True)
    return got[FIRST : FIRST + heads]


def local(
    inputs,
    pre_gain,
    w_query,
    w_key,
    w_value,
    mix_gate,
    w_rate,
    rate_bias,
    inner_gain,
    inner_bias,
    init_w_one,
    init_b_one,
    init_w_two,
    init_b_two,
    post_gain,
    post_bias,
    w_out,
    ffn_gain,
    w_gate,
    w_up,
    w_down,
    cotangent,
):
    full_width = pre_gain.shape[0]
    rows, local_cols = inputs.shape
    heads, head_dim = inner_gain.shape
    head_index = lax.axis_index("head")
    position = lax.axis_index("seq") % CHAIN
    mine = jnp.clip(position - FIRST, 0, heads - 1)
    is_owner = (position >= FIRST) & (position < FIRST + heads)
    whole_in = lax.all_gather(inputs, "head", axis=1, tiled=True).astype(f32)
    grad_whole = lax.all_gather(cotangent, "head", axis=1, tiled=True)
    rms_one = lax.rsqrt(jnp.mean(whole_in * whole_in, axis=1, keepdims=True) + eps_norm)
    normed_one = (whole_in * rms_one * pre_gain).astype(bf16)
    queries = bf_product("rd,dc->rc", normed_one, w_query).astype(bf16)
    keys_in = bf_product("rd,dc->rc", normed_one, w_key).astype(bf16)
    values_in = bf_product("rd,dc->rc", normed_one, w_value).astype(bf16)
    gate_pre = bf_product("rd,dc->rc", normed_one, mix_gate)
    logits = bf_product("rd,dc->rc", normed_one, w_rate) + rate_bias

    def split_heads(block):
        return block.reshape(rows, heads, -1).transpose(1, 0, 2)

    logit_high = lax.reduce_precision(logits, 8, 7)
    logit_low = (logits - logit_high).astype(bf16)
    payload = jnp.concatenate(
        [split_heads(block) for block in (queries, keys_in, values_in)]
        + [split_heads(logit_high.astype(bf16)), split_heads(logit_low)], axis=2)
    got = to_owners(payload)
    query_h = got[:, :head_dim]
    key_h = got[:, head_dim : 2 * head_dim]
    value_h = got[:, 2 * head_dim : 3 * head_dim]
    logit_h = got[:, 3 * head_dim : 3 * head_dim + 1].astype(f32) + got[:, 3 * head_dim + 1 :].astype(f32)
    total = query_h.shape[0]

    def augment(block):
        lane = lax.broadcasted_iota(jnp.int32, (block.shape[0], AUG), 1)
        wide = jnp.pad(block, ((0, 0), (0, AUG - head_dim)))
        return jnp.where(lane == head_dim, jnp.ones_like(wide), wide)

    query_aug = augment(query_h)
    key_aug = augment(jnp.pad(key_h, ((0, MINI), (0, 0))))
    gain_h = lax.dynamic_slice_in_dim(inner_gain, mine, 1, 0)
    bias_h = lax.dynamic_slice_in_dim(inner_bias, mine, 1, 0)
    target = value_h.astype(f32) - key_h.astype(f32)
    base = (bias_h - target) * gain_h
    sig = jax.nn.sigmoid(logit_h)
    rate = sig / head_dim
    keep = 1.0 - sig
    start_one = jnp.pad(
        jnp.concatenate(
            [lax.dynamic_index_in_dim(init_w_one, mine, 0, False), lax.dynamic_slice_in_dim(init_b_one, mine, 1, 0)], 0),
        ((0, AUG - head_dim - 1), (0, 0)))
    start_two = lax.dynamic_index_in_dim(init_w_two, mine, 0, False).T
    start_two = start_two - jnp.mean(start_two, axis=0, keepdims=True)
    start_b_two = lax.dynamic_slice_in_dim(init_b_two, mine, 1, 0)
    start_b_two = start_b_two - jnp.mean(start_b_two)
    mixed_h, *saved = chain_forward(
        query_aug, key_aug, base, rate, start_one, start_two, start_b_two, gain_h, bias_h)
    mixed = from_owners(mixed_h, heads).transpose(1, 0, 2).reshape(rows, local_cols).astype(f32)
    totals = lax.psum((jnp.sum(mixed, axis=1), jnp.sum(mixed * mixed, axis=1)), "head")
    mean_z = totals[0][:, None] / full_width
    var_z = totals[1][:, None] / full_width - mean_z * mean_z
    inv_z = lax.rsqrt(var_z + eps_norm)
    z_hat = (mixed - mean_z) * inv_z
    post_out = z_hat * post_gain + post_bias
    gate_act = gelu_tanh(gate_pre)
    gated_low = (post_out * gate_act).astype(bf16)
    out_whole = lax.psum(bf_product("rc,cd->rd", gated_low, w_out), "head")
    resid = whole_in + out_whole
    rms_two = lax.rsqrt(jnp.mean(resid * resid, axis=1, keepdims=True) + eps_norm)
    normed_two = (resid * rms_two * ffn_gain).astype(bf16)
    gate_val = bf_product("rd,df->rf", normed_two, w_gate)
    up_val = bf_product("rd,df->rf", normed_two, w_up)
    silu_gate = jax.nn.silu(gate_val)
    hidden_ffn = (silu_gate * up_val).astype(bf16)
    down_local = lax.psum_scatter(
        bf_product("rf,fd->rd", hidden_ffn, w_down).astype(bf16), "head", scatter_dimension=1, tiled=True
    ).astype(f32)
    resid_local = lax.dynamic_slice_in_dim(resid, head_index * local_cols, local_cols, 1)
    outputs = resid_local + down_local
    grad_down_t = bf_product("rd,rf->df", grad_whole, hidden_ffn)
    grad_hidden = bf_product("rd,fd->rf", grad_whole, w_down)
    sig_gate = jax.nn.sigmoid(gate_val)
    grad_gate_val = (grad_hidden * up_val * sig_gate * (1.0 + gate_val * (1.0 - sig_gate))).astype(bf16)
    grad_up_val = (grad_hidden * silu_gate).astype(bf16)
    gate_term = bf_product("rd,rf->df", normed_two, grad_gate_val)
    up_term = bf_product("rd,rf->df", normed_two, grad_up_val)
    grad_normed_two = bf_product("rf,df->rd", grad_gate_val, w_gate) + bf_product(
        "rf,df->rd", grad_up_val, w_up
    )
    scaled_two = grad_normed_two * ffn_gain
    resid_back = rms_two * (
        scaled_two - resid * rms_two * rms_two * jnp.mean(scaled_two * resid, axis=1, keepdims=True)
    )
    gain_two_term = jnp.sum(grad_normed_two * resid * rms_two, axis=0)
    resid_sum = lax.psum(resid_back.astype(bf16), "head").astype(f32)
    grad_resid = grad_whole.astype(f32) + resid_sum
    grad_out_val = grad_resid.astype(bf16)
    grad_out_t = bf_product("rd,rc->dc", grad_out_val, gated_low)
    grad_gated = bf_product("rd,cd->rc", grad_out_val, w_out)
    grad_post = grad_gated * gate_act
    grad_gate_pre = (grad_gated * post_out * gelu_derivative(gate_pre)).astype(bf16)
    post_gain_term = jnp.sum(grad_post * z_hat, axis=0)
    post_bias_term = jnp.sum(grad_post, axis=0)
    grad_zhat = grad_post * post_gain
    sums_back = lax.psum((jnp.sum(grad_zhat, axis=1), jnp.sum(grad_zhat * z_hat, axis=1)), "head")
    grad_mixed = inv_z * (
        grad_zhat - sums_back[0][:, None] / full_width - z_hat * sums_back[1][:, None] / full_width
    )
    mixgate_term = bf_product("rd,rc->dc", normed_one, grad_gate_pre)
    early = jnp.concatenate(
        [block.astype(bf16) for block in (mixgate_term, grad_out_t, gate_term, up_term, grad_down_t)], axis=1)
    early_sum = lax.psum_scatter(early, "seq", scatter_dimension=0, tiled=True).astype(f32)
    grad_mixed_h = to_owners(split_heads(grad_mixed.astype(bf16)))
    dq_h, dk_h, dv_h, dl_h, end_one, end_two, end_b_two, end_gain, end_bias = chain_backward(
        grad_mixed_h, query_aug, key_aug, target, rate, keep, gain_h, bias_h, saved)
    dl_high = lax.reduce_precision(dl_h, 8, 7)
    back = from_owners(
        jnp.concatenate([dq_h, dk_h, dv_h, dl_high.astype(bf16), (dl_h - dl_high).astype(bf16)], axis=1), heads)

    def join_heads(lo, hi):
        return back[:, :, lo:hi].transpose(1, 0, 2).reshape(rows, -1)

    grad_q_low = join_heads(0, head_dim)
    grad_k_low = join_heads(head_dim, 2 * head_dim)
    grad_v_low = join_heads(2 * head_dim, 3 * head_dim)
    grad_logits = join_heads(3 * head_dim, 3 * head_dim + 1).astype(f32) + join_heads(
        3 * head_dim + 1, 3 * head_dim + 2).astype(f32)
    rate_bias_term = jnp.sum(grad_logits, axis=0)
    grad_logit_low = grad_logits.astype(bf16)
    query_term = bf_product("rd,rc->dc", normed_one, grad_q_low)
    key_term = bf_product("rd,rc->dc", normed_one, grad_k_low)
    value_term = bf_product("rd,rc->dc", normed_one, grad_v_low)
    rate_weight_term = bf_product("rd,rc->dc", normed_one, grad_logit_low)
    grad_normed_one = (
        bf_product("rc,dc->rd", grad_q_low, w_query)
        + bf_product("rc,dc->rd", grad_k_low, w_key)
        + bf_product("rc,dc->rd", grad_v_low, w_value)
        + bf_product("rc,dc->rd", grad_gate_pre, mix_gate)
        + bf_product("rc,dc->rd", grad_logit_low, w_rate)
    )
    scaled_one = grad_normed_one * pre_gain
    input_back = rms_one * (
        scaled_one
        - whole_in * rms_one * rms_one * jnp.mean(scaled_one * whole_in, axis=1, keepdims=True)
    )
    gain_one_term = jnp.sum(grad_normed_one * whole_in * rms_one, axis=0)
    input_local = lax.psum_scatter(
        input_back.astype(bf16), "head", scatter_dimension=1, tiled=True).astype(f32)
    grad_inputs = (
        lax.dynamic_slice_in_dim(grad_resid, head_index * local_cols, local_cols, 1) + input_local
    )
    late = jnp.concatenate([block.astype(bf16) for block in (query_term, key_term, value_term)], axis=1)
    late_sum = lax.psum_scatter(late, "seq", scatter_dimension=0, tiled=True).astype(f32)

    def place(part):
        slot = lax.broadcasted_iota(jnp.int32, (heads,) + part.shape, 0)
        return jnp.where((slot == mine) & is_owner, part[None], 0.0)

    end_one_w = place(end_one[:head_dim])
    end_two_w = place((end_two - jnp.mean(end_two, axis=0, keepdims=True)).T)
    hidden = end_one.shape[1]
    flat = jnp.concatenate(
        [end_one_w.reshape(-1), end_two_w.reshape(-1), place(end_one[head_dim]).reshape(-1),
         place(end_b_two[0] - jnp.mean(end_b_two)).reshape(-1), place(end_gain[0]).reshape(-1),
         place(end_bias[0]).reshape(-1), post_gain_term, post_bias_term, rate_weight_term.reshape(-1),
         rate_bias_term])
    flat = lax.psum(flat, "seq")
    at = 0

    def take(shape):
        nonlocal at
        size = 1
        for extent in shape:
            size *= extent
        at += size
        return flat[at - size : at].reshape(shape)

    grad_one = take((heads, head_dim, hidden))
    grad_two = take((heads, hidden, head_dim))
    grad_b_one = take((heads, hidden))
    grad_b_two = take((heads, head_dim))
    grad_gain = take((heads, head_dim))
    grad_bias = take((heads, head_dim))
    grad_post_gain = take((local_cols,))
    grad_post_bias = take((local_cols,))
    grad_rate_w = take((full_width, heads))
    grad_rate_b = take((heads,))
    gain_both = lax.psum(jnp.concatenate([gain_one_term, gain_two_term]), ("seq", "head"))
    gain_one = lax.dynamic_slice_in_dim(gain_both, head_index * local_cols, local_cols, 0)
    gain_two = gain_both[full_width:]
    ffn = gate_term.shape[1]
    return (
        outputs,
        grad_inputs,
        gain_one,
        late_sum[:, :local_cols],
        late_sum[:, local_cols : 2 * local_cols],
        late_sum[:, 2 * local_cols :],
        early_sum[:, :local_cols],
        grad_rate_w,
        grad_rate_b,
        grad_gain,
        grad_bias,
        grad_one,
        grad_b_one,
        grad_two,
        grad_b_two,
        grad_post_gain,
        grad_post_bias,
        early_sum[:, local_cols : 2 * local_cols].T,
        gain_two,
        early_sum[:, 2 * local_cols : 2 * local_cols + ffn],
        early_sum[:, 2 * local_cols + ffn : 2 * local_cols + 2 * ffn],
        early_sum[:, 2 * local_cols + 2 * ffn :].T,
    )


def solution(mesh):
    in_specs = (
        P("seq", "head"),
        P(),
        P(None, "head"),
        P(None, "head"),
        P(None, "head"),
        P(None, "head"),
        P(None, "head"),
        P("head"),
        P("head", None),
        P("head", None),
        P("head", None, None),
        P("head", None),
        P("head", None, None),
        P("head", None),
        P("head"),
        P("head"),
        P("head", None),
        P(),
        P(None, "head"),
        P(None, "head"),
        P("head", None),
        P("seq", "head"),
    )
    out_specs = (
        P("seq", "head"),
        P("seq", "head"),
        P("head"),
        P("seq", "head"),
        P("seq", "head"),
        P("seq", "head"),
        P("seq", "head"),
        P(None, "head"),
        P("head"),
        P("head", None),
        P("head", None),
        P("head", None, None),
        P("head", None),
        P("head", None, None),
        P("head", None),
        P("head"),
        P("head"),
        P("head", "seq"),
        P(),
        P("seq", "head"),
        P("seq", "head"),
        P("head", "seq"),
    )
    return jax.shard_map(local, mesh=mesh, in_specs=in_specs, out_specs=out_specs, check_vma=False)
```

```python
import functools

import jax
import jax.numpy as jnp
from jax import lax
from jax.experimental import pallas as pl
from jax.experimental.pallas import tpu as pltpu
from jax.sharding import PartitionSpec as P

MINI = 16
CHAIN = 8
FIRST = 2
AUG = 80
eps_norm = 1e-06
gelu_scale = 0.7978845608028654
f32 = jnp.float32
bf16 = jnp.bfloat16


def dot_nn(a, b):
    return lax.dot_general(a, b, (((1,), (0,)), ((), ())), preferred_element_type=f32)


def dot_nt(a, b):
    return lax.dot_general(a, b, (((1,), (1,)), ((), ())), preferred_element_type=f32)


def dot_tn(a, b):
    return lax.dot_general(a, b, (((0,), (0,)), ((), ())), preferred_element_type=f32)


def mean_row(x):
    return jnp.sum(x, axis=1, keepdims=True) * (1.0 / x.shape[1])


def gelu_first(z):
    sq = z * z
    th = jnp.tanh(gelu_scale * z * (1.0 + 0.044715 * sq))
    half = 0.5 * (1.0 + th)
    act = z * half
    der = half + (0.5 * gelu_scale) * z * (1.0 - th * th) * (1.0 + 0.134145 * sq)
    return act, der


def gelu_second(z):
    sq = z * z
    th = jnp.tanh(gelu_scale * z * (1.0 + 0.044715 * sq))
    half = 0.5 * (1.0 + th)
    act = z * half
    slope = gelu_scale * (1.0 + 0.134145 * sq)
    sech = 1.0 - th * th
    der = half + 0.5 * z * sech * slope
    curve = sech * (slope + z * (0.5 * gelu_scale * 0.26829 * z) - z * th * slope * slope)
    return act, der, curve


def tri_mask():
    rows = lax.broadcasted_iota(jnp.int32, (MINI, MINI), 0)
    cols = lax.broadcasted_iota(jnp.int32, (MINI, MINI), 1)
    return jnp.where(rows >= cols, 1.0, 0.0).astype(f32)


def inner_target_grad(z, base, gain_sq, rate):
    mz = mean_row(z)
    m_zz = mean_row(z * z)
    zg = z * gain_sq
    m_zg = mean_row(zg)
    m_zzg = mean_row(zg * z)
    m_zb = mean_row(z * base)
    m_b = mean_row(base)
    m_sq = mean_row(gain_sq)
    inv = lax.rsqrt(m_zz - mz * mz + eps_norm)
    c_zg = m_zg - mz * m_sq
    c_zzg = m_zzg - mz * (m_zg + c_zg)
    c_zb = m_zb - mz * m_b
    m_g = inv * c_zg + m_b
    m_gn = inv * (inv * c_zzg + c_zb)
    zc = z - mz
    n = zc * inv
    grad = inv * (n * (gain_sq - m_gn) + (base - m_g))
    return rate * grad, zc


def forward_step(state, z1, key_aug, key_next, query_aug, base, rate, gain, gain_sq, bias, tri):
    w1, w2t, b2 = state
    act, der = gelu_first(z1)
    act_h = act.astype(bf16)
    w1_h = w1.astype(bf16)
    w2_h = w2t.astype(bf16)
    s2, zc = inner_target_grad(dot_nt(act_h, w2_h) + b2, base, gain_sq, rate)
    s2_h = s2.astype(bf16)
    upd = dot_nn(s2_h, w2_h)
    s1_h = (upd * der).astype(bf16)
    both = jnp.concatenate([key_next, query_aug], axis=0)
    coef = dot_nt(both, key_aug)
    coef = jnp.concatenate([coef[:MINI], coef[MINI:] * tri], axis=0)
    zz = dot_nn(both, w1_h) - dot_nn(coef.astype(bf16), s1_h)
    z1_next = zz[:MINI]
    z1b = zz[MINI:]
    new_w1 = w1 - dot_tn(key_aug, s1_h)
    new_w2t = w2t - dot_tn(s2_h, act_h)
    new_b2 = b2 - jnp.sum(s2, axis=0, keepdims=True)
    actb, _ = gelu_first(z1b)
    actb_h = actb.astype(bf16)
    att = (dot_nt(actb_h, act_h) + 1.0) * tri
    z2b = dot_nt(actb_h, w2_h) + b2 - dot_nn(att.astype(bf16), s2_h)
    z2b = z2b - mean_row(z2b)
    invb = lax.rsqrt(mean_row(z2b * z2b) + eps_norm)
    out = z2b * invb * gain + bias
    return (new_w1, new_w2t, new_b2), z1_next, out, (w1_h, w2_h, upd, zc, s2, z1b, z2b)


def backward_step(carry, saved, d_out, key_aug, query_aug, target, rate, keep, gain, gain_sq, bias, tri):
    p1, p2t, p2 = carry
    w1_h, w2_h, z1, upd, zc, s2, z1b, z2b = saved
    act, der, curve = gelu_second(z1)
    act_h = act.astype(bf16)
    actb, derb = gelu_first(z1b)
    actb_h = actb.astype(bf16)
    s2_h = s2.astype(bf16)
    s1_h = (upd * der).astype(bf16)
    p1_h = p1.astype(bf16)
    p2_h = p2t.astype(bf16)
    invb = lax.rsqrt(mean_row(z2b * z2b) + eps_norm)
    nb = z2b * invb
    dn = d_out * gain
    d_z2b = invb * (dn - mean_row(dn) - nb * mean_row(dn * nb))
    d_z2b_h = d_z2b.astype(bf16)
    d_att2 = (-dot_nt(d_z2b_h, s2_h) * tri).astype(bf16)
    d_actb = dot_nn(d_z2b_h, w2_h) + dot_nn(d_att2, act_h)
    d_z1b_h = (d_actb * derb).astype(bf16)
    att2 = ((dot_nt(actb_h, act_h) + 1.0) * tri).astype(bf16)
    att1 = (dot_nt(query_aug, key_aug) * tri).astype(bf16)
    c2 = dot_tn(att2, d_z2b_h)
    c3 = dot_tn(d_att2, actb_h)
    c1 = dot_tn(att1, d_z1b_h)
    d_att1 = (-dot_nt(d_z1b_h, s1_h) * tri).astype(bf16)
    d_query = dot_nt(d_z1b_h, w1_h) + dot_nn(d_att1, key_aug)
    d_key = dot_tn(d_att1, query_aug)
    d_s1 = -c1 - dot_nn(key_aug, p1_h)
    d_upd = d_s1 * der
    d_upd_h = d_upd.astype(bf16)
    d_s2 = dot_nt(d_upd_h, w2_h) - c2 - dot_nt(act_h, p2_h) - p2
    h = rate * d_s2
    inv = lax.rsqrt(mean_row(zc * zc) + eps_norm)
    n = zc * inv
    base = (bias - target) * gain
    big_g = n * gain_sq + base
    m_g = mean_row(big_g)
    m_gn = mean_row(big_g * n)
    m_sq = mean_row(gain_sq)
    ng = n * gain_sq
    m_ng = mean_row(ng)
    m_nng = mean_row(n * ng)
    g = inv * (big_g - m_g - n * m_gn)
    a1 = mean_row(h)
    a2 = mean_row(h * n)
    a3 = mean_row(h * gain_sq)
    a4 = mean_row(h * ng)
    a5 = mean_row(h * g)
    proj = h - a1 - n * a2
    d_g = inv * proj
    dnn = inv * (proj * gain_sq - h * m_gn - big_g * a2)
    m_dn = inv * (a3 - a1 * (m_sq + m_gn) - a2 * (m_ng + m_g))
    m_dnn = inv * (a4 - a1 * m_ng - a2 * (m_nng + 2.0 * m_gn))
    d_zc = inv * (dnn - m_dn - n * (m_dnn + a5))
    d_zc_h = d_zc.astype(bf16)
    d_act = dot_nn(d_zc_h, w2_h) + c3 - dot_nn(s2_h, p2_h)
    d_z1 = d_act * der + d_s1 * upd * curve
    d_z1_h = d_z1.astype(bf16)
    d_gg = d_g * gain
    d_key = d_key + dot_nt(d_z1_h, w1_h) - dot_nt(s1_h, p1_h)
    d_key = d_key[:, : gain.shape[1]] + d_gg
    d_query = d_query[:, : gain.shape[1]] + d_out
    d_value = -d_gg
    d_logit = keep * jnp.sum(d_s2 * s2, axis=1, keepdims=True)
    new_p1 = p1 + dot_tn(
        jnp.concatenate([key_aug, query_aug], axis=0), jnp.concatenate([d_z1_h, d_z1b_h], axis=0)
    )
    new_p2t = p2t + dot_tn(
        jnp.concatenate([s2_h, d_zc_h, d_z2b_h], axis=0),
        jnp.concatenate([d_upd_h, act_h, actb_h], axis=0),
    )
    new_p2 = p2 + jnp.sum(d_zc + d_z2b, axis=0, keepdims=True)
    d_bias = jnp.sum(d_out + d_gg, axis=0, keepdims=True)
    d_gain = jnp.sum(d_out * nb + d_g * (2.0 * n * gain + bias - target), axis=0, keepdims=True)
    return (new_p1, new_p2t, new_p2), (d_query, d_key, d_value, d_logit), d_gain, d_bias


MESH = pl.DeviceIdType.MESH
PACK = 256
ENDS = 160


def seq_place():
    index = lax.axis_index("seq")
    pos = lax.rem(index, CHAIN)
    return pos, index - pos


def meet_group(pos, base):
    barrier = pltpu.get_barrier_semaphore()
    for d in range(1, CHAIN):
        pl.semaphore_signal(
            barrier, inc=1, device_id={"seq": base + lax.rem(pos + d, CHAIN)}, device_id_type=MESH)
    pl.semaphore_wait(barrier, CHAIN - 1)


def push(src, dst, send_sem, recv_sem, target):
    return pltpu.make_async_remote_copy(
        src_ref=src, dst_ref=dst, send_sem=send_sem, recv_sem=recv_sem,
        device_id={"seq": target}, device_id_type=MESH)


def await_bytes(ref, sem):
    pltpu.make_async_copy(ref, ref, sem).wait()


def swap_start(src, dst, send, recv, local_sem, pos, base):
    for d in range(1, CHAIN):
        peer = lax.rem(pos + d, CHAIN)
        push(src.at[peer], dst.at[pos], send.at[d - 1], recv.at[d - 1], base + peer).start()
    pltpu.make_async_copy(src.at[pos], dst.at[pos], local_sem).start()


def swap_wait(src, dst, send, recv, local_sem, pos, base):
    for d in range(1, CHAIN):
        peer = lax.rem(pos + d, CHAIN)
        origin = lax.rem(pos + CHAIN - d, CHAIN)
        push(src.at[peer], dst.at[pos], send.at[d - 1], recv.at[d - 1], base + peer).wait_send()
        await_bytes(dst.at[origin], recv.at[d - 1])
    await_bytes(dst.at[pos], local_sem)


def fwd_kernel(block, unroll, heads, pay_ref, w1_in, b1_in, w2_in, b2_in, gain_in, bias_in,
               mixed_ref, k_out, q_out, aux_out, w1s_ref, w2s_ref, z1s_ref, upd_ref, zc_ref, s2_ref, z1b_ref, z2b_ref,
               got, k_all, q_all, base_all, aux_all, mixed_all, w1, w2t, b2, z1,
               pay_send, pay_recv, mix_send, mix_recv):
    blk = pl.program_id(0)
    last = pl.num_programs(0) - 1
    pos, base = seq_place()
    width = gain_in.shape[1]
    hidden = w1.shape[1]
    rows_each = pay_ref.shape[0]
    per = rows_each // block
    owner = (pos >= FIRST) & (pos < FIRST + heads)
    mine = jnp.clip(pos - FIRST, 0, heads - 1)
    gain = gain_in[pl.ds(mine, 1), :]
    bias = bias_in[pl.ds(mine, 1), :]
    gain_sq = gain * gain
    tri = tri_mask()

    @pl.when(blk == 0)
    def _():
        meet_group(pos, base)
        for j in range(heads):
            src = pay_ref.at[:, pl.ds(j * PACK, PACK)]
            dst = got.at[pos]

            @pl.when(pos != FIRST + j)
            def _():
                push(src, dst, pay_send.at[j], pay_recv.at[pos], base + FIRST + j).start()

            @pl.when(pos == FIRST + j)
            def _():
                pltpu.make_async_copy(src, dst, pay_recv.at[pos]).start()

    def take_in(p):
        await_bytes(got.at[p], pay_recv.at[p])
        part = got[p]
        rows = pl.ds(pl.multiple_of(p * rows_each, rows_each), rows_each)
        lane = lax.broadcasted_iota(jnp.int32, (rows_each, AUG), 1)
        one = jnp.ones((), bf16)
        zero = jnp.zeros((), bf16)
        tail = jnp.where(lane == width, one, zero)
        query = part[:, :AUG]
        key = part[:, width : width + AUG]
        q_all[rows, :] = jnp.where(lane < width, query, tail)
        k_all[rows, :] = jnp.where(lane < width, key, tail)
        key_f = part[:, width : 2 * width].astype(f32)
        target = part[:, 2 * width : 3 * width].astype(f32) - key_f
        logit = part[:, 3 * width : 3 * width + 1].astype(f32) + part[:, 3 * width + 1 : 3 * width + 2].astype(f32)
        sig = 1.0 / (1.0 + jnp.exp(-logit))
        base_all[rows, :] = (bias - target) * gain
        spot = lax.broadcasted_iota(jnp.int32, (rows_each, 2 * width), 1)
        wide = jnp.concatenate([target, target], axis=1)
        aux_all[rows, :] = jnp.where(
            spot < width, wide, jnp.where(spot == width, sig * (1.0 / width), 1.0 - sig))

    def send_mixed(b):
        p = lax.div(b, per)
        src = mixed_all.at[pl.ds(pl.multiple_of(b * block, block), block), :]
        dst = mixed_ref.at[mine, pl.ds(pl.multiple_of(lax.rem(b, per) * block, block), block), :]

        @pl.when(p != pos)
        def _():
            push(src, dst, mix_send, mix_recv.at[mine], base + p).start()

        @pl.when(p == pos)
        def _():
            pltpu.make_async_copy(src, dst, mix_recv.at[mine]).start()

    @pl.when(owner)
    def _():
        @pl.when(blk == 0)
        def _():
            row = lax.broadcasted_iota(jnp.int32, (AUG - width, hidden), 0)
            w1[pl.ds(0, width), :] = w1_in[mine]
            w1[pl.ds(width, AUG - width), :] = jnp.where(row == 0, b1_in[pl.ds(mine, 1), :], 0.0)
            turned = w2_in[mine].T
            w2t[...] = turned - jnp.mean(turned, axis=0, keepdims=True)
            start = b2_in[pl.ds(mine, 1), :]
            b2[...] = start - mean_row(start)
            k_all[pl.ds(CHAIN * rows_each, MINI), :] = jnp.zeros((MINI, AUG), bf16)
            take_in(0)
            z1[...] = dot_nn(k_all[0:MINI, :], w1[...].astype(bf16))

        @pl.when((lax.rem(blk, per) == 0) & (blk < last + 1 - per))
        def _():
            take_in(lax.div(blk, per) + 1)

        @pl.when(blk > 0)
        def _():
            send_mixed(blk - 1)

        brows = pl.ds(pl.multiple_of(blk * block, block), block)
        k_out[...] = k_all[brows, :]
        q_out[...] = q_all[brows, :]
        aux_out[...] = aux_all[brows, :]

        def group(it, _):
            for u in range(unroll):
                loc = it * unroll + u
                row = pl.multiple_of(blk * block + loc * MINI, MINI)
                rows = pl.ds(row, MINI)
                lrows = pl.ds(pl.multiple_of(loc * MINI, MINI), MINI)
                q_aug = q_all[rows, :]
                z1_now = z1[...]
                state, z1_next, out, saved = forward_step(
                    (w1[...], w2t[...], b2[...]), z1_now, k_all[rows, :], k_all[pl.ds(row + MINI, MINI), :], q_aug,
                    base_all[rows, :], aux_all[rows, width : width + 1], gain, gain_sq, bias, tri)
                w1[...], w2t[...], b2[...] = state
                z1[...] = z1_next
                mixed_all[rows, :] = (out + q_aug[:, :width].astype(f32)).astype(bf16)
                w1s_ref[loc], w2s_ref[loc], upd, zc, s2, z1b, z2b = saved
                z1s_ref[lrows, :] = z1_now
                upd_ref[lrows, :] = upd
                zc_ref[lrows, :] = zc
                s2_ref[lrows, :] = s2
                z1b_ref[lrows, :] = z1b
                z2b_ref[lrows, :] = z2b
            return 0

        lax.fori_loop(0, block // MINI // unroll, group, 0)

    @pl.when(blk == last)
    def _():
        @pl.when(owner)
        def _():
            send_mixed(last)
            others = mixed_all.at[pl.ds(0, (CHAIN - 1) * rows_each), :]
            await_bytes(others, mix_send)

        for j in range(heads):
            @pl.when(pos != FIRST + j)
            def _():
                await_bytes(got.at[pos], pay_send.at[j])

            await_bytes(mixed_ref.at[j], mix_recv.at[j])


def chain_forward(payload, w1, b1, w2, b2, gain, bias, block=128, unroll=8):
    rows = payload.shape[0]
    heads, width, hidden = w1.shape
    tokens = rows * CHAIN
    steps = tokens // MINI
    nb = block // MINI
    whole = lambda a: pl.BlockSpec(a.shape, lambda i: (0,) * a.ndim)
    rowblk = lambda w: pl.BlockSpec((block, w), lambda i: (i, 0))
    stepblk = lambda r: pl.BlockSpec((nb, r, hidden), lambda i: (i, 0, 0))
    anywhere = pl.BlockSpec(memory_space=pl.ANY)
    small = (w1, b1, w2, b2, gain, bias)
    dma = pltpu.SemaphoreType.DMA
    wide = jax.ShapeDtypeStruct((tokens, hidden), f32)
    narrow = jax.ShapeDtypeStruct((tokens, width), f32)
    return pl.pallas_call(
        functools.partial(fwd_kernel, block, unroll, heads),
        grid=(tokens // block,),
        in_specs=[anywhere] + [whole(a) for a in small],
        out_specs=[anywhere, rowblk(AUG), rowblk(AUG), rowblk(2 * width), stepblk(AUG), stepblk(width),
                   rowblk(hidden), rowblk(hidden), rowblk(width), rowblk(width), rowblk(hidden), rowblk(width)],
        out_shape=[jax.ShapeDtypeStruct((heads, rows, width), bf16),
                   jax.ShapeDtypeStruct((tokens, AUG), bf16),
                   jax.ShapeDtypeStruct((tokens, AUG), bf16),
                   jax.ShapeDtypeStruct((tokens, 2 * width), f32),
                   jax.ShapeDtypeStruct((steps, AUG, hidden), bf16),
                   jax.ShapeDtypeStruct((steps, width, hidden), bf16),
                   wide, wide, narrow, narrow, wide, narrow],
        scratch_shapes=[pltpu.VMEM((CHAIN, rows, PACK), bf16),
                        pltpu.VMEM((tokens + MINI, AUG), bf16), pltpu.VMEM((tokens, AUG), bf16),
                        pltpu.VMEM((tokens, width), f32), pltpu.VMEM((tokens, 2 * width), f32),
                        pltpu.VMEM((tokens, width), bf16),
                        pltpu.VMEM((AUG, hidden), f32), pltpu.VMEM((width, hidden), f32),
                        pltpu.VMEM((1, width), f32), pltpu.VMEM((MINI, hidden), f32),
                        dma((heads,)), dma((CHAIN,)), dma, dma((heads,))],
        compiler_params=pltpu.CompilerParams(collective_id=0, has_side_effects=True),
        name="inner_forward",
    )(payload, *small)


def bwd_kernel(block, unroll, heads, gm_ref, early_ref, norm_ref, gain_in, bias_in,
               k_ref, q_ref, aux_ref, w1s_ref, w2s_ref, z1s_ref, upd_ref, zc_ref, s2_ref, z1b_ref, z2b_ref,
               grads_ref, ends_ref, early_out, norm_out,
               dout, early_got, packed, ends, p1, p2t, p2, dg, db,
               gm_send, gm_recv, ea_send, ea_recv, ea_loc, no_send, no_recv, no_loc, bc_send, bc_recv, en_send, en_recv):
    pid = pl.program_id(0)
    last = pl.num_programs(0) - 1
    blk = last - pid
    pos, base = seq_place()
    width = gain_in.shape[1]
    rows_each = gm_ref.shape[1]
    per = rows_each // block
    owner = (pos >= FIRST) & (pos < FIRST + heads)
    mine = jnp.clip(pos - FIRST, 0, heads - 1)
    gain = gain_in[pl.ds(mine, 1), :]
    bias = bias_in[pl.ds(mine, 1), :]
    gain_sq = gain * gain
    tri = tri_mask()
    count = block // MINI

    @pl.when(pid == 0)
    def _():
        meet_group(pos, base)
        for j in range(heads):
            @pl.when(pos != FIRST + j)
            def _():
                push(gm_ref.at[j], dout.at[pos], gm_send.at[j], gm_recv.at[pos], base + FIRST + j).start()

            @pl.when(pos == FIRST + j)
            def _():
                pltpu.make_async_copy(gm_ref.at[j], dout.at[pos], gm_recv.at[pos]).start()

        swap_start(early_ref, early_got, ea_send, ea_recv, ea_loc, pos, base)
        swap_start(norm_ref, norm_out, no_send, no_recv, no_loc, pos, base)

    def share_block(b):
        rows = pl.ds(pl.multiple_of(b * block, block), block)
        for d in range(1, CHAIN):
            push(packed.at[rows, :], grads_ref.at[mine, rows, :], bc_send.at[d - 1], bc_recv.at[mine],
                 base + lax.rem(pos + d, CHAIN)).start()
        pltpu.make_async_copy(packed.at[rows, :], grads_ref.at[mine, rows, :], bc_recv.at[mine]).start()

    @pl.when(owner)
    def _():
        @pl.when(pid == 0)
        def _():
            for r in (p1, p2t, p2, dg, db):
                r[...] = jnp.zeros_like(r)

        @pl.when(lax.rem(pid, per) == 0)
        def _():
            p = lax.div(blk, per)
            await_bytes(dout.at[p], gm_recv.at[p])

        @pl.when(pid > 0)
        def _():
            share_block(blk + 1)

        def group(it, _):
            for u in range(unroll):
                loc = count - 1 - (it * unroll + u)
                row = pl.multiple_of(blk * block + loc * MINI, MINI)
                lr = pl.ds(pl.multiple_of(loc * MINI, MINI), MINI)
                inner = pl.ds(pl.multiple_of(lax.rem(blk, per) * block + loc * MINI, MINI), MINI)
                saved = (w1s_ref[loc], w2s_ref[loc], z1s_ref[lr, :], upd_ref[lr, :], zc_ref[lr, :], s2_ref[lr, :],
                         z1b_ref[lr, :], z2b_ref[lr, :])
                aux = aux_ref[lr, :]
                carry, outs, dgn, dbn = backward_step(
                    (p1[...], p2t[...], p2[...]), saved, dout[lax.div(blk, per), inner, :].astype(f32), k_ref[lr, :],
                    q_ref[lr, :], aux[:, :width], aux[:, width : width + 1], aux[:, width + 1 : width + 2],
                    gain, gain_sq, bias, tri)
                p1[...], p2t[...], p2[...] = carry
                dg[...] += dgn
                db[...] += dbn
                d_query, d_key, d_value, d_logit = outs
                high = d_logit.astype(bf16).astype(f32)
                lane = lax.broadcasted_iota(jnp.int32, (MINI, width), 1)
                extra = jnp.where(lane == 0, high, jnp.where(lane == 1, d_logit - high, 0.0))
                packed[pl.ds(row, MINI), :] = jnp.concatenate([d_query, d_key, d_value, extra], axis=1).astype(bf16)
            return 0

        lax.fori_loop(0, count // unroll, group, 0)

        @pl.when(pid == last)
        def _():
            ends[pl.ds(0, AUG), :] = p1[...].astype(bf16)
            ends[pl.ds(AUG, width), :] = p2t[...].astype(bf16)
            rest = ENDS - AUG - width
            row = lax.broadcasted_iota(jnp.int32, (rest, width), 0)
            tailing = jnp.where(row == 0, p2[...], jnp.where(row == 1, dg[...], jnp.where(row == 2, db[...], 0.0)))
            ends[pl.ds(AUG + width, rest), :] = jnp.concatenate([tailing] * 4, axis=1).astype(bf16)
            share_block(0)
            for d in range(1, CHAIN):
                push(ends, ends_ref.at[mine], en_send.at[d - 1], en_recv.at[mine],
                     base + lax.rem(pos + d, CHAIN)).start()
            pltpu.make_async_copy(ends, ends_ref.at[mine], en_recv.at[mine]).start()

    @pl.when(pid == last)
    def _():
        swap_wait(early_ref, early_got, ea_send, ea_recv, ea_loc, pos, base)
        swap_wait(norm_ref, norm_out, no_send, no_recv, no_loc, pos, base)

        def add_up(c, _):
            rows = pl.ds(pl.multiple_of(c * MINI, MINI), MINI)
            acc = early_got[0, rows, :].astype(f32)
            for p in range(1, CHAIN):
                acc = acc + early_got[p, rows, :].astype(f32)
            early_out[rows, :] = acc
            return 0

        lax.fori_loop(0, early_out.shape[0] // MINI, add_up, 0)
        for j in range(heads):
            @pl.when(pos != FIRST + j)
            def _():
                await_bytes(dout.at[pos], gm_send.at[j])

            await_bytes(grads_ref.at[j], bc_recv.at[j])
            await_bytes(ends_ref.at[j], en_recv.at[j])

        @pl.when(owner)
        def _():
            for d in range(1, CHAIN):
                await_bytes(packed, bc_send.at[d - 1])
                await_bytes(ends, en_send.at[d - 1])


def chain_backward(grad_mixed, early, normed, gain, bias, saved, block=128, unroll=4):
    heads, rows, width = grad_mixed.shape
    tokens = rows * CHAIN
    hidden = saved[5].shape[1]
    nblk = tokens // block
    nb = block // MINI
    whole = lambda a: pl.BlockSpec(a.shape, lambda i: (0,) * a.ndim)
    rowblk = lambda w: pl.BlockSpec((block, w), lambda i: (nblk - 1 - i, 0))
    stepblk = lambda r: pl.BlockSpec((nb, r, hidden), lambda i: (nblk - 1 - i, 0, 0))
    anywhere = pl.BlockSpec(memory_space=pl.ANY)
    dma = pltpu.SemaphoreType.DMA
    seven = dma((CHAIN - 1,))
    share = early.shape[1:]
    return pl.pallas_call(
        functools.partial(bwd_kernel, block, unroll, heads),
        grid=(nblk,),
        in_specs=[anywhere] * 3 + [whole(gain), whole(bias), rowblk(AUG), rowblk(AUG), rowblk(2 * width),
                                   stepblk(AUG), stepblk(width), rowblk(hidden), rowblk(hidden), rowblk(width),
                                   rowblk(width), rowblk(hidden), rowblk(width)],
        out_specs=[anywhere, anywhere, pl.BlockSpec(share, lambda i: (0, 0)), anywhere],
        out_shape=[jax.ShapeDtypeStruct((heads, tokens, PACK), bf16),
                   jax.ShapeDtypeStruct((heads, ENDS, hidden), bf16),
                   jax.ShapeDtypeStruct(share, f32),
                   jax.ShapeDtypeStruct(normed.shape, bf16)],
        scratch_shapes=[pltpu.VMEM((CHAIN, rows, width), bf16), pltpu.VMEM(early.shape, bf16),
                        pltpu.VMEM((tokens, PACK), bf16), pltpu.VMEM((ENDS, hidden), bf16),
                        pltpu.VMEM((AUG, hidden), f32), pltpu.VMEM((width, hidden), f32), pltpu.VMEM((1, width), f32),
                        pltpu.VMEM((1, width), f32), pltpu.VMEM((1, width), f32),
                        dma((heads,)), dma((CHAIN,)), seven, seven, dma, seven, seven, dma,
                        seven, dma((heads,)), seven, dma((heads,))],
        compiler_params=pltpu.CompilerParams(collective_id=1, has_side_effects=True),
        name="inner_backward",
    )(grad_mixed, early, normed, gain, bias, *saved)


def head_place():
    return lax.axis_index("head"), lax.axis_size("head")


def meet_heads(me, count):
    barrier = pltpu.get_barrier_semaphore()
    for d in range(1, count):
        pl.semaphore_signal(barrier, inc=1, device_id={"head": lax.rem(me + d, count)}, device_id_type=MESH)
    pl.semaphore_wait(barrier, count - 1)


def push_head(src, dst, send_sem, recv_sem, target):
    return pltpu.make_async_remote_copy(
        src_ref=src, dst_ref=dst, send_sem=send_sem, recv_sem=recv_sem,
        device_id={"head": target}, device_id_type=MESH)


def row_totals(first, second):
    ones = jnp.ones((8, first.shape[1]), f32)

    def total(x):
        return lax.dot_general(ones, x, (((1,), (1,)), ((), ())), precision=lax.Precision.HIGHEST,
                               preferred_element_type=f32)

    top, low = total(first), total(second)
    row = lax.broadcasted_iota(jnp.int32, top.shape, 0)
    return jnp.where(row == 0, top, low)


def mid_kernel(count, mixed_ref, x_ref, ct_ref, gate_pre_ref, normed_ref, w_out_ref, w_gate_ref, w_up_ref, w_down_ref,
               post_gain_ref, post_bias_ref, ffn_gain_ref,
               gm_ref, early_ref, ggp_ref, out_ref, grc_ref, small_ref,
               st_mine, st_got, pa_mine, pa_got, nt_all, rc_mine, rc_all, gn_mine, gn_got, dn_mine, dn_got, gov_all,
               gc_mine, gc_all, sb_mine, sb_got, gt_mine, gt_got, gh, gated, hidden, ggv, guv, resid,
               st_s, st_r, pa_s, pa_r, nt_s, nt_r, rc_s, rc_r, gn_s, gn_r, dn_s, dn_r, go_s, go_r, gc_s, gc_r, sb_s, sb_r,
               gt_s, gt_r):
    me, _ = head_place()
    heads, rows, width = mixed_ref.shape
    cols = heads * width
    full = cols * count
    part = rows // count
    peers = [(d, lax.rem(me + d, count)) for d in range(1, count)]
    meet_heads(me, count)

    def rows_of(device):
        return pl.ds(pl.multiple_of(device * part, part), part)

    def send_all(src, dst, send, recv):
        for d, peer in peers:
            push_head(src, dst.at[d - 1], send.at[d - 1], recv.at[d - 1], peer).start()

    def wait_all(src, dst, send, recv):
        for d, peer in peers:
            push_head(src, dst.at[d - 1], send.at[d - 1], recv.at[d - 1], peer).wait()

    z = jnp.concatenate([mixed_ref[j] for j in range(heads)], axis=1).astype(f32)
    st_mine[...] = row_totals(z, z * z)
    send_all(st_mine, st_got, st_s, st_r)
    gate_pre = gate_pre_ref[...]
    gate_act, gate_der = gelu_first(gate_pre)
    gh[...] = dot_nt(ct_ref[...], w_down_ref[...])
    wait_all(st_mine, st_got, st_s, st_r)
    tot = st_mine[...]
    for d, _ in peers:
        tot = tot + st_got[d - 1]
    tot = tot.T * (1.0 / full)
    mean_z = tot[:, 0:1]
    inv_z = lax.rsqrt(tot[:, 1:2] - mean_z * mean_z + eps_norm)
    z_hat = (z - mean_z) * inv_z
    post_out = z_hat * post_gain_ref[...] + post_bias_ref[...]
    gated[...] = (post_out * gate_act).astype(bf16)

    def spread_rows(make, mine, got, send, recv):
        pending = None
        for d, peer in peers:
            mine[d - 1] = make(rows_of(peer)).astype(bf16)
            if pending is not None:
                pending.start()
            pending = push_head(mine.at[d - 1], got.at[d - 1], send.at[d - 1], recv.at[d - 1], peer)
        own = make(rows_of(me))
        pending.start()
        return own

    def add_rows(own, mine, got, send, recv):
        for d, peer in peers:
            push_head(mine.at[d - 1], got.at[d - 1], send.at[d - 1], recv.at[d - 1], peer).wait()
            own = own + got[d - 1].astype(f32)
        return own

    def gather_rows(all_ref, send, recv):
        for d, peer in peers:
            view = all_ref.at[rows_of(me), :]
            push_head(view, view, send.at[d - 1], recv.at[d - 1], peer).start()

    def gather_wait(all_ref, send, recv):
        for d, peer in peers:
            view = all_ref.at[rows_of(me), :]
            push_head(view, view, send.at[d - 1], recv.at[d - 1], peer).wait_send()
            await_bytes(all_ref.at[rows_of(lax.rem(me + count - d, count)), :], recv.at[d - 1])

    def turn_columns(value, mine, all_ref, send, recv):
        for b in range(count):
            mine[b] = value[:, b * cols : (b + 1) * cols]
        all_ref[rows_of(me), :] = mine[me]

    def turn_start(mine, all_ref, send, recv):
        for d, peer in peers:
            push_head(mine.at[peer], all_ref.at[rows_of(me), :], send.at[d - 1], recv.at[d - 1], peer).start()

    def turn_wait(mine, all_ref, send, recv):
        for d, peer in peers:
            push_head(mine.at[peer], all_ref.at[rows_of(me), :], send.at[d - 1], recv.at[d - 1], peer).wait_send()
            await_bytes(all_ref.at[rows_of(lax.rem(me + count - d, count)), :], recv.at[d - 1])

    w_out = w_out_ref[...]
    own = spread_rows(lambda r: dot_nn(gated[r, :], w_out), pa_mine, pa_got, pa_s, pa_r)
    res = x_ref[rows_of(me), :].astype(f32) + add_rows(own, pa_mine, pa_got, pa_s, pa_r)
    rms_two = lax.rsqrt(mean_row(res * res) + eps_norm)
    ffn_gain = ffn_gain_ref[...]
    nt_all[rows_of(me), :] = (res * rms_two * ffn_gain).astype(bf16)
    turn_columns(res, rc_mine, rc_all, rc_s, rc_r)
    resid[...] = res
    gather_rows(nt_all, nt_s, nt_r)
    turn_start(rc_mine, rc_all, rc_s, rc_r)
    gather_wait(nt_all, nt_s, nt_r)
    def forward_rows(b, _):
        r = pl.ds(pl.multiple_of(b * part, part), part)
        nt = nt_all[r, :]
        gate_val = dot_nn(nt, w_gate_ref[...])
        up_val = dot_nn(nt, w_up_ref[...])
        sig = 1.0 / (1.0 + jnp.exp(-gate_val))
        silu = gate_val * sig
        hidden[r, :] = (silu * up_val).astype(bf16)
        g = gh[r, :]
        ggv[r, :] = (g * up_val * sig * (1.0 + gate_val * (1.0 - sig))).astype(bf16)
        guv[r, :] = (g * silu).astype(bf16)
        return 0

    lax.fori_loop(0, count, forward_rows, 0)
    own = spread_rows(lambda r: dot_nt(ggv[r, :], w_gate_ref[...]) + dot_nt(guv[r, :], w_up_ref[...]),
                      gn_mine, gn_got, gn_s, gn_r)
    for b in range(count):
        r = pl.ds(b * part, part)
        down = dot_nn(hidden[r, :], w_down_ref[...]).astype(bf16)
        for c in range(count):
            dn_mine[c, r, :] = down[:, c * cols : (c + 1) * cols]
    ffn = w_gate_ref.shape[1]
    half = full // 2
    for b in range(2):
        r = slice(b * half, (b + 1) * half)
        early_ref[r, 0:ffn] = dot_tn(nt_all[:, r], ggv[...]).astype(bf16)
    for d, peer in peers:
        push_head(dn_mine.at[peer], dn_got.at[d - 1], dn_s.at[d - 1], dn_r.at[d - 1], peer).start()
    gnt = add_rows(own, gn_mine, gn_got, gn_s, gn_r)
    res = resid[...]
    rms_two = lax.rsqrt(mean_row(res * res) + eps_norm)
    scaled = gnt * ffn_gain
    grad_res = ct_ref[rows_of(me), :].astype(f32) + rms_two * (
        scaled - res * rms_two * rms_two * mean_row(scaled * res))
    gov_all[rows_of(me), :] = grad_res.astype(bf16)
    gt_mine[...] = jnp.broadcast_to(jnp.sum(gnt * res * rms_two, axis=0, keepdims=True), gt_mine.shape)
    turn_columns(grad_res, gc_mine, gc_all, gc_s, gc_r)
    gather_rows(gov_all, go_s, go_r)
    turn_start(gc_mine, gc_all, gc_s, gc_r)
    send_all(gt_mine, gt_got, gt_s, gt_r)
    for b in range(2):
        r = slice(b * half, (b + 1) * half)
        early_ref[r, ffn : 2 * ffn] = dot_tn(nt_all[:, r], guv[...]).astype(bf16)
    gather_wait(gov_all, go_s, go_r)
    gov = gov_all[...]
    grad_gated = dot_nt(gov, w_out_ref[...])
    grad_post = grad_gated * gate_act
    grad_zhat = grad_post * post_gain_ref[...]
    sb_mine[...] = row_totals(grad_zhat, grad_zhat * z_hat)
    ggp = (grad_gated * post_out * gate_der).astype(bf16)
    ggp_ref[...] = ggp
    send_all(sb_mine, sb_got, sb_s, sb_r)
    early_ref[:, 3 * ffn : 3 * ffn + 2 * cols] = jnp.concatenate(
        [dot_tn(normed_ref[...], ggp).astype(bf16), dot_tn(gov, gated[...]).astype(bf16)], axis=1)
    row = lax.broadcasted_iota(jnp.int32, (8, cols), 0)
    wait_all(sb_mine, sb_got, sb_s, sb_r)
    tot = sb_mine[...]
    for d, _ in peers:
        tot = tot + sb_got[d - 1]
    tot = tot.T * (1.0 / full)
    grad_mixed = (inv_z * (grad_zhat - tot[:, 0:1] - z_hat * tot[:, 1:2])).astype(bf16)
    for j in range(heads):
        gm_ref[j] = grad_mixed[:, j * width : (j + 1) * width]
    for b in range(2):
        r = slice(b * half, (b + 1) * half)
        early_ref[r, 2 * ffn : 3 * ffn] = dot_tn(ct_ref[:, r], hidden[...]).astype(bf16)
    turn_wait(rc_mine, rc_all, rc_s, rc_r)
    out = rc_all[...] + dn_mine[me].astype(f32)
    for d, peer in peers:
        push_head(dn_mine.at[peer], dn_got.at[d - 1], dn_s.at[d - 1], dn_r.at[d - 1], peer).wait()
        out = out + dn_got[d - 1].astype(f32)
    out_ref[...] = out
    turn_wait(gc_mine, gc_all, gc_s, gc_r)
    grc_ref[...] = gc_all[...]
    wait_all(gt_mine, gt_got, gt_s, gt_r)
    gain_two = gt_mine[...]
    for d, _ in peers:
        gain_two = gain_two + gt_got[d - 1]
    post = jnp.where(row == 1, jnp.sum(grad_post * z_hat, axis=0, keepdims=True),
                     jnp.sum(grad_post, axis=0, keepdims=True))
    line = lax.broadcasted_iota(jnp.int32, (8, full), 0)
    small_ref[...] = jnp.where(
        line == 0, gain_two, jnp.concatenate([post] + [jnp.zeros_like(post)] * (count - 1), axis=1))


def middle(mixed, x, ct, gate_pre, normed, w_out, w_gate, w_up, w_down, post_gain, post_bias, ffn_gain):
    count = lax.axis_size("head")
    heads, rows, width = mixed.shape
    cols = heads * width
    full = cols * count
    part = rows // count
    ffn = w_gate.shape[1]
    ins = (mixed, x, ct, gate_pre, normed, w_out, w_gate, w_up, w_down, post_gain, post_bias, ffn_gain)
    vmem = pl.BlockSpec(memory_space=pltpu.VMEM)
    V = pltpu.VMEM
    trio = count - 1
    sem = pltpu.SemaphoreType.DMA((trio,))
    return pl.pallas_call(
        functools.partial(mid_kernel, count),
        in_specs=[vmem] * len(ins),
        out_specs=[vmem] * 6,
        out_shape=[jax.ShapeDtypeStruct((heads, rows, width), bf16),
                   jax.ShapeDtypeStruct((full, 3 * ffn + 2 * cols), bf16),
                   jax.ShapeDtypeStruct((rows, cols), bf16),
                   jax.ShapeDtypeStruct((rows, cols), f32),
                   jax.ShapeDtypeStruct((rows, cols), f32),
                   jax.ShapeDtypeStruct((8, full), f32)],
        scratch_shapes=[
            V((8, rows), f32), V((trio, 8, rows), f32),
            V((trio, part, full), bf16), V((trio, part, full), bf16),
            V((rows, full), bf16),
            V((count, part, cols), f32), V((rows, cols), f32),
            V((trio, part, full), bf16), V((trio, part, full), bf16),
            V((count, rows, cols), bf16), V((trio, rows, cols), bf16),
            V((rows, full), bf16),
            V((count, part, cols), f32), V((rows, cols), f32),
            V((8, rows), f32), V((trio, 8, rows), f32),
            V((8, full), f32), V((trio, 8, full), f32),
            V((rows, ffn), f32), V((rows, cols), bf16),
            V((rows, ffn), bf16), V((rows, ffn), bf16), V((rows, ffn), bf16),
            V((part, full), f32)] + [sem] * 20,
        compiler_params=pltpu.CompilerParams(
            collective_id=2, has_side_effects=True, vmem_limit_bytes=56 * 1024 * 1024),
        name="middle",
    )(*ins)


def stretch_groups(axis):
    count = lax.axis_size(axis)
    return [[start + step for step in range(0, count, CHAIN)] for start in range(CHAIN)]


def bf_product(form, left, right):
    return jnp.einsum(form, left, right, preferred_element_type=f32)


def local(
    inputs,
    pre_gain,
    w_query,
    w_key,
    w_value,
    mix_gate,
    w_rate,
    rate_bias,
    inner_gain,
    inner_bias,
    init_w_one,
    init_b_one,
    init_w_two,
    init_b_two,
    post_gain,
    post_bias,
    w_out,
    ffn_gain,
    w_gate,
    w_up,
    w_down,
    cotangent,
):
    full_width = pre_gain.shape[0]
    rows, local_cols = inputs.shape
    heads, head_dim = inner_gain.shape
    head_index = lax.axis_index("head")
    position = lax.axis_index("seq") % CHAIN
    whole_low = lax.all_gather(inputs, "head", axis=1, tiled=True)
    whole_in = whole_low.astype(f32)
    grad_whole = lax.all_gather(cotangent, "head", axis=1, tiled=True)
    rms_one = lax.rsqrt(jnp.mean(whole_in * whole_in, axis=1, keepdims=True) + eps_norm)
    normed_one = (whole_in * rms_one * pre_gain).astype(bf16)
    stretches = lax.axis_size("seq") // CHAIN
    spare = PACK - 3 * head_dim

    def by_head(weight):
        return weight.reshape(full_width, heads, -1)

    rate_cols = by_head(w_rate)
    packed_w = jnp.concatenate(
        [by_head(w_query), by_head(w_key), by_head(w_value), rate_cols, rate_cols,
         jnp.zeros((full_width, heads, spare - 2), bf16)], axis=2).reshape(full_width, heads * PACK)
    lane = lax.broadcasted_iota(jnp.int32, (1, heads, PACK), 2)
    rate_lane = (lane == 3 * head_dim) | (lane == 3 * head_dim + 1)
    packed_bias = jnp.where(rate_lane, rate_bias[None, :, None], 0.0).reshape(1, heads * PACK)
    low_lane = (lane == 3 * head_dim + 1).reshape(1, heads * PACK)
    pre = bf_product("rd,dc->rc", normed_one, packed_w) + packed_bias
    payload = (pre - jnp.where(low_lane, lax.reduce_precision(pre, 8, 7), 0.0)).astype(bf16)
    gate_pre = bf_product("rd,dc->rc", normed_one, mix_gate)
    mixed_h, *saved = chain_forward(
        payload, init_w_one, init_b_one, init_w_two, init_b_two, inner_gain, inner_bias)
    grad_mixed, early, grad_gate_pre, outputs, grad_resid_cols, small = middle(
        mixed_h, whole_low, grad_whole, gate_pre, normed_one, w_out, w_gate, w_up, w_down,
        post_gain[None], post_bias[None], ffn_gain[None])
    share = full_width // CHAIN
    grads, ends, early_sum, normed_cols = chain_backward(
        grad_mixed,
        early.reshape(CHAIN, share, early.shape[1]),
        normed_one.reshape(rows, CHAIN, share).transpose(1, 0, 2), inner_gain, inner_bias, saved)
    wide = 3 * head_dim
    late = bf_product("tc,jtk->jck", normed_cols.reshape(CHAIN * rows, share), grads[:, :, :wide])
    back = lax.dynamic_slice_in_dim(grads, position * rows, rows, 1)

    def join_heads(lo, hi):
        return back[:, :, lo:hi].transpose(1, 0, 2).reshape(rows, -1)

    grad_q_low = join_heads(0, head_dim)
    grad_k_low = join_heads(head_dim, 2 * head_dim)
    grad_v_low = join_heads(2 * head_dim, 3 * head_dim)
    grad_logits = join_heads(3 * head_dim, 3 * head_dim + 1).astype(f32) + join_heads(
        3 * head_dim + 1, 3 * head_dim + 2).astype(f32)
    rate_bias_term = jnp.sum(grad_logits, axis=0)
    grad_logit_low = grad_logits.astype(bf16)
    rate_weight_term = bf_product("rd,rc->dc", normed_one, grad_logit_low)
    grad_normed_one = (
        bf_product("rc,dc->rd", grad_q_low, w_query)
        + bf_product("rc,dc->rd", grad_k_low, w_key)
        + bf_product("rc,dc->rd", grad_v_low, w_value)
        + bf_product("rc,dc->rd", grad_gate_pre, mix_gate)
        + bf_product("rc,dc->rd", grad_logit_low, w_rate)
    )
    scaled_one = grad_normed_one * pre_gain
    input_back = rms_one * (
        scaled_one
        - whole_in * rms_one * rms_one * jnp.mean(scaled_one * whole_in, axis=1, keepdims=True)
    )
    gain_one_term = jnp.sum(grad_normed_one * whole_in * rms_one, axis=0)
    input_local = lax.psum_scatter(
        input_back.astype(bf16), "head", scatter_dimension=1, tiled=True).astype(f32)
    grad_inputs = grad_resid_cols + input_local
    ends = ends.astype(f32)
    hidden = ends.shape[2]
    late = late.reshape(heads, share, 3, head_dim).transpose(2, 1, 0, 3).reshape(3, share, local_cols)
    if stretches > 1:
        ends = lax.psum(ends, "seq", axis_index_groups=stretch_groups("seq"))
        seq_index = lax.axis_index("seq")

        def spread(mine_rows):
            summed = lax.psum(mine_rows, "seq", axis_index_groups=stretch_groups("seq"))
            total = lax.all_gather(
                summed, "seq", axis=summed.ndim - 2, tiled=True,
                axis_index_groups=[list(range(s, s + CHAIN)) for s in range(0, stretches * CHAIN, CHAIN)])
            return lax.dynamic_slice_in_dim(
                total, seq_index * (share // stretches), share // stretches, summed.ndim - 2)

        late = spread(late)
        early_sum = spread(early_sum)
    end_two = ends[:, AUG : AUG + head_dim]
    tails = ends[:, AUG + head_dim :, :head_dim]
    grad_one = ends[:, :head_dim]
    grad_b_one = ends[:, head_dim]
    grad_two = (end_two - jnp.mean(end_two, axis=1, keepdims=True)).transpose(0, 2, 1)
    grad_b_two = tails[:, 0] - jnp.mean(tails[:, 0], axis=1, keepdims=True)
    grad_gain = tails[:, 1]
    grad_bias = tails[:, 2]
    flat = lax.psum(
        jnp.concatenate([small[1, :local_cols], small[2, :local_cols], rate_weight_term.reshape(-1), rate_bias_term]), "seq")
    at = 0

    def take(shape):
        nonlocal at
        size = 1
        for extent in shape:
            size *= extent
        at += size
        return flat[at - size : at].reshape(shape)

    grad_post_gain = take((local_cols,))
    grad_post_bias = take((local_cols,))
    grad_rate_w = take((full_width, heads))
    grad_rate_b = take((heads,))
    gain_both = lax.psum(
        jnp.concatenate([gain_one_term, small[0] / lax.axis_size("head")]), ("seq", "head"))
    gain_one = lax.dynamic_slice_in_dim(gain_both, head_index * local_cols, local_cols, 0)
    gain_two = gain_both[full_width:]
    ffn = w_gate.shape[1]
    return (
        outputs,
        grad_inputs,
        gain_one,
        late[0],
        late[1],
        late[2],
        early_sum[:, 3 * ffn : 3 * ffn + local_cols],
        grad_rate_w,
        grad_rate_b,
        grad_gain,
        grad_bias,
        grad_one,
        grad_b_one,
        grad_two,
        grad_b_two,
        grad_post_gain,
        grad_post_bias,
        early_sum[:, 3 * ffn + local_cols :].T,
        gain_two,
        early_sum[:, :ffn],
        early_sum[:, ffn : 2 * ffn],
        early_sum[:, 2 * ffn : 3 * ffn].T,
    )


def solution(mesh):
    in_specs = (
        P("seq", "head"),
        P(),
        P(None, "head"),
        P(None, "head"),
        P(None, "head"),
        P(None, "head"),
        P(None, "head"),
        P("head"),
        P("head", None),
        P("head", None),
        P("head", None, None),
        P("head", None),
        P("head", None, None),
        P("head", None),
        P("head"),
        P("head"),
        P("head", None),
        P(),
        P(None, "head"),
        P(None, "head"),
        P("head", None),
        P("seq", "head"),
    )
    out_specs = (
        P("seq", "head"),
        P("seq", "head"),
        P("head"),
        P("seq", "head"),
        P("seq", "head"),
        P("seq", "head"),
        P("seq", "head"),
        P(None, "head"),
        P("head"),
        P("head", None),
        P("head", None),
        P("head", None, None),
        P("head", None),
        P("head", None, None),
        P("head", None),
        P("head"),
        P("head"),
        P("head", "seq"),
        P(),
        P("seq", "head"),
        P("seq", "head"),
        P("head", "seq"),
    )
    return jax.shard_map(local, mesh=mesh, in_specs=in_specs, out_specs=out_specs, check_vma=False)
```

```python
import functools

import jax
import jax.numpy as jnp
from jax import lax
from jax.experimental import pallas as pl
from jax.experimental.pallas import tpu as pltpu
from jax.sharding import PartitionSpec as P

MINI = 16
CHAIN = 8
FIRST = 2
AUG = 80
eps_norm = 1e-06
gelu_scale = 0.7978845608028654
f32 = jnp.float32
bf16 = jnp.bfloat16


def dot_nn(a, b):
    return lax.dot_general(a, b, (((1,), (0,)), ((), ())), preferred_element_type=f32)


def dot_nt(a, b):
    return lax.dot_general(a, b, (((1,), (1,)), ((), ())), preferred_element_type=f32)


def dot_tn(a, b):
    return lax.dot_general(a, b, (((0,), (0,)), ((), ())), preferred_element_type=f32)


def mean_row(x):
    return jnp.sum(x, axis=1, keepdims=True) * (1.0 / x.shape[1])


def gelu_first(z):
    sq = z * z
    th = jnp.tanh(gelu_scale * z * (1.0 + 0.044715 * sq))
    half = 0.5 * (1.0 + th)
    act = z * half
    der = half + (0.5 * gelu_scale) * z * (1.0 - th * th) * (1.0 + 0.134145 * sq)
    return act, der


def gelu_second(z):
    sq = z * z
    th = jnp.tanh(gelu_scale * z * (1.0 + 0.044715 * sq))
    half = 0.5 * (1.0 + th)
    act = z * half
    slope = gelu_scale * (1.0 + 0.134145 * sq)
    sech = 1.0 - th * th
    der = half + 0.5 * z * sech * slope
    curve = sech * (slope + z * (0.5 * gelu_scale * 0.26829 * z) - z * th * slope * slope)
    return act, der, curve


def tri_mask():
    rows = lax.broadcasted_iota(jnp.int32, (MINI, MINI), 0)
    cols = lax.broadcasted_iota(jnp.int32, (MINI, MINI), 1)
    return jnp.where(rows >= cols, 1.0, 0.0).astype(f32)


def inner_target_grad(z, base, gain_sq, rate):
    mz = mean_row(z)
    m_zz = mean_row(z * z)
    zg = z * gain_sq
    m_zg = mean_row(zg)
    m_zzg = mean_row(zg * z)
    m_zb = mean_row(z * base)
    m_b = mean_row(base)
    m_sq = mean_row(gain_sq)
    inv = lax.rsqrt(m_zz - mz * mz + eps_norm)
    c_zg = m_zg - mz * m_sq
    c_zzg = m_zzg - mz * (m_zg + c_zg)
    c_zb = m_zb - mz * m_b
    m_g = inv * c_zg + m_b
    m_gn = inv * (inv * c_zzg + c_zb)
    zc = z - mz
    n = zc * inv
    grad = inv * (n * (gain_sq - m_gn) + (base - m_g))
    return rate * grad, zc


def forward_step(state, z1, key_aug, key_next, query_aug, base, rate, gain, gain_sq, bias, tri):
    w1, w2t, b2 = state
    act, der = gelu_first(z1)
    act_h = act.astype(bf16)
    w1_h = w1.astype(bf16)
    w2_h = w2t.astype(bf16)
    s2, zc = inner_target_grad(dot_nt(act_h, w2_h) + b2, base, gain_sq, rate)
    s2_h = s2.astype(bf16)
    upd = dot_nn(s2_h, w2_h)
    s1_h = (upd * der).astype(bf16)
    both = jnp.concatenate([key_next, query_aug], axis=0)
    coef = dot_nt(both, key_aug)
    coef = jnp.concatenate([coef[:MINI], coef[MINI:] * tri], axis=0)
    zz = dot_nn(both, w1_h) - dot_nn(coef.astype(bf16), s1_h)
    z1_next = zz[:MINI]
    z1b = zz[MINI:]
    new_w1 = w1 - dot_tn(key_aug, s1_h)
    new_w2t = w2t - dot_tn(s2_h, act_h)
    new_b2 = b2 - jnp.sum(s2, axis=0, keepdims=True)
    actb, _ = gelu_first(z1b)
    actb_h = actb.astype(bf16)
    att = (dot_nt(actb_h, act_h) + 1.0) * tri
    z2b = dot_nt(actb_h, w2_h) + b2 - dot_nn(att.astype(bf16), s2_h)
    z2b = z2b - mean_row(z2b)
    invb = lax.rsqrt(mean_row(z2b * z2b) + eps_norm)
    out = z2b * invb * gain + bias
    return (new_w1, new_w2t, new_b2), z1_next, out, (w1_h, w2_h, upd, zc, s2, z1b, z2b)


def backward_step(carry, saved, d_out, key_aug, query_aug, target, rate, keep, gain, gain_sq, bias, tri):
    p1, p2t, p2 = carry
    w1_h, w2_h, z1, upd, zc, s2, z1b, z2b = saved
    act, der, curve = gelu_second(z1)
    act_h = act.astype(bf16)
    actb, derb = gelu_first(z1b)
    actb_h = actb.astype(bf16)
    s2_h = s2.astype(bf16)
    s1_h = (upd * der).astype(bf16)
    p1_h = p1.astype(bf16)
    p2_h = p2t.astype(bf16)
    invb = lax.rsqrt(mean_row(z2b * z2b) + eps_norm)
    nb = z2b * invb
    dn = d_out * gain
    d_z2b = invb * (dn - mean_row(dn) - nb * mean_row(dn * nb))
    d_z2b_h = d_z2b.astype(bf16)
    d_att2 = (-dot_nt(d_z2b_h, s2_h) * tri).astype(bf16)
    d_actb = dot_nn(d_z2b_h, w2_h) + dot_nn(d_att2, act_h)
    d_z1b_h = (d_actb * derb).astype(bf16)
    att2 = ((dot_nt(actb_h, act_h) + 1.0) * tri).astype(bf16)
    att1 = (dot_nt(query_aug, key_aug) * tri).astype(bf16)
    c2 = dot_tn(att2, d_z2b_h)
    c3 = dot_tn(d_att2, actb_h)
    c1 = dot_tn(att1, d_z1b_h)
    d_att1 = (-dot_nt(d_z1b_h, s1_h) * tri).astype(bf16)
    d_query = dot_nt(d_z1b_h, w1_h) + dot_nn(d_att1, key_aug)
    d_key = dot_tn(d_att1, query_aug)
    d_s1 = -c1 - dot_nn(key_aug, p1_h)
    d_upd = d_s1 * der
    d_upd_h = d_upd.astype(bf16)
    d_s2 = dot_nt(d_upd_h, w2_h) - c2 - dot_nt(act_h, p2_h) - p2
    h = rate * d_s2
    inv = lax.rsqrt(mean_row(zc * zc) + eps_norm)
    n = zc * inv
    base = (bias - target) * gain
    big_g = n * gain_sq + base
    m_g = mean_row(big_g)
    m_gn = mean_row(big_g * n)
    m_sq = mean_row(gain_sq)
    ng = n * gain_sq
    m_ng = mean_row(ng)
    m_nng = mean_row(n * ng)
    g = inv * (big_g - m_g - n * m_gn)
    a1 = mean_row(h)
    a2 = mean_row(h * n)
    a3 = mean_row(h * gain_sq)
    a4 = mean_row(h * ng)
    a5 = mean_row(h * g)
    proj = h - a1 - n * a2
    d_g = inv * proj
    dnn = inv * (proj * gain_sq - h * m_gn - big_g * a2)
    m_dn = inv * (a3 - a1 * (m_sq + m_gn) - a2 * (m_ng + m_g))
    m_dnn = inv * (a4 - a1 * m_ng - a2 * (m_nng + 2.0 * m_gn))
    d_zc = inv * (dnn - m_dn - n * (m_dnn + a5))
    d_zc_h = d_zc.astype(bf16)
    d_act = dot_nn(d_zc_h, w2_h) + c3 - dot_nn(s2_h, p2_h)
    d_z1 = d_act * der + d_s1 * upd * curve
    d_z1_h = d_z1.astype(bf16)
    d_gg = d_g * gain
    d_key = d_key + dot_nt(d_z1_h, w1_h) - dot_nt(s1_h, p1_h)
    d_key = d_key[:, : gain.shape[1]] + d_gg
    d_query = d_query[:, : gain.shape[1]] + d_out
    d_value = -d_gg
    d_logit = keep * jnp.sum(d_s2 * s2, axis=1, keepdims=True)
    new_p1 = p1 + dot_tn(
        jnp.concatenate([key_aug, query_aug], axis=0), jnp.concatenate([d_z1_h, d_z1b_h], axis=0)
    )
    new_p2t = p2t + dot_tn(
        jnp.concatenate([s2_h, d_zc_h, d_z2b_h], axis=0),
        jnp.concatenate([d_upd_h, act_h, actb_h], axis=0),
    )
    new_p2 = p2 + jnp.sum(d_zc + d_z2b, axis=0, keepdims=True)
    d_bias = jnp.sum(d_out + d_gg, axis=0, keepdims=True)
    d_gain = jnp.sum(d_out * nb + d_g * (2.0 * n * gain + bias - target), axis=0, keepdims=True)
    return (new_p1, new_p2t, new_p2), (d_query, d_key, d_value, d_logit), d_gain, d_bias


MESH = pl.DeviceIdType.MESH
PACK = 256
ENDS = 160


def seq_place():
    index = lax.axis_index("seq")
    pos = lax.rem(index, CHAIN)
    return pos, index - pos


def meet_group(pos, base):
    barrier = pltpu.get_barrier_semaphore()
    for d in range(1, CHAIN):
        pl.semaphore_signal(
            barrier, inc=1, device_id={"seq": base + lax.rem(pos + d, CHAIN)}, device_id_type=MESH)
    pl.semaphore_wait(barrier, CHAIN - 1)


def push(src, dst, send_sem, recv_sem, target):
    return pltpu.make_async_remote_copy(
        src_ref=src, dst_ref=dst, send_sem=send_sem, recv_sem=recv_sem,
        device_id={"seq": target}, device_id_type=MESH)


def await_bytes(ref, sem):
    pltpu.make_async_copy(ref, ref, sem).wait()


def swap_start(src, dst, send, recv, local_sem, pos, base):
    for d in range(1, CHAIN):
        peer = lax.rem(pos + d, CHAIN)
        push(src.at[peer], dst.at[pos], send.at[d - 1], recv.at[d - 1], base + peer).start()
    pltpu.make_async_copy(src.at[pos], dst.at[pos], local_sem).start()


def swap_wait(src, dst, send, recv, local_sem, pos, base):
    for d in range(1, CHAIN):
        peer = lax.rem(pos + d, CHAIN)
        origin = lax.rem(pos + CHAIN - d, CHAIN)
        push(src.at[peer], dst.at[pos], send.at[d - 1], recv.at[d - 1], base + peer).wait_send()
        await_bytes(dst.at[origin], recv.at[d - 1])
    await_bytes(dst.at[pos], local_sem)


def fwd_kernel(block, unroll, heads, pay_ref, norm_ref, w1_in, b1_in, w2_in, b2_in, gain_in, bias_in,
               mixed_ref, norm_out, k_out, q_out, aux_out, w1s_ref, w2s_ref, z1s_ref, upd_ref, zc_ref, s2_ref, z1b_ref, z2b_ref,
               got, k_all, q_all, base_all, aux_all, mixed_all, w1, w2t, b2, z1,
               pay_send, pay_recv, mix_send, mix_recv, no_send, no_recv, no_loc):
    blk = pl.program_id(0)
    last = pl.num_programs(0) - 1
    pos, base = seq_place()
    width = gain_in.shape[1]
    hidden = w1.shape[1]
    rows_each = pay_ref.shape[0]
    per = rows_each // block
    owner = (pos >= FIRST) & (pos < FIRST + heads)
    mine = jnp.clip(pos - FIRST, 0, heads - 1)
    gain = gain_in[pl.ds(mine, 1), :]
    bias = bias_in[pl.ds(mine, 1), :]
    gain_sq = gain * gain
    tri = tri_mask()

    @pl.when(blk == 0)
    def _():
        meet_group(pos, base)
        for j in range(heads):
            src = pay_ref.at[:, pl.ds(j * PACK, PACK)]
            dst = got.at[pos]

            @pl.when(pos != FIRST + j)
            def _():
                push(src, dst, pay_send.at[j], pay_recv.at[pos], base + FIRST + j).start()

            @pl.when(pos == FIRST + j)
            def _():
                pltpu.make_async_copy(src, dst, pay_recv.at[pos]).start()

        swap_start(norm_ref, norm_out, no_send, no_recv, no_loc, pos, base)

    def take_in(p):
        await_bytes(got.at[p], pay_recv.at[p])
        part = got[p]
        rows = pl.ds(pl.multiple_of(p * rows_each, rows_each), rows_each)
        lane = lax.broadcasted_iota(jnp.int32, (rows_each, AUG), 1)
        one = jnp.ones((), bf16)
        zero = jnp.zeros((), bf16)
        tail = jnp.where(lane == width, one, zero)
        query = part[:, :AUG]
        key = part[:, width : width + AUG]
        q_all[rows, :] = jnp.where(lane < width, query, tail)
        k_all[rows, :] = jnp.where(lane < width, key, tail)
        key_f = part[:, width : 2 * width].astype(f32)
        target = part[:, 2 * width : 3 * width].astype(f32) - key_f
        logit = part[:, 3 * width : 3 * width + 1].astype(f32) + part[:, 3 * width + 1 : 3 * width + 2].astype(f32)
        sig = 1.0 / (1.0 + jnp.exp(-logit))
        base_all[rows, :] = (bias - target) * gain
        spot = lax.broadcasted_iota(jnp.int32, (rows_each, 2 * width), 1)
        wide = jnp.concatenate([target, target], axis=1)
        aux_all[rows, :] = jnp.where(
            spot < width, wide, jnp.where(spot == width, sig * (1.0 / width), 1.0 - sig))

    def send_mixed(b):
        p = lax.div(b, per)
        src = mixed_all.at[pl.ds(pl.multiple_of(b * block, block), block), :]
        dst = mixed_ref.at[mine, pl.ds(pl.multiple_of(lax.rem(b, per) * block, block), block), :]

        @pl.when(p != pos)
        def _():
            push(src, dst, mix_send, mix_recv.at[mine], base + p).start()

        @pl.when(p == pos)
        def _():
            pltpu.make_async_copy(src, dst, mix_recv.at[mine]).start()

    @pl.when(owner)
    def _():
        @pl.when(blk == 0)
        def _():
            row = lax.broadcasted_iota(jnp.int32, (AUG - width, hidden), 0)
            w1[pl.ds(0, width), :] = w1_in[mine]
            w1[pl.ds(width, AUG - width), :] = jnp.where(row == 0, b1_in[pl.ds(mine, 1), :], 0.0)
            turned = w2_in[mine].T
            w2t[...] = turned - jnp.mean(turned, axis=0, keepdims=True)
            start = b2_in[pl.ds(mine, 1), :]
            b2[...] = start - mean_row(start)
            k_all[pl.ds(CHAIN * rows_each, MINI), :] = jnp.zeros((MINI, AUG), bf16)
            take_in(0)
            z1[...] = dot_nn(k_all[0:MINI, :], w1[...].astype(bf16))

        @pl.when((lax.rem(blk, per) == 0) & (blk < last + 1 - per))
        def _():
            take_in(lax.div(blk, per) + 1)

        @pl.when(blk > 0)
        def _():
            send_mixed(blk - 1)

        brows = pl.ds(pl.multiple_of(blk * block, block), block)
        k_out[...] = k_all[brows, :]
        q_out[...] = q_all[brows, :]
        aux_out[...] = aux_all[brows, :]

        def group(it, _):
            for u in range(unroll):
                loc = it * unroll + u
                row = pl.multiple_of(blk * block + loc * MINI, MINI)
                rows = pl.ds(row, MINI)
                lrows = pl.ds(pl.multiple_of(loc * MINI, MINI), MINI)
                q_aug = q_all[rows, :]
                z1_now = z1[...]
                state, z1_next, out, saved = forward_step(
                    (w1[...], w2t[...], b2[...]), z1_now, k_all[rows, :], k_all[pl.ds(row + MINI, MINI), :], q_aug,
                    base_all[rows, :], aux_all[rows, width : width + 1], gain, gain_sq, bias, tri)
                w1[...], w2t[...], b2[...] = state
                z1[...] = z1_next
                mixed_all[rows, :] = (out + q_aug[:, :width].astype(f32)).astype(bf16)
                w1s_ref[loc], w2s_ref[loc], upd, zc, s2, z1b, z2b = saved
                z1s_ref[lrows, :] = z1_now
                upd_ref[lrows, :] = upd
                zc_ref[lrows, :] = zc
                s2_ref[lrows, :] = s2
                z1b_ref[lrows, :] = z1b
                z2b_ref[lrows, :] = z2b
            return 0

        lax.fori_loop(0, block // MINI // unroll, group, 0)

    @pl.when(blk == last)
    def _():
        @pl.when(owner)
        def _():
            send_mixed(last)
            others = mixed_all.at[pl.ds(0, (CHAIN - 1) * rows_each), :]
            await_bytes(others, mix_send)

        swap_wait(norm_ref, norm_out, no_send, no_recv, no_loc, pos, base)
        for j in range(heads):
            @pl.when(pos != FIRST + j)
            def _():
                await_bytes(got.at[pos], pay_send.at[j])

            await_bytes(mixed_ref.at[j], mix_recv.at[j])


def chain_forward(payload, normed, w1, b1, w2, b2, gain, bias, block=128, unroll=8):
    rows = payload.shape[0]
    heads, width, hidden = w1.shape
    tokens = rows * CHAIN
    steps = tokens // MINI
    nb = block // MINI
    whole = lambda a: pl.BlockSpec(a.shape, lambda i: (0,) * a.ndim)
    rowblk = lambda w: pl.BlockSpec((block, w), lambda i: (i, 0))
    stepblk = lambda r: pl.BlockSpec((nb, r, hidden), lambda i: (i, 0, 0))
    anywhere = pl.BlockSpec(memory_space=pl.ANY)
    small = (w1, b1, w2, b2, gain, bias)
    dma = pltpu.SemaphoreType.DMA
    wide = jax.ShapeDtypeStruct((tokens, hidden), f32)
    narrow = jax.ShapeDtypeStruct((tokens, width), f32)
    return pl.pallas_call(
        functools.partial(fwd_kernel, block, unroll, heads),
        grid=(tokens // block,),
        in_specs=[anywhere, anywhere] + [whole(a) for a in small],
        out_specs=[anywhere, anywhere, rowblk(AUG), rowblk(AUG), rowblk(2 * width), stepblk(AUG), stepblk(width),
                   rowblk(hidden), rowblk(hidden), rowblk(width), rowblk(width), rowblk(hidden), rowblk(width)],
        out_shape=[jax.ShapeDtypeStruct((heads, rows, width), bf16),
                   jax.ShapeDtypeStruct(normed.shape, bf16),
                   jax.ShapeDtypeStruct((tokens, AUG), bf16),
                   jax.ShapeDtypeStruct((tokens, AUG), bf16),
                   jax.ShapeDtypeStruct((tokens, 2 * width), f32),
                   jax.ShapeDtypeStruct((steps, AUG, hidden), bf16),
                   jax.ShapeDtypeStruct((steps, width, hidden), bf16),
                   wide, wide, narrow, narrow, wide, narrow],
        scratch_shapes=[pltpu.VMEM((CHAIN, rows, PACK), bf16),
                        pltpu.VMEM((tokens + MINI, AUG), bf16), pltpu.VMEM((tokens, AUG), bf16),
                        pltpu.VMEM((tokens, width), f32), pltpu.VMEM((tokens, 2 * width), f32),
                        pltpu.VMEM((tokens, width), bf16),
                        pltpu.VMEM((AUG, hidden), f32), pltpu.VMEM((width, hidden), f32),
                        pltpu.VMEM((1, width), f32), pltpu.VMEM((MINI, hidden), f32),
                        dma((heads,)), dma((CHAIN,)), dma, dma((heads,)),
                        dma((CHAIN - 1,)), dma((CHAIN - 1,)), dma],
        compiler_params=pltpu.CompilerParams(collective_id=0, has_side_effects=True),
        name="inner_forward",
    )(payload, normed, *small)


def bwd_kernel(block, unroll, heads, turn, gm_ref, early_ref, small_ref, gain_in, bias_in,
               k_ref, q_ref, aux_ref, w1s_ref, w2s_ref, z1s_ref, upd_ref, zc_ref, s2_ref, z1b_ref, z2b_ref,
               grads_ref, ends_ref, early_out, small_out,
               dout, half_got, half_mine, quarter, quarter_got, packed, ends, p1, p2t, p2, dg, db,
               gm_send, gm_recv, ha_send, ha_recv, ha_loc, qu_send, qu_recv, sm_send, sm_recv, sm_loc, bc_send, bc_recv, en_send, en_recv):
    pid = pl.program_id(0)
    last = pl.num_programs(0) - 1
    blk = last - pid
    pos, base = seq_place()
    width = gain_in.shape[1]
    rows_each = gm_ref.shape[1]
    per = rows_each // block
    owner = (pos >= FIRST) & (pos < FIRST + heads)
    mine = jnp.clip(pos - FIRST, 0, heads - 1)
    gain = gain_in[pl.ds(mine, 1), :]
    bias = bias_in[pl.ds(mine, 1), :]
    gain_sq = gain * gain
    tri = tri_mask()
    count = block // MINI
    side = lax.rem(pos, 2)
    rank = lax.div(pos, 2)
    partner = pos + 1 - 2 * side

    @pl.when(pid == 0)
    def _():
        meet_group(pos, base)
        for j in range(heads):
            @pl.when(pos != FIRST + j)
            def _():
                push(gm_ref.at[j], dout.at[pos], gm_send.at[j], gm_recv.at[pos], base + FIRST + j).start()

            @pl.when(pos == FIRST + j)
            def _():
                pltpu.make_async_copy(gm_ref.at[j], dout.at[pos], gm_recv.at[pos]).start()

        for d in range(1, CHAIN):
            push(small_ref, small_out.at[pos], sm_send.at[d - 1], sm_recv.at[d - 1],
                 base + lax.rem(pos + d, CHAIN)).start()
        pltpu.make_async_copy(small_ref, small_out.at[pos], sm_loc).start()
        push(early_ref.at[:, 1 - side], half_got, ha_send, ha_recv, base + partner).start()
        pltpu.make_async_copy(early_ref.at[:, side], half_mine, ha_loc).start()

    @pl.when(pid == turn)
    def _():
        push(early_ref.at[:, 1 - side], half_got, ha_send, ha_recv, base + partner).wait()
        await_bytes(half_mine, ha_loc)

        def pair_up(c, _):
            rows = pl.ds(pl.multiple_of(c * MINI, MINI), MINI)
            for r in range(CHAIN // 2):
                quarter[r, rows, :] = (half_mine[r, rows, :].astype(f32) + half_got[r, rows, :].astype(f32)).astype(bf16)
            return 0

        lax.fori_loop(0, half_mine.shape[1] // MINI, pair_up, 0)
        for d in range(1, CHAIN // 2):
            other = lax.rem(rank + d, CHAIN // 2)
            push(quarter.at[other], quarter_got.at[d - 1], qu_send.at[d - 1], qu_recv.at[d - 1],
                 base + 2 * other + side).start()

    def share_block(b):
        rows = pl.ds(pl.multiple_of(b * block, block), block)
        for d in range(1, CHAIN):
            push(packed.at[rows, :], grads_ref.at[mine, rows, :], bc_send.at[d - 1], bc_recv.at[mine],
                 base + lax.rem(pos + d, CHAIN)).start()
        pltpu.make_async_copy(packed.at[rows, :], grads_ref.at[mine, rows, :], bc_recv.at[mine]).start()

    @pl.when(owner)
    def _():
        @pl.when(pid == 0)
        def _():
            for r in (p1, p2t, p2, dg, db):
                r[...] = jnp.zeros_like(r)

        @pl.when(lax.rem(pid, per) == 0)
        def _():
            p = lax.div(blk, per)
            await_bytes(dout.at[p], gm_recv.at[p])

        @pl.when(pid > 0)
        def _():
            share_block(blk + 1)

        def group(it, _):
            for u in range(unroll):
                loc = count - 1 - (it * unroll + u)
                row = pl.multiple_of(blk * block + loc * MINI, MINI)
                lr = pl.ds(pl.multiple_of(loc * MINI, MINI), MINI)
                inner = pl.ds(pl.multiple_of(lax.rem(blk, per) * block + loc * MINI, MINI), MINI)
                saved = (w1s_ref[loc], w2s_ref[loc], z1s_ref[lr, :], upd_ref[lr, :], zc_ref[lr, :], s2_ref[lr, :],
                         z1b_ref[lr, :], z2b_ref[lr, :])
                aux = aux_ref[lr, :]
                carry, outs, dgn, dbn = backward_step(
                    (p1[...], p2t[...], p2[...]), saved, dout[lax.div(blk, per), inner, :].astype(f32), k_ref[lr, :],
                    q_ref[lr, :], aux[:, :width], aux[:, width : width + 1], aux[:, width + 1 : width + 2],
                    gain, gain_sq, bias, tri)
                p1[...], p2t[...], p2[...] = carry
                dg[...] += dgn
                db[...] += dbn
                d_query, d_key, d_value, d_logit = outs
                high = d_logit.astype(bf16).astype(f32)
                lane = lax.broadcasted_iota(jnp.int32, (MINI, width), 1)
                extra = jnp.where(lane == 0, high, jnp.where(lane == 1, d_logit - high, 0.0))
                packed[pl.ds(row, MINI), :] = jnp.concatenate([d_query, d_key, d_value, extra], axis=1).astype(bf16)
            return 0

        lax.fori_loop(0, count // unroll, group, 0)

        @pl.when(pid == last)
        def _():
            ends[pl.ds(0, AUG), :] = p1[...].astype(bf16)
            ends[pl.ds(AUG, width), :] = p2t[...].astype(bf16)
            rest = ENDS - AUG - width
            row = lax.broadcasted_iota(jnp.int32, (rest, width), 0)
            tailing = jnp.where(row == 0, p2[...], jnp.where(row == 1, dg[...], jnp.where(row == 2, db[...], 0.0)))
            ends[pl.ds(AUG + width, rest), :] = jnp.concatenate([tailing] * 4, axis=1).astype(bf16)
            share_block(0)
            for d in range(1, CHAIN):
                push(ends, ends_ref.at[mine], en_send.at[d - 1], en_recv.at[mine],
                     base + lax.rem(pos + d, CHAIN)).start()
            pltpu.make_async_copy(ends, ends_ref.at[mine], en_recv.at[mine]).start()

    @pl.when(pid == last)
    def _():
        for d in range(1, CHAIN // 2):
            other = lax.rem(rank + d, CHAIN // 2)
            push(quarter.at[other], quarter_got.at[d - 1], qu_send.at[d - 1], qu_recv.at[d - 1],
                 base + 2 * other + side).wait()
        for d in range(1, CHAIN):
            push(small_ref, small_out.at[pos], sm_send.at[d - 1], sm_recv.at[d - 1],
                 base + lax.rem(pos + d, CHAIN)).wait_send()
            await_bytes(small_out.at[lax.rem(pos + CHAIN - d, CHAIN)], sm_recv.at[d - 1])
        await_bytes(small_out.at[pos], sm_loc)

        def add_up(c, _):
            rows = pl.ds(pl.multiple_of(c * MINI, MINI), MINI)
            acc = quarter[rank, rows, :].astype(f32)
            for d in range(1, CHAIN // 2):
                acc = acc + quarter_got[d - 1, rows, :].astype(f32)
            early_out[rows, :] = acc
            return 0

        lax.fori_loop(0, early_out.shape[0] // MINI, add_up, 0)
        for j in range(heads):
            @pl.when(pos != FIRST + j)
            def _():
                await_bytes(dout.at[pos], gm_send.at[j])

            await_bytes(grads_ref.at[j], bc_recv.at[j])
            await_bytes(ends_ref.at[j], en_recv.at[j])

        @pl.when(owner)
        def _():
            for d in range(1, CHAIN):
                await_bytes(packed, bc_send.at[d - 1])
                await_bytes(ends, en_send.at[d - 1])


def chain_backward(grad_mixed, early, small, gain, bias, saved, block=128, unroll=4, turn=6):
    heads, rows, width = grad_mixed.shape
    tokens = rows * CHAIN
    hidden = saved[5].shape[1]
    nblk = tokens // block
    nb = block // MINI
    whole = lambda a: pl.BlockSpec(a.shape, lambda i: (0,) * a.ndim)
    rowblk = lambda w: pl.BlockSpec((block, w), lambda i: (nblk - 1 - i, 0))
    stepblk = lambda r: pl.BlockSpec((nb, r, hidden), lambda i: (nblk - 1 - i, 0, 0))
    anywhere = pl.BlockSpec(memory_space=pl.ANY)
    dma = pltpu.SemaphoreType.DMA
    seven = dma((CHAIN - 1,))
    share = early.shape[2:]
    three = dma((CHAIN // 2 - 1,))
    return pl.pallas_call(
        functools.partial(bwd_kernel, block, unroll, heads, turn),
        grid=(nblk,),
        in_specs=[anywhere] * 3 + [whole(gain), whole(bias), rowblk(AUG), rowblk(AUG), rowblk(2 * width),
                                   stepblk(AUG), stepblk(width), rowblk(hidden), rowblk(hidden), rowblk(width),
                                   rowblk(width), rowblk(hidden), rowblk(width)],
        out_specs=[anywhere, anywhere, pl.BlockSpec(share, lambda i: (0, 0)), anywhere],
        out_shape=[jax.ShapeDtypeStruct((heads, tokens, PACK), bf16),
                   jax.ShapeDtypeStruct((heads, ENDS, hidden), bf16),
                   jax.ShapeDtypeStruct(share, f32),
                   jax.ShapeDtypeStruct((CHAIN,) + small.shape, f32)],
        scratch_shapes=[pltpu.VMEM((CHAIN, rows, width), bf16), pltpu.VMEM((CHAIN // 2,) + share, bf16),
                        pltpu.VMEM((CHAIN // 2,) + share, bf16), pltpu.VMEM((CHAIN // 2,) + share, bf16),
                        pltpu.VMEM((CHAIN // 2 - 1,) + share, bf16),
                        pltpu.VMEM((tokens, PACK), bf16), pltpu.VMEM((ENDS, hidden), bf16),
                        pltpu.VMEM((AUG, hidden), f32), pltpu.VMEM((width, hidden), f32), pltpu.VMEM((1, width), f32),
                        pltpu.VMEM((1, width), f32), pltpu.VMEM((1, width), f32),
                        dma((heads,)), dma((CHAIN,)), dma, dma, dma, three, three, seven, seven, dma,
                        seven, dma((heads,)), seven, dma((heads,))],
        compiler_params=pltpu.CompilerParams(collective_id=1, has_side_effects=True),
        name="inner_backward",
    )(grad_mixed, early, small, gain, bias, *saved)


def head_place():
    return lax.axis_index("head"), lax.axis_size("head")


def meet_heads(me, count):
    barrier = pltpu.get_barrier_semaphore()
    for d in range(1, count):
        pl.semaphore_signal(barrier, inc=1, device_id={"head": lax.rem(me + d, count)}, device_id_type=MESH)
    pl.semaphore_wait(barrier, count - 1)


def push_head(src, dst, send_sem, recv_sem, target):
    return pltpu.make_async_remote_copy(
        src_ref=src, dst_ref=dst, send_sem=send_sem, recv_sem=recv_sem,
        device_id={"head": target}, device_id_type=MESH)


def row_totals(first, second):
    ones = jnp.ones((8, first.shape[1]), f32)

    def total(x):
        return lax.dot_general(ones, x, (((1,), (1,)), ((), ())), precision=lax.Precision.HIGHEST,
                               preferred_element_type=f32)

    top, low = total(first), total(second)
    row = lax.broadcasted_iota(jnp.int32, top.shape, 0)
    return jnp.where(row == 0, top, low)


def mid_kernel(count, mixed_ref, x_ref, ct_ref, gate_pre_ref, normed_ref, w_out_ref, w_gate_ref, w_up_ref, w_down_ref,
               post_gain_ref, post_bias_ref, ffn_gain_ref,
               gm_ref, early_ref, ggp_ref, out_ref, rco_ref, grc_ref, small_ref,
               st_mine, st_got, pa_mine, pa_got, nt_all, rc_mine, rc_all, gn_mine, gn_got, dn_mine, dn_got, gov_all,
               gc_mine, gc_all, sb_mine, sb_got, gt_all, gh, gated, hidden, ggv, guv, resid,
               st_s, st_r, pa_s, pa_r, nt_s, nt_r, rc_s, rc_r, gn_s, gn_r, dn_s, dn_r, go_s, go_r, gc_s, gc_r, sb_s, sb_r,
               gt_s, gt_r):
    me, _ = head_place()
    heads, rows, width = mixed_ref.shape
    cols = heads * width
    full = cols * count
    part = rows // count
    peers = [(d, lax.rem(me + d, count)) for d in range(1, count)]
    meet_heads(me, count)

    def rows_of(device):
        return pl.ds(pl.multiple_of(device * part, part), part)

    def send_all(src, dst, send, recv):
        for d, peer in peers:
            push_head(src, dst.at[d - 1], send.at[d - 1], recv.at[d - 1], peer).start()

    def wait_all(src, dst, send, recv):
        for d, peer in peers:
            push_head(src, dst.at[d - 1], send.at[d - 1], recv.at[d - 1], peer).wait()

    z = jnp.concatenate([mixed_ref[j] for j in range(heads)], axis=1).astype(f32)
    st_mine[...] = row_totals(z, z * z)
    send_all(st_mine, st_got, st_s, st_r)
    gate_pre = gate_pre_ref[...]
    gate_act, gate_der = gelu_first(gate_pre)
    gh[...] = dot_nt(ct_ref[...], w_down_ref[...])
    wait_all(st_mine, st_got, st_s, st_r)
    tot = st_mine[...]
    for d, _ in peers:
        tot = tot + st_got[d - 1]
    tot = tot.T * (1.0 / full)
    mean_z = tot[:, 0:1]
    inv_z = lax.rsqrt(tot[:, 1:2] - mean_z * mean_z + eps_norm)
    z_hat = (z - mean_z) * inv_z
    post_out = z_hat * post_gain_ref[...] + post_bias_ref[...]
    gated[...] = (post_out * gate_act).astype(bf16)

    def spread_rows(make, mine, got, send, recv):
        pending = None
        for d, peer in peers:
            mine[d - 1] = make(rows_of(peer)).astype(bf16)
            if pending is not None:
                pending.start()
            pending = push_head(mine.at[d - 1], got.at[d - 1], send.at[d - 1], recv.at[d - 1], peer)
        own = make(rows_of(me))
        pending.start()
        return own

    def add_rows(own, mine, got, send, recv):
        for d, peer in peers:
            push_head(mine.at[d - 1], got.at[d - 1], send.at[d - 1], recv.at[d - 1], peer).wait()
            own = own + got[d - 1].astype(f32)
        return own

    def gather_rows(all_ref, send, recv):
        for d, peer in peers:
            view = all_ref.at[rows_of(me), :]
            push_head(view, view, send.at[d - 1], recv.at[d - 1], peer).start()

    def gather_wait(all_ref, send, recv):
        for d, peer in peers:
            view = all_ref.at[rows_of(me), :]
            push_head(view, view, send.at[d - 1], recv.at[d - 1], peer).wait_send()
            await_bytes(all_ref.at[rows_of(lax.rem(me + count - d, count)), :], recv.at[d - 1])

    def turn_columns(value, mine, all_ref, send, recv):
        for b in range(count):
            mine[b] = value[:, b * cols : (b + 1) * cols]
        all_ref[rows_of(me), :] = mine[me]

    def turn_start(mine, all_ref, send, recv):
        for d, peer in peers:
            push_head(mine.at[peer], all_ref.at[rows_of(me), :], send.at[d - 1], recv.at[d - 1], peer).start()

    def turn_wait(mine, all_ref, send, recv):
        for d, peer in peers:
            push_head(mine.at[peer], all_ref.at[rows_of(me), :], send.at[d - 1], recv.at[d - 1], peer).wait_send()
            await_bytes(all_ref.at[rows_of(lax.rem(me + count - d, count)), :], recv.at[d - 1])

    w_out = w_out_ref[...]
    own = spread_rows(lambda r: dot_nn(gated[r, :], w_out), pa_mine, pa_got, pa_s, pa_r)
    res = x_ref[rows_of(me), :].astype(f32) + add_rows(own, pa_mine, pa_got, pa_s, pa_r)
    rms_two = lax.rsqrt(mean_row(res * res) + eps_norm)
    ffn_gain = ffn_gain_ref[...]
    nt_all[rows_of(me), :] = (res * rms_two * ffn_gain).astype(bf16)
    turn_columns(res, rc_mine, rc_all, rc_s, rc_r)
    resid[...] = res
    gather_rows(nt_all, nt_s, nt_r)
    turn_start(rc_mine, rc_all, rc_s, rc_r)
    gather_wait(nt_all, nt_s, nt_r)
    def forward_rows(b, _):
        r = pl.ds(pl.multiple_of(b * part, part), part)
        nt = nt_all[r, :]
        gate_val = dot_nn(nt, w_gate_ref[...])
        up_val = dot_nn(nt, w_up_ref[...])
        sig = 1.0 / (1.0 + jnp.exp(-gate_val))
        silu = gate_val * sig
        hidden[r, :] = (silu * up_val).astype(bf16)
        g = gh[r, :]
        ggv[r, :] = (g * up_val * sig * (1.0 + gate_val * (1.0 - sig))).astype(bf16)
        guv[r, :] = (g * silu).astype(bf16)
        return 0

    lax.fori_loop(0, count, forward_rows, 0)
    own = spread_rows(lambda r: dot_nt(ggv[r, :], w_gate_ref[...]) + dot_nt(guv[r, :], w_up_ref[...]),
                      gn_mine, gn_got, gn_s, gn_r)
    for b in range(count):
        r = pl.ds(b * part, part)
        down = dot_nn(hidden[r, :], w_down_ref[...]).astype(bf16)
        for c in range(count):
            dn_mine[c, r, :] = down[:, c * cols : (c + 1) * cols]
    ffn = w_gate_ref.shape[1]
    half = full // 2
    for b in range(2):
        r = slice(b * half, (b + 1) * half)
        early_ref[r, 0:ffn] = dot_tn(nt_all[:, r], ggv[...]).astype(bf16)
    for d, peer in peers:
        push_head(dn_mine.at[peer], dn_got.at[d - 1], dn_s.at[d - 1], dn_r.at[d - 1], peer).start()
    gnt = add_rows(own, gn_mine, gn_got, gn_s, gn_r)
    res = resid[...]
    rms_two = lax.rsqrt(mean_row(res * res) + eps_norm)
    scaled = gnt * ffn_gain
    grad_res = ct_ref[rows_of(me), :].astype(f32) + rms_two * (
        scaled - res * rms_two * rms_two * mean_row(scaled * res))
    gov_all[rows_of(me), :] = grad_res.astype(bf16)
    gt_all[me] = jnp.broadcast_to(jnp.sum(gnt * res * rms_two, axis=0, keepdims=True), gt_all.shape[1:])
    turn_columns(grad_res, gc_mine, gc_all, gc_s, gc_r)
    gather_rows(gov_all, go_s, go_r)
    turn_start(gc_mine, gc_all, gc_s, gc_r)
    for d, peer in peers:
        push_head(gt_all.at[me], gt_all.at[me], gt_s.at[d - 1], gt_r.at[d - 1], peer).start()
    for b in range(2):
        r = slice(b * half, (b + 1) * half)
        early_ref[r, ffn : 2 * ffn] = dot_tn(nt_all[:, r], guv[...]).astype(bf16)
    gather_wait(gov_all, go_s, go_r)
    gov = gov_all[...]
    grad_gated = dot_nt(gov, w_out_ref[...])
    grad_post = grad_gated * gate_act
    grad_zhat = grad_post * post_gain_ref[...]
    sb_mine[...] = row_totals(grad_zhat, grad_zhat * z_hat)
    ggp = (grad_gated * post_out * gate_der).astype(bf16)
    ggp_ref[...] = ggp
    send_all(sb_mine, sb_got, sb_s, sb_r)
    early_ref[:, 3 * ffn : 3 * ffn + 2 * cols] = jnp.concatenate(
        [dot_tn(normed_ref[...], ggp).astype(bf16), dot_tn(gov, gated[...]).astype(bf16)], axis=1)
    row = lax.broadcasted_iota(jnp.int32, (8, cols), 0)
    wait_all(sb_mine, sb_got, sb_s, sb_r)
    tot = sb_mine[...]
    for d, _ in peers:
        tot = tot + sb_got[d - 1]
    tot = tot.T * (1.0 / full)
    grad_mixed = (inv_z * (grad_zhat - tot[:, 0:1] - z_hat * tot[:, 1:2])).astype(bf16)
    for j in range(heads):
        gm_ref[j] = grad_mixed[:, j * width : (j + 1) * width]
    for b in range(2):
        r = slice(b * half, (b + 1) * half)
        early_ref[r, 2 * ffn : 3 * ffn] = dot_tn(ct_ref[:, r], hidden[...]).astype(bf16)
    turn_wait(rc_mine, rc_all, rc_s, rc_r)
    rco_ref[...] = rc_all[...]
    out = dn_mine[me].astype(f32)
    for d, peer in peers:
        push_head(dn_mine.at[peer], dn_got.at[d - 1], dn_s.at[d - 1], dn_r.at[d - 1], peer).wait()
        out = out + dn_got[d - 1].astype(f32)
    out_ref[...] = out
    turn_wait(gc_mine, gc_all, gc_s, gc_r)
    grc_ref[...] = gc_all[...]
    for d, peer in peers:
        push_head(gt_all.at[me], gt_all.at[me], gt_s.at[d - 1], gt_r.at[d - 1], peer).wait_send()
        await_bytes(gt_all.at[lax.rem(me + count - d, count)], gt_r.at[d - 1])
    gain_two = gt_all[0]
    for b in range(1, count):
        gain_two = gain_two + gt_all[b]
    post = jnp.where(row == 1, jnp.sum(grad_post * z_hat, axis=0, keepdims=True),
                     jnp.sum(grad_post, axis=0, keepdims=True))
    line = lax.broadcasted_iota(jnp.int32, (8, full), 0)
    small_ref[...] = jnp.where(
        line == 0, gain_two, jnp.concatenate([post] + [jnp.zeros_like(post)] * (count - 1), axis=1))


def middle(mixed, x, ct, gate_pre, normed, w_out, w_gate, w_up, w_down, post_gain, post_bias, ffn_gain):
    count = lax.axis_size("head")
    heads, rows, width = mixed.shape
    cols = heads * width
    full = cols * count
    part = rows // count
    ffn = w_gate.shape[1]
    ins = (mixed, x, ct, gate_pre, normed, w_out, w_gate, w_up, w_down, post_gain, post_bias, ffn_gain)
    vmem = pl.BlockSpec(memory_space=pltpu.VMEM)
    V = pltpu.VMEM
    trio = count - 1
    sem = pltpu.SemaphoreType.DMA((trio,))
    return pl.pallas_call(
        functools.partial(mid_kernel, count),
        in_specs=[vmem] * len(ins),
        out_specs=[vmem] * 7,
        out_shape=[jax.ShapeDtypeStruct((heads, rows, width), bf16),
                   jax.ShapeDtypeStruct((full, 3 * ffn + 2 * cols), bf16),
                   jax.ShapeDtypeStruct((rows, cols), bf16),
                   jax.ShapeDtypeStruct((rows, cols), f32),
                   jax.ShapeDtypeStruct((rows, cols), f32),
                   jax.ShapeDtypeStruct((rows, cols), f32),
                   jax.ShapeDtypeStruct((8, full), f32)],
        scratch_shapes=[
            V((8, rows), f32), V((trio, 8, rows), f32),
            V((trio, part, full), bf16), V((trio, part, full), bf16),
            V((rows, full), bf16),
            V((count, part, cols), f32), V((rows, cols), f32),
            V((trio, part, full), bf16), V((trio, part, full), bf16),
            V((count, rows, cols), bf16), V((trio, rows, cols), bf16),
            V((rows, full), bf16),
            V((count, part, cols), f32), V((rows, cols), f32),
            V((8, rows), f32), V((trio, 8, rows), f32),
            V((count, 8, full), f32),
            V((rows, ffn), f32), V((rows, cols), bf16),
            V((rows, ffn), bf16), V((rows, ffn), bf16), V((rows, ffn), bf16),
            V((part, full), f32)] + [sem] * 20,
        compiler_params=pltpu.CompilerParams(
            collective_id=2, has_side_effects=True, vmem_limit_bytes=56 * 1024 * 1024),
        name="middle",
    )(*ins)


def tail_kernel(count, at_mix, grads_ref, packed_w_ref, mix_gate_ref, ggp_ref, x_ref, pre_gain_ref, cols_ref, early_ref,
                late_ref, back_ref, tiles_ref,
                near, mine, got, tile, tile_got, near_sem, ib_s, ib_r, th_s, th_r, ts_s, ts_r, ts_loc):
    me, _ = head_place()
    pos, base = seq_place()
    heads = grads_ref.shape[0]
    rows = x_ref.shape[0]
    cols = ggp_ref.shape[1]
    full = x_ref.shape[1]
    share = early_ref.shape[0]
    rate_lane = PACK - PACK // 4
    peers = [(d, lax.rem(me + d, count)) for d in range(1, count)]
    barrier = pltpu.get_barrier_semaphore()
    for d, peer in peers:
        pl.semaphore_signal(barrier, inc=1, device_id={"head": peer}, device_id_type=MESH)
    for d in range(1, CHAIN):
        pl.semaphore_signal(
            barrier, inc=1, device_id={"seq": base + lax.rem(pos + d, CHAIN)}, device_id_type=MESH)
    pl.semaphore_wait(barrier, count - 1 + CHAIN - 1)
    here = pl.ds(pl.multiple_of(pos * rows, rows), rows)
    part = rows // count

    def back_rows(b, _):
        r = pl.ds(pl.multiple_of(b * part, part), part)
        away = pl.ds(pl.multiple_of(pos * rows + b * part, part), part)
        grad = dot_nt(ggp_ref[r, :], mix_gate_ref[...])
        for j in range(heads):
            grad = grad + dot_nt(grads_ref[j, away, :], packed_w_ref[:, j * PACK : (j + 1) * PACK])
        x = x_ref[r, :].astype(f32)
        rms = lax.rsqrt(mean_row(x * x) + eps_norm)
        scaled = grad * pre_gain_ref[...]
        back = (rms * (scaled - x * rms * rms * mean_row(scaled * x))).astype(bf16)
        for c in range(count):
            mine[c, r, :] = back[:, c * cols : (c + 1) * cols]
        return 0

    lax.fori_loop(0, count, back_rows, 0)
    turned = cols_ref[...]
    ones = jnp.ones((MINI, turned.shape[0]), bf16)
    lane = lax.broadcasted_iota(jnp.int32, (share, 128), 1)
    spot = lax.broadcasted_iota(jnp.int32, (8, 128), 1)
    line = lax.broadcasted_iota(jnp.int32, (8, 128), 0)
    w_rows = pl.ds(pl.multiple_of(pos * share, share), share)
    gain = jnp.sum(early_ref[:, at_mix : at_mix + cols] * mix_gate_ref[w_rows, :].astype(f32), axis=1, keepdims=True)
    table = jnp.zeros((share, 128), f32)
    extra = jnp.zeros((8, 128), f32)
    for j in range(heads):
        late = dot_tn(turned, grads_ref[j])
        late_ref[j] = late
        gain = gain + jnp.sum(
            late * packed_w_ref[w_rows, j * PACK : (j + 1) * PACK].astype(f32), axis=1, keepdims=True)
        rate = late[:, rate_lane : rate_lane + 1] + late[:, rate_lane + 1 : rate_lane + 2]
        table = jnp.where(lane == j, rate, table)
        if j == 0:
            for d, peer in peers:
                push_head(mine.at[peer], got.at[d - 1], ib_s.at[d - 1], ib_r.at[d - 1], peer).start()
        total = dot_nn(ones, grads_ref[j])[0:8]
        total = total[:, rate_lane : rate_lane + 1] + total[:, rate_lane + 1 : rate_lane + 2]
        extra = jnp.where((line == heads + 1) & (spot == j), total, extra)
    table = jnp.where(lane == heads, gain, table)
    flat = jnp.concatenate([table, jnp.zeros((128 - share, 128), f32)], axis=0).T[0:8]
    tile[...] = flat + extra
    for d, peer in peers:
        push_head(tile, tile_got.at[d - 1], th_s.at[d - 1], th_r.at[d - 1], peer).start()
    back = mine[me].astype(f32)
    for d, peer in peers:
        push_head(tile, tile_got.at[d - 1], th_s.at[d - 1], th_r.at[d - 1], peer).wait()
    summed = flat
    for d, peer in peers:
        summed = summed + tile_got[d - 1]
    tile[...] = jnp.where(line == heads, summed, flat + extra)
    for d in range(1, CHAIN):
        push(tile, tiles_ref.at[pos], ts_s.at[d - 1], ts_r.at[d - 1], base + lax.rem(pos + d, CHAIN)).start()
    pltpu.make_async_copy(tile, tiles_ref.at[pos], ts_loc).start()
    for d, peer in peers:
        push_head(mine.at[peer], got.at[d - 1], ib_s.at[d - 1], ib_r.at[d - 1], peer).wait()
        back = back + got[d - 1].astype(f32)
    back_ref[...] = back
    for d in range(1, CHAIN):
        push(tile, tiles_ref.at[pos], ts_s.at[d - 1], ts_r.at[d - 1], base + lax.rem(pos + d, CHAIN)).wait_send()
        await_bytes(tiles_ref.at[lax.rem(pos + CHAIN - d, CHAIN)], ts_r.at[d - 1])
    await_bytes(tiles_ref.at[pos], ts_loc)


def tail(at_mix, grads, packed_w, mix_gate, ggp, x, pre_gain, cols, early):
    count = lax.axis_size("head")
    heads, tokens, _ = grads.shape
    rows, full = x.shape
    width = ggp.shape[1]
    share = early.shape[0]
    vmem = pl.BlockSpec(memory_space=pltpu.VMEM)
    V = pltpu.VMEM
    dma = pltpu.SemaphoreType.DMA
    trio, seven = dma((count - 1,)), dma((CHAIN - 1,))
    return pl.pallas_call(
        functools.partial(tail_kernel, count, at_mix),
        in_specs=[vmem] * 8,
        out_specs=[vmem] * 3,
        out_shape=[jax.ShapeDtypeStruct((heads, share, PACK), f32),
                   jax.ShapeDtypeStruct((rows, width), f32),
                   jax.ShapeDtypeStruct((CHAIN, 8, 128), f32)],
        scratch_shapes=[V((8, 128), f32), V((count, rows, width), bf16), V((count - 1, rows, width), bf16),
                        V((8, 128), f32), V((count - 1, 8, 128), f32),
                        dma, trio, trio, trio, trio, seven, seven, dma],
        compiler_params=pltpu.CompilerParams(
            collective_id=3, has_side_effects=True, vmem_limit_bytes=56 * 1024 * 1024),
        name="tail",
    )(grads, packed_w, mix_gate, ggp, x, pre_gain, cols, early)


def final_kernel(at_mix, ffn, down_ref, resid_ref, back_ref, grc_ref, late_ref, early_ref, ends_ref, tiles_ref, small_ref,
                 out_ref, gin_ref, gq_ref, gk_ref, gv_ref, gmix_ref, rate_ref, gwout_ref, gwg_ref, gwu_ref, gwd_ref,
                 w1_ref, b1_ref, w2_ref, b2_ref, ig_ref, ib_ref, vec_ref):
    heads, width, hidden = w1_ref.shape
    cols = heads * width
    out_ref[...] = down_ref[...] + resid_ref[...]
    gin_ref[...] = back_ref[...] + grc_ref[...]
    for i, ref in enumerate((gq_ref, gk_ref, gv_ref)):
        ref[...] = jnp.concatenate([late_ref[j, :, i * width : (i + 1) * width] for j in range(heads)], axis=1)
    gwg_ref[...] = early_ref[:, 0:ffn]
    gwu_ref[...] = early_ref[:, ffn : 2 * ffn]
    gwd_ref[...] = early_ref[:, 2 * ffn : 3 * ffn].T
    both = early_ref[:, at_mix : at_mix + 2 * cols]
    gmix_ref[...] = both[:, 0:cols]
    gwout_ref[...] = both[:, cols:].T
    for j in range(heads):
        w1_ref[j] = ends_ref[j, 0:width, :].astype(f32)
        b1_ref[pl.ds(j, 1), :] = ends_ref[j, width : AUG, :].astype(f32)[0:1]
        second = ends_ref[j, AUG : AUG + width, :].astype(f32)
        w2_ref[j] = (second - jnp.mean(second, axis=0, keepdims=True)).T
        rest = ends_ref[j, AUG + width :, :].astype(f32)[0:8, 0:width]
        b2_ref[pl.ds(j, 1), :] = rest[0:1] - mean_row(rest[0:1])
        ig_ref[pl.ds(j, 1), :] = rest[1:2]
        ib_ref[pl.ds(j, 1), :] = rest[2:3]
    each = rate_ref.shape[0] // CHAIN
    for p in range(CHAIN):
        turned = jnp.concatenate([tiles_ref[p]] * 16, axis=0).T
        rate_ref[pl.ds(p * each, each), :] = turned[0:each, 0:heads]
    acc = small_ref[0]
    for p in range(1, CHAIN):
        acc = acc + small_ref[p]
    vec_ref[...] = acc


def finish(at_mix, ffn, down, resid, back, grc, late, early, ends, tiles, small, shapes):
    ins = (down, resid, back, grc, late, early, ends, tiles, small)
    vmem = pl.BlockSpec(memory_space=pltpu.VMEM)
    return pl.pallas_call(
        functools.partial(final_kernel, at_mix, ffn),
        in_specs=[vmem] * len(ins),
        out_specs=[vmem] * len(shapes),
        out_shape=[jax.ShapeDtypeStruct(s, f32) for s in shapes],
        compiler_params=pltpu.CompilerParams(vmem_limit_bytes=48 * 1024 * 1024),
        name="final",
    )(*ins)


def stretch_groups(axis):
    count = lax.axis_size(axis)
    return [[start + step for step in range(0, count, CHAIN)] for start in range(CHAIN)]


def bf_product(form, left, right):
    return jnp.einsum(form, left, right, preferred_element_type=f32)


def local(
    inputs,
    pre_gain,
    w_query,
    w_key,
    w_value,
    mix_gate,
    w_rate,
    rate_bias,
    inner_gain,
    inner_bias,
    init_w_one,
    init_b_one,
    init_w_two,
    init_b_two,
    post_gain,
    post_bias,
    w_out,
    ffn_gain,
    w_gate,
    w_up,
    w_down,
    cotangent,
):
    full_width = pre_gain.shape[0]
    rows, local_cols = inputs.shape
    heads, head_dim = inner_gain.shape
    head_index = lax.axis_index("head")
    whole_low = lax.all_gather(inputs, "head", axis=1, tiled=True)
    whole_in = whole_low.astype(f32)
    grad_whole = lax.all_gather(cotangent, "head", axis=1, tiled=True)
    rms_one = lax.rsqrt(jnp.mean(whole_in * whole_in, axis=1, keepdims=True) + eps_norm)
    normed_one = (whole_in * rms_one * pre_gain).astype(bf16)
    stretches = lax.axis_size("seq") // CHAIN
    spare = PACK - 3 * head_dim

    def by_head(weight):
        return weight.reshape(full_width, heads, -1)

    rate_cols = by_head(w_rate)
    packed_w = jnp.concatenate(
        [by_head(w_query), by_head(w_key), by_head(w_value), rate_cols, rate_cols,
         jnp.zeros((full_width, heads, spare - 2), bf16)], axis=2).reshape(full_width, heads * PACK)
    lane = lax.broadcasted_iota(jnp.int32, (1, heads, PACK), 2)
    rate_lane = (lane == 3 * head_dim) | (lane == 3 * head_dim + 1)
    packed_bias = jnp.where(rate_lane, rate_bias[None, :, None], 0.0).reshape(1, heads * PACK)
    low_lane = (lane == 3 * head_dim + 1).reshape(1, heads * PACK)
    pre = bf_product("rd,dc->rc", normed_one, packed_w) + packed_bias
    payload = (pre - jnp.where(low_lane, lax.reduce_precision(pre, 8, 7), 0.0)).astype(bf16)
    gate_pre = bf_product("rd,dc->rc", normed_one, mix_gate)
    share = full_width // CHAIN
    mixed_h, normed_cols, *saved = chain_forward(
        payload, normed_one.reshape(rows, CHAIN, share).transpose(1, 0, 2), init_w_one, init_b_one, init_w_two, init_b_two, inner_gain, inner_bias)
    ffn = w_gate.shape[1]
    at_mix = 3 * ffn
    grad_mixed, early, grad_gate_pre, down_cols, resid_cols, grad_resid_cols, small = middle(
        mixed_h, whole_low, grad_whole, gate_pre, normed_one, w_out, w_gate, w_up, w_down,
        post_gain[None], post_bias[None], ffn_gain[None])
    grads, ends, early_sum, small = chain_backward(
        grad_mixed, early.reshape(CHAIN // 2, 2, share, early.shape[1]), small, inner_gain, inner_bias, saved)
    late, back_cols, tiles = tail(
        at_mix, grads, packed_w, mix_gate, grad_gate_pre, whole_low, pre_gain[None],
        normed_cols.reshape(CHAIN * rows, share), early_sum)
    if stretches > 1:
        groups = stretch_groups("seq")
        ends, tiles, small = lax.psum((ends.astype(f32), tiles, small), "seq", axis_index_groups=groups)
        seq_index = lax.axis_index("seq")
        stretch_lists = [list(range(s, s + CHAIN)) for s in range(0, stretches * CHAIN, CHAIN)]

        def spread(mine_rows):
            summed = lax.psum(mine_rows, "seq", axis_index_groups=groups)
            total = lax.all_gather(
                summed, "seq", axis=summed.ndim - 2, tiled=True, axis_index_groups=stretch_lists)
            return lax.dynamic_slice_in_dim(
                total, seq_index * (share // stretches), share // stretches, summed.ndim - 2)

        late = spread(late)
        early_sum = spread(early_sum)
    held = share // stretches
    hidden = init_w_one.shape[2]
    square = (held, local_cols)
    (outputs, grad_inputs, grad_q, grad_k, grad_v, grad_mix, grad_rate_w, grad_w_out, grad_w_gate, grad_w_up, grad_w_down,
     grad_one, grad_b_one, grad_two, grad_b_two, grad_gain, grad_bias, vectors) = finish(
        at_mix, ffn, down_cols, resid_cols, back_cols, grad_resid_cols, late, early_sum, ends, tiles, small,
        ((rows, local_cols), (rows, local_cols), square, square, square, square, (full_width, heads),
         (local_cols, held), (held, ffn), (held, ffn), (ffn, held),
         (heads, head_dim, hidden), (heads, hidden), (heads, hidden, head_dim), (heads, head_dim),
         (heads, head_dim), (heads, head_dim), (8, full_width)))
    gain_all = tiles[:, heads, :share].reshape(full_width) / pre_gain
    gain_one = lax.dynamic_slice_in_dim(gain_all, head_index * local_cols, local_cols, 0)
    return (
        outputs,
        grad_inputs,
        gain_one,
        grad_q,
        grad_k,
        grad_v,
        grad_mix,
        grad_rate_w,
        tiles[0, heads + 1, :heads],
        grad_gain,
        grad_bias,
        grad_one,
        grad_b_one,
        grad_two,
        grad_b_two,
        vectors[1, :local_cols],
        vectors[2, :local_cols],
        grad_w_out,
        vectors[0],
        grad_w_gate,
        grad_w_up,
        grad_w_down,
    )


def solution(mesh):
    in_specs = (
        P("seq", "head"),
        P(),
        P(None, "head"),
        P(None, "head"),
        P(None, "head"),
        P(None, "head"),
        P(None, "head"),
        P("head"),
        P("head", None),
        P("head", None),
        P("head", None, None),
        P("head", None),
        P("head", None, None),
        P("head", None),
        P("head"),
        P("head"),
        P("head", None),
        P(),
        P(None, "head"),
        P(None, "head"),
        P("head", None),
        P("seq", "head"),
    )
    out_specs = (
        P("seq", "head"),
        P("seq", "head"),
        P("head"),
        P("seq", "head"),
        P("seq", "head"),
        P("seq", "head"),
        P("seq", "head"),
        P(None, "head"),
        P("head"),
        P("head", None),
        P("head", None),
        P("head", None, None),
        P("head", None),
        P("head", None, None),
        P("head", None),
        P("head"),
        P("head"),
        P("head", "seq"),
        P(),
        P("seq", "head"),
        P("seq", "head"),
        P("head", "seq"),
    )
    return jax.shard_map(local, mesh=mesh, in_specs=in_specs, out_specs=out_specs, check_vma=False)
```

```python
import functools

import jax
import jax.numpy as jnp
from jax import lax
from jax.experimental import pallas as pl
from jax.experimental.pallas import tpu as pltpu
from jax.sharding import PartitionSpec as P

MINI = 16
CHAIN = 8
FIRST = 2
AUG = 80
eps_norm = 1e-06
gelu_scale = 0.7978845608028654
f32 = jnp.float32
bf16 = jnp.bfloat16


def dot_nn(a, b):
    return lax.dot_general(a, b, (((1,), (0,)), ((), ())), preferred_element_type=f32)


def dot_nt(a, b):
    return lax.dot_general(a, b, (((1,), (1,)), ((), ())), preferred_element_type=f32)


def dot_tn(a, b):
    return lax.dot_general(a, b, (((0,), (0,)), ((), ())), preferred_element_type=f32)


def mean_row(x):
    return jnp.sum(x, axis=1, keepdims=True) * (1.0 / x.shape[1])


def gelu_first(z):
    sq = z * z
    th = jnp.tanh(gelu_scale * z * (1.0 + 0.044715 * sq))
    half = 0.5 * (1.0 + th)
    act = z * half
    der = half + (0.5 * gelu_scale) * z * (1.0 - th * th) * (1.0 + 0.134145 * sq)
    return act, der


def gelu_second(z):
    sq = z * z
    th = jnp.tanh(gelu_scale * z * (1.0 + 0.044715 * sq))
    half = 0.5 * (1.0 + th)
    act = z * half
    slope = gelu_scale * (1.0 + 0.134145 * sq)
    sech = 1.0 - th * th
    der = half + 0.5 * z * sech * slope
    curve = sech * (slope + z * (0.5 * gelu_scale * 0.26829 * z) - z * th * slope * slope)
    return act, der, curve


def tri_mask():
    rows = lax.broadcasted_iota(jnp.int32, (MINI, MINI), 0)
    cols = lax.broadcasted_iota(jnp.int32, (MINI, MINI), 1)
    return jnp.where(rows >= cols, 1.0, 0.0).astype(f32)


def inner_target_grad(z, base, gain_sq, rate):
    mz = mean_row(z)
    m_zz = mean_row(z * z)
    zg = z * gain_sq
    m_zg = mean_row(zg)
    m_zzg = mean_row(zg * z)
    m_zb = mean_row(z * base)
    m_b = mean_row(base)
    m_sq = mean_row(gain_sq)
    inv = lax.rsqrt(m_zz - mz * mz + eps_norm)
    c_zg = m_zg - mz * m_sq
    c_zzg = m_zzg - mz * (m_zg + c_zg)
    c_zb = m_zb - mz * m_b
    m_g = inv * c_zg + m_b
    m_gn = inv * (inv * c_zzg + c_zb)
    zc = z - mz
    n = zc * inv
    grad = inv * (n * (gain_sq - m_gn) + (base - m_g))
    return rate * grad, zc


def forward_step(state, z1, key_aug, key_next, query_aug, base, rate, gain, gain_sq, bias, tri):
    w1, w2t, b2 = state
    act, der = gelu_first(z1)
    act_h = act.astype(bf16)
    w1_h = w1.astype(bf16)
    w2_h = w2t.astype(bf16)
    s2, zc = inner_target_grad(dot_nt(act_h, w2_h) + b2, base, gain_sq, rate)
    s2_h = s2.astype(bf16)
    upd = dot_nn(s2_h, w2_h)
    s1_h = (upd * der).astype(bf16)
    both = jnp.concatenate([key_next, query_aug], axis=0)
    coef = dot_nt(both, key_aug)
    coef = jnp.concatenate([coef[:MINI], coef[MINI:] * tri], axis=0)
    zz = dot_nn(both, w1_h) - dot_nn(coef.astype(bf16), s1_h)
    z1_next = zz[:MINI]
    z1b = zz[MINI:]
    new_w1 = w1 - dot_tn(key_aug, s1_h)
    new_w2t = w2t - dot_tn(s2_h, act_h)
    new_b2 = b2 - jnp.sum(s2, axis=0, keepdims=True)
    actb, _ = gelu_first(z1b)
    actb_h = actb.astype(bf16)
    att = (dot_nt(actb_h, act_h) + 1.0) * tri
    z2b = dot_nt(actb_h, w2_h) + b2 - dot_nn(att.astype(bf16), s2_h)
    z2b = z2b - mean_row(z2b)
    invb = lax.rsqrt(mean_row(z2b * z2b) + eps_norm)
    out = z2b * invb * gain + bias
    return (new_w1, new_w2t, new_b2), z1_next, out, (w1_h, w2_h, upd, zc, s2, z1b, z2b)


def prepare_back(store, saved, d_out, key_aug, query_aug, target, rate, gain, gain_sq, bias, tri):
    w1_h, w2_h, z1, upd, zc, s2, z1b, z2b = saved
    width = gain.shape[1]
    s2_h = s2.astype(bf16)
    actb, derb = gelu_first(z1b)
    actb_h = actb.astype(bf16)
    invb = lax.rsqrt(mean_row(z2b * z2b) + eps_norm)
    dn = d_out * gain
    m_dn = mean_row(dn)
    yield
    act, der, curve = gelu_second(z1)
    act_h = act.astype(bf16)
    s1_h = (upd * der).astype(bf16)
    store.update(act=act_h, der=der, bend=upd * curve, actb=actb_h, s1=s1_h, s2=s2_h)
    yield
    att2 = dot_nt(actb_h, act_h)
    att1 = dot_nt(query_aug, key_aug)
    nb = z2b * invb
    d_z2b = invb * (dn - m_dn - nb * mean_row(dn * nb))
    d_z2b_h = d_z2b.astype(bf16)
    yield
    inv = lax.rsqrt(mean_row(zc * zc) + eps_norm)
    d_att2 = dot_nt(d_z2b_h, s2_h)
    d_actb = dot_nn(d_z2b_h, w2_h)
    base = (bias - target) * gain
    m_sq = mean_row(gain_sq)
    yield
    att2 = ((att2 + 1.0) * tri).astype(bf16)
    att1 = (att1 * tri).astype(bf16)
    n = zc * inv
    ng = n * gain_sq
    big_g = ng + base
    m_g = mean_row(big_g)
    m_gn = mean_row(big_g * n)
    yield
    d_att2 = (-d_att2 * tri).astype(bf16)
    d_actb = d_actb + dot_nn(d_att2, act_h)
    c2 = dot_tn(att2, d_z2b_h)
    m_ng = mean_row(ng)
    m_nng = mean_row(n * ng)
    yield
    c3 = dot_tn(d_att2, actb_h)
    inv2 = inv * inv
    g = inv * (big_g - m_g - n * m_gn)
    fac = rate * inv2 * (gain_sq - m_gn)
    scale = rate * (1.0 / width)
    weights = (jnp.broadcast_to(scale, n.shape), scale * n, scale * gain_sq, scale * (ng * inv2 + g * inv))
    store.update(c2=c2, c3=c3, fac=fac, weights=weights, inv=inv, inv2=inv2, n=n)
    yield
    d_z1b_h = (d_actb * derb).astype(bf16)
    c1 = dot_tn(att1, d_z1b_h)
    row1 = inv2 * (gain_sq - (m_sq + m_gn) - n * m_ng)
    row2 = inv2 * (ng + big_g - (m_ng + m_g) - n * (m_nng + 2.0 * m_gn))
    store.update(dz2b=d_z2b_h, dz2bf=d_z2b, dz1b=d_z1b_h, c1=c1, row1=row1, row2=row2)
    yield
    fixed = dot_nn(jnp.concatenate([row1, row2, jnp.broadcast_to(inv2, n.shape), n], axis=0).astype(bf16), w2_h)
    d_att1 = dot_nt(d_z1b_h, s1_h)
    d_query = dot_nt(d_z1b_h, w1_h)
    yield
    prods = tuple(fixed[i * MINI : (i + 1) * MINI] for i in range(4))
    store.update(prods=prods)
    d_att1 = (-d_att1 * tri).astype(bf16)
    d_query = (d_query + dot_nn(d_att1, key_aug))[:, :width] + d_out
    d_key = dot_tn(d_att1, query_aug)[:, :width]
    yield
    d_gain = jnp.sum(d_out * nb, axis=0, keepdims=True)
    d_bias = jnp.sum(d_out, axis=0, keepdims=True)
    store.update(dq=d_query, dk=d_key, d_gain=d_gain, d_bias=d_bias, rate=rate, w1=w1_h, w2=w2_h, s2f=s2,
                 key=key_aug, query=query_aug, gslope=2.0 * n * gain + bias - target)
    yield


PIECES = 11


def settle(post, width):
    if post is None:
        return
    pre, d_s2, a1, a2, d_z1_h, p1_h, keep, gain, sink = post
    d_g = pre["inv"] * (pre["rate"] * d_s2 - a1 - pre["n"] * a2)
    d_gg = d_g * gain
    key_part = dot_nt(d_z1_h, pre["w1"])
    late_part = dot_nt(pre["s1"], p1_h)
    d_logit = keep * jnp.sum(d_s2 * pre["s2f"], axis=1, keepdims=True)
    yield
    d_gain = pre["d_gain"] + jnp.sum(d_g * pre["gslope"], axis=0, keepdims=True)
    d_bias = pre["d_bias"] + jnp.sum(d_gg, axis=0, keepdims=True)
    d_key = pre["dk"] + d_gg + (key_part - late_part)[:, :width]
    sink(pre["dq"], d_key, -d_gg, d_logit, d_gain, d_bias)
    yield


def drain(maker):
    for _ in maker:
        pass


def backward_chain(carry, pre, post, fill, keep, gain, sink):
    p1, p2t, p2, dz, kq, left, right, dsum = carry
    width = gain.shape[1]
    key, act, der, w2_h = pre["key"], pre["act"], pre["der"], pre["w2"]
    after = settle(post, width)
    p1_h = p1.astype(bf16)
    coef1 = dot_nt(key, kq).astype(bf16)
    base1 = pre["c1"] + dot_nn(key, p1_h)
    d_s1 = -base1 - dot_nn(coef1, dz)
    p2_h = p2t.astype(bf16)
    coef2 = dot_nt(act, right).astype(bf16)
    p2 = p2 + dsum
    base2 = pre["c2"] + p2 + dot_nt(act, p2_h)
    fill(2)
    side = base2 + dot_nn(coef2, left)
    p1 = p1 + dot_tn(kq, dz)
    p2t = p2t + dot_tn(left, right)
    next(after, None)
    fill(1)
    d_upd = d_s1 * der
    d_upd_h = d_upd.astype(bf16)
    d_s2 = dot_nt(d_upd_h, w2_h) - side
    rest = pre["c3"] - dot_nn(pre["s2"], p2t.astype(bf16))
    p1_h = p1.astype(bf16)
    bend = d_s1 * pre["bend"]
    next(after, None)
    fill(3)
    d_fac = d_s2 * pre["fac"]
    main = dot_nn(d_fac.astype(bf16), w2_h)
    a1, a2, a3, a4 = (jnp.sum(d_s2 * w, axis=1, keepdims=True) for w in pre["weights"])
    fill(5)
    y1, y2, y3, y4 = pre["prods"]
    d_act = (main + rest) - ((a1 * y1 + a2 * y2) + (a3 * y3 + a4 * y4))
    d_z1_h = (d_act * der + bend).astype(bf16)
    d_zc = d_fac - ((a1 * pre["row1"] + a2 * pre["row2"]) + (a3 * pre["inv2"] + a4 * pre["n"]))
    d_zc_h = d_zc.astype(bf16)
    carry = (p1, p2t, p2, jnp.concatenate([d_z1_h, pre["dz1b"]], axis=0),
             jnp.concatenate([key, pre["query"]], axis=0),
             jnp.concatenate([pre["s2"], d_zc_h, pre["dz2b"]], axis=0),
             jnp.concatenate([d_upd_h, act, pre["actb"]], axis=0),
             jnp.sum(d_zc + pre["dz2bf"], axis=0, keepdims=True))
    return carry, (pre, d_s2, a1, a2, d_z1_h, p1_h, keep, gain, sink)


def backward_close(carry):
    p1, p2t, p2, dz, kq, left, right, dsum = carry
    return p1 + dot_tn(kq, dz), p2t + dot_tn(left, right), p2 + dsum


MESH = pl.DeviceIdType.MESH
PACK = 256
ENDS = 160


def seq_place():
    index = lax.axis_index("seq")
    pos = lax.rem(index, CHAIN)
    return pos, index - pos


def meet_group(pos, base):
    barrier = pltpu.get_barrier_semaphore()
    for d in range(1, CHAIN):
        pl.semaphore_signal(
            barrier, inc=1, device_id={"seq": base + lax.rem(pos + d, CHAIN)}, device_id_type=MESH)
    pl.semaphore_wait(barrier, CHAIN - 1)


def push(src, dst, send_sem, recv_sem, target):
    return pltpu.make_async_remote_copy(
        src_ref=src, dst_ref=dst, send_sem=send_sem, recv_sem=recv_sem,
        device_id={"seq": target}, device_id_type=MESH)


def await_bytes(ref, sem):
    pltpu.make_async_copy(ref, ref, sem).wait()


def swap_start(src, dst, send, recv, local_sem, pos, base):
    for d in range(1, CHAIN):
        peer = lax.rem(pos + d, CHAIN)
        push(src.at[peer], dst.at[pos], send.at[d - 1], recv.at[d - 1], base + peer).start()
    pltpu.make_async_copy(src.at[pos], dst.at[pos], local_sem).start()


def swap_wait(src, dst, send, recv, local_sem, pos, base):
    for d in range(1, CHAIN):
        peer = lax.rem(pos + d, CHAIN)
        origin = lax.rem(pos + CHAIN - d, CHAIN)
        push(src.at[peer], dst.at[pos], send.at[d - 1], recv.at[d - 1], base + peer).wait_send()
        await_bytes(dst.at[origin], recv.at[d - 1])
    await_bytes(dst.at[pos], local_sem)


def fwd_kernel(block, unroll, heads, pay_ref, norm_ref, w1_in, b1_in, w2_in, b2_in, gain_in, bias_in,
               mixed_ref, norm_out, k_out, q_out, aux_out, w1s_ref, w2s_ref, z1s_ref, upd_ref, zc_ref, s2_ref, z1b_ref, z2b_ref,
               got, k_all, q_all, base_all, aux_all, mixed_all, w1, w2t, b2, z1,
               pay_send, pay_recv, mix_send, mix_recv, no_send, no_recv):
    blk = pl.program_id(0)
    last = pl.num_programs(0) - 1
    pos, base = seq_place()
    width = gain_in.shape[1]
    hidden = w1.shape[1]
    rows_each = pay_ref.shape[0]
    per = rows_each // block
    owner = (pos >= FIRST) & (pos < FIRST + heads)
    mine = jnp.clip(pos - FIRST, 0, heads - 1)
    gain = gain_in[pl.ds(mine, 1), :]
    bias = bias_in[pl.ds(mine, 1), :]
    gain_sq = gain * gain
    tri = tri_mask()

    @pl.when(blk == 0)
    def _():
        meet_group(pos, base)
        for j in range(heads):
            src = pay_ref.at[:, pl.ds(j * PACK, PACK)]
            dst = got.at[pos]

            @pl.when(pos != FIRST + j)
            def _():
                push(src, dst, pay_send.at[j], pay_recv.at[pos], base + FIRST + j).start()

            @pl.when(pos == FIRST + j)
            def _():
                pltpu.make_async_copy(src, dst, pay_recv.at[pos]).start()

        for j in range(heads):
            @pl.when(pos != FIRST + j)
            def _():
                push(norm_ref, norm_out.at[pos], no_send.at[j], no_recv.at[pos], base + FIRST + j).start()

            @pl.when(pos == FIRST + j)
            def _():
                pltpu.make_async_copy(norm_ref, norm_out.at[pos], no_recv.at[pos]).start()

    def take_in(p):
        await_bytes(got.at[p], pay_recv.at[p])
        part = got[p]
        rows = pl.ds(pl.multiple_of(p * rows_each, rows_each), rows_each)
        lane = lax.broadcasted_iota(jnp.int32, (rows_each, AUG), 1)
        one = jnp.ones((), bf16)
        zero = jnp.zeros((), bf16)
        tail = jnp.where(lane == width, one, zero)
        query = part[:, :AUG]
        key = part[:, width : width + AUG]
        q_all[rows, :] = jnp.where(lane < width, query, tail)
        k_all[rows, :] = jnp.where(lane < width, key, tail)
        key_f = part[:, width : 2 * width].astype(f32)
        target = part[:, 2 * width : 3 * width].astype(f32) - key_f
        logit = part[:, 3 * width : 3 * width + 1].astype(f32) + part[:, 3 * width + 1 : 3 * width + 2].astype(f32)
        sig = 1.0 / (1.0 + jnp.exp(-logit))
        base_all[rows, :] = (bias - target) * gain
        spot = lax.broadcasted_iota(jnp.int32, (rows_each, 2 * width), 1)
        wide = jnp.concatenate([target, target], axis=1)
        aux_all[rows, :] = jnp.where(
            spot < width, wide, jnp.where(spot == width, sig * (1.0 / width), 1.0 - sig))

    def send_mixed(b):
        p = lax.div(b, per)
        src = mixed_all.at[pl.ds(pl.multiple_of(b * block, block), block), :]
        dst = mixed_ref.at[mine, pl.ds(pl.multiple_of(lax.rem(b, per) * block, block), block), :]

        @pl.when(p != pos)
        def _():
            push(src, dst, mix_send, mix_recv.at[mine], base + p).start()

        @pl.when(p == pos)
        def _():
            pltpu.make_async_copy(src, dst, mix_recv.at[mine]).start()

    @pl.when(owner)
    def _():
        @pl.when(blk == 0)
        def _():
            row = lax.broadcasted_iota(jnp.int32, (AUG - width, hidden), 0)
            w1[pl.ds(0, width), :] = w1_in[mine]
            w1[pl.ds(width, AUG - width), :] = jnp.where(row == 0, b1_in[pl.ds(mine, 1), :], 0.0)
            turned = w2_in[mine].T
            w2t[...] = turned - jnp.mean(turned, axis=0, keepdims=True)
            start = b2_in[pl.ds(mine, 1), :]
            b2[...] = start - mean_row(start)
            k_all[pl.ds(CHAIN * rows_each, MINI), :] = jnp.zeros((MINI, AUG), bf16)
            take_in(0)
            z1[...] = dot_nn(k_all[0:MINI, :], w1[...].astype(bf16))

        @pl.when((lax.rem(blk, per) == 0) & (blk < last + 1 - per))
        def _():
            take_in(lax.div(blk, per) + 1)

        @pl.when(blk > 0)
        def _():
            send_mixed(blk - 1)

        brows = pl.ds(pl.multiple_of(blk * block, block), block)
        k_out[...] = k_all[brows, :]
        q_out[...] = q_all[brows, :]
        aux_out[...] = aux_all[brows, :]

        def group(it, _):
            for u in range(unroll):
                loc = it * unroll + u
                row = pl.multiple_of(blk * block + loc * MINI, MINI)
                rows = pl.ds(row, MINI)
                lrows = pl.ds(pl.multiple_of(loc * MINI, MINI), MINI)
                q_aug = q_all[rows, :]
                z1_now = z1[...]
                state, z1_next, out, saved = forward_step(
                    (w1[...], w2t[...], b2[...]), z1_now, k_all[rows, :], k_all[pl.ds(row + MINI, MINI), :], q_aug,
                    base_all[rows, :], aux_all[rows, width : width + 1], gain, gain_sq, bias, tri)
                w1[...], w2t[...], b2[...] = state
                z1[...] = z1_next
                mixed_all[rows, :] = (out + q_aug[:, :width].astype(f32)).astype(bf16)
                w1s_ref[loc], w2s_ref[loc], upd, zc, s2, z1b, z2b = saved
                z1s_ref[lrows, :] = z1_now
                upd_ref[lrows, :] = upd
                zc_ref[lrows, :] = zc
                s2_ref[lrows, :] = s2
                z1b_ref[lrows, :] = z1b
                z2b_ref[lrows, :] = z2b
            return 0

        lax.fori_loop(0, block // MINI // unroll, group, 0)

    @pl.when(blk == last)
    def _():
        @pl.when(owner)
        def _():
            send_mixed(last)
            others = mixed_all.at[pl.ds(0, (CHAIN - 1) * rows_each), :]
            await_bytes(others, mix_send)
            for p in range(CHAIN):
                await_bytes(norm_out.at[p], no_recv.at[p])

        for j in range(heads):
            @pl.when(pos != FIRST + j)
            def _():
                await_bytes(got.at[pos], pay_send.at[j])
                await_bytes(norm_ref, no_send.at[j])

            await_bytes(mixed_ref.at[j], mix_recv.at[j])


def chain_forward(payload, normed, w1, b1, w2, b2, gain, bias, block=128, unroll=8):
    rows = payload.shape[0]
    heads, width, hidden = w1.shape
    tokens = rows * CHAIN
    steps = tokens // MINI
    nb = block // MINI
    whole = lambda a: pl.BlockSpec(a.shape, lambda i: (0,) * a.ndim)
    rowblk = lambda w: pl.BlockSpec((block, w), lambda i: (i, 0))
    stepblk = lambda r: pl.BlockSpec((nb, r, hidden), lambda i: (i, 0, 0))
    anywhere = pl.BlockSpec(memory_space=pl.ANY)
    small = (w1, b1, w2, b2, gain, bias)
    dma = pltpu.SemaphoreType.DMA
    wide = jax.ShapeDtypeStruct((tokens, hidden), f32)
    narrow = jax.ShapeDtypeStruct((tokens, width), f32)
    return pl.pallas_call(
        functools.partial(fwd_kernel, block, unroll, heads),
        grid=(tokens // block,),
        in_specs=[anywhere, anywhere] + [whole(a) for a in small],
        out_specs=[anywhere, anywhere, rowblk(AUG), rowblk(AUG), rowblk(2 * width), stepblk(AUG), stepblk(width),
                   rowblk(hidden), rowblk(hidden), rowblk(width), rowblk(width), rowblk(hidden), rowblk(width)],
        out_shape=[jax.ShapeDtypeStruct((heads, rows, width), bf16),
                   jax.ShapeDtypeStruct((CHAIN,) + normed.shape, bf16),
                   jax.ShapeDtypeStruct((tokens, AUG), bf16),
                   jax.ShapeDtypeStruct((tokens, AUG), bf16),
                   jax.ShapeDtypeStruct((tokens, 2 * width), f32),
                   jax.ShapeDtypeStruct((steps, AUG, hidden), bf16),
                   jax.ShapeDtypeStruct((steps, width, hidden), bf16),
                   wide, wide, narrow, narrow, wide, narrow],
        scratch_shapes=[pltpu.VMEM((CHAIN, rows, PACK), bf16),
                        pltpu.VMEM((tokens + MINI, AUG), bf16), pltpu.VMEM((tokens, AUG), bf16),
                        pltpu.VMEM((tokens, width), f32), pltpu.VMEM((tokens, 2 * width), f32),
                        pltpu.VMEM((tokens, width), bf16),
                        pltpu.VMEM((AUG, hidden), f32), pltpu.VMEM((width, hidden), f32),
                        pltpu.VMEM((1, width), f32), pltpu.VMEM((MINI, hidden), f32),
                        dma((heads,)), dma((CHAIN,)), dma, dma((heads,)),
                        dma((heads,)), dma((CHAIN,))],
        compiler_params=pltpu.CompilerParams(collective_id=0, has_side_effects=True),
        name="inner_forward",
    )(payload, normed, *small)


def bwd_kernel(block, heads, turn, gm_ref, early_ref, small_ref, gain_in, bias_in, norm_ref,
               k_ref, q_ref, aux_ref, w1s_ref, w2s_ref, z1s_ref, upd_ref, zc_ref, s2_ref, z1b_ref, z2b_ref,
               grads_ref, ends_ref, late_ref, early_out, small_out,
               dout, half_got, half_mine, quarter, quarter_got, packed, ends, weights, late,
               p1, p2t, p2, dz, kq, left, right, dsum, dg, db, dl,
               gm_send, gm_recv, ha_send, ha_recv, ha_loc, qu_send, qu_recv, sm_send, sm_recv, sm_loc, bc_send, bc_recv, en_send, en_recv, la_send, la_recv):
    pid = pl.program_id(0)
    last = pl.num_programs(0) - 1
    blk = last - pid
    pos, base = seq_place()
    width = gain_in.shape[1]
    rows_each = gm_ref.shape[1]
    per = rows_each // block
    owner = (pos >= FIRST) & (pos < FIRST + heads)
    mine = jnp.clip(pos - FIRST, 0, heads - 1)
    gain = gain_in[pl.ds(mine, 1), :]
    bias = bias_in[pl.ds(mine, 1), :]
    gain_sq = gain * gain
    tri = tri_mask()
    count = block // MINI
    side = lax.rem(pos, 2)
    rank = lax.div(pos, 2)
    partner = pos + 1 - 2 * side
    state = (p1, p2t, p2, dz, kq, left, right, dsum)

    @pl.when(pid == 0)
    def _():
        meet_group(pos, base)
        for j in range(heads):
            @pl.when(pos != FIRST + j)
            def _():
                push(gm_ref.at[j], dout.at[pos], gm_send.at[j], gm_recv.at[pos], base + FIRST + j).start()

            @pl.when(pos == FIRST + j)
            def _():
                pltpu.make_async_copy(gm_ref.at[j], dout.at[pos], gm_recv.at[pos]).start()

        for d in range(1, CHAIN):
            push(small_ref, small_out.at[pos], sm_send.at[d - 1], sm_recv.at[d - 1],
                 base + lax.rem(pos + d, CHAIN)).start()
        pltpu.make_async_copy(small_ref, small_out.at[pos], sm_loc).start()
        push(early_ref.at[:, 1 - side], half_got, ha_send, ha_recv, base + partner).start()
        pltpu.make_async_copy(early_ref.at[:, side], half_mine, ha_loc).start()

    @pl.when(pid == turn)
    def _():
        push(early_ref.at[:, 1 - side], half_got, ha_send, ha_recv, base + partner).wait()
        await_bytes(half_mine, ha_loc)

        def pair_up(c, _):
            rows = pl.ds(pl.multiple_of(c * MINI, MINI), MINI)
            for r in range(CHAIN // 2):
                quarter[r, rows, :] = (half_mine[r, rows, :].astype(f32) + half_got[r, rows, :].astype(f32)).astype(bf16)
            return 0

        lax.fori_loop(0, half_mine.shape[1] // MINI, pair_up, 0)
        for d in range(1, CHAIN // 2):
            other = lax.rem(rank + d, CHAIN // 2)
            push(quarter.at[other], quarter_got.at[d - 1], qu_send.at[d - 1], qu_recv.at[d - 1],
                 base + 2 * other + side).start()

    def share_block(b):
        p = lax.div(b, per)
        src = packed.at[pl.ds(pl.multiple_of(b * block, block), block), :]
        dst = grads_ref.at[mine, pl.ds(pl.multiple_of(lax.rem(b, per) * block, block), block), :]

        @pl.when(p != pos)
        def _():
            push(src, dst, bc_send, bc_recv.at[mine], base + p).start()

        @pl.when(p == pos)
        def _():
            pltpu.make_async_copy(src, dst, bc_recv.at[mine]).start()

    share = late.shape[1]

    def weigh(b, lo, hi):
        rows = pl.ds(pl.multiple_of(b * block, block), block)
        weights[lo:hi, :] += dot_tn(norm_ref[:, lo:hi], packed[rows, :])

    @pl.when(owner)
    def _():
        @pl.when(pid == 0)
        def _():
            for r in state + (dg, db, dl, weights):
                r[...] = jnp.zeros_like(r)

        @pl.when(lax.rem(pid, per) == 0)
        def _():
            p = lax.div(blk, per)
            await_bytes(dout.at[p], gm_recv.at[p])

        @pl.when(pid > 0)
        def _():
            share_block(blk + 1)

        carry = tuple(r[...] for r in state)
        totals = [dg[...], db[...], dl[...]]
        made = {}

        def start(loc):
            made[loc] = {}
            lr = pl.ds(loc * MINI, MINI)
            inner = pl.ds(pl.multiple_of(lax.rem(blk, per) * block + loc * MINI, MINI), MINI)
            saved = (w1s_ref[loc], w2s_ref[loc], z1s_ref[lr, :], upd_ref[lr, :], zc_ref[lr, :], s2_ref[lr, :],
                     z1b_ref[lr, :], z2b_ref[lr, :])
            return prepare_back(made[loc], saved, dout[lax.div(blk, per), inner, :].astype(f32), k_ref[lr, :],
                                q_ref[lr, :], aux_ref[lr, 0:width], aux_ref[lr, width : width + 1],
                                gain, gain_sq, bias, tri)

        drain(start(count - 1))
        post = None
        for loc in range(count - 1, -1, -1):
            ahead = start(loc - 1) if loc > 0 else iter(())

            def fill(pieces, ahead=ahead):
                for _ in range(pieces):
                    next(ahead, None)

            def sink(d_query, d_key, d_value, d_logit, d_gain, d_bias, loc=loc):
                totals[0] = totals[0] + d_gain
                totals[1] = totals[1] + d_bias
                totals[2] = totals[2] + jnp.sum(d_logit, axis=0, keepdims=True)
                high = d_logit.astype(bf16).astype(f32)
                lane = lax.broadcasted_iota(jnp.int32, (MINI, width), 1)
                extra = jnp.where(lane == 0, high, jnp.where(lane == 1, d_logit - high, 0.0))
                rows = pl.ds(pl.multiple_of(blk * block + loc * MINI, MINI), MINI)
                packed[rows, :] = jnp.concatenate([d_query, d_key, d_value, extra], axis=1).astype(bf16)

            carry, post = backward_chain(
                carry, made.pop(loc), post, fill, aux_ref[pl.ds(loc * MINI, MINI), width + 1 : width + 2], gain, sink)
        drain(settle(post, width))
        for r, v in zip(state, carry):
            r[...] = v
        dg[...], db[...], dl[...] = totals
        quarter_rows = norm_ref.shape[1] // 4
        for i in range(4):
            weigh(blk, i * quarter_rows, (i + 1) * quarter_rows)

        @pl.when(pid == last)
        def _():
            end_one, end_two, end_b_two = backward_close(tuple(r[...] for r in state))
            ends[pl.ds(0, AUG), :] = end_one.astype(bf16)
            ends[pl.ds(AUG, width), :] = end_two.astype(bf16)
            rest = ENDS - AUG - width
            row = lax.broadcasted_iota(jnp.int32, (rest, width), 0)
            tailing = jnp.where(row == 0, end_b_two, jnp.where(row == 1, dg[...], jnp.where(row == 2, db[...], 0.0)))
            high = dl[...].astype(bf16).astype(f32)
            tailing = tailing + jnp.where(row == 3, high, jnp.where(row == 4, dl[...] - high, 0.0))
            ends[pl.ds(AUG + width, rest), :] = jnp.concatenate([tailing] * 4, axis=1).astype(bf16)
            share_block(0)
            for p in range(CHAIN):
                late[p] = weights[p * share : (p + 1) * share, :].astype(bf16)
            for d in range(1, CHAIN):
                peer = lax.rem(pos + d, CHAIN)
                push(late.at[peer], late_ref.at[mine], la_send.at[d - 1], la_recv.at[mine], base + peer).start()
            pltpu.make_async_copy(late.at[pos], late_ref.at[mine], la_recv.at[mine]).start()
            for d in range(1, CHAIN):
                push(ends, ends_ref.at[mine], en_send.at[d - 1], en_recv.at[mine],
                     base + lax.rem(pos + d, CHAIN)).start()
            pltpu.make_async_copy(ends, ends_ref.at[mine], en_recv.at[mine]).start()

    @pl.when(pid == last)
    def _():
        for d in range(1, CHAIN // 2):
            other = lax.rem(rank + d, CHAIN // 2)
            push(quarter.at[other], quarter_got.at[d - 1], qu_send.at[d - 1], qu_recv.at[d - 1],
                 base + 2 * other + side).wait()
        for d in range(1, CHAIN):
            push(small_ref, small_out.at[pos], sm_send.at[d - 1], sm_recv.at[d - 1],
                 base + lax.rem(pos + d, CHAIN)).wait_send()
            await_bytes(small_out.at[lax.rem(pos + CHAIN - d, CHAIN)], sm_recv.at[d - 1])
        await_bytes(small_out.at[pos], sm_loc)

        def add_up(c, _):
            rows = pl.ds(pl.multiple_of(c * MINI, MINI), MINI)
            acc = quarter[rank, rows, :].astype(f32)
            for d in range(1, CHAIN // 2):
                acc = acc + quarter_got[d - 1, rows, :].astype(f32)
            early_out[rows, :] = acc
            return 0

        lax.fori_loop(0, early_out.shape[0] // MINI, add_up, 0)
        for j in range(heads):
            @pl.when(pos != FIRST + j)
            def _():
                await_bytes(dout.at[pos], gm_send.at[j])

            await_bytes(grads_ref.at[j], bc_recv.at[j])
            await_bytes(ends_ref.at[j], en_recv.at[j])
            await_bytes(late_ref.at[j], la_recv.at[j])

        @pl.when(owner)
        def _():
            await_bytes(packed.at[pl.ds(0, (CHAIN - 1) * rows_each), :], bc_send)
            for d in range(1, CHAIN):
                await_bytes(ends, en_send.at[d - 1])
                await_bytes(late.at[0], la_send.at[d - 1])


def chain_backward(grad_mixed, early, small, gain, bias, normed, saved, block=128, turn=6):
    heads, rows, width = grad_mixed.shape
    tokens = rows * CHAIN
    hidden = saved[5].shape[1]
    nblk = tokens // block
    nb = block // MINI
    whole = lambda a: pl.BlockSpec(a.shape, lambda i: (0,) * a.ndim)
    rowblk = lambda w: pl.BlockSpec((block, w), lambda i: (nblk - 1 - i, 0))
    stepblk = lambda r: pl.BlockSpec((nb, r, hidden), lambda i: (nblk - 1 - i, 0, 0))
    anywhere = pl.BlockSpec(memory_space=pl.ANY)
    dma = pltpu.SemaphoreType.DMA
    seven = dma((CHAIN - 1,))
    share = early.shape[2:]
    three = dma((CHAIN // 2 - 1,))
    return pl.pallas_call(
        functools.partial(bwd_kernel, block, heads, turn),
        grid=(nblk,),
        in_specs=[anywhere] * 3 + [whole(gain), whole(bias), rowblk(normed.shape[1]), rowblk(AUG), rowblk(AUG),
                                   rowblk(2 * width), stepblk(AUG), stepblk(width), rowblk(hidden), rowblk(hidden), rowblk(width),
                                   rowblk(width), rowblk(hidden), rowblk(width)],
        out_specs=[anywhere, anywhere, anywhere, pl.BlockSpec(share, lambda i: (0, 0)), anywhere],
        out_shape=[jax.ShapeDtypeStruct((heads, rows, PACK), bf16),
                   jax.ShapeDtypeStruct((heads, ENDS, hidden), bf16),
                   jax.ShapeDtypeStruct((heads, share[0], PACK), bf16),
                   jax.ShapeDtypeStruct(share, f32),
                   jax.ShapeDtypeStruct((CHAIN,) + small.shape, f32)],
        scratch_shapes=[pltpu.VMEM((CHAIN, rows, width), bf16), pltpu.VMEM((CHAIN // 2,) + share, bf16),
                        pltpu.VMEM((CHAIN // 2,) + share, bf16), pltpu.VMEM((CHAIN // 2,) + share, bf16),
                        pltpu.VMEM((CHAIN // 2 - 1,) + share, bf16),
                        pltpu.VMEM((tokens, PACK), bf16), pltpu.VMEM((ENDS, hidden), bf16),
                        pltpu.VMEM((CHAIN * share[0], PACK), f32), pltpu.VMEM((CHAIN, share[0], PACK), bf16),
                        pltpu.VMEM((AUG, hidden), f32), pltpu.VMEM((width, hidden), f32), pltpu.VMEM((1, width), f32),
                        pltpu.VMEM((2 * MINI, hidden), bf16), pltpu.VMEM((2 * MINI, AUG), bf16),
                        pltpu.VMEM((3 * MINI, width), bf16), pltpu.VMEM((3 * MINI, hidden), bf16),
                        pltpu.VMEM((1, width), f32), pltpu.VMEM((1, width), f32), pltpu.VMEM((1, width), f32),
                        pltpu.VMEM((1, 1), f32),
                        dma((heads,)), dma((CHAIN,)), dma, dma, dma, three, three, seven, seven, dma,
                        dma, dma((heads,)), seven, dma((heads,)), seven, dma((heads,))],
        compiler_params=pltpu.CompilerParams(collective_id=1, has_side_effects=True),
        name="inner_backward",
    )(grad_mixed, early, small, gain, bias, normed, *saved)


def head_place():
    return lax.axis_index("head"), lax.axis_size("head")


def meet_heads(me, count):
    barrier = pltpu.get_barrier_semaphore()
    for d in range(1, count):
        pl.semaphore_signal(barrier, inc=1, device_id={"head": lax.rem(me + d, count)}, device_id_type=MESH)
    pl.semaphore_wait(barrier, count - 1)


def push_head(src, dst, send_sem, recv_sem, target):
    return pltpu.make_async_remote_copy(
        src_ref=src, dst_ref=dst, send_sem=send_sem, recv_sem=recv_sem,
        device_id={"head": target}, device_id_type=MESH)


def row_totals(first, second):
    ones = jnp.ones((8, first.shape[1]), f32)

    def total(x):
        return lax.dot_general(ones, x, (((1,), (1,)), ((), ())), precision=lax.Precision.HIGHEST,
                               preferred_element_type=f32)

    top, low = total(first), total(second)
    row = lax.broadcasted_iota(jnp.int32, top.shape, 0)
    return jnp.where(row == 0, top, low)


def mid_kernel(count, mixed_ref, x_ref, ct_ref, gate_pre_ref, normed_ref, w_out_ref, w_gate_ref, w_up_ref, w_down_ref,
               post_gain_ref, post_bias_ref, ffn_gain_ref,
               gm_ref, early_ref, ggp_ref, out_ref, rco_ref, grc_ref, small_ref,
               st_mine, st_got, pa_mine, pa_got, nt_all, rc_mine, rc_all, gn_mine, gn_got, dn_mine, dn_got, gov_all,
               gc_mine, gc_all, sb_mine, sb_got, gt_all, gh, gated, hidden, ggv, guv, resid,
               st_s, st_r, pa_s, pa_r, nt_s, nt_r, rc_s, rc_r, gn_s, gn_r, dn_s, dn_r, go_s, go_r, gc_s, gc_r, sb_s, sb_r,
               gt_s, gt_r):
    me, _ = head_place()
    heads, rows, width = mixed_ref.shape
    cols = heads * width
    full = cols * count
    part = rows // count
    peers = [(d, lax.rem(me + d, count)) for d in range(1, count)]
    meet_heads(me, count)

    def rows_of(device):
        return pl.ds(pl.multiple_of(device * part, part), part)

    def send_all(src, dst, send, recv):
        for d, peer in peers:
            push_head(src, dst.at[d - 1], send.at[d - 1], recv.at[d - 1], peer).start()

    def wait_all(src, dst, send, recv):
        for d, peer in peers:
            push_head(src, dst.at[d - 1], send.at[d - 1], recv.at[d - 1], peer).wait()

    z = jnp.concatenate([mixed_ref[j] for j in range(heads)], axis=1).astype(f32)
    st_mine[...] = row_totals(z, z * z)
    send_all(st_mine, st_got, st_s, st_r)
    gate_pre = gate_pre_ref[...]
    gate_act, gate_der = gelu_first(gate_pre)
    gh[...] = dot_nt(ct_ref[...], w_down_ref[...])
    wait_all(st_mine, st_got, st_s, st_r)
    tot = st_mine[...]
    for d, _ in peers:
        tot = tot + st_got[d - 1]
    tot = tot.T * (1.0 / full)
    mean_z = tot[:, 0:1]
    inv_z = lax.rsqrt(tot[:, 1:2] - mean_z * mean_z + eps_norm)
    z_hat = (z - mean_z) * inv_z
    post_out = z_hat * post_gain_ref[...] + post_bias_ref[...]
    gated[...] = (post_out * gate_act).astype(bf16)

    def spread_rows(make, mine, got, send, recv):
        pending = None
        for d, peer in peers:
            mine[d - 1] = make(rows_of(peer)).astype(bf16)
            if pending is not None:
                pending.start()
            pending = push_head(mine.at[d - 1], got.at[d - 1], send.at[d - 1], recv.at[d - 1], peer)
        own = make(rows_of(me))
        pending.start()
        return own

    def add_rows(own, mine, got, send, recv):
        for d, peer in peers:
            push_head(mine.at[d - 1], got.at[d - 1], send.at[d - 1], recv.at[d - 1], peer).wait()
            own = own + got[d - 1].astype(f32)
        return own

    def gather_rows(all_ref, send, recv):
        for d, peer in peers:
            view = all_ref.at[rows_of(me), :]
            push_head(view, view, send.at[d - 1], recv.at[d - 1], peer).start()

    def gather_wait(all_ref, send, recv):
        for d, peer in peers:
            view = all_ref.at[rows_of(me), :]
            push_head(view, view, send.at[d - 1], recv.at[d - 1], peer).wait_send()
            await_bytes(all_ref.at[rows_of(lax.rem(me + count - d, count)), :], recv.at[d - 1])

    def turn_columns(value, mine, all_ref, send, recv):
        for b in range(count):
            mine[b] = value[:, b * cols : (b + 1) * cols]
        all_ref[rows_of(me), :] = mine[me]

    def turn_start(mine, all_ref, send, recv):
        for d, peer in peers:
            push_head(mine.at[peer], all_ref.at[rows_of(me), :], send.at[d - 1], recv.at[d - 1], peer).start()

    def turn_wait(mine, all_ref, send, recv):
        for d, peer in peers:
            push_head(mine.at[peer], all_ref.at[rows_of(me), :], send.at[d - 1], recv.at[d - 1], peer).wait_send()
            await_bytes(all_ref.at[rows_of(lax.rem(me + count - d, count)), :], recv.at[d - 1])

    w_out = w_out_ref[...]
    own = spread_rows(lambda r: dot_nn(gated[r, :], w_out), pa_mine, pa_got, pa_s, pa_r)
    res = x_ref[rows_of(me), :].astype(f32) + add_rows(own, pa_mine, pa_got, pa_s, pa_r)
    rms_two = lax.rsqrt(mean_row(res * res) + eps_norm)
    ffn_gain = ffn_gain_ref[...]
    nt_all[rows_of(me), :] = (res * rms_two * ffn_gain).astype(bf16)
    turn_columns(res, rc_mine, rc_all, rc_s, rc_r)
    resid[...] = res
    gather_rows(nt_all, nt_s, nt_r)
    turn_start(rc_mine, rc_all, rc_s, rc_r)
    gather_wait(nt_all, nt_s, nt_r)
    def forward_rows(b, _):
        r = pl.ds(pl.multiple_of(b * part, part), part)
        nt = nt_all[r, :]
        gate_val = dot_nn(nt, w_gate_ref[...])
        up_val = dot_nn(nt, w_up_ref[...])
        sig = 1.0 / (1.0 + jnp.exp(-gate_val))
        silu = gate_val * sig
        hidden[r, :] = (silu * up_val).astype(bf16)
        g = gh[r, :]
        ggv[r, :] = (g * up_val * sig * (1.0 + gate_val * (1.0 - sig))).astype(bf16)
        guv[r, :] = (g * silu).astype(bf16)
        return 0

    lax.fori_loop(0, count, forward_rows, 0)
    own = spread_rows(lambda r: dot_nt(ggv[r, :], w_gate_ref[...]) + dot_nt(guv[r, :], w_up_ref[...]),
                      gn_mine, gn_got, gn_s, gn_r)
    for b in range(count):
        r = pl.ds(b * part, part)
        down = dot_nn(hidden[r, :], w_down_ref[...]).astype(bf16)
        for c in range(count):
            dn_mine[c, r, :] = down[:, c * cols : (c + 1) * cols]
    ffn = w_gate_ref.shape[1]
    half = full // 2
    for b in range(2):
        r = slice(b * half, (b + 1) * half)
        early_ref[r, 0:ffn] = dot_tn(nt_all[:, r], ggv[...]).astype(bf16)
    for d, peer in peers:
        push_head(dn_mine.at[peer], dn_got.at[d - 1], dn_s.at[d - 1], dn_r.at[d - 1], peer).start()
    gnt = add_rows(own, gn_mine, gn_got, gn_s, gn_r)
    res = resid[...]
    rms_two = lax.rsqrt(mean_row(res * res) + eps_norm)
    scaled = gnt * ffn_gain
    grad_res = ct_ref[rows_of(me), :].astype(f32) + rms_two * (
        scaled - res * rms_two * rms_two * mean_row(scaled * res))
    gov_all[rows_of(me), :] = grad_res.astype(bf16)
    gt_all[me] = jnp.broadcast_to(jnp.sum(gnt * res * rms_two, axis=0, keepdims=True), gt_all.shape[1:])
    turn_columns(grad_res, gc_mine, gc_all, gc_s, gc_r)
    gather_rows(gov_all, go_s, go_r)
    turn_start(gc_mine, gc_all, gc_s, gc_r)
    for d, peer in peers:
        push_head(gt_all.at[me], gt_all.at[me], gt_s.at[d - 1], gt_r.at[d - 1], peer).start()
    for b in range(2):
        r = slice(b * half, (b + 1) * half)
        early_ref[r, ffn : 2 * ffn] = dot_tn(nt_all[:, r], guv[...]).astype(bf16)
    gather_wait(gov_all, go_s, go_r)
    gov = gov_all[...]
    grad_gated = dot_nt(gov, w_out_ref[...])
    grad_post = grad_gated * gate_act
    grad_zhat = grad_post * post_gain_ref[...]
    sb_mine[...] = row_totals(grad_zhat, grad_zhat * z_hat)
    ggp = (grad_gated * post_out * gate_der).astype(bf16)
    ggp_ref[...] = ggp
    send_all(sb_mine, sb_got, sb_s, sb_r)
    early_ref[:, 3 * ffn : 3 * ffn + 2 * cols] = jnp.concatenate(
        [dot_tn(normed_ref[...], ggp).astype(bf16), dot_tn(gov, gated[...]).astype(bf16)], axis=1)
    row = lax.broadcasted_iota(jnp.int32, (8, cols), 0)
    wait_all(sb_mine, sb_got, sb_s, sb_r)
    tot = sb_mine[...]
    for d, _ in peers:
        tot = tot + sb_got[d - 1]
    tot = tot.T * (1.0 / full)
    grad_mixed = (inv_z * (grad_zhat - tot[:, 0:1] - z_hat * tot[:, 1:2])).astype(bf16)
    for j in range(heads):
        gm_ref[j] = grad_mixed[:, j * width : (j + 1) * width]
    for b in range(2):
        r = slice(b * half, (b + 1) * half)
        early_ref[r, 2 * ffn : 3 * ffn] = dot_tn(ct_ref[:, r], hidden[...]).astype(bf16)
    turn_wait(rc_mine, rc_all, rc_s, rc_r)
    rco_ref[...] = rc_all[...]
    out = dn_mine[me].astype(f32)
    for d, peer in peers:
        push_head(dn_mine.at[peer], dn_got.at[d - 1], dn_s.at[d - 1], dn_r.at[d - 1], peer).wait()
        out = out + dn_got[d - 1].astype(f32)
    out_ref[...] = out
    turn_wait(gc_mine, gc_all, gc_s, gc_r)
    grc_ref[...] = gc_all[...]
    for d, peer in peers:
        push_head(gt_all.at[me], gt_all.at[me], gt_s.at[d - 1], gt_r.at[d - 1], peer).wait_send()
        await_bytes(gt_all.at[lax.rem(me + count - d, count)], gt_r.at[d - 1])
    gain_two = gt_all[0]
    for b in range(1, count):
        gain_two = gain_two + gt_all[b]
    post = jnp.where(row == 1, jnp.sum(grad_post * z_hat, axis=0, keepdims=True),
                     jnp.sum(grad_post, axis=0, keepdims=True))
    line = lax.broadcasted_iota(jnp.int32, (8, full), 0)
    small_ref[...] = jnp.where(
        line == 0, gain_two, jnp.concatenate([post] + [jnp.zeros_like(post)] * (count - 1), axis=1))


def middle(mixed, x, ct, gate_pre, normed, w_out, w_gate, w_up, w_down, post_gain, post_bias, ffn_gain):
    count = lax.axis_size("head")
    heads, rows, width = mixed.shape
    cols = heads * width
    full = cols * count
    part = rows // count
    ffn = w_gate.shape[1]
    ins = (mixed, x, ct, gate_pre, normed, w_out, w_gate, w_up, w_down, post_gain, post_bias, ffn_gain)
    vmem = pl.BlockSpec(memory_space=pltpu.VMEM)
    V = pltpu.VMEM
    trio = count - 1
    sem = pltpu.SemaphoreType.DMA((trio,))
    return pl.pallas_call(
        functools.partial(mid_kernel, count),
        in_specs=[vmem] * len(ins),
        out_specs=[vmem] * 7,
        out_shape=[jax.ShapeDtypeStruct((heads, rows, width), bf16),
                   jax.ShapeDtypeStruct((full, 3 * ffn + 2 * cols), bf16),
                   jax.ShapeDtypeStruct((rows, cols), bf16),
                   jax.ShapeDtypeStruct((rows, cols), f32),
                   jax.ShapeDtypeStruct((rows, cols), f32),
                   jax.ShapeDtypeStruct((rows, cols), f32),
                   jax.ShapeDtypeStruct((8, full), f32)],
        scratch_shapes=[
            V((8, rows), f32), V((trio, 8, rows), f32),
            V((trio, part, full), bf16), V((trio, part, full), bf16),
            V((rows, full), bf16),
            V((count, part, cols), f32), V((rows, cols), f32),
            V((trio, part, full), bf16), V((trio, part, full), bf16),
            V((count, rows, cols), bf16), V((trio, rows, cols), bf16),
            V((rows, full), bf16),
            V((count, part, cols), f32), V((rows, cols), f32),
            V((8, rows), f32), V((trio, 8, rows), f32),
            V((count, 8, full), f32),
            V((rows, ffn), f32), V((rows, cols), bf16),
            V((rows, ffn), bf16), V((rows, ffn), bf16), V((rows, ffn), bf16),
            V((part, full), f32)] + [sem] * 20,
        compiler_params=pltpu.CompilerParams(
            collective_id=2, has_side_effects=True, vmem_limit_bytes=56 * 1024 * 1024),
        name="middle",
    )(*ins)


def tail_kernel(count, at_mix, grads_ref, packed_w_ref, mix_gate_ref, ggp_ref, x_ref, pre_gain_ref, late_ref, early_ref,
                back_ref, tiles_ref,
                mine, got, tile, tile_got, ib_s, ib_r, th_s, th_r, ts_s, ts_r, ts_loc):
    me, _ = head_place()
    pos, base = seq_place()
    heads = grads_ref.shape[0]
    rows = x_ref.shape[0]
    cols = ggp_ref.shape[1]
    full = x_ref.shape[1]
    share = early_ref.shape[0]
    rate_lane = PACK - PACK // 4
    peers = [(d, lax.rem(me + d, count)) for d in range(1, count)]
    barrier = pltpu.get_barrier_semaphore()
    for d, peer in peers:
        pl.semaphore_signal(barrier, inc=1, device_id={"head": peer}, device_id_type=MESH)
    for d in range(1, CHAIN):
        pl.semaphore_signal(
            barrier, inc=1, device_id={"seq": base + lax.rem(pos + d, CHAIN)}, device_id_type=MESH)
    pl.semaphore_wait(barrier, count - 1 + CHAIN - 1)
    part = rows // count

    def back_rows(b, _):
        r = pl.ds(pl.multiple_of(b * part, part), part)
        grad = dot_nt(ggp_ref[r, :], mix_gate_ref[...])
        for j in range(heads):
            grad = grad + dot_nt(grads_ref[j, r, :], packed_w_ref[:, j * PACK : (j + 1) * PACK])
        x = x_ref[r, :].astype(f32)
        rms = lax.rsqrt(mean_row(x * x) + eps_norm)
        scaled = grad * pre_gain_ref[...]
        back = (rms * (scaled - x * rms * rms * mean_row(scaled * x))).astype(bf16)
        for c in range(count):
            mine[c, r, :] = back[:, c * cols : (c + 1) * cols]
        return 0

    lax.fori_loop(0, count, back_rows, 0)
    lane = lax.broadcasted_iota(jnp.int32, (share, 128), 1)
    line = lax.broadcasted_iota(jnp.int32, (8, 128), 0)
    w_rows = pl.ds(pl.multiple_of(pos * share, share), share)
    gain = jnp.sum(early_ref[:, at_mix : at_mix + cols] * mix_gate_ref[w_rows, :].astype(f32), axis=1, keepdims=True)
    table = jnp.zeros((share, 128), f32)
    for j in range(heads):
        late = late_ref[j].astype(f32)
        gain = gain + jnp.sum(
            late * packed_w_ref[w_rows, j * PACK : (j + 1) * PACK].astype(f32), axis=1, keepdims=True)
        rate = late[:, rate_lane : rate_lane + 1] + late[:, rate_lane + 1 : rate_lane + 2]
        table = jnp.where(lane == j, rate, table)
        if j == 0:
            for d, peer in peers:
                push_head(mine.at[peer], got.at[d - 1], ib_s.at[d - 1], ib_r.at[d - 1], peer).start()
    table = jnp.where(lane == heads, gain, table)
    flat = jnp.concatenate([table, jnp.zeros((128 - share, 128), f32)], axis=0).T[0:8]
    tile[...] = flat
    for d, peer in peers:
        push_head(tile, tile_got.at[d - 1], th_s.at[d - 1], th_r.at[d - 1], peer).start()
    back = mine[me].astype(f32)
    for d, peer in peers:
        push_head(tile, tile_got.at[d - 1], th_s.at[d - 1], th_r.at[d - 1], peer).wait()
    summed = flat
    for d, peer in peers:
        summed = summed + tile_got[d - 1]
    tile[...] = jnp.where(line == heads, summed, flat)
    for d in range(1, CHAIN):
        push(tile, tiles_ref.at[pos], ts_s.at[d - 1], ts_r.at[d - 1], base + lax.rem(pos + d, CHAIN)).start()
    pltpu.make_async_copy(tile, tiles_ref.at[pos], ts_loc).start()
    for d, peer in peers:
        push_head(mine.at[peer], got.at[d - 1], ib_s.at[d - 1], ib_r.at[d - 1], peer).wait()
        back = back + got[d - 1].astype(f32)
    back_ref[...] = back
    for d in range(1, CHAIN):
        push(tile, tiles_ref.at[pos], ts_s.at[d - 1], ts_r.at[d - 1], base + lax.rem(pos + d, CHAIN)).wait_send()
        await_bytes(tiles_ref.at[lax.rem(pos + CHAIN - d, CHAIN)], ts_r.at[d - 1])
    await_bytes(tiles_ref.at[pos], ts_loc)


def tail(at_mix, grads, packed_w, mix_gate, ggp, x, pre_gain, late, early):
    count = lax.axis_size("head")
    rows, full = x.shape
    width = ggp.shape[1]
    vmem = pl.BlockSpec(memory_space=pltpu.VMEM)
    V = pltpu.VMEM
    dma = pltpu.SemaphoreType.DMA
    trio, seven = dma((count - 1,)), dma((CHAIN - 1,))
    return pl.pallas_call(
        functools.partial(tail_kernel, count, at_mix),
        in_specs=[vmem] * 8,
        out_specs=[vmem] * 2,
        out_shape=[jax.ShapeDtypeStruct((rows, width), f32),
                   jax.ShapeDtypeStruct((CHAIN, 8, 128), f32)],
        scratch_shapes=[V((count, rows, width), bf16), V((count - 1, rows, width), bf16),
                        V((8, 128), f32), V((count - 1, 8, 128), f32),
                        trio, trio, trio, trio, seven, seven, dma],
        compiler_params=pltpu.CompilerParams(
            collective_id=3, has_side_effects=True, vmem_limit_bytes=56 * 1024 * 1024),
        name="tail",
    )(grads, packed_w, mix_gate, ggp, x, pre_gain, late, early)


def final_kernel(at_mix, ffn, down_ref, resid_ref, back_ref, grc_ref, late_ref, early_ref, ends_ref, tiles_ref, small_ref,
                 out_ref, gin_ref, gq_ref, gk_ref, gv_ref, gmix_ref, rate_ref, gwout_ref, gwg_ref, gwu_ref, gwd_ref,
                 w1_ref, b1_ref, w2_ref, b2_ref, ig_ref, ib_ref, rb_ref, vec_ref):
    heads, width, hidden = w1_ref.shape
    cols = heads * width
    out_ref[...] = down_ref[...] + resid_ref[...]
    gin_ref[...] = back_ref[...] + grc_ref[...]
    for i, ref in enumerate((gq_ref, gk_ref, gv_ref)):
        ref[...] = jnp.concatenate([late_ref[j, :, i * width : (i + 1) * width].astype(f32) for j in range(heads)], axis=1)
    gwg_ref[...] = early_ref[:, 0:ffn]
    gwu_ref[...] = early_ref[:, ffn : 2 * ffn]
    gwd_ref[...] = early_ref[:, 2 * ffn : 3 * ffn].T
    both = early_ref[:, at_mix : at_mix + 2 * cols]
    gmix_ref[...] = both[:, 0:cols]
    gwout_ref[...] = both[:, cols:].T
    for j in range(heads):
        w1_ref[j] = ends_ref[j, 0:width, :].astype(f32)
        b1_ref[pl.ds(j, 1), :] = ends_ref[j, width : AUG, :].astype(f32)[0:1]
        second = ends_ref[j, AUG : AUG + width, :].astype(f32)
        w2_ref[j] = (second - jnp.mean(second, axis=0, keepdims=True)).T
        rest = ends_ref[j, AUG + width :, :].astype(f32)[0:8, 0:width]
        b2_ref[pl.ds(j, 1), :] = rest[0:1] - mean_row(rest[0:1])
        ig_ref[pl.ds(j, 1), :] = rest[1:2]
        ib_ref[pl.ds(j, 1), :] = rest[2:3]
        rb_ref[pl.ds(j, 1), :] = rest[3:4] + rest[4:5]
    each = rate_ref.shape[0] // CHAIN
    for p in range(CHAIN):
        turned = jnp.concatenate([tiles_ref[p]] * 16, axis=0).T
        rate_ref[pl.ds(p * each, each), :] = turned[0:each, 0:heads]
    acc = small_ref[0]
    for p in range(1, CHAIN):
        acc = acc + small_ref[p]
    vec_ref[...] = acc


def finish(at_mix, ffn, down, resid, back, grc, late, early, ends, tiles, small, shapes):
    ins = (down, resid, back, grc, late, early, ends, tiles, small)
    vmem = pl.BlockSpec(memory_space=pltpu.VMEM)
    return pl.pallas_call(
        functools.partial(final_kernel, at_mix, ffn),
        in_specs=[vmem] * len(ins),
        out_specs=[vmem] * len(shapes),
        out_shape=[jax.ShapeDtypeStruct(s, f32) for s in shapes],
        compiler_params=pltpu.CompilerParams(vmem_limit_bytes=48 * 1024 * 1024),
        name="final",
    )(*ins)


def stretch_groups(axis):
    count = lax.axis_size(axis)
    return [[start + step for step in range(0, count, CHAIN)] for start in range(CHAIN)]


def bf_product(form, left, right):
    return jnp.einsum(form, left, right, preferred_element_type=f32)


def local(
    inputs,
    pre_gain,
    w_query,
    w_key,
    w_value,
    mix_gate,
    w_rate,
    rate_bias,
    inner_gain,
    inner_bias,
    init_w_one,
    init_b_one,
    init_w_two,
    init_b_two,
    post_gain,
    post_bias,
    w_out,
    ffn_gain,
    w_gate,
    w_up,
    w_down,
    cotangent,
):
    full_width = pre_gain.shape[0]
    rows, local_cols = inputs.shape
    heads, head_dim = inner_gain.shape
    head_index = lax.axis_index("head")
    whole_low = lax.all_gather(inputs, "head", axis=1, tiled=True)
    whole_in = whole_low.astype(f32)
    grad_whole = lax.all_gather(cotangent, "head", axis=1, tiled=True)
    rms_one = lax.rsqrt(jnp.mean(whole_in * whole_in, axis=1, keepdims=True) + eps_norm)
    normed_one = (whole_in * rms_one * pre_gain).astype(bf16)
    stretches = lax.axis_size("seq") // CHAIN
    spare = PACK - 3 * head_dim

    def by_head(weight):
        return weight.reshape(full_width, heads, -1)

    rate_cols = by_head(w_rate)
    packed_w = jnp.concatenate(
        [by_head(w_query), by_head(w_key), by_head(w_value), rate_cols, rate_cols,
         jnp.zeros((full_width, heads, spare - 2), bf16)], axis=2).reshape(full_width, heads * PACK)
    lane = lax.broadcasted_iota(jnp.int32, (1, heads, PACK), 2)
    rate_lane = (lane == 3 * head_dim) | (lane == 3 * head_dim + 1)
    packed_bias = jnp.where(rate_lane, rate_bias[None, :, None], 0.0).reshape(1, heads * PACK)
    low_lane = (lane == 3 * head_dim + 1).reshape(1, heads * PACK)
    pre = bf_product("rd,dc->rc", normed_one, packed_w) + packed_bias
    payload = (pre - jnp.where(low_lane, lax.reduce_precision(pre, 8, 7), 0.0)).astype(bf16)
    gate_pre = bf_product("rd,dc->rc", normed_one, mix_gate)
    share = full_width // CHAIN
    mixed_h, normed_all, *saved = chain_forward(
        payload, normed_one, init_w_one, init_b_one, init_w_two, init_b_two, inner_gain, inner_bias)
    ffn = w_gate.shape[1]
    at_mix = 3 * ffn
    grad_mixed, early, grad_gate_pre, down_cols, resid_cols, grad_resid_cols, small = middle(
        mixed_h, whole_low, grad_whole, gate_pre, normed_one, w_out, w_gate, w_up, w_down,
        post_gain[None], post_bias[None], ffn_gain[None])
    grads, ends, late, early_sum, small = chain_backward(
        grad_mixed, early.reshape(CHAIN // 2, 2, share, early.shape[1]), small, inner_gain, inner_bias,
        normed_all.reshape(CHAIN * rows, full_width), saved)
    back_cols, tiles = tail(
        at_mix, grads, packed_w, mix_gate, grad_gate_pre, whole_low, pre_gain[None],
        late, early_sum)
    if stretches > 1:
        groups = stretch_groups("seq")
        ends, tiles, small = lax.psum((ends.astype(f32), tiles, small), "seq", axis_index_groups=groups)
        seq_index = lax.axis_index("seq")
        stretch_lists = [list(range(s, s + CHAIN)) for s in range(0, stretches * CHAIN, CHAIN)]

        def spread(mine_rows):
            summed = lax.psum(mine_rows, "seq", axis_index_groups=groups)
            total = lax.all_gather(
                summed, "seq", axis=summed.ndim - 2, tiled=True, axis_index_groups=stretch_lists)
            return lax.dynamic_slice_in_dim(
                total, seq_index * (share // stretches), share // stretches, summed.ndim - 2)

        late = spread(late.astype(f32))
        early_sum = spread(early_sum)
    held = share // stretches
    hidden = init_w_one.shape[2]
    square = (held, local_cols)
    (outputs, grad_inputs, grad_q, grad_k, grad_v, grad_mix, grad_rate_w, grad_w_out, grad_w_gate, grad_w_up, grad_w_down,
     grad_one, grad_b_one, grad_two, grad_b_two, grad_gain, grad_bias, rate_b, vectors) = finish(
        at_mix, ffn, down_cols, resid_cols, back_cols, grad_resid_cols, late, early_sum, ends, tiles, small,
        ((rows, local_cols), (rows, local_cols), square, square, square, square, (full_width, heads),
         (local_cols, held), (held, ffn), (held, ffn), (ffn, held),
         (heads, head_dim, hidden), (heads, hidden), (heads, hidden, head_dim), (heads, head_dim),
         (heads, head_dim), (heads, head_dim), (heads, head_dim), (8, full_width)))
    gain_all = tiles[:, heads, :share].reshape(full_width) / pre_gain
    gain_one = lax.dynamic_slice_in_dim(gain_all, head_index * local_cols, local_cols, 0)
    return (
        outputs,
        grad_inputs,
        gain_one,
        grad_q,
        grad_k,
        grad_v,
        grad_mix,
        grad_rate_w,
        rate_b[:, 0],
        grad_gain,
        grad_bias,
        grad_one,
        grad_b_one,
        grad_two,
        grad_b_two,
        vectors[1, :local_cols],
        vectors[2, :local_cols],
        grad_w_out,
        vectors[0],
        grad_w_gate,
        grad_w_up,
        grad_w_down,
    )


def solution(mesh):
    in_specs = (
        P("seq", "head"),
        P(),
        P(None, "head"),
        P(None, "head"),
        P(None, "head"),
        P(None, "head"),
        P(None, "head"),
        P("head"),
        P("head", None),
        P("head", None),
        P("head", None, None),
        P("head", None),
        P("head", None, None),
        P("head", None),
        P("head"),
        P("head"),
        P("head", None),
        P(),
        P(None, "head"),
        P(None, "head"),
        P("head", None),
        P("seq", "head"),
    )
    out_specs = (
        P("seq", "head"),
        P("seq", "head"),
        P("head"),
        P("seq", "head"),
        P("seq", "head"),
        P("seq", "head"),
        P("seq", "head"),
        P(None, "head"),
        P("head"),
        P("head", None),
        P("head", None),
        P("head", None, None),
        P("head", None),
        P("head", None, None),
        P("head", None),
        P("head"),
        P("head"),
        P("head", "seq"),
        P(),
        P("seq", "head"),
        P("seq", "head"),
        P("head", "seq"),
    )
    return jax.shard_map(local, mesh=mesh, in_specs=in_specs, out_specs=out_specs, check_vma=False)
```

```python
import functools

import jax
import jax.numpy as jnp
from jax import lax
from jax.experimental import pallas as pl
from jax.experimental.pallas import tpu as pltpu
from jax.sharding import PartitionSpec as P

MINI = 16
CHAIN = 8
FIRST = 2
AUG = 80
eps_norm = 1e-06
gelu_scale = 0.7978845608028654
f32 = jnp.float32
bf16 = jnp.bfloat16


def dot_nn(a, b):
    return lax.dot_general(a, b, (((1,), (0,)), ((), ())), preferred_element_type=f32)


def dot_nt(a, b):
    return lax.dot_general(a, b, (((1,), (1,)), ((), ())), preferred_element_type=f32)


def dot_tn(a, b):
    return lax.dot_general(a, b, (((0,), (0,)), ((), ())), preferred_element_type=f32)


def mean_row(x):
    return jnp.sum(x, axis=1, keepdims=True) * (1.0 / x.shape[1])


def gelu_first(z):
    sq = z * z
    th = jnp.tanh(gelu_scale * z * (1.0 + 0.044715 * sq))
    half = 0.5 * (1.0 + th)
    act = z * half
    der = half + (0.5 * gelu_scale) * z * (1.0 - th * th) * (1.0 + 0.134145 * sq)
    return act, der


def gelu_second(z):
    sq = z * z
    th = jnp.tanh(gelu_scale * z * (1.0 + 0.044715 * sq))
    half = 0.5 * (1.0 + th)
    act = z * half
    slope = gelu_scale * (1.0 + 0.134145 * sq)
    sech = 1.0 - th * th
    der = half + 0.5 * z * sech * slope
    curve = sech * (slope + z * (0.5 * gelu_scale * 0.26829 * z) - z * th * slope * slope)
    return act, der, curve


def tri_mask():
    rows = lax.broadcasted_iota(jnp.int32, (MINI, MINI), 0)
    cols = lax.broadcasted_iota(jnp.int32, (MINI, MINI), 1)
    return jnp.where(rows >= cols, 1.0, 0.0).astype(f32)


def forward_output(kept, gain, bias, tri, sink):
    z1b, act_h, w2_h, b2, s2_h = kept
    actb, _ = gelu_first(z1b)
    actb_h = actb.astype(bf16)
    yield
    att = dot_nt(actb_h, act_h)
    z2b = dot_nt(actb_h, w2_h) + b2
    yield
    z2b = z2b - dot_nn(((att + 1.0) * tri).astype(bf16), s2_h)
    yield
    z2b = z2b - mean_row(z2b)
    yield
    invb = lax.rsqrt(mean_row(z2b * z2b) + eps_norm)
    sink(z2b * invb * gain + bias, z2b)
    yield


def forward_chain(state, z1, post, key_aug, key_next, query_aug, base, rate, gain_sq, tri, save):
    w1, w2t, b2 = state
    width = gain_sq.shape[1]
    scale = 1.0 / width
    w2_h = w2t.astype(bf16)
    act, der = gelu_first(z1)
    act_h = act.astype(bf16)
    z = dot_nt(act_h, w2_h) + b2
    next(post, None)
    fixed = dot_nn(
        jnp.concatenate([base, jnp.broadcast_to(gain_sq, (8, width)), jnp.ones((8, width), f32)], axis=0).astype(bf16),
        w2_h)
    both = jnp.concatenate([key_next, query_aug], axis=0)
    coef = dot_nt(both, key_aug)
    coef = jnp.concatenate([coef[:MINI], coef[MINI:] * tri], axis=0).astype(bf16)
    m_b = mean_row(base)
    m_sq = mean_row(gain_sq)
    w1_h = w1.astype(bf16)
    next(post, None)
    zg = z * gain_sq
    prods = dot_nn(jnp.concatenate([zg, z], axis=0).astype(bf16), w2_h)
    mz = mean_row(z)
    m_zz = mean_row(z * z)
    m_zg = mean_row(zg)
    m_zzg = mean_row(zg * z)
    m_zb = mean_row(z * base)
    zz = dot_nn(both, w1_h)
    next(post, None)
    inv = lax.rsqrt(m_zz - mz * mz + eps_norm)
    c_zg = m_zg - mz * m_sq
    c_zzg = m_zzg - mz * (m_zg + c_zg)
    c_zb = m_zb - mz * m_b
    m_g = inv * c_zg + m_b
    m_gn = inv * (inv * c_zzg + c_zb)
    rinv = rate * inv
    rinv2 = rinv * inv
    skew = rinv2 * m_gn
    shift = skew * mz - rinv * m_g
    upd = (rinv2 * prods[:MINI] - skew * prods[MINI:]) + (
        (rinv * fixed[:MINI] + shift * fixed[MINI + 8 : MINI + 9]) - (rinv2 * mz) * fixed[MINI : MINI + 1])
    s1_h = (upd * der).astype(bf16)
    zz = zz - dot_nn(coef, s1_h)
    zc = z - mz
    s2 = rinv2 * zc * gain_sq - skew * zc + (rinv * base - rinv * m_g)
    s2_h = s2.astype(bf16)
    new_w2t = w2t - dot_tn(s2_h, act_h)
    new_w1 = w1 - dot_tn(key_aug, s1_h)
    new_b2 = b2 - jnp.sum(s2, axis=0, keepdims=True)
    next(post, None)
    next(post, None)
    z1b = zz[MINI:]
    save(w1_h, w2_h, z1, upd, zc, s2, z1b)
    return (new_w1, new_w2t, new_b2), zz[:MINI], (z1b, act_h, w2_h, b2, s2_h)


def prepare_back(store, saved, d_out, key_aug, query_aug, target, rate, gain, gain_sq, bias, tri):
    w1_h, w2_h, z1, upd, zc, s2, z1b, z2b = saved
    width = gain.shape[1]
    s2_h = s2.astype(bf16)
    actb, derb = gelu_first(z1b)
    actb_h = actb.astype(bf16)
    invb = lax.rsqrt(mean_row(z2b * z2b) + eps_norm)
    dn = d_out * gain
    m_dn = mean_row(dn)
    yield
    act, der, curve = gelu_second(z1)
    act_h = act.astype(bf16)
    s1_h = (upd * der).astype(bf16)
    store.update(act=act_h, der=der, bend=upd * curve, actb=actb_h, s1=s1_h, s2=s2_h)
    yield
    att2 = dot_nt(actb_h, act_h)
    att1 = dot_nt(query_aug, key_aug)
    nb = z2b * invb
    d_z2b = invb * (dn - m_dn - nb * mean_row(dn * nb))
    d_z2b_h = d_z2b.astype(bf16)
    yield
    inv = lax.rsqrt(mean_row(zc * zc) + eps_norm)
    d_att2 = dot_nt(d_z2b_h, s2_h)
    d_actb = dot_nn(d_z2b_h, w2_h)
    base = (bias - target) * gain
    m_sq = mean_row(gain_sq)
    yield
    att2 = ((att2 + 1.0) * tri).astype(bf16)
    att1 = (att1 * tri).astype(bf16)
    n = zc * inv
    ng = n * gain_sq
    big_g = ng + base
    m_g = mean_row(big_g)
    m_gn = mean_row(big_g * n)
    yield
    d_att2 = (-d_att2 * tri).astype(bf16)
    d_actb = d_actb + dot_nn(d_att2, act_h)
    c2 = dot_tn(att2, d_z2b_h)
    m_ng = mean_row(ng)
    m_nng = mean_row(n * ng)
    yield
    c3 = dot_tn(d_att2, actb_h)
    inv2 = inv * inv
    g = inv * (big_g - m_g - n * m_gn)
    fac = rate * inv2 * (gain_sq - m_gn)
    scale = rate * (1.0 / width)
    weights = (jnp.broadcast_to(scale, n.shape), scale * n, scale * gain_sq, scale * (ng * inv2 + g * inv))
    store.update(c2=c2, c3=c3, fac=fac, weights=weights, inv=inv, inv2=inv2, n=n)
    yield
    d_z1b_h = (d_actb * derb).astype(bf16)
    c1 = dot_tn(att1, d_z1b_h)
    row1 = inv2 * (gain_sq - (m_sq + m_gn) - n * m_ng)
    row2 = inv2 * (ng + big_g - (m_ng + m_g) - n * (m_nng + 2.0 * m_gn))
    store.update(dz2b=d_z2b_h, dz2bf=d_z2b, dz1b=d_z1b_h, c1=c1, row1=row1, row2=row2)
    yield
    fixed = dot_nn(jnp.concatenate([row1, row2, jnp.broadcast_to(inv2, n.shape), n], axis=0).astype(bf16), w2_h)
    d_att1 = dot_nt(d_z1b_h, s1_h)
    d_query = dot_nt(d_z1b_h, w1_h)
    yield
    prods = tuple(fixed[i * MINI : (i + 1) * MINI] for i in range(4))
    store.update(prods=prods)
    d_att1 = (-d_att1 * tri).astype(bf16)
    d_query = (d_query + dot_nn(d_att1, key_aug))[:, :width] + d_out
    d_key = dot_tn(d_att1, query_aug)[:, :width]
    yield
    d_gain = jnp.sum(d_out * nb, axis=0, keepdims=True)
    d_bias = jnp.sum(d_out, axis=0, keepdims=True)
    store.update(dq=d_query, dk=d_key, d_gain=d_gain, d_bias=d_bias, rate=rate, w1=w1_h, w2=w2_h, s2f=s2,
                 key=key_aug, query=query_aug, gslope=2.0 * n * gain + bias - target)
    yield


PIECES = 11


def settle(post, width):
    if post is None:
        return
    pre, d_s2, a1, a2, d_z1_h, p1_h, keep, gain, sink = post
    d_g = pre["inv"] * (pre["rate"] * d_s2 - a1 - pre["n"] * a2)
    d_gg = d_g * gain
    key_part = dot_nt(d_z1_h, pre["w1"])
    late_part = dot_nt(pre["s1"], p1_h)
    d_logit = keep * jnp.sum(d_s2 * pre["s2f"], axis=1, keepdims=True)
    yield
    d_gain = pre["d_gain"] + jnp.sum(d_g * pre["gslope"], axis=0, keepdims=True)
    d_bias = pre["d_bias"] + jnp.sum(d_gg, axis=0, keepdims=True)
    d_key = pre["dk"] + d_gg + (key_part - late_part)[:, :width]
    sink(pre["dq"], d_key, -d_gg, d_logit, d_gain, d_bias)
    yield


def drain(maker):
    for _ in maker:
        pass


def backward_chain(carry, pre, post, fill, keep, gain, sink):
    p1, p2t, p2, dz, kq, left, right, dsum = carry
    width = gain.shape[1]
    key, act, der, w2_h = pre["key"], pre["act"], pre["der"], pre["w2"]
    after = settle(post, width)
    p1_h = p1.astype(bf16)
    coef1 = dot_nt(key, kq).astype(bf16)
    base1 = pre["c1"] + dot_nn(key, p1_h)
    d_s1 = -base1 - dot_nn(coef1, dz)
    p2_h = p2t.astype(bf16)
    coef2 = dot_nt(act, right).astype(bf16)
    p2 = p2 + dsum
    base2 = pre["c2"] + p2 + dot_nt(act, p2_h)
    fill(2)
    side = base2 + dot_nn(coef2, left)
    p1 = p1 + dot_tn(kq, dz)
    p2t = p2t + dot_tn(left, right)
    next(after, None)
    fill(1)
    d_upd = d_s1 * der
    d_upd_h = d_upd.astype(bf16)
    d_s2 = dot_nt(d_upd_h, w2_h) - side
    rest = pre["c3"] - dot_nn(pre["s2"], p2t.astype(bf16))
    p1_h = p1.astype(bf16)
    bend = d_s1 * pre["bend"]
    next(after, None)
    fill(3)
    d_fac = d_s2 * pre["fac"]
    main = dot_nn(d_fac.astype(bf16), w2_h)
    a1, a2, a3, a4 = (jnp.sum(d_s2 * w, axis=1, keepdims=True) for w in pre["weights"])
    fill(5)
    y1, y2, y3, y4 = pre["prods"]
    d_act = (main + rest) - ((a1 * y1 + a2 * y2) + (a3 * y3 + a4 * y4))
    d_z1_h = (d_act * der + bend).astype(bf16)
    d_zc = d_fac - ((a1 * pre["row1"] + a2 * pre["row2"]) + (a3 * pre["inv2"] + a4 * pre["n"]))
    d_zc_h = d_zc.astype(bf16)
    carry = (p1, p2t, p2, jnp.concatenate([d_z1_h, pre["dz1b"]], axis=0),
             jnp.concatenate([key, pre["query"]], axis=0),
             jnp.concatenate([pre["s2"], d_zc_h, pre["dz2b"]], axis=0),
             jnp.concatenate([d_upd_h, act, pre["actb"]], axis=0),
             jnp.sum(d_zc + pre["dz2bf"], axis=0, keepdims=True))
    return carry, (pre, d_s2, a1, a2, d_z1_h, p1_h, keep, gain, sink)


def backward_close(carry):
    p1, p2t, p2, dz, kq, left, right, dsum = carry
    return p1 + dot_tn(kq, dz), p2t + dot_tn(left, right), p2 + dsum


MESH = pl.DeviceIdType.MESH
PACK = 256
ENDS = 160


def seq_place():
    index = lax.axis_index("seq")
    pos = lax.rem(index, CHAIN)
    return pos, index - pos


def meet_group(pos, base):
    barrier = pltpu.get_barrier_semaphore()
    for d in range(1, CHAIN):
        pl.semaphore_signal(
            barrier, inc=1, device_id={"seq": base + lax.rem(pos + d, CHAIN)}, device_id_type=MESH)
    pl.semaphore_wait(barrier, CHAIN - 1)


def push(src, dst, send_sem, recv_sem, target):
    return pltpu.make_async_remote_copy(
        src_ref=src, dst_ref=dst, send_sem=send_sem, recv_sem=recv_sem,
        device_id={"seq": target}, device_id_type=MESH)


def await_bytes(ref, sem):
    pltpu.make_async_copy(ref, ref, sem).wait()


def swap_start(src, dst, send, recv, local_sem, pos, base):
    for d in range(1, CHAIN):
        peer = lax.rem(pos + d, CHAIN)
        push(src.at[peer], dst.at[pos], send.at[d - 1], recv.at[d - 1], base + peer).start()
    pltpu.make_async_copy(src.at[pos], dst.at[pos], local_sem).start()


def swap_wait(src, dst, send, recv, local_sem, pos, base):
    for d in range(1, CHAIN):
        peer = lax.rem(pos + d, CHAIN)
        origin = lax.rem(pos + CHAIN - d, CHAIN)
        push(src.at[peer], dst.at[pos], send.at[d - 1], recv.at[d - 1], base + peer).wait_send()
        await_bytes(dst.at[origin], recv.at[d - 1])
    await_bytes(dst.at[pos], local_sem)


def fwd_kernel(block, heads, count, pay_ref, ct_ref, w1_in, b1_in, w2_in, b2_in, gain_in, bias_in,
               mixed_ref, ct_out, k_out, q_out, aux_out, w1s_ref, w2s_ref, z1s_ref, upd_ref, zc_ref, s2_ref, z1b_ref, z2b_ref,
               got, k_all, q_all, base_all, aux_all, mixed_all, w1, w2t, b2, z1,
               pay_send, pay_recv, mix_send, mix_recv, ct_send, ct_recv, ct_loc):
    blk = pl.program_id(0)
    last = pl.num_programs(0) - 1
    pos, base = seq_place()
    width = gain_in.shape[1]
    hidden = w1.shape[1]
    rows_each = pay_ref.shape[0]
    per = rows_each // block
    piece = got.shape[1]
    parts = rows_each // piece
    owner = (pos >= FIRST) & (pos < FIRST + heads)
    mine = jnp.clip(pos - FIRST, 0, heads - 1)
    gain = gain_in[pl.ds(mine, 1), :]
    bias = bias_in[pl.ds(mine, 1), :]
    gain_sq = gain * gain
    tri = tri_mask()

    me, _ = head_place()

    @pl.when(blk == 0)
    def _():
        barrier = pltpu.get_barrier_semaphore()
        for d in range(1, count):
            pl.semaphore_signal(barrier, inc=1, device_id={"head": lax.rem(me + d, count)}, device_id_type=MESH)
        for d in range(1, CHAIN):
            pl.semaphore_signal(
                barrier, inc=1, device_id={"seq": base + lax.rem(pos + d, CHAIN)}, device_id_type=MESH)
        pl.semaphore_wait(barrier, CHAIN - 1 + count - 1)
        for s in range(parts):
            for j in range(heads):
                src = pay_ref.at[s * piece : (s + 1) * piece, j * PACK : (j + 1) * PACK]
                dst = got.at[pos * parts + s]

                @pl.when(pos != FIRST + j)
                def _():
                    push(src, dst, pay_send.at[j], pay_recv.at[pos * parts + s], base + FIRST + j).start()

                @pl.when(pos == FIRST + j)
                def _():
                    pltpu.make_async_copy(src, dst, pay_recv.at[pos * parts + s]).start()

    @pl.when(blk == 1)
    def _():
        for d in range(1, count):
            push_head(ct_ref, ct_out.at[me], ct_send.at[d - 1], ct_recv.at[d - 1], lax.rem(me + d, count)).start()
        pltpu.make_async_copy(ct_ref, ct_out.at[me], ct_loc).start()

    def take_in(p):
        await_bytes(got.at[p], pay_recv.at[p])
        part = got[p]
        rows = pl.ds(pl.multiple_of(p * piece, piece), piece)
        lane = lax.broadcasted_iota(jnp.int32, (piece, AUG), 1)
        one = jnp.ones((), bf16)
        zero = jnp.zeros((), bf16)
        tail = jnp.where(lane == width, one, zero)
        query = part[:, :AUG]
        key = part[:, width : width + AUG]
        q_all[rows, :] = jnp.where(lane < width, query, tail)
        k_all[rows, :] = jnp.where(lane < width, key, tail)
        key_f = part[:, width : 2 * width].astype(f32)
        target = part[:, 2 * width : 3 * width].astype(f32) - key_f
        logit = part[:, 3 * width : 3 * width + 1].astype(f32) + part[:, 3 * width + 1 : 3 * width + 2].astype(f32)
        sig = 1.0 / (1.0 + jnp.exp(-logit))
        base_all[rows, :] = (bias - target) * gain
        spot = lax.broadcasted_iota(jnp.int32, (piece, 2 * width), 1)
        wide = jnp.concatenate([target, target], axis=1)
        aux_all[rows, :] = jnp.where(
            spot < width, wide, jnp.where(spot == width, sig * (1.0 / width), 1.0 - sig))

    def send_mixed(b):
        p = lax.div(b, per)
        src = mixed_all.at[pl.ds(pl.multiple_of(b * block, block), block), :]
        dst = mixed_ref.at[mine, pl.ds(pl.multiple_of(lax.rem(b, per) * block, block), block), :]

        @pl.when(p != pos)
        def _():
            push(src, dst, mix_send, mix_recv.at[mine], base + p).start()

        @pl.when(p == pos)
        def _():
            pltpu.make_async_copy(src, dst, mix_recv.at[mine]).start()

    @pl.when(owner)
    def _():
        @pl.when(blk == 0)
        def _():
            row = lax.broadcasted_iota(jnp.int32, (AUG - width, hidden), 0)
            w1[pl.ds(0, width), :] = w1_in[mine]
            w1[pl.ds(width, AUG - width), :] = jnp.where(row == 0, b1_in[pl.ds(mine, 1), :], 0.0)
            turned = w2_in[mine]
            w2t[...] = turned - jnp.mean(turned, axis=0, keepdims=True)
            start = b2_in[pl.ds(mine, 1), :]
            b2[...] = start - mean_row(start)
            k_all[pl.ds(CHAIN * rows_each, MINI), :] = jnp.zeros((MINI, AUG), bf16)

        @pl.when(blk > 0)
        def _():
            send_mixed(blk - 1)

        def bring(p, _):
            take_in(p)
            return 0

        lax.fori_loop(jnp.where(blk == 0, 0, 2 * blk + 1), jnp.minimum(2 * blk + 3, 2 * last + 2), bring, 0)

        @pl.when(blk == 0)
        def _():
            z1[...] = dot_nn(k_all[0:MINI, :], w1[...].astype(bf16))

        state = (w1[...], w2t[...], b2[...])
        z1_now = z1[...]
        post = iter(())
        for loc in range(block // MINI):
            row = pl.multiple_of(blk * block + loc * MINI, MINI)
            rows = pl.ds(row, MINI)
            lr = pl.ds(loc * MINI, MINI)
            q_aug = q_all[rows, :]

            def save(w1_h, w2_h, z1_v, upd, zc, s2, z1b, loc=loc, lr=lr):
                w1s_ref[loc] = w1_h
                w2s_ref[loc] = w2_h
                z1s_ref[lr, :] = z1_v
                upd_ref[lr, :] = upd
                zc_ref[lr, :] = zc
                s2_ref[lr, :] = s2
                z1b_ref[lr, :] = z1b

            state, z1_now, kept = forward_chain(
                state, z1_now, post, k_all[rows, :], k_all[pl.ds(row + MINI, MINI), :], q_aug,
                base_all[rows, :], aux_all[rows, width : width + 1], gain_sq, tri, save)

            def sink(out, z2b, lr=lr, rows=rows, q_aug=q_aug):
                z2b_ref[lr, :] = z2b
                mixed_all[rows, :] = (out + q_aug[:, :width].astype(f32)).astype(bf16)

            post = forward_output(kept, gain, bias, tri, sink)
        drain(post)
        w1[...], w2t[...], b2[...] = state
        z1[...] = z1_now

        brows = pl.ds(pl.multiple_of(blk * block, block), block)
        k_out[...] = k_all[brows, :]
        q_out[...] = q_all[brows, :]
        aux_out[...] = aux_all[brows, :]

    @pl.when(blk == last)
    def _():
        @pl.when(owner)
        def _():
            send_mixed(last)
            others = mixed_all.at[pl.ds(0, (CHAIN - 1) * rows_each), :]
            await_bytes(others, mix_send)
        for j in range(heads):
            @pl.when(pos != FIRST + j)
            def _():
                await_bytes(got.at[pl.ds(0, parts)], pay_send.at[j])

            await_bytes(mixed_ref.at[j], mix_recv.at[j])

        for d in range(1, count):
            push_head(ct_ref, ct_out.at[me], ct_send.at[d - 1], ct_recv.at[d - 1],
                      lax.rem(me + d, count)).wait_send()
            await_bytes(ct_out.at[lax.rem(me + count - d, count)], ct_recv.at[d - 1])
        await_bytes(ct_out.at[me], ct_loc)


def chain_forward(payload, ct, w1, b1, w2, b2, gain, bias, block=256):
    rows = payload.shape[0]
    heads, width, hidden = w1.shape
    count = lax.axis_size("head")
    tokens = rows * CHAIN
    steps = tokens // MINI
    nb = block // MINI
    whole = lambda a: pl.BlockSpec(a.shape, lambda i: (0,) * a.ndim)
    rowblk = lambda w: pl.BlockSpec((block, w), lambda i: (i, 0))
    stepblk = lambda r: pl.BlockSpec((nb, r, hidden), lambda i: (i, 0, 0))
    anywhere = pl.BlockSpec(memory_space=pl.ANY)
    small = (w1, b1, w2, b2, gain, bias)
    dma = pltpu.SemaphoreType.DMA
    wide = jax.ShapeDtypeStruct((tokens, hidden), f32)
    narrow = jax.ShapeDtypeStruct((tokens, width), f32)
    return pl.pallas_call(
        functools.partial(fwd_kernel, block, heads, count),
        grid=(tokens // block,),
        in_specs=[anywhere, anywhere] + [whole(a) for a in small],
        out_specs=[anywhere, anywhere, rowblk(AUG), rowblk(AUG), rowblk(2 * width), stepblk(AUG), stepblk(width),
                   rowblk(hidden), rowblk(hidden), rowblk(width), rowblk(width), rowblk(hidden), rowblk(width)],
        out_shape=[jax.ShapeDtypeStruct((heads, rows, width), bf16),
                   jax.ShapeDtypeStruct((count,) + ct.shape, bf16),
                   jax.ShapeDtypeStruct((tokens, AUG), bf16),
                   jax.ShapeDtypeStruct((tokens, AUG), bf16),
                   jax.ShapeDtypeStruct((tokens, 2 * width), f32),
                   jax.ShapeDtypeStruct((steps, AUG, hidden), bf16),
                   jax.ShapeDtypeStruct((steps, width, hidden), bf16),
                   wide, wide, narrow, narrow, wide, narrow],
        scratch_shapes=[pltpu.VMEM((2 * tokens // block, block // 2, PACK), bf16),
                        pltpu.VMEM((tokens + MINI, AUG), bf16), pltpu.VMEM((tokens, AUG), bf16),
                        pltpu.VMEM((tokens, width), f32), pltpu.VMEM((tokens, 2 * width), f32),
                        pltpu.VMEM((tokens, width), bf16),
                        pltpu.VMEM((AUG, hidden), f32), pltpu.VMEM((width, hidden), f32),
                        pltpu.VMEM((1, width), f32), pltpu.VMEM((MINI, hidden), f32),
                        dma((heads,)), dma((2 * tokens // block,)), dma, dma((heads,)),
                        dma((count - 1,)), dma((count - 1,)), dma],
        compiler_params=pltpu.CompilerParams(collective_id=0, has_side_effects=True),
        name="inner_forward",
    )(payload, ct, *small)


def bwd_kernel(block, heads, turn, gm_ref, early_ref, small_ref, gain_in, bias_in, norm_ref, norm_last_ref,
               k_ref, q_ref, aux_ref, w1s_ref, w2s_ref, z1s_ref, upd_ref, zc_ref, s2_ref, z1b_ref, z2b_ref,
               grads_ref, ends_ref, late_ref, early_out, small_out,
               dout, half_got, half_mine, quarter, quarter_got, packed, ends, weights, late,
               p1, p2t, p2, dz, kq, left, right, dsum, dg, db, dl,
               gm_send, gm_recv, ha_send, ha_recv, ha_loc, qu_send, qu_recv, sm_send, sm_recv, sm_loc, bc_send, bc_recv, en_send, en_recv, la_send, la_recv):
    pid = pl.program_id(0)
    last = pl.num_programs(0) - 1
    blk = last - pid
    pos, base = seq_place()
    width = gain_in.shape[1]
    rows_each = gm_ref.shape[1]
    per = rows_each // block
    owner = (pos >= FIRST) & (pos < FIRST + heads)
    mine = jnp.clip(pos - FIRST, 0, heads - 1)
    gain = gain_in[pl.ds(mine, 1), :]
    bias = bias_in[pl.ds(mine, 1), :]
    gain_sq = gain * gain
    tri = tri_mask()
    count = block // MINI
    side = lax.rem(pos, 2)
    rank = lax.div(pos, 2)
    partner = pos + 1 - 2 * side
    state = (p1, p2t, p2, dz, kq, left, right, dsum)

    @pl.when(pid == 0)
    def _():
        meet_group(pos, base)
        for j in range(heads):
            @pl.when(pos != FIRST + j)
            def _():
                push(gm_ref.at[j], dout.at[pos], gm_send.at[j], gm_recv.at[pos], base + FIRST + j).start()

            @pl.when(pos == FIRST + j)
            def _():
                pltpu.make_async_copy(gm_ref.at[j], dout.at[pos], gm_recv.at[pos]).start()

        for d in range(1, CHAIN):
            push(small_ref, small_out.at[pos], sm_send.at[d - 1], sm_recv.at[d - 1],
                 base + lax.rem(pos + d, CHAIN)).start()
        pltpu.make_async_copy(small_ref, small_out.at[pos], sm_loc).start()
        push(early_ref.at[:, 1 - side], half_got, ha_send, ha_recv, base + partner).start()
        pltpu.make_async_copy(early_ref.at[:, side], half_mine, ha_loc).start()

    @pl.when(pid == turn)
    def _():
        push(early_ref.at[:, 1 - side], half_got, ha_send, ha_recv, base + partner).wait()
        await_bytes(half_mine, ha_loc)

        def pair_up(c, _):
            rows = pl.ds(pl.multiple_of(c * MINI, MINI), MINI)
            for r in range(CHAIN // 2):
                quarter[r, rows, :] = (half_mine[r, rows, :].astype(f32) + half_got[r, rows, :].astype(f32)).astype(bf16)
            return 0

        lax.fori_loop(0, half_mine.shape[1] // MINI, pair_up, 0)
        for d in range(1, CHAIN // 2):
            other = lax.rem(rank + d, CHAIN // 2)
            push(quarter.at[other], quarter_got.at[d - 1], qu_send.at[d - 1], qu_recv.at[d - 1],
                 base + 2 * other + side).start()

    def share_block(b):
        p = lax.div(b, per)
        src = packed.at[pl.ds(pl.multiple_of(b * block, block), block), :]
        dst = grads_ref.at[mine, pl.ds(pl.multiple_of(lax.rem(b, per) * block, block), block), :]

        @pl.when(p != pos)
        def _():
            push(src, dst, bc_send, bc_recv.at[mine], base + p).start()

        @pl.when(p == pos)
        def _():
            pltpu.make_async_copy(src, dst, bc_recv.at[mine]).start()

    share = late.shape[1]

    def weigh(norm, b, lo, hi):
        rows = pl.ds(pl.multiple_of(b * block, block), block)
        weights[lo:hi, :] += dot_tn(norm[:, lo:hi], packed[rows, :])

    slabs = [(i * 128, i * 128 + 128) for i in range(norm_ref.shape[1] // 128)]

    @pl.when(owner)
    def _():
        @pl.when(pid == 0)
        def _():
            for r in state + (dg, db, dl, weights):
                r[...] = jnp.zeros_like(r)
            packed[pl.ds(0, block), :] = jnp.zeros((block, PACK), bf16)

        @pl.when(lax.rem(pid, per) == 0)
        def _():
            p = lax.div(blk, per)
            await_bytes(dout.at[p], gm_recv.at[p])

        @pl.when(pid > 0)
        def _():
            share_block(blk + 1)

        carry = tuple(r[...] for r in state)
        totals = [dg[...], db[...], dl[...]]
        made = {}

        def start(loc):
            made[loc] = {}
            lr = pl.ds(loc * MINI, MINI)
            inner = pl.ds(pl.multiple_of(lax.rem(blk, per) * block + loc * MINI, MINI), MINI)
            saved = (w1s_ref[loc], w2s_ref[loc], z1s_ref[lr, :], upd_ref[lr, :], zc_ref[lr, :], s2_ref[lr, :],
                     z1b_ref[lr, :], z2b_ref[lr, :])
            return prepare_back(made[loc], saved, dout[lax.div(blk, per), inner, :].astype(f32), k_ref[lr, :],
                                q_ref[lr, :], aux_ref[lr, 0:width], aux_ref[lr, width : width + 1],
                                gain, gain_sq, bias, tri)

        drain(start(count - 1))
        post = None
        for loc in range(count - 1, -1, -1):
            ahead = start(loc - 1) if loc > 0 else iter(())

            def fill(pieces, ahead=ahead):
                for _ in range(pieces):
                    next(ahead, None)

            def sink(d_query, d_key, d_value, d_logit, d_gain, d_bias, loc=loc):
                totals[0] = totals[0] + d_gain
                totals[1] = totals[1] + d_bias
                totals[2] = totals[2] + jnp.sum(d_logit, axis=0, keepdims=True)
                high = d_logit.astype(bf16).astype(f32)
                lane = lax.broadcasted_iota(jnp.int32, (MINI, width), 1)
                extra = jnp.where(lane == 0, high, jnp.where(lane == 1, d_logit - high, 0.0))
                rows = pl.ds(pl.multiple_of(blk * block + loc * MINI, MINI), MINI)
                packed[rows, :] = jnp.concatenate([d_query, d_key, d_value, extra], axis=1).astype(bf16)

            if (count - 1 - loc) % 2 == 0 and (count - 1 - loc) // 2 < len(slabs):
                weigh(norm_ref, jnp.where(pid == 0, 0, blk + 1), *slabs[(count - 1 - loc) // 2])
            carry, post = backward_chain(
                carry, made.pop(loc), post, fill, aux_ref[pl.ds(loc * MINI, MINI), width + 1 : width + 2], gain, sink)
        drain(settle(post, width))
        for r, v in zip(state, carry):
            r[...] = v
        dg[...], db[...], dl[...] = totals

        @pl.when(pid == last)
        def _():
            end_one, end_two, end_b_two = backward_close(tuple(r[...] for r in state))
            ends[pl.ds(0, AUG), :] = end_one.astype(bf16)
            ends[pl.ds(AUG, width), :] = end_two.astype(bf16)
            rest = ENDS - AUG - width
            row = lax.broadcasted_iota(jnp.int32, (rest, width), 0)
            tailing = jnp.where(row == 0, end_b_two, jnp.where(row == 1, dg[...], jnp.where(row == 2, db[...], 0.0)))
            high = dl[...].astype(bf16).astype(f32)
            tailing = tailing + jnp.where(row == 3, high, jnp.where(row == 4, dl[...] - high, 0.0))
            ends[pl.ds(AUG + width, rest), :] = jnp.concatenate([tailing] * 4, axis=1).astype(bf16)
            share_block(0)
            for slab in slabs:
                weigh(norm_last_ref, 0, *slab)
            for p in range(CHAIN):
                late[p] = weights[p * share : (p + 1) * share, :].astype(bf16)
            for d in range(1, CHAIN):
                peer = lax.rem(pos + d, CHAIN)
                push(late.at[peer], late_ref.at[mine], la_send.at[d - 1], la_recv.at[mine], base + peer).start()
            pltpu.make_async_copy(late.at[pos], late_ref.at[mine], la_recv.at[mine]).start()
            for d in range(1, CHAIN):
                push(ends, ends_ref.at[mine], en_send.at[d - 1], en_recv.at[mine],
                     base + lax.rem(pos + d, CHAIN)).start()
            pltpu.make_async_copy(ends, ends_ref.at[mine], en_recv.at[mine]).start()

    @pl.when(pid == last)
    def _():
        for d in range(1, CHAIN // 2):
            other = lax.rem(rank + d, CHAIN // 2)
            push(quarter.at[other], quarter_got.at[d - 1], qu_send.at[d - 1], qu_recv.at[d - 1],
                 base + 2 * other + side).wait()
        for d in range(1, CHAIN):
            push(small_ref, small_out.at[pos], sm_send.at[d - 1], sm_recv.at[d - 1],
                 base + lax.rem(pos + d, CHAIN)).wait_send()
            await_bytes(small_out.at[lax.rem(pos + CHAIN - d, CHAIN)], sm_recv.at[d - 1])
        await_bytes(small_out.at[pos], sm_loc)

        def add_up(c, _):
            rows = pl.ds(pl.multiple_of(c * MINI, MINI), MINI)
            acc = quarter[rank, rows, :].astype(f32)
            for d in range(1, CHAIN // 2):
                acc = acc + quarter_got[d - 1, rows, :].astype(f32)
            early_out[rows, :] = acc
            return 0

        lax.fori_loop(0, early_out.shape[0] // MINI, add_up, 0)
        for j in range(heads):
            @pl.when(pos != FIRST + j)
            def _():
                await_bytes(dout.at[pos], gm_send.at[j])

            await_bytes(grads_ref.at[j], bc_recv.at[j])
            await_bytes(ends_ref.at[j], en_recv.at[j])
            await_bytes(late_ref.at[j], la_recv.at[j])

        @pl.when(owner)
        def _():
            await_bytes(packed.at[pl.ds(0, (CHAIN - 1) * rows_each), :], bc_send)
            for d in range(1, CHAIN):
                await_bytes(ends, en_send.at[d - 1])
                await_bytes(late.at[0], la_send.at[d - 1])


def chain_backward(grad_mixed, early, small, gain, bias, normed, saved, block=256, turn=3):
    heads, rows, width = grad_mixed.shape
    tokens = rows * CHAIN
    hidden = saved[5].shape[1]
    nblk = tokens // block
    nb = block // MINI
    whole = lambda a: pl.BlockSpec(a.shape, lambda i: (0,) * a.ndim)
    rowblk = lambda w: pl.BlockSpec((block, w), lambda i: (nblk - 1 - i, 0))
    stepblk = lambda r: pl.BlockSpec((nb, r, hidden), lambda i: (nblk - 1 - i, 0, 0))
    behind = pl.BlockSpec((block, normed.shape[1]), lambda i: (jnp.minimum(nblk - i, nblk - 1), 0))
    first = pl.BlockSpec((block, normed.shape[1]), lambda i: (0, 0))
    anywhere = pl.BlockSpec(memory_space=pl.ANY)
    dma = pltpu.SemaphoreType.DMA
    seven = dma((CHAIN - 1,))
    share = early.shape[2:]
    three = dma((CHAIN // 2 - 1,))
    return pl.pallas_call(
        functools.partial(bwd_kernel, block, heads, turn),
        grid=(nblk,),
        in_specs=[anywhere] * 3 + [whole(gain), whole(bias), behind, first, rowblk(AUG), rowblk(AUG),
                                   rowblk(2 * width), stepblk(AUG), stepblk(width), rowblk(hidden), rowblk(hidden), rowblk(width),
                                   rowblk(width), rowblk(hidden), rowblk(width)],
        out_specs=[anywhere, anywhere, anywhere, pl.BlockSpec(share, lambda i: (0, 0)), anywhere],
        out_shape=[jax.ShapeDtypeStruct((heads, rows, PACK), bf16),
                   jax.ShapeDtypeStruct((heads, ENDS, hidden), bf16),
                   jax.ShapeDtypeStruct((heads, share[0], PACK), bf16),
                   jax.ShapeDtypeStruct(share, f32),
                   jax.ShapeDtypeStruct((CHAIN,) + small.shape, f32)],
        scratch_shapes=[pltpu.VMEM((CHAIN, rows, width), bf16), pltpu.VMEM((CHAIN // 2,) + share, bf16),
                        pltpu.VMEM((CHAIN // 2,) + share, bf16), pltpu.VMEM((CHAIN // 2,) + share, bf16),
                        pltpu.VMEM((CHAIN // 2 - 1,) + share, bf16),
                        pltpu.VMEM((tokens, PACK), bf16), pltpu.VMEM((ENDS, hidden), bf16),
                        pltpu.VMEM((CHAIN * share[0], PACK), f32), pltpu.VMEM((CHAIN, share[0], PACK), bf16),
                        pltpu.VMEM((AUG, hidden), f32), pltpu.VMEM((width, hidden), f32), pltpu.VMEM((1, width), f32),
                        pltpu.VMEM((2 * MINI, hidden), bf16), pltpu.VMEM((2 * MINI, AUG), bf16),
                        pltpu.VMEM((3 * MINI, width), bf16), pltpu.VMEM((3 * MINI, hidden), bf16),
                        pltpu.VMEM((1, width), f32), pltpu.VMEM((1, width), f32), pltpu.VMEM((1, width), f32),
                        pltpu.VMEM((1, 1), f32),
                        dma((heads,)), dma((CHAIN,)), dma, dma, dma, three, three, seven, seven, dma,
                        dma, dma((heads,)), seven, dma((heads,)), seven, dma((heads,))],
        compiler_params=pltpu.CompilerParams(collective_id=1, has_side_effects=True),
        name="inner_backward",
    )(grad_mixed, early, small, gain, bias, normed, normed, *saved)


def head_place():
    return lax.axis_index("head"), lax.axis_size("head")


def meet_heads(me, count):
    barrier = pltpu.get_barrier_semaphore()
    for d in range(1, count):
        pl.semaphore_signal(barrier, inc=1, device_id={"head": lax.rem(me + d, count)}, device_id_type=MESH)
    pl.semaphore_wait(barrier, count - 1)


def push_head(src, dst, send_sem, recv_sem, target):
    return pltpu.make_async_remote_copy(
        src_ref=src, dst_ref=dst, send_sem=send_sem, recv_sem=recv_sem,
        device_id={"head": target}, device_id_type=MESH)


def row_totals(first, second):
    ones = jnp.ones((8, first.shape[1]), f32)

    def total(x):
        return lax.dot_general(ones, x, (((1,), (1,)), ((), ())), precision=lax.Precision.HIGHEST,
                               preferred_element_type=f32)

    top, low = total(first), total(second)
    row = lax.broadcasted_iota(jnp.int32, top.shape, 0)
    return jnp.where(row == 0, top, low)


def mid_kernel(count, mixed_ref, x_ref, ctt_ref, mix_gate_ref, normed_ref, w_out_ref, w_gate_ref, w_up_ref, w_down_ref,
               post_gain_ref, post_bias_ref, ffn_gain_ref,
               gm_ref, early_ref, ggp_ref, out_ref, rco_ref, grc_ref, small_ref, norm_out,
               st_mine, st_got, pa_mine, pa_got, nt_all, rc_mine, rc_all, gn_mine, gn_got, dn_mine, dn_got, gov_all,
               gc_mine, gc_all, sb_mine, sb_got, gt_all, ct_ref, gh, gated, hidden, ggv, guv, resid,
               st_s, st_r, pa_s, pa_r, nt_s, nt_r, rc_s, rc_r, gn_s, gn_r, dn_s, dn_r, go_s, go_r, gc_s, gc_r, sb_s, sb_r,
               gt_s, gt_r, no_s, no_r):
    me, _ = head_place()
    heads, rows, width = mixed_ref.shape
    cols = heads * width
    full = cols * count
    part = rows // count
    peers = [(d, lax.rem(me + d, count)) for d in range(1, count)]
    pos, base = seq_place()
    owner = (pos >= FIRST) & (pos < FIRST + heads)
    barrier = pltpu.get_barrier_semaphore()
    for d in range(1, count):
        pl.semaphore_signal(barrier, inc=1, device_id={"head": lax.rem(me + d, count)}, device_id_type=MESH)
    for d in range(1, CHAIN):
        pl.semaphore_signal(
            barrier, inc=1, device_id={"seq": base + lax.rem(pos + d, CHAIN)}, device_id_type=MESH)
    pl.semaphore_wait(barrier, CHAIN - 1 + count - 1)
    ffn_gain = ffn_gain_ref[...][None, :]
    post_gain = post_gain_ref[...][None, :]
    post_bias = post_bias_ref[...][None, :]

    def rows_of(device):
        return pl.ds(pl.multiple_of(device * part, part), part)

    def send_all(src, dst, send, recv):
        for d, peer in peers:
            push_head(src, dst.at[d - 1], send.at[d - 1], recv.at[d - 1], peer).start()

    def wait_all(src, dst, send, recv):
        for d, peer in peers:
            push_head(src, dst.at[d - 1], send.at[d - 1], recv.at[d - 1], peer).wait()

    z = jnp.concatenate([mixed_ref[j] for j in range(heads)], axis=1).astype(f32)
    st_mine[...] = row_totals(z, z * z)
    send_all(st_mine, st_got, st_s, st_r)
    for j in range(heads):
        @pl.when(pos != FIRST + j)
        def _():
            push(normed_ref, norm_out.at[pos], no_s.at[j], no_r.at[pos], base + FIRST + j).start()

        @pl.when(pos == FIRST + j)
        def _():
            pltpu.make_async_copy(normed_ref, norm_out.at[pos], no_r.at[pos]).start()

    ct_ref[...] = ctt_ref[...].T
    gate_act, gate_der = gelu_first(dot_nt(normed_ref[...], mix_gate_ref[...]))
    gh[...] = dot_nt(ct_ref[...], w_down_ref[...])
    wait_all(st_mine, st_got, st_s, st_r)
    tot = st_mine[...]
    for d, _ in peers:
        tot = tot + st_got[d - 1]
    tot = tot.T * (1.0 / full)
    mean_z = tot[:, 0:1]
    inv_z = lax.rsqrt(tot[:, 1:2] - mean_z * mean_z + eps_norm)
    z_hat = (z - mean_z) * inv_z
    post_out = z_hat * post_gain + post_bias
    gated[...] = (post_out * gate_act).astype(bf16)

    def spread_rows(make, mine, got, send, recv):
        pending = None
        for d, peer in peers:
            mine[d - 1] = make(rows_of(peer)).astype(bf16)
            if pending is not None:
                pending.start()
            pending = push_head(mine.at[d - 1], got.at[d - 1], send.at[d - 1], recv.at[d - 1], peer)
        own = make(rows_of(me))
        pending.start()
        return own

    def add_rows(own, mine, got, send, recv):
        for d, peer in peers:
            push_head(mine.at[d - 1], got.at[d - 1], send.at[d - 1], recv.at[d - 1], peer).wait()
            own = own + got[d - 1].astype(f32)
        return own

    def gather_rows(all_ref, send, recv):
        for d, peer in peers:
            view = all_ref.at[rows_of(me), :]
            push_head(view, view, send.at[d - 1], recv.at[d - 1], peer).start()

    def gather_wait(all_ref, send, recv):
        for d, peer in peers:
            view = all_ref.at[rows_of(me), :]
            push_head(view, view, send.at[d - 1], recv.at[d - 1], peer).wait_send()
            await_bytes(all_ref.at[rows_of(lax.rem(me + count - d, count)), :], recv.at[d - 1])

    def turn_columns(value, mine, all_ref, send, recv):
        for b in range(count):
            mine[b] = value[:, b * cols : (b + 1) * cols]
        all_ref[rows_of(me), :] = mine[me]

    def turn_start(mine, all_ref, send, recv):
        for d, peer in peers:
            push_head(mine.at[peer], all_ref.at[rows_of(me), :], send.at[d - 1], recv.at[d - 1], peer).start()

    def turn_wait(mine, all_ref, send, recv):
        for d, peer in peers:
            push_head(mine.at[peer], all_ref.at[rows_of(me), :], send.at[d - 1], recv.at[d - 1], peer).wait_send()
            await_bytes(all_ref.at[rows_of(lax.rem(me + count - d, count)), :], recv.at[d - 1])

    w_out = w_out_ref[...]
    own = spread_rows(lambda r: dot_nn(gated[r, :], w_out), pa_mine, pa_got, pa_s, pa_r)
    res = x_ref[rows_of(me), :].astype(f32) + add_rows(own, pa_mine, pa_got, pa_s, pa_r)
    rms_two = lax.rsqrt(mean_row(res * res) + eps_norm)
    nt_all[rows_of(me), :] = (res * rms_two * ffn_gain).astype(bf16)
    turn_columns(res, rc_mine, rc_all, rc_s, rc_r)
    resid[...] = res
    gather_rows(nt_all, nt_s, nt_r)
    turn_start(rc_mine, rc_all, rc_s, rc_r)
    gather_wait(nt_all, nt_s, nt_r)
    def forward_rows(b, _):
        r = pl.ds(pl.multiple_of(b * part, part), part)
        nt = nt_all[r, :]
        gate_val = dot_nn(nt, w_gate_ref[...])
        up_val = dot_nn(nt, w_up_ref[...])
        sig = 1.0 / (1.0 + jnp.exp(-gate_val))
        silu = gate_val * sig
        hidden[r, :] = (silu * up_val).astype(bf16)
        g = gh[r, :]
        ggv[r, :] = (g * up_val * sig * (1.0 + gate_val * (1.0 - sig))).astype(bf16)
        guv[r, :] = (g * silu).astype(bf16)
        return 0

    lax.fori_loop(0, count, forward_rows, 0)
    own = spread_rows(lambda r: dot_nt(ggv[r, :], w_gate_ref[...]) + dot_nt(guv[r, :], w_up_ref[...]),
                      gn_mine, gn_got, gn_s, gn_r)
    for b in range(count):
        r = pl.ds(b * part, part)
        down = dot_nn(hidden[r, :], w_down_ref[...]).astype(bf16)
        for c in range(count):
            dn_mine[c, r, :] = down[:, c * cols : (c + 1) * cols]
    ffn = w_gate_ref.shape[1]
    half = full // 2
    for b in range(2):
        r = slice(b * half, (b + 1) * half)
        early_ref[r, 0:ffn] = dot_tn(nt_all[:, r], ggv[...]).astype(bf16)
    for d, peer in peers:
        push_head(dn_mine.at[peer], dn_got.at[d - 1], dn_s.at[d - 1], dn_r.at[d - 1], peer).start()
    gnt = add_rows(own, gn_mine, gn_got, gn_s, gn_r)
    res = resid[...]
    rms_two = lax.rsqrt(mean_row(res * res) + eps_norm)
    scaled = gnt * ffn_gain
    grad_res = ct_ref[rows_of(me), :].astype(f32) + rms_two * (
        scaled - res * rms_two * rms_two * mean_row(scaled * res))
    gov_all[rows_of(me), :] = grad_res.astype(bf16)
    gt_all[me] = jnp.broadcast_to(jnp.sum(gnt * res * rms_two, axis=0, keepdims=True), gt_all.shape[1:])
    turn_columns(grad_res, gc_mine, gc_all, gc_s, gc_r)
    gather_rows(gov_all, go_s, go_r)
    turn_start(gc_mine, gc_all, gc_s, gc_r)
    for d, peer in peers:
        push_head(gt_all.at[me], gt_all.at[me], gt_s.at[d - 1], gt_r.at[d - 1], peer).start()
    for b in range(2):
        r = slice(b * half, (b + 1) * half)
        early_ref[r, ffn : 2 * ffn] = dot_tn(nt_all[:, r], guv[...]).astype(bf16)
    gather_wait(gov_all, go_s, go_r)
    gov = gov_all[...]
    grad_gated = dot_nt(gov, w_out_ref[...])
    grad_post = grad_gated * gate_act
    grad_zhat = grad_post * post_gain
    sb_mine[...] = row_totals(grad_zhat, grad_zhat * z_hat)
    ggp = (grad_gated * post_out * gate_der).astype(bf16)
    ggp_ref[...] = ggp
    send_all(sb_mine, sb_got, sb_s, sb_r)
    early_ref[:, 3 * ffn : 3 * ffn + 2 * cols] = jnp.concatenate(
        [dot_tn(normed_ref[...], ggp).astype(bf16), dot_tn(gov, gated[...]).astype(bf16)], axis=1)
    row = lax.broadcasted_iota(jnp.int32, (8, cols), 0)
    wait_all(sb_mine, sb_got, sb_s, sb_r)
    tot = sb_mine[...]
    for d, _ in peers:
        tot = tot + sb_got[d - 1]
    tot = tot.T * (1.0 / full)
    grad_mixed = (inv_z * (grad_zhat - tot[:, 0:1] - z_hat * tot[:, 1:2])).astype(bf16)
    for j in range(heads):
        gm_ref[j] = grad_mixed[:, j * width : (j + 1) * width]
    for b in range(2):
        r = slice(b * half, (b + 1) * half)
        early_ref[r, 2 * ffn : 3 * ffn] = dot_nn(ctt_ref[r, :], hidden[...]).astype(bf16)
    turn_wait(rc_mine, rc_all, rc_s, rc_r)
    rco_ref[...] = rc_all[...]
    out = dn_mine[me].astype(f32)
    for d, peer in peers:
        push_head(dn_mine.at[peer], dn_got.at[d - 1], dn_s.at[d - 1], dn_r.at[d - 1], peer).wait()
        out = out + dn_got[d - 1].astype(f32)
    out_ref[...] = out
    turn_wait(gc_mine, gc_all, gc_s, gc_r)
    grc_ref[...] = gc_all[...]
    for d, peer in peers:
        push_head(gt_all.at[me], gt_all.at[me], gt_s.at[d - 1], gt_r.at[d - 1], peer).wait_send()
        await_bytes(gt_all.at[lax.rem(me + count - d, count)], gt_r.at[d - 1])
    gain_two = gt_all[0]
    for b in range(1, count):
        gain_two = gain_two + gt_all[b]
    post = jnp.where(row == 1, jnp.sum(grad_post * z_hat, axis=0, keepdims=True),
                     jnp.sum(grad_post, axis=0, keepdims=True))
    line = lax.broadcasted_iota(jnp.int32, (8, full), 0)
    small_ref[...] = jnp.where(
        line == 0, gain_two, jnp.concatenate([post] + [jnp.zeros_like(post)] * (count - 1), axis=1))
    for j in range(heads):
        @pl.when(pos != FIRST + j)
        def _():
            await_bytes(normed_ref, no_s.at[j])

    @pl.when(owner)
    def _():
        for p in range(CHAIN):
            await_bytes(norm_out.at[p], no_r.at[p])


def middle(mixed, x, ct, mix_gate, normed, w_out, w_gate, w_up, w_down, post_gain, post_bias, ffn_gain):
    count = lax.axis_size("head")
    heads, rows, width = mixed.shape
    cols = heads * width
    full = cols * count
    part = rows // count
    ffn = w_gate.shape[1]
    ins = (mixed, x, ct, mix_gate, normed, w_out, w_gate, w_up, w_down, post_gain, post_bias, ffn_gain)
    vmem = pl.BlockSpec(memory_space=pltpu.VMEM)
    V = pltpu.VMEM
    trio = count - 1
    sem = pltpu.SemaphoreType.DMA((trio,))
    return pl.pallas_call(
        functools.partial(mid_kernel, count),
        in_specs=[vmem] * len(ins),
        out_specs=[vmem] * 7 + [pl.BlockSpec(memory_space=pl.ANY)],
        out_shape=[jax.ShapeDtypeStruct((heads, rows, width), bf16),
                   jax.ShapeDtypeStruct((full, 3 * ffn + 2 * cols), bf16),
                   jax.ShapeDtypeStruct((rows, cols), bf16),
                   jax.ShapeDtypeStruct((rows, cols), f32),
                   jax.ShapeDtypeStruct((rows, cols), f32),
                   jax.ShapeDtypeStruct((rows, cols), f32),
                   jax.ShapeDtypeStruct((8, full), f32),
                   jax.ShapeDtypeStruct((CHAIN, rows, full), bf16)],
        scratch_shapes=[
            V((8, rows), f32), V((trio, 8, rows), f32),
            V((trio, part, full), bf16), V((trio, part, full), bf16),
            V((rows, full), bf16),
            V((count, part, cols), f32), V((rows, cols), f32),
            V((trio, part, full), bf16), V((trio, part, full), bf16),
            V((count, rows, cols), bf16), V((trio, rows, cols), bf16),
            V((rows, full), bf16),
            V((count, part, cols), f32), V((rows, cols), f32),
            V((8, rows), f32), V((trio, 8, rows), f32),
            V((count, 8, full), f32),
            V((rows, full), bf16), V((rows, ffn), f32), V((rows, cols), bf16),
            V((rows, ffn), bf16), V((rows, ffn), bf16), V((rows, ffn), bf16),
            V((part, full), f32)] + [sem] * 20 + [
            pltpu.SemaphoreType.DMA((heads,)), pltpu.SemaphoreType.DMA((CHAIN,))],
        compiler_params=pltpu.CompilerParams(
            collective_id=2, has_side_effects=True, vmem_limit_bytes=56 * 1024 * 1024),
        name="middle",
    )(*ins)


def front_kernel(count, in_ref, gain_ref, bias_ref, wq_ref, wk_ref, wv_ref, wr_ref, x_ref, normed_ref, pay_ref, gathered, send, recv):
    me, _ = head_place()
    cols, rows = in_ref.shape
    heads = wr_ref.shape[0]
    width = cols // heads
    part = rows // count
    meet_heads(me, count)
    here = pl.ds(pl.multiple_of(me * cols, cols), cols)
    for d in range(1, count):
        push_head(in_ref, gathered.at[here, :], send.at[d - 1], recv.at[d - 1], lax.rem(me + d, count)).start()
    gathered[here, :] = in_ref[...]
    for d in range(1, count):
        push_head(in_ref, gathered.at[here, :], send.at[d - 1], recv.at[d - 1], lax.rem(me + d, count)).wait_send()
        origin = lax.rem(me + count - d, count)
        await_bytes(gathered.at[pl.ds(pl.multiple_of(origin * cols, cols), cols), :], recv.at[d - 1])
    gain = gain_ref[...][None, :]
    rate_bias = bias_ref[...][None, :]
    x_ref[...] = gathered[...].T

    def project(b, _):
        r = pl.ds(pl.multiple_of(b * part, part), part)
        x = x_ref[r, :].astype(f32)
        nt = (x * lax.rsqrt(mean_row(x * x) + eps_norm) * gain).astype(bf16)
        normed_ref[r, :] = nt
        query = dot_nt(nt, wq_ref[...]).astype(bf16)
        key = dot_nt(nt, wk_ref[...]).astype(bf16)
        value = dot_nt(nt, wv_ref[...]).astype(bf16)
        logit = dot_nt(nt, wr_ref[...]) + rate_bias
        high = logit.astype(bf16)
        low = (logit - high.astype(f32)).astype(bf16)
        lane = lax.broadcasted_iota(jnp.int32, (part, width), 1)
        for j in range(heads):
            own = slice(j * width, (j + 1) * width)
            extra = jnp.where(lane == 0, high[:, j : j + 1].astype(f32),
                              jnp.where(lane == 1, low[:, j : j + 1].astype(f32), 0.0)).astype(bf16)
            pay_ref[r, j * PACK : (j + 1) * PACK] = jnp.concatenate(
                [query[:, own], key[:, own], value[:, own], extra], axis=1)
        return 0

    lax.fori_loop(0, count, project, 0)


def front(inputs_t, pre_gain, rate_bias, wq, wk, wv, wr):
    count = lax.axis_size("head")
    cols, rows = inputs_t.shape
    heads = wr.shape[0]
    vmem = pl.BlockSpec(memory_space=pltpu.VMEM)
    sem = pltpu.SemaphoreType.DMA((count - 1,))
    wide = jax.ShapeDtypeStruct((rows, cols * count), bf16)
    return pl.pallas_call(
        functools.partial(front_kernel, count),
        in_specs=[vmem] * 7,
        out_specs=[vmem] * 3,
        out_shape=[wide, wide, jax.ShapeDtypeStruct((rows, heads * PACK), bf16)],
        scratch_shapes=[pltpu.VMEM((cols * count, rows), bf16), sem, sem],
        compiler_params=pltpu.CompilerParams(collective_id=4, has_side_effects=True),
        name="front",
    )(inputs_t, pre_gain, rate_bias, wq, wk, wv, wr)


def tail_kernel(count, at_mix, grads_ref, wq_ref, wk_ref, wv_ref, wr_ref, mix_gate_ref, ggp_ref, x_ref, gain_ref,
                late_ref, early_ref,
                back_ref, tiles_ref,
                mine, got, tile, tile_got, wcols, ib_s, ib_r, th_s, th_r, ts_s, ts_r, ts_loc):
    me, _ = head_place()
    pos, base = seq_place()
    heads = grads_ref.shape[0]
    rows = x_ref.shape[0]
    cols = ggp_ref.shape[1]
    full = x_ref.shape[1]
    share = early_ref.shape[0]
    rate_lane = PACK - PACK // 4
    peers = [(d, lax.rem(me + d, count)) for d in range(1, count)]
    barrier = pltpu.get_barrier_semaphore()
    for d, peer in peers:
        pl.semaphore_signal(barrier, inc=1, device_id={"head": peer}, device_id_type=MESH)
    for d in range(1, CHAIN):
        pl.semaphore_signal(
            barrier, inc=1, device_id={"seq": base + lax.rem(pos + d, CHAIN)}, device_id_type=MESH)
    pl.semaphore_wait(barrier, count - 1 + CHAIN - 1)
    part = rows // count
    width = PACK // 4
    pre_gain = gain_ref[...][None, :]
    sides = (wq_ref, wk_ref, wv_ref)

    def back_rows(b, _):
        r = pl.ds(pl.multiple_of(b * part, part), part)
        grad = dot_nn(ggp_ref[r, :], mix_gate_ref[...])
        blocks = [grads_ref[j, r, :] for j in range(heads)]
        for i, side in enumerate(sides):
            joined = jnp.concatenate([b[:, i * width : (i + 1) * width] for b in blocks], axis=1)
            grad = grad + dot_nn(joined, side[...])
        for j in range(heads):
            rate = blocks[j][:, rate_lane : rate_lane + 1].astype(f32) + blocks[j][
                :, rate_lane + 1 : rate_lane + 2].astype(f32)
            grad = grad + rate.astype(bf16).astype(f32) * wr_ref[j : j + 1, :].astype(f32)
        x = x_ref[r, :].astype(f32)
        rms = lax.rsqrt(mean_row(x * x) + eps_norm)
        scaled = grad * pre_gain
        back = (rms * (scaled - x * rms * rms * mean_row(scaled * x))).astype(bf16)
        for c in range(count):
            mine[c, r, :] = back[:, c * cols : (c + 1) * cols]
        return 0

    lax.fori_loop(0, count, back_rows, 0)
    for d, peer in peers:
        push_head(mine.at[peer], got.at[d - 1], ib_s.at[d - 1], ib_r.at[d - 1], peer).start()
    lane = lax.broadcasted_iota(jnp.int32, (share, 128), 1)
    line = lax.broadcasted_iota(jnp.int32, (8, 128), 0)
    w_rows = pl.ds(pl.multiple_of(pos * share, share), share)
    slim = jnp.concatenate([wr_ref[j : j + 1, :].astype(f32) for j in range(heads)] + [pre_gain] * (8 - heads), axis=0)
    wcols[4, :, 0:8] = slim.T
    for i, side in enumerate(sides + (mix_gate_ref,)):
        wcols[i] = side[...].astype(f32).T
    gain = jnp.sum(early_ref[:, at_mix : at_mix + cols] * wcols[3, w_rows, :], axis=1, keepdims=True)
    table = jnp.zeros((share, 128), f32)
    blocks = [late_ref[j].astype(f32) for j in range(heads)]
    for i in range(3):
        joined = jnp.concatenate([b[:, i * width : (i + 1) * width] for b in blocks], axis=1)
        gain = gain + jnp.sum(joined * wcols[i, w_rows, :], axis=1, keepdims=True)
    for j in range(heads):
        rate = blocks[j][:, rate_lane : rate_lane + 1] + blocks[j][:, rate_lane + 1 : rate_lane + 2]
        gain = gain + rate * wcols[4, w_rows, j : j + 1]
        table = jnp.where(lane == j, rate, table)
    gain = gain / wcols[4, w_rows, heads : heads + 1]
    table = jnp.where(lane == heads, gain, table)
    flat = jnp.concatenate([table, jnp.zeros((128 - share, 128), f32)], axis=0).T[0:8]
    tile[...] = flat
    for d, peer in peers:
        push_head(tile, tile_got.at[d - 1], th_s.at[d - 1], th_r.at[d - 1], peer).start()
    back = mine[me].astype(f32)
    for d, peer in peers:
        push_head(tile, tile_got.at[d - 1], th_s.at[d - 1], th_r.at[d - 1], peer).wait()
    summed = flat
    for d, peer in peers:
        summed = summed + tile_got[d - 1]
    tile[...] = jnp.where(line == heads, summed, flat)
    for d in range(1, CHAIN):
        push(tile, tiles_ref.at[pos], ts_s.at[d - 1], ts_r.at[d - 1], base + lax.rem(pos + d, CHAIN)).start()
    pltpu.make_async_copy(tile, tiles_ref.at[pos], ts_loc).start()
    for d, peer in peers:
        push_head(mine.at[peer], got.at[d - 1], ib_s.at[d - 1], ib_r.at[d - 1], peer).wait()
        back = back + got[d - 1].astype(f32)
    back_ref[...] = back
    for d in range(1, CHAIN):
        push(tile, tiles_ref.at[pos], ts_s.at[d - 1], ts_r.at[d - 1], base + lax.rem(pos + d, CHAIN)).wait_send()
        await_bytes(tiles_ref.at[lax.rem(pos + CHAIN - d, CHAIN)], ts_r.at[d - 1])
    await_bytes(tiles_ref.at[pos], ts_loc)


def tail(at_mix, grads, wq, wk, wv, wr, mix_gate, ggp, x, pre_gain, late, early):
    count = lax.axis_size("head")
    rows, full = x.shape
    width = ggp.shape[1]
    vmem = pl.BlockSpec(memory_space=pltpu.VMEM)
    V = pltpu.VMEM
    dma = pltpu.SemaphoreType.DMA
    trio, seven = dma((count - 1,)), dma((CHAIN - 1,))
    return pl.pallas_call(
        functools.partial(tail_kernel, count, at_mix),
        in_specs=[vmem] * 11,
        out_specs=[vmem] * 2,
        out_shape=[jax.ShapeDtypeStruct((rows, width), f32),
                   jax.ShapeDtypeStruct((CHAIN, 8, 128), f32)],
        scratch_shapes=[V((count, rows, width), bf16), V((count - 1, rows, width), bf16),
                        V((8, 128), f32), V((count - 1, 8, 128), f32), V((5, full, width), f32),
                        trio, trio, trio, trio, seven, seven, dma],
        compiler_params=pltpu.CompilerParams(
            collective_id=3, has_side_effects=True, vmem_limit_bytes=56 * 1024 * 1024),
        name="tail",
    )(grads, wq, wk, wv, wr, mix_gate, ggp, x, pre_gain, late, early)


def final_kernel(at_mix, ffn, down_ref, resid_ref, back_ref, grc_ref, late_ref, early_ref, ends_ref, tiles_ref, small_ref,
                 out_ref, gin_ref, gq_ref, gk_ref, gv_ref, gmix_ref, rate_ref, gwout_ref, gwg_ref, gwu_ref, gwd_ref,
                 w1_ref, b1_ref, w2_ref, b2_ref, ig_ref, ib_ref, rb_ref, pre_ref, pg_ref, pb_ref, fg_ref):
    heads, width, hidden = w1_ref.shape
    cols = heads * width
    out_ref[...] = (down_ref[...] + resid_ref[...]).T
    gin_ref[...] = (back_ref[...] + grc_ref[...]).T
    for i, ref in enumerate((gq_ref, gk_ref, gv_ref)):
        ref[...] = jnp.concatenate([late_ref[j, :, i * width : (i + 1) * width].astype(f32) for j in range(heads)], axis=1)
    gwg_ref[...] = early_ref[:, 0:ffn]
    gwu_ref[...] = early_ref[:, ffn : 2 * ffn]
    rates = []
    gwd_ref[...] = early_ref[:, 2 * ffn : 3 * ffn]
    both = early_ref[:, at_mix : at_mix + 2 * cols]
    gmix_ref[...] = both[:, 0:cols]
    gwout_ref[...] = both[:, cols:].T
    for j in range(heads):
        w1_ref[j] = ends_ref[j, 0:width, :].astype(f32)
        b1_ref[pl.ds(j, 1), :] = ends_ref[j, width : AUG, :].astype(f32)[0:1]
        second = ends_ref[j, AUG : AUG + width, :].astype(f32)
        w2_ref[j] = second - jnp.mean(second, axis=0, keepdims=True)
        rest = ends_ref[j, AUG + width :, :].astype(f32)[0:8, 0:width]
        b2_ref[pl.ds(j, 1), :] = rest[0:1] - mean_row(rest[0:1])
        ig_ref[pl.ds(j, 1), :] = rest[1:2]
        ib_ref[pl.ds(j, 1), :] = rest[2:3]
        rates.append((rest[3:4] + rest[4:5])[:, 0:1])
    each = rate_ref.shape[1] // CHAIN
    strips = jnp.concatenate([tiles_ref[p, :, 0:each] for p in range(CHAIN)], axis=1)
    rate_ref[...] = strips[0:heads]
    me, count = head_place()
    pick = [tiles_ref[me * (CHAIN // count) + i, heads : heads + 1, 0:each] for i in range(CHAIN // count)]
    pre_ref[...] = jnp.concatenate(pick, axis=1)[0]
    rb_ref[...] = jnp.concatenate(rates, axis=1)[0]
    acc = small_ref[0]
    for p in range(1, CHAIN):
        acc = acc + small_ref[p]
    fg_ref[...] = acc[0]
    pg_ref[...] = acc[1:2, 0:cols][0]
    pb_ref[...] = acc[2:3, 0:cols][0]


def finish(at_mix, ffn, down, resid, back, grc, late, early, ends, tiles, small, shapes):
    ins = (down, resid, back, grc, late, early, ends, tiles, small)
    vmem = pl.BlockSpec(memory_space=pltpu.VMEM)
    return pl.pallas_call(
        functools.partial(final_kernel, at_mix, ffn),
        in_specs=[vmem] * len(ins),
        out_specs=[vmem] * len(shapes),
        out_shape=[jax.ShapeDtypeStruct(s, f32) for s in shapes],
        compiler_params=pltpu.CompilerParams(vmem_limit_bytes=48 * 1024 * 1024),
        name="final",
    )(*ins)


def stretch_groups(axis):
    count = lax.axis_size(axis)
    return [[start + step for step in range(0, count, CHAIN)] for start in range(CHAIN)]


def local(
    inputs,
    pre_gain,
    w_query,
    w_key,
    w_value,
    mix_gate,
    w_rate,
    rate_bias,
    inner_gain,
    inner_bias,
    init_w_one,
    init_b_one,
    init_w_two,
    init_b_two,
    post_gain,
    post_bias,
    w_out,
    ffn_gain,
    w_gate,
    w_up,
    w_down,
    cotangent,
):
    full_width = pre_gain.shape[0]
    rows, local_cols = inputs.shape
    heads, head_dim = inner_gain.shape
    stretches = lax.axis_size("seq") // CHAIN
    share = full_width // CHAIN

    sides = (w_query.T, w_key.T, w_value.T, w_rate.T)
    whole_low, normed_one, payload = front(inputs.T, pre_gain, rate_bias, *sides)
    mixed_h, ct_blocks, *saved = chain_forward(
        payload, cotangent.T, init_w_one, init_b_one, init_w_two.transpose(0, 2, 1), init_b_two,
        inner_gain, inner_bias)
    ffn = w_gate.shape[1]
    at_mix = 3 * ffn
    grad_mixed, early, grad_gate_pre, down_cols, resid_cols, grad_resid_cols, small, normed_all = middle(
        mixed_h, whole_low, ct_blocks.reshape(full_width, rows), mix_gate.T, normed_one, w_out, w_gate, w_up, w_down,
        post_gain, post_bias, ffn_gain)
    grads, ends, late, early_sum, small = chain_backward(
        grad_mixed, early.reshape(CHAIN // 2, 2, share, early.shape[1]), small, inner_gain, inner_bias,
        normed_all.reshape(CHAIN * rows, full_width), saved)
    back_cols, tiles = tail(
        at_mix, grads, *sides, mix_gate.T, grad_gate_pre, whole_low, pre_gain,
        late, early_sum)
    if stretches > 1:
        groups = stretch_groups("seq")
        ends, tiles, small = lax.psum((ends.astype(f32), tiles, small), "seq", axis_index_groups=groups)
        seq_index = lax.axis_index("seq")
        stretch_lists = [list(range(s, s + CHAIN)) for s in range(0, stretches * CHAIN, CHAIN)]

        def spread(mine_rows):
            summed = lax.psum(mine_rows, "seq", axis_index_groups=groups)
            total = lax.all_gather(
                summed, "seq", axis=summed.ndim - 2, tiled=True, axis_index_groups=stretch_lists)
            return lax.dynamic_slice_in_dim(
                total, seq_index * (share // stretches), share // stretches, summed.ndim - 2)

        late = spread(late.astype(f32))
        early_sum = spread(early_sum)
    held = share // stretches
    hidden = init_w_one.shape[2]
    square = (held, local_cols)
    (outputs, grad_inputs, grad_q, grad_k, grad_v, grad_mix, grad_rate_w, grad_w_out, grad_w_gate, grad_w_up, grad_w_down,
     grad_one, grad_b_one, grad_two, grad_b_two, grad_gain, grad_bias, rate_b, grad_pre, grad_post_gain, grad_post_bias,
     grad_ffn_gain) = finish(
        at_mix, ffn, down_cols, resid_cols, back_cols, grad_resid_cols, late, early_sum, ends, tiles, small,
        ((local_cols, rows), (local_cols, rows), square, square, square, square, (heads, full_width),
         (local_cols, held), (held, ffn), (held, ffn), (held, ffn),
         (heads, head_dim, hidden), (heads, hidden), (heads, head_dim, hidden), (heads, head_dim),
         (heads, head_dim), (heads, head_dim), (heads,), (local_cols,), (local_cols,), (local_cols,), (full_width,)))
    return (
        outputs.T,
        grad_inputs.T,
        grad_pre,
        grad_q,
        grad_k,
        grad_v,
        grad_mix,
        grad_rate_w.T,
        rate_b,
        grad_gain,
        grad_bias,
        grad_one,
        grad_b_one,
        grad_two.transpose(0, 2, 1),
        grad_b_two,
        grad_post_gain,
        grad_post_bias,
        grad_w_out,
        grad_ffn_gain,
        grad_w_gate,
        grad_w_up,
        grad_w_down.T,
    )


def solution(mesh):
    in_specs = (
        P("seq", "head"),
        P(),
        P(None, "head"),
        P(None, "head"),
        P(None, "head"),
        P(None, "head"),
        P(None, "head"),
        P("head"),
        P("head", None),
        P("head", None),
        P("head", None, None),
        P("head", None),
        P("head", None, None),
        P("head", None),
        P("head"),
        P("head"),
        P("head", None),
        P(),
        P(None, "head"),
        P(None, "head"),
        P("head", None),
        P("seq", "head"),
    )
    out_specs = (
        P("seq", "head"),
        P("seq", "head"),
        P("head"),
        P("seq", "head"),
        P("seq", "head"),
        P("seq", "head"),
        P("seq", "head"),
        P(None, "head"),
        P("head"),
        P("head", None),
        P("head", None),
        P("head", None, None),
        P("head", None),
        P("head", None, None),
        P("head", None),
        P("head"),
        P("head"),
        P("head", "seq"),
        P(),
        P("seq", "head"),
        P("seq", "head"),
        P("head", "seq"),
    )
    return jax.shard_map(local, mesh=mesh, in_specs=in_specs, out_specs=out_specs, check_vma=False)
```

```python
import functools

import jax
import jax.numpy as jnp
from jax import lax
from jax.experimental import pallas as pl
from jax.experimental.pallas import tpu as pltpu
from jax.sharding import PartitionSpec as P

MINI = 16
CHAIN = 8
FIRST = 2
AUG = 80
eps_norm = 1e-06
gelu_scale = 0.7978845608028654
f32 = jnp.float32
bf16 = jnp.bfloat16


def dot_nn(a, b):
    return lax.dot_general(a, b, (((1,), (0,)), ((), ())), preferred_element_type=f32)


def dot_nt(a, b):
    return lax.dot_general(a, b, (((1,), (1,)), ((), ())), preferred_element_type=f32)


def dot_tn(a, b):
    return lax.dot_general(a, b, (((0,), (0,)), ((), ())), preferred_element_type=f32)


def mean_row(x):
    return jnp.sum(x, axis=1, keepdims=True) * (1.0 / x.shape[1])


def gelu_first(z):
    sq = z * z
    th = jnp.tanh(gelu_scale * z * (1.0 + 0.044715 * sq))
    half = 0.5 * (1.0 + th)
    act = z * half
    der = half + (0.5 * gelu_scale) * z * (1.0 - th * th) * (1.0 + 0.134145 * sq)
    return act, der


def gelu_second(z):
    sq = z * z
    th = jnp.tanh(gelu_scale * z * (1.0 + 0.044715 * sq))
    half = 0.5 * (1.0 + th)
    act = z * half
    slope = gelu_scale * (1.0 + 0.134145 * sq)
    sech = 1.0 - th * th
    der = half + 0.5 * z * sech * slope
    curve = sech * (slope + z * (0.5 * gelu_scale * 0.26829 * z) - z * th * slope * slope)
    return act, der, curve


def tri_mask():
    rows = lax.broadcasted_iota(jnp.int32, (MINI, MINI), 0)
    cols = lax.broadcasted_iota(jnp.int32, (MINI, MINI), 1)
    return jnp.where(rows >= cols, 1.0, 0.0).astype(f32)


def forward_output(kept, gain, bias, tri, sink):
    z1b, act_h, w2_h, b2, s2_h = kept
    actb, _ = gelu_first(z1b)
    actb_h = actb.astype(bf16)
    yield
    att = dot_nt(actb_h, act_h)
    z2b = dot_nt(actb_h, w2_h) + b2
    yield
    z2b = z2b - dot_nn(((att + 1.0) * tri).astype(bf16), s2_h)
    yield
    z2b = z2b - mean_row(z2b)
    yield
    invb = lax.rsqrt(mean_row(z2b * z2b) + eps_norm)
    sink(z2b * invb * gain + bias, z2b)
    yield


def forward_chain(state, z1, post, key_aug, key_next, query_aug, base, rate, gain_sq, tri, save):
    w1, w2t, b2 = state
    width = gain_sq.shape[1]
    scale = 1.0 / width
    w2_h = w2t.astype(bf16)
    act, der = gelu_first(z1)
    act_h = act.astype(bf16)
    z = dot_nt(act_h, w2_h) + b2
    next(post, None)
    fixed = dot_nn(
        jnp.concatenate([base, jnp.broadcast_to(gain_sq, (8, width)), jnp.ones((8, width), f32)], axis=0).astype(bf16),
        w2_h)
    both = jnp.concatenate([key_next, query_aug], axis=0)
    coef = dot_nt(both, key_aug)
    coef = jnp.concatenate([coef[:MINI], coef[MINI:] * tri], axis=0).astype(bf16)
    m_b = mean_row(base)
    m_sq = mean_row(gain_sq)
    w1_h = w1.astype(bf16)
    next(post, None)
    zg = z * gain_sq
    prods = dot_nn(jnp.concatenate([zg, z], axis=0).astype(bf16), w2_h)
    mz = mean_row(z)
    m_zz = mean_row(z * z)
    m_zg = mean_row(zg)
    m_zzg = mean_row(zg * z)
    m_zb = mean_row(z * base)
    zz = dot_nn(both, w1_h)
    next(post, None)
    inv = lax.rsqrt(m_zz - mz * mz + eps_norm)
    c_zg = m_zg - mz * m_sq
    c_zzg = m_zzg - mz * (m_zg + c_zg)
    c_zb = m_zb - mz * m_b
    m_g = inv * c_zg + m_b
    m_gn = inv * (inv * c_zzg + c_zb)
    rinv = rate * inv
    rinv2 = rinv * inv
    skew = rinv2 * m_gn
    shift = skew * mz - rinv * m_g
    upd = (rinv2 * prods[:MINI] - skew * prods[MINI:]) + (
        (rinv * fixed[:MINI] + shift * fixed[MINI + 8 : MINI + 9]) - (rinv2 * mz) * fixed[MINI : MINI + 1])
    s1_h = (upd * der).astype(bf16)
    zz = zz - dot_nn(coef, s1_h)
    zc = z - mz
    s2 = rinv2 * zc * gain_sq - skew * zc + (rinv * base - rinv * m_g)
    s2_h = s2.astype(bf16)
    new_w2t = w2t - dot_tn(s2_h, act_h)
    new_w1 = w1 - dot_tn(key_aug, s1_h)
    new_b2 = b2 - jnp.sum(s2, axis=0, keepdims=True)
    next(post, None)
    next(post, None)
    z1b = zz[MINI:]
    save(w1_h, w2_h, z1, upd, zc, s2, z1b)
    return (new_w1, new_w2t, new_b2), zz[:MINI], (z1b, act_h, w2_h, b2, s2_h)


def prepare_back(store, saved, d_out, key_aug, query_aug, target, rate, gain, gain_sq, bias, tri):
    w1_h, w2_h, z1, upd, zc, s2, z1b, z2b = saved
    width = gain.shape[1]
    s2_h = s2.astype(bf16)
    actb, derb = gelu_first(z1b)
    actb_h = actb.astype(bf16)
    invb = lax.rsqrt(mean_row(z2b * z2b) + eps_norm)
    dn = d_out * gain
    m_dn = mean_row(dn)
    yield
    act, der, curve = gelu_second(z1)
    act_h = act.astype(bf16)
    s1_h = (upd * der).astype(bf16)
    store.update(act=act_h, der=der, bend=upd * curve, actb=actb_h, s1=s1_h, s2=s2_h)
    yield
    att2 = dot_nt(actb_h, act_h)
    att1 = dot_nt(query_aug, key_aug)
    nb = z2b * invb
    d_z2b = invb * (dn - m_dn - nb * mean_row(dn * nb))
    d_z2b_h = d_z2b.astype(bf16)
    yield
    inv = lax.rsqrt(mean_row(zc * zc) + eps_norm)
    d_att2 = dot_nt(d_z2b_h, s2_h)
    d_actb = dot_nn(d_z2b_h, w2_h)
    base = (bias - target) * gain
    m_sq = mean_row(gain_sq)
    yield
    att2 = ((att2 + 1.0) * tri).astype(bf16)
    att1 = (att1 * tri).astype(bf16)
    n = zc * inv
    ng = n * gain_sq
    big_g = ng + base
    m_g = mean_row(big_g)
    m_gn = mean_row(big_g * n)
    yield
    d_att2 = (-d_att2 * tri).astype(bf16)
    d_actb = d_actb + dot_nn(d_att2, act_h)
    c2 = dot_tn(att2, d_z2b_h)
    m_ng = mean_row(ng)
    m_nng = mean_row(n * ng)
    yield
    c3 = dot_tn(d_att2, actb_h)
    inv2 = inv * inv
    g = inv * (big_g - m_g - n * m_gn)
    fac = rate * inv2 * (gain_sq - m_gn)
    scale = rate * (1.0 / width)
    weights = (jnp.broadcast_to(scale, n.shape), scale * n, scale * gain_sq, scale * (ng * inv2 + g * inv))
    store.update(c2=c2, c3=c3, fac=fac, weights=weights, inv=inv, inv2=inv2, n=n)
    yield
    d_z1b_h = (d_actb * derb).astype(bf16)
    c1 = dot_tn(att1, d_z1b_h)
    row1 = inv2 * (gain_sq - (m_sq + m_gn) - n * m_ng)
    row2 = inv2 * (ng + big_g - (m_ng + m_g) - n * (m_nng + 2.0 * m_gn))
    store.update(dz2b=d_z2b_h, dz2bf=d_z2b, dz1b=d_z1b_h, c1=c1, row1=row1, row2=row2)
    yield
    fixed = dot_nn(jnp.concatenate([row1, row2, jnp.broadcast_to(inv2, n.shape), n], axis=0).astype(bf16), w2_h)
    d_att1 = dot_nt(d_z1b_h, s1_h)
    d_query = dot_nt(d_z1b_h, w1_h)
    yield
    prods = tuple(fixed[i * MINI : (i + 1) * MINI] for i in range(4))
    store.update(prods=prods)
    d_att1 = (-d_att1 * tri).astype(bf16)
    d_query = (d_query + dot_nn(d_att1, key_aug))[:, :width] + d_out
    d_key = dot_tn(d_att1, query_aug)[:, :width]
    yield
    d_gain = d_out * nb
    d_bias = d_out
    store.update(dq=d_query, dk=d_key, d_gain=d_gain, d_bias=d_bias, rate=rate, w1=w1_h, w2=w2_h, s2f=s2,
                 key=key_aug, query=query_aug, gslope=2.0 * n * gain + bias - target)
    yield


PIECES = 11


def settle(post, width):
    if post is None:
        return
    pre, d_s2, a1, a2, d_z1_h, p1_h, keep, gain, sink = post
    d_g = pre["inv"] * (pre["rate"] * d_s2 - a1 - pre["n"] * a2)
    d_gg = d_g * gain
    key_part = dot_nt(d_z1_h, pre["w1"])
    late_part = dot_nt(pre["s1"], p1_h)
    d_logit = keep * jnp.sum(d_s2 * pre["s2f"], axis=1, keepdims=True)
    yield
    d_gain = pre["d_gain"] + d_g * pre["gslope"]
    d_bias = pre["d_bias"] + d_gg
    d_key = pre["dk"] + d_gg + (key_part - late_part)[:, :width]
    sink(pre["dq"], d_key, -d_gg, d_logit, d_gain, d_bias)
    yield


def drain(maker):
    for _ in maker:
        pass


def backward_chain(carry, pre, post, fill, keep, gain, sink):
    p1, p2t, p2, dz, kq, left, right, dsum = carry
    width = gain.shape[1]
    key, act, der, w2_h = pre["key"], pre["act"], pre["der"], pre["w2"]
    after = settle(post, width)
    p1_h = p1.astype(bf16)
    coef1 = dot_nt(key, kq).astype(bf16)
    base1 = pre["c1"] + dot_nn(key, p1_h)
    d_s1 = -base1 - dot_nn(coef1, dz)
    p2_h = p2t.astype(bf16)
    coef2 = dot_nt(act, right).astype(bf16)
    p2 = p2 + dsum
    base2 = pre["c2"] + p2 + dot_nt(act, p2_h)
    fill(2)
    side = base2 + dot_nn(coef2, left)
    p1 = p1 + dot_tn(kq, dz)
    p2t = p2t + dot_tn(left, right)
    next(after, None)
    fill(1)
    d_upd = d_s1 * der
    d_upd_h = d_upd.astype(bf16)
    d_s2 = dot_nt(d_upd_h, w2_h) - side
    rest = pre["c3"] - dot_nn(pre["s2"], p2t.astype(bf16))
    p1_h = p1.astype(bf16)
    bend = d_s1 * pre["bend"]
    next(after, None)
    fill(3)
    d_fac = d_s2 * pre["fac"]
    main = dot_nn(d_fac.astype(bf16), w2_h)
    a1, a2, a3, a4 = (jnp.sum(d_s2 * w, axis=1, keepdims=True) for w in pre["weights"])
    fill(5)
    y1, y2, y3, y4 = pre["prods"]
    d_act = (main + rest) - ((a1 * y1 + a2 * y2) + (a3 * y3 + a4 * y4))
    d_z1_h = (d_act * der + bend).astype(bf16)
    d_zc = d_fac - ((a1 * pre["row1"] + a2 * pre["row2"]) + (a3 * pre["inv2"] + a4 * pre["n"]))
    d_zc_h = d_zc.astype(bf16)
    carry = (p1, p2t, p2, jnp.concatenate([d_z1_h, pre["dz1b"]], axis=0),
             jnp.concatenate([key, pre["query"]], axis=0),
             jnp.concatenate([pre["s2"], d_zc_h, pre["dz2b"]], axis=0),
             jnp.concatenate([d_upd_h, act, pre["actb"]], axis=0),
             jnp.sum(d_zc + pre["dz2bf"], axis=0, keepdims=True))
    return carry, (pre, d_s2, a1, a2, d_z1_h, p1_h, keep, gain, sink)


def backward_close(carry):
    p1, p2t, p2, dz, kq, left, right, dsum = carry
    return p1 + dot_tn(kq, dz), p2t + dot_tn(left, right), p2 + dsum


MESH = pl.DeviceIdType.MESH
PACK = 256
ENDS = 160


def seq_place():
    index = lax.axis_index("seq")
    pos = lax.rem(index, CHAIN)
    return pos, index - pos


def meet_group(pos, base):
    barrier = pltpu.get_barrier_semaphore()
    for d in range(1, CHAIN):
        pl.semaphore_signal(
            barrier, inc=1, device_id={"seq": base + lax.rem(pos + d, CHAIN)}, device_id_type=MESH)
    pl.semaphore_wait(barrier, CHAIN - 1)


def push(src, dst, send_sem, recv_sem, target):
    return pltpu.make_async_remote_copy(
        src_ref=src, dst_ref=dst, send_sem=send_sem, recv_sem=recv_sem,
        device_id={"seq": target}, device_id_type=MESH)


def await_bytes(ref, sem):
    pltpu.make_async_copy(ref, ref, sem).wait()


def swap_start(src, dst, send, recv, local_sem, pos, base):
    for d in range(1, CHAIN):
        peer = lax.rem(pos + d, CHAIN)
        push(src.at[peer], dst.at[pos], send.at[d - 1], recv.at[d - 1], base + peer).start()
    pltpu.make_async_copy(src.at[pos], dst.at[pos], local_sem).start()


def swap_wait(src, dst, send, recv, local_sem, pos, base):
    for d in range(1, CHAIN):
        peer = lax.rem(pos + d, CHAIN)
        origin = lax.rem(pos + CHAIN - d, CHAIN)
        push(src.at[peer], dst.at[pos], send.at[d - 1], recv.at[d - 1], base + peer).wait_send()
        await_bytes(dst.at[origin], recv.at[d - 1])
    await_bytes(dst.at[pos], local_sem)


def fwd_kernel(block, heads, count, pay_ref, ct_ref, w1_in, b1_in, w2_in, b2_in, gain_in, bias_in,
               mixed_ref, ct_out, k_out, q_out, aux_out, w1s_ref, w2s_ref, z1s_ref, upd_ref, zc_ref, s2_ref, z1b_ref, z2b_ref,
               got, k_all, q_all, base_all, aux_all, mixed_all, w1, w2t, b2, z1,
               pay_send, pay_recv, mix_send, mix_recv, ct_send, ct_recv, ct_loc):
    blk = pl.program_id(0)
    last = pl.num_programs(0) - 1
    pos, base = seq_place()
    width = gain_in.shape[1]
    hidden = w1.shape[1]
    rows_each = pay_ref.shape[0]
    per = rows_each // block
    piece = got.shape[1]
    parts = rows_each // piece
    owner = (pos >= FIRST) & (pos < FIRST + heads)
    mine = jnp.clip(pos - FIRST, 0, heads - 1)
    gain = gain_in[pl.ds(mine, 1), :]
    bias = bias_in[pl.ds(mine, 1), :]
    gain_sq = gain * gain
    tri = tri_mask()

    me, _ = head_place()

    @pl.when(blk == 0)
    def _():
        barrier = pltpu.get_barrier_semaphore()
        for d in range(1, count):
            pl.semaphore_signal(barrier, inc=1, device_id={"head": lax.rem(me + d, count)}, device_id_type=MESH)
        for d in range(1, CHAIN):
            pl.semaphore_signal(
                barrier, inc=1, device_id={"seq": base + lax.rem(pos + d, CHAIN)}, device_id_type=MESH)
        pl.semaphore_wait(barrier, CHAIN - 1 + count - 1)
        for s in range(parts):
            for j in range(heads):
                src = pay_ref.at[s * piece : (s + 1) * piece, j * PACK : (j + 1) * PACK]
                dst = got.at[pos * parts + s]

                @pl.when(pos != FIRST + j)
                def _():
                    push(src, dst, pay_send.at[j], pay_recv.at[pos * parts + s], base + FIRST + j).start()

                @pl.when(pos == FIRST + j)
                def _():
                    pltpu.make_async_copy(src, dst, pay_recv.at[pos * parts + s]).start()

    @pl.when(blk == 1)
    def _():
        for d in range(1, count):
            push_head(ct_ref, ct_out.at[me], ct_send.at[d - 1], ct_recv.at[d - 1], lax.rem(me + d, count)).start()
        pltpu.make_async_copy(ct_ref, ct_out.at[me], ct_loc).start()

    def take_in(p):
        await_bytes(got.at[p], pay_recv.at[p])
        part = got[p]
        rows = pl.ds(pl.multiple_of(p * piece, piece), piece)
        lane = lax.broadcasted_iota(jnp.int32, (piece, AUG), 1)
        one = jnp.ones((), bf16)
        zero = jnp.zeros((), bf16)
        tail = jnp.where(lane == width, one, zero)
        query = part[:, :AUG]
        key = part[:, width : width + AUG]
        q_all[rows, :] = jnp.where(lane < width, query, tail)
        k_all[rows, :] = jnp.where(lane < width, key, tail)
        key_f = part[:, width : 2 * width].astype(f32)
        target = part[:, 2 * width : 3 * width].astype(f32) - key_f
        logit = part[:, 3 * width : 3 * width + 1].astype(f32) + part[:, 3 * width + 1 : 3 * width + 2].astype(f32)
        sig = 1.0 / (1.0 + jnp.exp(-logit))
        base_all[rows, :] = (bias - target) * gain
        spot = lax.broadcasted_iota(jnp.int32, (piece, 2 * width), 1)
        wide = jnp.concatenate([target, target], axis=1)
        aux_all[rows, :] = jnp.where(
            spot < width, wide, jnp.where(spot == width, sig * (1.0 / width), 1.0 - sig))

    def send_mixed(b):
        p = lax.div(b, per)
        src = mixed_all.at[pl.ds(pl.multiple_of(b * block, block), block), :]
        dst = mixed_ref.at[mine, pl.ds(pl.multiple_of(lax.rem(b, per) * block, block), block), :]

        @pl.when(p != pos)
        def _():
            push(src, dst, mix_send, mix_recv.at[mine], base + p).start()

        @pl.when(p == pos)
        def _():
            pltpu.make_async_copy(src, dst, mix_recv.at[mine]).start()

    @pl.when(owner)
    def _():
        @pl.when(blk == 0)
        def _():
            row = lax.broadcasted_iota(jnp.int32, (AUG - width, hidden), 0)
            w1[pl.ds(0, width), :] = w1_in[mine]
            w1[pl.ds(width, AUG - width), :] = jnp.where(row == 0, b1_in[pl.ds(mine, 1), :], 0.0)
            turned = w2_in[mine]
            w2t[...] = turned - jnp.mean(turned, axis=0, keepdims=True)
            start = b2_in[pl.ds(mine, 1), :]
            b2[...] = start - mean_row(start)
            k_all[pl.ds(CHAIN * rows_each, MINI), :] = jnp.zeros((MINI, AUG), bf16)

        @pl.when(blk > 0)
        def _():
            send_mixed(blk - 1)

        def bring(p, _):
            take_in(p)
            return 0

        lax.fori_loop(jnp.where(blk == 0, 0, 2 * blk + 1), jnp.minimum(2 * blk + 3, 2 * last + 2), bring, 0)

        @pl.when(blk == 0)
        def _():
            z1[...] = dot_nn(k_all[0:MINI, :], w1[...].astype(bf16))

        state = (w1[...], w2t[...], b2[...])
        z1_now = z1[...]
        post = iter(())
        for loc in range(block // MINI):
            row = pl.multiple_of(blk * block + loc * MINI, MINI)
            rows = pl.ds(row, MINI)
            lr = pl.ds(loc * MINI, MINI)
            q_aug = q_all[rows, :]

            def save(w1_h, w2_h, z1_v, upd, zc, s2, z1b, loc=loc, lr=lr):
                w1s_ref[loc] = w1_h
                w2s_ref[loc] = w2_h
                z1s_ref[lr, :] = z1_v
                upd_ref[lr, :] = upd
                zc_ref[lr, :] = zc
                s2_ref[lr, :] = s2
                z1b_ref[lr, :] = z1b

            state, z1_now, kept = forward_chain(
                state, z1_now, post, k_all[rows, :], k_all[pl.ds(row + MINI, MINI), :], q_aug,
                base_all[rows, :], aux_all[rows, width : width + 1], gain_sq, tri, save)

            def sink(out, z2b, lr=lr, rows=rows, q_aug=q_aug):
                z2b_ref[lr, :] = z2b
                mixed_all[rows, :] = (out + q_aug[:, :width].astype(f32)).astype(bf16)

            post = forward_output(kept, gain, bias, tri, sink)
        drain(post)
        w1[...], w2t[...], b2[...] = state
        z1[...] = z1_now

        brows = pl.ds(pl.multiple_of(blk * block, block), block)
        k_out[...] = k_all[brows, :]
        q_out[...] = q_all[brows, :]
        aux_out[...] = aux_all[brows, :]

    @pl.when(blk == last)
    def _():
        @pl.when(owner)
        def _():
            send_mixed(last)
            others = mixed_all.at[pl.ds(0, (CHAIN - 1) * rows_each), :]
            await_bytes(others, mix_send)
        for j in range(heads):
            @pl.when(pos != FIRST + j)
            def _():
                await_bytes(got.at[pl.ds(0, parts)], pay_send.at[j])

            await_bytes(mixed_ref.at[j], mix_recv.at[j])

        for d in range(1, count):
            push_head(ct_ref, ct_out.at[me], ct_send.at[d - 1], ct_recv.at[d - 1],
                      lax.rem(me + d, count)).wait_send()
            await_bytes(ct_out.at[lax.rem(me + count - d, count)], ct_recv.at[d - 1])
        await_bytes(ct_out.at[me], ct_loc)


def chain_forward(payload, ct, w1, b1, w2, b2, gain, bias, block=256):
    rows = payload.shape[0]
    heads, width, hidden = w1.shape
    count = lax.axis_size("head")
    tokens = rows * CHAIN
    steps = tokens // MINI
    nb = block // MINI
    whole = lambda a: pl.BlockSpec(a.shape, lambda i: (0,) * a.ndim)
    rowblk = lambda w: pl.BlockSpec((block, w), lambda i: (i, 0))
    stepblk = lambda r: pl.BlockSpec((nb, r, hidden), lambda i: (i, 0, 0))
    anywhere = pl.BlockSpec(memory_space=pl.ANY)
    small = (w1, b1, w2, b2, gain, bias)
    dma = pltpu.SemaphoreType.DMA
    wide = jax.ShapeDtypeStruct((tokens, hidden), f32)
    narrow = jax.ShapeDtypeStruct((tokens, width), f32)
    return pl.pallas_call(
        functools.partial(fwd_kernel, block, heads, count),
        grid=(tokens // block,),
        in_specs=[anywhere, anywhere] + [whole(a) for a in small],
        out_specs=[anywhere, anywhere, rowblk(AUG), rowblk(AUG), rowblk(2 * width), stepblk(AUG), stepblk(width),
                   rowblk(hidden), rowblk(hidden), rowblk(width), rowblk(width), rowblk(hidden), rowblk(width)],
        out_shape=[jax.ShapeDtypeStruct((heads, rows, width), bf16),
                   jax.ShapeDtypeStruct((count,) + ct.shape, bf16),
                   jax.ShapeDtypeStruct((tokens, AUG), bf16),
                   jax.ShapeDtypeStruct((tokens, AUG), bf16),
                   jax.ShapeDtypeStruct((tokens, 2 * width), f32),
                   jax.ShapeDtypeStruct((steps, AUG, hidden), bf16),
                   jax.ShapeDtypeStruct((steps, width, hidden), bf16),
                   wide, wide, narrow, narrow, wide, narrow],
        scratch_shapes=[pltpu.VMEM((2 * tokens // block, block // 2, PACK), bf16),
                        pltpu.VMEM((tokens + MINI, AUG), bf16), pltpu.VMEM((tokens, AUG), bf16),
                        pltpu.VMEM((tokens, width), f32), pltpu.VMEM((tokens, 2 * width), f32),
                        pltpu.VMEM((tokens, width), bf16),
                        pltpu.VMEM((AUG, hidden), f32), pltpu.VMEM((width, hidden), f32),
                        pltpu.VMEM((1, width), f32), pltpu.VMEM((MINI, hidden), f32),
                        dma((heads,)), dma((2 * tokens // block,)), dma, dma((heads,)),
                        dma((count - 1,)), dma((count - 1,)), dma],
        compiler_params=pltpu.CompilerParams(collective_id=0, has_side_effects=True),
        name="inner_forward",
    )(payload, ct, *small)


def bwd_kernel(block, heads, turn, gm_ref, early_ref, small_ref, gain_in, bias_in, norm_ref, norm_last_ref,
               k_ref, q_ref, aux_ref, w1s_ref, w2s_ref, z1s_ref, upd_ref, zc_ref, s2_ref, z1b_ref, z2b_ref,
               grads_ref, ends_ref, late_ref, early_out, small_out,
               dout, half_got, half_mine, quarter, quarter_got, packed, ends, weights, late,
               p1, p2t, p2, dz, kq, left, right, dsum, dg, db, dl,
               gm_send, gm_recv, ha_send, ha_recv, ha_loc, qu_send, qu_recv, sm_send, sm_recv, sm_loc, bc_send, bc_recv, en_send, en_recv, la_send, la_recv):
    pid = pl.program_id(0)
    last = pl.num_programs(0) - 1
    blk = last - pid
    pos, base = seq_place()
    width = gain_in.shape[1]
    rows_each = gm_ref.shape[1]
    per = rows_each // block
    owner = (pos >= FIRST) & (pos < FIRST + heads)
    mine = jnp.clip(pos - FIRST, 0, heads - 1)
    gain = gain_in[pl.ds(mine, 1), :]
    bias = bias_in[pl.ds(mine, 1), :]
    gain_sq = gain * gain
    tri = tri_mask()
    count = block // MINI
    side = lax.rem(pos, 2)
    rank = lax.div(pos, 2)
    partner = pos + 1 - 2 * side
    state = (p1, p2t, p2, dz, kq, left, right, dsum)

    @pl.when(pid == 0)
    def _():
        meet_group(pos, base)
        for j in range(heads):
            @pl.when(pos != FIRST + j)
            def _():
                push(gm_ref.at[j], dout.at[pos], gm_send.at[j], gm_recv.at[pos], base + FIRST + j).start()

            @pl.when(pos == FIRST + j)
            def _():
                pltpu.make_async_copy(gm_ref.at[j], dout.at[pos], gm_recv.at[pos]).start()

        for d in range(1, CHAIN):
            push(small_ref, small_out.at[pos], sm_send.at[d - 1], sm_recv.at[d - 1],
                 base + lax.rem(pos + d, CHAIN)).start()
        pltpu.make_async_copy(small_ref, small_out.at[pos], sm_loc).start()
        push(early_ref.at[:, 1 - side], half_got, ha_send, ha_recv, base + partner).start()
        pltpu.make_async_copy(early_ref.at[:, side], half_mine, ha_loc).start()

    @pl.when(pid == turn)
    def _():
        push(early_ref.at[:, 1 - side], half_got, ha_send, ha_recv, base + partner).wait()
        await_bytes(half_mine, ha_loc)

        def pair_up(c, _):
            rows = pl.ds(pl.multiple_of(c * MINI, MINI), MINI)
            for r in range(CHAIN // 2):
                quarter[r, rows, :] = (half_mine[r, rows, :].astype(f32) + half_got[r, rows, :].astype(f32)).astype(bf16)
            return 0

        lax.fori_loop(0, half_mine.shape[1] // MINI, pair_up, 0)
        for d in range(1, CHAIN // 2):
            other = lax.rem(rank + d, CHAIN // 2)
            push(quarter.at[other], quarter_got.at[d - 1], qu_send.at[d - 1], qu_recv.at[d - 1],
                 base + 2 * other + side).start()

    def share_block(b):
        p = lax.div(b, per)
        src = packed.at[pl.ds(pl.multiple_of(b * block, block), block), :]
        dst = grads_ref.at[mine, pl.ds(pl.multiple_of(lax.rem(b, per) * block, block), block), :]

        @pl.when(p != pos)
        def _():
            push(src, dst, bc_send, bc_recv.at[mine], base + p).start()

        @pl.when(p == pos)
        def _():
            pltpu.make_async_copy(src, dst, bc_recv.at[mine]).start()

    share = late.shape[1]

    def weigh(norm, b, lo, hi):
        rows = pl.ds(pl.multiple_of(b * block, block), block)
        weights[lo:hi, :] += dot_tn(norm[:, lo:hi], packed[rows, :])

    slabs = [(i * 128, i * 128 + 128) for i in range(norm_ref.shape[1] // 128)]

    @pl.when(owner)
    def _():
        @pl.when(pid == 0)
        def _():
            for r in state + (dg, db, dl, weights):
                r[...] = jnp.zeros_like(r)
            packed[pl.ds(0, block), :] = jnp.zeros((block, PACK), bf16)

        @pl.when(lax.rem(pid, per) == 0)
        def _():
            p = lax.div(blk, per)
            await_bytes(dout.at[p], gm_recv.at[p])

        @pl.when(pid > 0)
        def _():
            share_block(blk + 1)

        carry = tuple(r[...] for r in state)
        totals = [dg[...], db[...], dl[...]]
        made = {}

        def start(loc):
            made[loc] = {}
            lr = pl.ds(loc * MINI, MINI)
            inner = pl.ds(pl.multiple_of(lax.rem(blk, per) * block + loc * MINI, MINI), MINI)
            saved = (w1s_ref[loc], w2s_ref[loc], z1s_ref[lr, :], upd_ref[lr, :], zc_ref[lr, :], s2_ref[lr, :],
                     z1b_ref[lr, :], z2b_ref[lr, :])
            return prepare_back(made[loc], saved, dout[lax.div(blk, per), inner, :].astype(f32), k_ref[lr, :],
                                q_ref[lr, :], aux_ref[lr, 0:width], aux_ref[lr, width : width + 1],
                                gain, gain_sq, bias, tri)

        drain(start(count - 1))
        post = None
        for loc in range(count - 1, -1, -1):
            ahead = start(loc - 1) if loc > 0 else iter(())

            def fill(pieces, ahead=ahead):
                for _ in range(pieces):
                    next(ahead, None)

            def sink(d_query, d_key, d_value, d_logit, d_gain, d_bias, loc=loc):
                totals[0] = totals[0] + d_gain
                totals[1] = totals[1] + d_bias
                totals[2] = totals[2] + d_logit
                high = d_logit.astype(bf16).astype(f32)
                lane = lax.broadcasted_iota(jnp.int32, (MINI, width), 1)
                extra = jnp.where(lane == 0, high, jnp.where(lane == 1, d_logit - high, 0.0))
                rows = pl.ds(pl.multiple_of(blk * block + loc * MINI, MINI), MINI)
                packed[rows, :] = jnp.concatenate([d_query, d_key, d_value, extra], axis=1).astype(bf16)

            if (count - 1 - loc) % 2 == 0 and (count - 1 - loc) // 2 < len(slabs):
                weigh(norm_ref, jnp.where(pid == 0, 0, blk + 1), *slabs[(count - 1 - loc) // 2])
            carry, post = backward_chain(
                carry, made.pop(loc), post, fill, aux_ref[pl.ds(loc * MINI, MINI), width + 1 : width + 2], gain, sink)
        drain(settle(post, width))
        for r, v in zip(state, carry):
            r[...] = v
        dg[...], db[...], dl[...] = totals

        @pl.when(pid == last)
        def _():
            end_one, end_two, end_b_two = backward_close(tuple(r[...] for r in state))
            ends[pl.ds(0, AUG), :] = end_one.astype(bf16)
            ends[pl.ds(AUG, width), :] = end_two.astype(bf16)
            rest = ENDS - AUG - width
            row = lax.broadcasted_iota(jnp.int32, (rest, width), 0)
            sums = [jnp.sum(r[...], axis=0, keepdims=True) for r in (dg, db, dl)]
            tailing = jnp.where(row == 0, end_b_two, jnp.where(row == 1, sums[0], jnp.where(row == 2, sums[1], 0.0)))
            high = sums[2].astype(bf16).astype(f32)
            tailing = tailing + jnp.where(row == 3, high, jnp.where(row == 4, sums[2] - high, 0.0))
            ends[pl.ds(AUG + width, rest), :] = jnp.concatenate([tailing] * 4, axis=1).astype(bf16)
            share_block(0)
            for slab in slabs:
                weigh(norm_last_ref, 0, *slab)
            for p in range(CHAIN):
                late[p] = weights[p * share : (p + 1) * share, :].astype(bf16)
            for d in range(1, CHAIN):
                peer = lax.rem(pos + d, CHAIN)
                push(late.at[peer], late_ref.at[mine], la_send.at[d - 1], la_recv.at[mine], base + peer).start()
            pltpu.make_async_copy(late.at[pos], late_ref.at[mine], la_recv.at[mine]).start()
            for d in range(1, CHAIN):
                push(ends, ends_ref.at[mine], en_send.at[d - 1], en_recv.at[mine],
                     base + lax.rem(pos + d, CHAIN)).start()
            pltpu.make_async_copy(ends, ends_ref.at[mine], en_recv.at[mine]).start()

    @pl.when(pid == last)
    def _():
        for d in range(1, CHAIN // 2):
            other = lax.rem(rank + d, CHAIN // 2)
            push(quarter.at[other], quarter_got.at[d - 1], qu_send.at[d - 1], qu_recv.at[d - 1],
                 base + 2 * other + side).wait()
        for d in range(1, CHAIN):
            push(small_ref, small_out.at[pos], sm_send.at[d - 1], sm_recv.at[d - 1],
                 base + lax.rem(pos + d, CHAIN)).wait_send()
            await_bytes(small_out.at[lax.rem(pos + CHAIN - d, CHAIN)], sm_recv.at[d - 1])
        await_bytes(small_out.at[pos], sm_loc)

        def add_up(c, _):
            rows = pl.ds(pl.multiple_of(c * MINI, MINI), MINI)
            acc = quarter[rank, rows, :].astype(f32)
            for d in range(1, CHAIN // 2):
                acc = acc + quarter_got[d - 1, rows, :].astype(f32)
            early_out[rows, :] = acc
            return 0

        lax.fori_loop(0, early_out.shape[0] // MINI, add_up, 0)
        for j in range(heads):
            @pl.when(pos != FIRST + j)
            def _():
                await_bytes(dout.at[pos], gm_send.at[j])

            await_bytes(grads_ref.at[j], bc_recv.at[j])
            await_bytes(ends_ref.at[j], en_recv.at[j])
            await_bytes(late_ref.at[j], la_recv.at[j])

        @pl.when(owner)
        def _():
            await_bytes(packed.at[pl.ds(0, (CHAIN - 1) * rows_each), :], bc_send)
            for d in range(1, CHAIN):
                await_bytes(ends, en_send.at[d - 1])
                await_bytes(late.at[0], la_send.at[d - 1])


def chain_backward(grad_mixed, early, small, gain, bias, normed, saved, block=256, turn=3):
    heads, rows, width = grad_mixed.shape
    tokens = rows * CHAIN
    hidden = saved[5].shape[1]
    nblk = tokens // block
    nb = block // MINI
    whole = lambda a: pl.BlockSpec(a.shape, lambda i: (0,) * a.ndim)
    rowblk = lambda w: pl.BlockSpec((block, w), lambda i: (nblk - 1 - i, 0))
    stepblk = lambda r: pl.BlockSpec((nb, r, hidden), lambda i: (nblk - 1 - i, 0, 0))
    behind = pl.BlockSpec((block, normed.shape[1]), lambda i: (jnp.minimum(nblk - i, nblk - 1), 0))
    first = pl.BlockSpec((block, normed.shape[1]), lambda i: (0, 0))
    anywhere = pl.BlockSpec(memory_space=pl.ANY)
    dma = pltpu.SemaphoreType.DMA
    seven = dma((CHAIN - 1,))
    share = early.shape[2:]
    three = dma((CHAIN // 2 - 1,))
    return pl.pallas_call(
        functools.partial(bwd_kernel, block, heads, turn),
        grid=(nblk,),
        in_specs=[anywhere] * 3 + [whole(gain), whole(bias), behind, first, rowblk(AUG), rowblk(AUG),
                                   rowblk(2 * width), stepblk(AUG), stepblk(width), rowblk(hidden), rowblk(hidden), rowblk(width),
                                   rowblk(width), rowblk(hidden), rowblk(width)],
        out_specs=[anywhere, anywhere, anywhere, pl.BlockSpec(share, lambda i: (0, 0)), anywhere],
        out_shape=[jax.ShapeDtypeStruct((heads, rows, PACK), bf16),
                   jax.ShapeDtypeStruct((heads, ENDS, hidden), bf16),
                   jax.ShapeDtypeStruct((heads, share[0], PACK), bf16),
                   jax.ShapeDtypeStruct(share, f32),
                   jax.ShapeDtypeStruct((CHAIN,) + small.shape, f32)],
        scratch_shapes=[pltpu.VMEM((CHAIN, rows, width), bf16), pltpu.VMEM((CHAIN // 2,) + share, bf16),
                        pltpu.VMEM((CHAIN // 2,) + share, bf16), pltpu.VMEM((CHAIN // 2,) + share, bf16),
                        pltpu.VMEM((CHAIN // 2 - 1,) + share, bf16),
                        pltpu.VMEM((tokens, PACK), bf16), pltpu.VMEM((ENDS, hidden), bf16),
                        pltpu.VMEM((CHAIN * share[0], PACK), f32), pltpu.VMEM((CHAIN, share[0], PACK), bf16),
                        pltpu.VMEM((AUG, hidden), f32), pltpu.VMEM((width, hidden), f32), pltpu.VMEM((1, width), f32),
                        pltpu.VMEM((2 * MINI, hidden), bf16), pltpu.VMEM((2 * MINI, AUG), bf16),
                        pltpu.VMEM((3 * MINI, width), bf16), pltpu.VMEM((3 * MINI, hidden), bf16),
                        pltpu.VMEM((1, width), f32), pltpu.VMEM((MINI, width), f32), pltpu.VMEM((MINI, width), f32),
                        pltpu.VMEM((MINI, 1), f32),
                        dma((heads,)), dma((CHAIN,)), dma, dma, dma, three, three, seven, seven, dma,
                        dma, dma((heads,)), seven, dma((heads,)), seven, dma((heads,))],
        compiler_params=pltpu.CompilerParams(collective_id=1, has_side_effects=True),
        name="inner_backward",
    )(grad_mixed, early, small, gain, bias, normed, normed, *saved)


def head_place():
    return lax.axis_index("head"), lax.axis_size("head")


def meet_heads(me, count):
    barrier = pltpu.get_barrier_semaphore()
    for d in range(1, count):
        pl.semaphore_signal(barrier, inc=1, device_id={"head": lax.rem(me + d, count)}, device_id_type=MESH)
    pl.semaphore_wait(barrier, count - 1)


def push_head(src, dst, send_sem, recv_sem, target):
    return pltpu.make_async_remote_copy(
        src_ref=src, dst_ref=dst, send_sem=send_sem, recv_sem=recv_sem,
        device_id={"head": target}, device_id_type=MESH)


def row_totals(first, second):
    ones = jnp.ones((8, first.shape[1]), f32)

    def total(x):
        return lax.dot_general(ones, x, (((1,), (1,)), ((), ())), precision=lax.Precision.HIGHEST,
                               preferred_element_type=f32)

    top, low = total(first), total(second)
    row = lax.broadcasted_iota(jnp.int32, top.shape, 0)
    return jnp.where(row == 0, top, low)


def mid_kernel(count, mixed_ref, x_ref, ctt_ref, mix_gate_ref, normed_ref, w_out_ref, w_gate_ref, w_up_ref, w_down_ref,
               post_gain_ref, post_bias_ref, ffn_gain_ref,
               gm_ref, early_ref, ggp_ref, out_ref, rco_ref, grc_ref, small_ref, norm_out,
               st_mine, st_got, pa_mine, pa_got, nt_all, rc_mine, rc_all, gn_mine, gn_got, dn_mine, dn_got, gov_all,
               gc_mine, gc_all, sb_mine, sb_got, gt_all, ct_ref, gh, gated, hidden, ggv, guv, resid,
               st_s, st_r, pa_s, pa_r, nt_s, nt_r, rc_s, rc_r, gn_s, gn_r, dn_s, dn_r, go_s, go_r, gc_s, gc_r, sb_s, sb_r,
               gt_s, gt_r, no_s, no_r):
    me, _ = head_place()
    heads, rows, width = mixed_ref.shape
    cols = heads * width
    full = cols * count
    part = rows // count
    peers = [(d, lax.rem(me + d, count)) for d in range(1, count)]
    pos, base = seq_place()
    owner = (pos >= FIRST) & (pos < FIRST + heads)
    barrier = pltpu.get_barrier_semaphore()
    for d in range(1, count):
        pl.semaphore_signal(barrier, inc=1, device_id={"head": lax.rem(me + d, count)}, device_id_type=MESH)
    for d in range(1, CHAIN):
        pl.semaphore_signal(
            barrier, inc=1, device_id={"seq": base + lax.rem(pos + d, CHAIN)}, device_id_type=MESH)
    pl.semaphore_wait(barrier, CHAIN - 1 + count - 1)
    ffn_gain = ffn_gain_ref[...][None, :]
    post_gain = post_gain_ref[...][None, :]
    post_bias = post_bias_ref[...][None, :]

    def rows_of(device):
        return pl.ds(pl.multiple_of(device * part, part), part)

    def send_all(src, dst, send, recv):
        for d, peer in peers:
            push_head(src, dst.at[d - 1], send.at[d - 1], recv.at[d - 1], peer).start()

    def wait_all(src, dst, send, recv):
        for d, peer in peers:
            push_head(src, dst.at[d - 1], send.at[d - 1], recv.at[d - 1], peer).wait()

    z = jnp.concatenate([mixed_ref[j] for j in range(heads)], axis=1).astype(f32)
    st_mine[...] = row_totals(z, z * z)
    send_all(st_mine, st_got, st_s, st_r)
    for j in range(heads):
        @pl.when(pos != FIRST + j)
        def _():
            push(normed_ref, norm_out.at[pos], no_s.at[j], no_r.at[pos], base + FIRST + j).start()

        @pl.when(pos == FIRST + j)
        def _():
            pltpu.make_async_copy(normed_ref, norm_out.at[pos], no_r.at[pos]).start()

    ct_ref[...] = ctt_ref[...].T
    gate_act, gate_der = gelu_first(dot_nt(normed_ref[...], mix_gate_ref[...]))
    gh[...] = dot_nt(ct_ref[...], w_down_ref[...])
    wait_all(st_mine, st_got, st_s, st_r)
    tot = st_mine[...]
    for d, _ in peers:
        tot = tot + st_got[d - 1]
    tot = tot.T * (1.0 / full)
    mean_z = tot[:, 0:1]
    inv_z = lax.rsqrt(tot[:, 1:2] - mean_z * mean_z + eps_norm)
    z_hat = (z - mean_z) * inv_z
    post_out = z_hat * post_gain + post_bias
    gated[...] = (post_out * gate_act).astype(bf16)

    def spread_rows(make, mine, got, send, recv):
        pending = None
        for d, peer in peers:
            mine[d - 1] = make(rows_of(peer)).astype(bf16)
            if pending is not None:
                pending.start()
            pending = push_head(mine.at[d - 1], got.at[d - 1], send.at[d - 1], recv.at[d - 1], peer)
        own = make(rows_of(me))
        pending.start()
        return own

    def add_rows(own, mine, got, send, recv):
        for d, peer in peers:
            push_head(mine.at[d - 1], got.at[d - 1], send.at[d - 1], recv.at[d - 1], peer).wait()
            own = own + got[d - 1].astype(f32)
        return own

    def gather_rows(all_ref, send, recv):
        for d, peer in peers:
            view = all_ref.at[rows_of(me), :]
            push_head(view, view, send.at[d - 1], recv.at[d - 1], peer).start()

    def gather_wait(all_ref, send, recv):
        for d, peer in peers:
            view = all_ref.at[rows_of(me), :]
            push_head(view, view, send.at[d - 1], recv.at[d - 1], peer).wait_send()
            await_bytes(all_ref.at[rows_of(lax.rem(me + count - d, count)), :], recv.at[d - 1])

    def turn_columns(value, mine, all_ref, send, recv):
        for b in range(count):
            mine[b] = value[:, b * cols : (b + 1) * cols]
        all_ref[rows_of(me), :] = mine[me]

    def turn_start(mine, all_ref, send, recv):
        for d, peer in peers:
            push_head(mine.at[peer], all_ref.at[rows_of(me), :], send.at[d - 1], recv.at[d - 1], peer).start()

    def turn_wait(mine, all_ref, send, recv):
        for d, peer in peers:
            push_head(mine.at[peer], all_ref.at[rows_of(me), :], send.at[d - 1], recv.at[d - 1], peer).wait_send()
            await_bytes(all_ref.at[rows_of(lax.rem(me + count - d, count)), :], recv.at[d - 1])

    w_out = w_out_ref[...]
    own = spread_rows(lambda r: dot_nn(gated[r, :], w_out), pa_mine, pa_got, pa_s, pa_r)
    res = x_ref[rows_of(me), :].astype(f32) + add_rows(own, pa_mine, pa_got, pa_s, pa_r)
    rms_two = lax.rsqrt(mean_row(res * res) + eps_norm)
    nt_all[rows_of(me), :] = (res * rms_two * ffn_gain).astype(bf16)
    turn_columns(res, rc_mine, rc_all, rc_s, rc_r)
    resid[...] = res
    gather_rows(nt_all, nt_s, nt_r)
    turn_start(rc_mine, rc_all, rc_s, rc_r)
    gather_wait(nt_all, nt_s, nt_r)
    def forward_rows(b, _):
        r = pl.ds(pl.multiple_of(b * part, part), part)
        nt = nt_all[r, :]
        gate_val = dot_nn(nt, w_gate_ref[...])
        up_val = dot_nn(nt, w_up_ref[...])
        sig = 1.0 / (1.0 + jnp.exp(-gate_val))
        silu = gate_val * sig
        hidden[r, :] = (silu * up_val).astype(bf16)
        g = gh[r, :]
        ggv[r, :] = (g * up_val * sig * (1.0 + gate_val * (1.0 - sig))).astype(bf16)
        guv[r, :] = (g * silu).astype(bf16)
        return 0

    lax.fori_loop(0, count, forward_rows, 0)
    own = spread_rows(lambda r: dot_nt(ggv[r, :], w_gate_ref[...]) + dot_nt(guv[r, :], w_up_ref[...]),
                      gn_mine, gn_got, gn_s, gn_r)
    for b in range(count):
        r = pl.ds(b * part, part)
        down = dot_nn(hidden[r, :], w_down_ref[...]).astype(bf16)
        for c in range(count):
            dn_mine[c, r, :] = down[:, c * cols : (c + 1) * cols]
    ffn = w_gate_ref.shape[1]
    half = full // 2
    for b in range(2):
        r = slice(b * half, (b + 1) * half)
        early_ref[r, 0:ffn] = dot_tn(nt_all[:, r], ggv[...]).astype(bf16)
    for d, peer in peers:
        push_head(dn_mine.at[peer], dn_got.at[d - 1], dn_s.at[d - 1], dn_r.at[d - 1], peer).start()
    gnt = add_rows(own, gn_mine, gn_got, gn_s, gn_r)
    res = resid[...]
    rms_two = lax.rsqrt(mean_row(res * res) + eps_norm)
    scaled = gnt * ffn_gain
    grad_res = ct_ref[rows_of(me), :].astype(f32) + rms_two * (
        scaled - res * rms_two * rms_two * mean_row(scaled * res))
    gov_all[rows_of(me), :] = grad_res.astype(bf16)
    gt_all[me] = jnp.broadcast_to(jnp.sum(gnt * res * rms_two, axis=0, keepdims=True), gt_all.shape[1:])
    turn_columns(grad_res, gc_mine, gc_all, gc_s, gc_r)
    gather_rows(gov_all, go_s, go_r)
    turn_start(gc_mine, gc_all, gc_s, gc_r)
    for d, peer in peers:
        push_head(gt_all.at[me], gt_all.at[me], gt_s.at[d - 1], gt_r.at[d - 1], peer).start()
    for b in range(2):
        r = slice(b * half, (b + 1) * half)
        early_ref[r, ffn : 2 * ffn] = dot_tn(nt_all[:, r], guv[...]).astype(bf16)
    gather_wait(gov_all, go_s, go_r)
    gov = gov_all[...]
    grad_gated = dot_nt(gov, w_out_ref[...])
    grad_post = grad_gated * gate_act
    grad_zhat = grad_post * post_gain
    sb_mine[...] = row_totals(grad_zhat, grad_zhat * z_hat)
    ggp = (grad_gated * post_out * gate_der).astype(bf16)
    ggp_ref[...] = ggp
    send_all(sb_mine, sb_got, sb_s, sb_r)
    early_ref[:, 3 * ffn : 3 * ffn + 2 * cols] = jnp.concatenate(
        [dot_tn(normed_ref[...], ggp).astype(bf16), dot_tn(gov, gated[...]).astype(bf16)], axis=1)
    row = lax.broadcasted_iota(jnp.int32, (8, cols), 0)
    wait_all(sb_mine, sb_got, sb_s, sb_r)
    tot = sb_mine[...]
    for d, _ in peers:
        tot = tot + sb_got[d - 1]
    tot = tot.T * (1.0 / full)
    grad_mixed = (inv_z * (grad_zhat - tot[:, 0:1] - z_hat * tot[:, 1:2])).astype(bf16)
    for j in range(heads):
        gm_ref[j] = grad_mixed[:, j * width : (j + 1) * width]
    for b in range(2):
        r = slice(b * half, (b + 1) * half)
        early_ref[r, 2 * ffn : 3 * ffn] = dot_nn(ctt_ref[r, :], hidden[...]).astype(bf16)
    turn_wait(rc_mine, rc_all, rc_s, rc_r)
    rco_ref[...] = rc_all[...]
    out = dn_mine[me].astype(f32)
    for d, peer in peers:
        push_head(dn_mine.at[peer], dn_got.at[d - 1], dn_s.at[d - 1], dn_r.at[d - 1], peer).wait()
        out = out + dn_got[d - 1].astype(f32)
    out_ref[...] = out
    turn_wait(gc_mine, gc_all, gc_s, gc_r)
    grc_ref[...] = gc_all[...]
    for d, peer in peers:
        push_head(gt_all.at[me], gt_all.at[me], gt_s.at[d - 1], gt_r.at[d - 1], peer).wait_send()
        await_bytes(gt_all.at[lax.rem(me + count - d, count)], gt_r.at[d - 1])
    gain_two = gt_all[0]
    for b in range(1, count):
        gain_two = gain_two + gt_all[b]
    post = jnp.where(row == 1, jnp.sum(grad_post * z_hat, axis=0, keepdims=True),
                     jnp.sum(grad_post, axis=0, keepdims=True))
    line = lax.broadcasted_iota(jnp.int32, (8, full), 0)
    small_ref[...] = jnp.where(
        line == 0, gain_two, jnp.concatenate([post] + [jnp.zeros_like(post)] * (count - 1), axis=1))
    for j in range(heads):
        @pl.when(pos != FIRST + j)
        def _():
            await_bytes(normed_ref, no_s.at[j])

    @pl.when(owner)
    def _():
        for p in range(CHAIN):
            await_bytes(norm_out.at[p], no_r.at[p])


def middle(mixed, x, ct, mix_gate, normed, w_out, w_gate, w_up, w_down, post_gain, post_bias, ffn_gain):
    count = lax.axis_size("head")
    heads, rows, width = mixed.shape
    cols = heads * width
    full = cols * count
    part = rows // count
    ffn = w_gate.shape[1]
    ins = (mixed, x, ct, mix_gate, normed, w_out, w_gate, w_up, w_down, post_gain, post_bias, ffn_gain)
    vmem = pl.BlockSpec(memory_space=pltpu.VMEM)
    V = pltpu.VMEM
    trio = count - 1
    sem = pltpu.SemaphoreType.DMA((trio,))
    return pl.pallas_call(
        functools.partial(mid_kernel, count),
        in_specs=[vmem] * len(ins),
        out_specs=[vmem] * 7 + [pl.BlockSpec(memory_space=pl.ANY)],
        out_shape=[jax.ShapeDtypeStruct((heads, rows, width), bf16),
                   jax.ShapeDtypeStruct((full, 3 * ffn + 2 * cols), bf16),
                   jax.ShapeDtypeStruct((rows, cols), bf16),
                   jax.ShapeDtypeStruct((rows, cols), f32),
                   jax.ShapeDtypeStruct((rows, cols), f32),
                   jax.ShapeDtypeStruct((rows, cols), f32),
                   jax.ShapeDtypeStruct((8, full), f32),
                   jax.ShapeDtypeStruct((CHAIN, rows, full), bf16)],
        scratch_shapes=[
            V((8, rows), f32), V((trio, 8, rows), f32),
            V((trio, part, full), bf16), V((trio, part, full), bf16),
            V((rows, full), bf16),
            V((count, part, cols), f32), V((rows, cols), f32),
            V((trio, part, full), bf16), V((trio, part, full), bf16),
            V((count, rows, cols), bf16), V((trio, rows, cols), bf16),
            V((rows, full), bf16),
            V((count, part, cols), f32), V((rows, cols), f32),
            V((8, rows), f32), V((trio, 8, rows), f32),
            V((count, 8, full), f32),
            V((rows, full), bf16), V((rows, ffn), f32), V((rows, cols), bf16),
            V((rows, ffn), bf16), V((rows, ffn), bf16), V((rows, ffn), bf16),
            V((part, full), f32)] + [sem] * 20 + [
            pltpu.SemaphoreType.DMA((heads,)), pltpu.SemaphoreType.DMA((CHAIN,))],
        compiler_params=pltpu.CompilerParams(
            collective_id=2, has_side_effects=True, vmem_limit_bytes=56 * 1024 * 1024),
        name="middle",
    )(*ins)


def front_kernel(count, in_ref, gain_ref, bias_ref, wq_ref, wk_ref, wv_ref, wr_ref, x_ref, normed_ref, pay_ref, gathered, send, recv):
    me, _ = head_place()
    cols, rows = in_ref.shape
    heads = wr_ref.shape[0]
    width = cols // heads
    part = rows // count
    meet_heads(me, count)
    here = pl.ds(pl.multiple_of(me * cols, cols), cols)
    for d in range(1, count):
        push_head(in_ref, gathered.at[here, :], send.at[d - 1], recv.at[d - 1], lax.rem(me + d, count)).start()
    gathered[here, :] = in_ref[...]
    for d in range(1, count):
        push_head(in_ref, gathered.at[here, :], send.at[d - 1], recv.at[d - 1], lax.rem(me + d, count)).wait_send()
        origin = lax.rem(me + count - d, count)
        await_bytes(gathered.at[pl.ds(pl.multiple_of(origin * cols, cols), cols), :], recv.at[d - 1])
    gain = gain_ref[...][None, :]
    rate_bias = bias_ref[...][None, :]
    x_ref[...] = gathered[...].T

    def project(b, _):
        r = pl.ds(pl.multiple_of(b * part, part), part)
        x = x_ref[r, :].astype(f32)
        nt = (x * lax.rsqrt(mean_row(x * x) + eps_norm) * gain).astype(bf16)
        normed_ref[r, :] = nt
        query = dot_nt(nt, wq_ref[...]).astype(bf16)
        key = dot_nt(nt, wk_ref[...]).astype(bf16)
        value = dot_nt(nt, wv_ref[...]).astype(bf16)
        logit = dot_nt(nt, wr_ref[...]) + rate_bias
        high = logit.astype(bf16)
        low = (logit - high.astype(f32)).astype(bf16)
        lane = lax.broadcasted_iota(jnp.int32, (part, width), 1)
        for j in range(heads):
            own = slice(j * width, (j + 1) * width)
            extra = jnp.where(lane == 0, high[:, j : j + 1].astype(f32),
                              jnp.where(lane == 1, low[:, j : j + 1].astype(f32), 0.0)).astype(bf16)
            pay_ref[r, j * PACK : (j + 1) * PACK] = jnp.concatenate(
                [query[:, own], key[:, own], value[:, own], extra], axis=1)
        return 0

    lax.fori_loop(0, count, project, 0)


def front(inputs_t, pre_gain, rate_bias, wq, wk, wv, wr):
    count = lax.axis_size("head")
    cols, rows = inputs_t.shape
    heads = wr.shape[0]
    vmem = pl.BlockSpec(memory_space=pltpu.VMEM)
    sem = pltpu.SemaphoreType.DMA((count - 1,))
    wide = jax.ShapeDtypeStruct((rows, cols * count), bf16)
    return pl.pallas_call(
        functools.partial(front_kernel, count),
        in_specs=[vmem] * 7,
        out_specs=[vmem] * 3,
        out_shape=[wide, wide, jax.ShapeDtypeStruct((rows, heads * PACK), bf16)],
        scratch_shapes=[pltpu.VMEM((cols * count, rows), bf16), sem, sem],
        compiler_params=pltpu.CompilerParams(collective_id=4, has_side_effects=True),
        name="front",
    )(inputs_t, pre_gain, rate_bias, wq, wk, wv, wr)


def tail_kernel(count, at_mix, grads_ref, wq_ref, wk_ref, wv_ref, wr_ref, mix_gate_ref, ggp_ref, x_ref, gain_ref,
                late_ref, early_ref,
                back_ref, tiles_ref,
                mine, got, tile, tile_got, wcols, ib_s, ib_r, th_s, th_r, ts_s, ts_r, ts_loc):
    me, _ = head_place()
    pos, base = seq_place()
    heads = grads_ref.shape[0]
    rows = x_ref.shape[0]
    cols = ggp_ref.shape[1]
    full = x_ref.shape[1]
    share = early_ref.shape[0]
    rate_lane = PACK - PACK // 4
    peers = [(d, lax.rem(me + d, count)) for d in range(1, count)]
    barrier = pltpu.get_barrier_semaphore()
    for d, peer in peers:
        pl.semaphore_signal(barrier, inc=1, device_id={"head": peer}, device_id_type=MESH)
    for d in range(1, CHAIN):
        pl.semaphore_signal(
            barrier, inc=1, device_id={"seq": base + lax.rem(pos + d, CHAIN)}, device_id_type=MESH)
    part = rows // count
    width = PACK // 4
    pre_gain = gain_ref[...][None, :]
    sides = (wq_ref, wk_ref, wv_ref)

    def back_rows(b, _):
        r = pl.ds(pl.multiple_of(b * part, part), part)
        grad = dot_nn(ggp_ref[r, :], mix_gate_ref[...])
        blocks = [grads_ref[j, r, :] for j in range(heads)]
        for i, side in enumerate(sides):
            joined = jnp.concatenate([b[:, i * width : (i + 1) * width] for b in blocks], axis=1)
            grad = grad + dot_nn(joined, side[...])
        for j in range(heads):
            rate = blocks[j][:, rate_lane : rate_lane + 1].astype(f32) + blocks[j][
                :, rate_lane + 1 : rate_lane + 2].astype(f32)
            grad = grad + rate.astype(bf16).astype(f32) * wr_ref[j : j + 1, :].astype(f32)
        x = x_ref[r, :].astype(f32)
        rms = lax.rsqrt(mean_row(x * x) + eps_norm)
        scaled = grad * pre_gain
        back = (rms * (scaled - x * rms * rms * mean_row(scaled * x))).astype(bf16)
        for c in range(count):
            mine[c, r, :] = back[:, c * cols : (c + 1) * cols]
        return 0

    lane = lax.broadcasted_iota(jnp.int32, (share, 128), 1)
    line = lax.broadcasted_iota(jnp.int32, (8, 128), 0)
    w_rows = pl.ds(pl.multiple_of(pos * share, share), share)
    slim = jnp.concatenate([wr_ref[j : j + 1, :].astype(f32) for j in range(heads)] + [pre_gain] * (8 - heads), axis=0)
    wcols[4, :, 0:8] = slim.T
    for i, side in enumerate(sides + (mix_gate_ref,)):
        wcols[i] = side[...].astype(f32).T
    gain = jnp.sum(early_ref[:, at_mix : at_mix + cols] * wcols[3, w_rows, :], axis=1, keepdims=True)
    table = jnp.zeros((share, 128), f32)
    blocks = [late_ref[j].astype(f32) for j in range(heads)]
    for i in range(3):
        joined = jnp.concatenate([b[:, i * width : (i + 1) * width] for b in blocks], axis=1)
        gain = gain + jnp.sum(joined * wcols[i, w_rows, :], axis=1, keepdims=True)
    for j in range(heads):
        rate = blocks[j][:, rate_lane : rate_lane + 1] + blocks[j][:, rate_lane + 1 : rate_lane + 2]
        gain = gain + rate * wcols[4, w_rows, j : j + 1]
        table = jnp.where(lane == j, rate, table)
    gain = gain / wcols[4, w_rows, heads : heads + 1]
    table = jnp.where(lane == heads, gain, table)
    flat = jnp.concatenate([table, jnp.zeros((128 - share, 128), f32)], axis=0).T[0:8]
    tile[...] = flat
    pl.semaphore_wait(barrier, count - 1 + CHAIN - 1)
    for d, peer in peers:
        push_head(tile, tile_got.at[d - 1], th_s.at[d - 1], th_r.at[d - 1], peer).start()
    lax.fori_loop(0, count, back_rows, 0)
    for d, peer in peers:
        push_head(mine.at[peer], got.at[d - 1], ib_s.at[d - 1], ib_r.at[d - 1], peer).start()
    back = mine[me].astype(f32)
    for d, peer in peers:
        push_head(tile, tile_got.at[d - 1], th_s.at[d - 1], th_r.at[d - 1], peer).wait()
    summed = flat
    for d, peer in peers:
        summed = summed + tile_got[d - 1]
    tile[...] = jnp.where(line == heads, summed, flat)
    for d in range(1, CHAIN):
        push(tile, tiles_ref.at[pos], ts_s.at[d - 1], ts_r.at[d - 1], base + lax.rem(pos + d, CHAIN)).start()
    pltpu.make_async_copy(tile, tiles_ref.at[pos], ts_loc).start()
    for d, peer in peers:
        push_head(mine.at[peer], got.at[d - 1], ib_s.at[d - 1], ib_r.at[d - 1], peer).wait()
        back = back + got[d - 1].astype(f32)
    back_ref[...] = back
    for d in range(1, CHAIN):
        push(tile, tiles_ref.at[pos], ts_s.at[d - 1], ts_r.at[d - 1], base + lax.rem(pos + d, CHAIN)).wait_send()
        await_bytes(tiles_ref.at[lax.rem(pos + CHAIN - d, CHAIN)], ts_r.at[d - 1])
    await_bytes(tiles_ref.at[pos], ts_loc)


def tail(at_mix, grads, wq, wk, wv, wr, mix_gate, ggp, x, pre_gain, late, early):
    count = lax.axis_size("head")
    rows, full = x.shape
    width = ggp.shape[1]
    vmem = pl.BlockSpec(memory_space=pltpu.VMEM)
    V = pltpu.VMEM
    dma = pltpu.SemaphoreType.DMA
    trio, seven = dma((count - 1,)), dma((CHAIN - 1,))
    return pl.pallas_call(
        functools.partial(tail_kernel, count, at_mix),
        in_specs=[vmem] * 11,
        out_specs=[vmem] * 2,
        out_shape=[jax.ShapeDtypeStruct((rows, width), f32),
                   jax.ShapeDtypeStruct((CHAIN, 8, 128), f32)],
        scratch_shapes=[V((count, rows, width), bf16), V((count - 1, rows, width), bf16),
                        V((8, 128), f32), V((count - 1, 8, 128), f32), V((5, full, width), f32),
                        trio, trio, trio, trio, seven, seven, dma],
        compiler_params=pltpu.CompilerParams(
            collective_id=3, has_side_effects=True, vmem_limit_bytes=56 * 1024 * 1024),
        name="tail",
    )(grads, wq, wk, wv, wr, mix_gate, ggp, x, pre_gain, late, early)


def final_kernel(at_mix, ffn, down_ref, resid_ref, back_ref, grc_ref, late_ref, early_ref, ends_ref, tiles_ref, small_ref,
                 out_ref, gin_ref, gq_ref, gk_ref, gv_ref, gmix_ref, rate_ref, gwout_ref, gwg_ref, gwu_ref, gwd_ref,
                 w1_ref, b1_ref, w2_ref, b2_ref, ig_ref, ib_ref, rb_ref, pre_ref, pg_ref, pb_ref, fg_ref):
    heads, width, hidden = w1_ref.shape
    cols = heads * width
    out_ref[...] = (down_ref[...] + resid_ref[...]).T
    gin_ref[...] = (back_ref[...] + grc_ref[...]).T
    for i, ref in enumerate((gq_ref, gk_ref, gv_ref)):
        ref[...] = jnp.concatenate([late_ref[j, :, i * width : (i + 1) * width].astype(f32) for j in range(heads)], axis=1)
    gwg_ref[...] = early_ref[:, 0:ffn]
    gwu_ref[...] = early_ref[:, ffn : 2 * ffn]
    rates = []
    gwd_ref[...] = early_ref[:, 2 * ffn : 3 * ffn]
    both = early_ref[:, at_mix : at_mix + 2 * cols]
    gmix_ref[...] = both[:, 0:cols]
    gwout_ref[...] = both[:, cols:].T
    for j in range(heads):
        w1_ref[j] = ends_ref[j, 0:width, :].astype(f32)
        b1_ref[pl.ds(j, 1), :] = ends_ref[j, width : AUG, :].astype(f32)[0:1]
        second = ends_ref[j, AUG : AUG + width, :].astype(f32)
        w2_ref[j] = second - jnp.mean(second, axis=0, keepdims=True)
        rest = ends_ref[j, AUG + width :, :].astype(f32)[0:8, 0:width]
        b2_ref[pl.ds(j, 1), :] = rest[0:1] - mean_row(rest[0:1])
        ig_ref[pl.ds(j, 1), :] = rest[1:2]
        ib_ref[pl.ds(j, 1), :] = rest[2:3]
        rates.append((rest[3:4] + rest[4:5])[:, 0:1])
    each = rate_ref.shape[1] // CHAIN
    strips = jnp.concatenate([tiles_ref[p, :, 0:each] for p in range(CHAIN)], axis=1)
    rate_ref[...] = strips[0:heads]
    me, count = head_place()
    pick = [tiles_ref[me * (CHAIN // count) + i, heads : heads + 1, 0:each] for i in range(CHAIN // count)]
    pre_ref[...] = jnp.concatenate(pick, axis=1)[0]
    rb_ref[...] = jnp.concatenate(rates, axis=1)[0]
    acc = small_ref[0]
    for p in range(1, CHAIN):
        acc = acc + small_ref[p]
    fg_ref[...] = acc[0]
    pg_ref[...] = acc[1:2, 0:cols][0]
    pb_ref[...] = acc[2:3, 0:cols][0]


def finish(at_mix, ffn, down, resid, back, grc, late, early, ends, tiles, small, shapes):
    ins = (down, resid, back, grc, late, early, ends, tiles, small)
    vmem = pl.BlockSpec(memory_space=pltpu.VMEM)
    return pl.pallas_call(
        functools.partial(final_kernel, at_mix, ffn),
        in_specs=[vmem] * len(ins),
        out_specs=[vmem] * len(shapes),
        out_shape=[jax.ShapeDtypeStruct(s, f32) for s in shapes],
        compiler_params=pltpu.CompilerParams(vmem_limit_bytes=48 * 1024 * 1024),
        name="final",
    )(*ins)


def stretch_groups(axis):
    count = lax.axis_size(axis)
    return [[start + step for step in range(0, count, CHAIN)] for start in range(CHAIN)]


def local(
    inputs,
    pre_gain,
    w_query,
    w_key,
    w_value,
    mix_gate,
    w_rate,
    rate_bias,
    inner_gain,
    inner_bias,
    init_w_one,
    init_b_one,
    init_w_two,
    init_b_two,
    post_gain,
    post_bias,
    w_out,
    ffn_gain,
    w_gate,
    w_up,
    w_down,
    cotangent,
):
    full_width = pre_gain.shape[0]
    rows, local_cols = inputs.shape
    heads, head_dim = inner_gain.shape
    stretches = lax.axis_size("seq") // CHAIN
    share = full_width // CHAIN

    sides = (w_query.T, w_key.T, w_value.T, w_rate.T)
    whole_low, normed_one, payload = front(inputs.T, pre_gain, rate_bias, *sides)
    mixed_h, ct_blocks, *saved = chain_forward(
        payload, cotangent.T, init_w_one, init_b_one, init_w_two.transpose(0, 2, 1), init_b_two,
        inner_gain, inner_bias)
    ffn = w_gate.shape[1]
    at_mix = 3 * ffn
    grad_mixed, early, grad_gate_pre, down_cols, resid_cols, grad_resid_cols, small, normed_all = middle(
        mixed_h, whole_low, ct_blocks.reshape(full_width, rows), mix_gate.T, normed_one, w_out, w_gate, w_up, w_down,
        post_gain, post_bias, ffn_gain)
    grads, ends, late, early_sum, small = chain_backward(
        grad_mixed, early.reshape(CHAIN // 2, 2, share, early.shape[1]), small, inner_gain, inner_bias,
        normed_all.reshape(CHAIN * rows, full_width), saved)
    back_cols, tiles = tail(
        at_mix, grads, *sides, mix_gate.T, grad_gate_pre, whole_low, pre_gain,
        late, early_sum)
    if stretches > 1:
        groups = stretch_groups("seq")
        ends, tiles, small = lax.psum((ends.astype(f32), tiles, small), "seq", axis_index_groups=groups)
        seq_index = lax.axis_index("seq")
        stretch_lists = [list(range(s, s + CHAIN)) for s in range(0, stretches * CHAIN, CHAIN)]

        def spread(mine_rows):
            summed = lax.psum(mine_rows, "seq", axis_index_groups=groups)
            total = lax.all_gather(
                summed, "seq", axis=summed.ndim - 2, tiled=True, axis_index_groups=stretch_lists)
            return lax.dynamic_slice_in_dim(
                total, seq_index * (share // stretches), share // stretches, summed.ndim - 2)

        late = spread(late.astype(f32))
        early_sum = spread(early_sum)
    held = share // stretches
    hidden = init_w_one.shape[2]
    square = (held, local_cols)
    (outputs, grad_inputs, grad_q, grad_k, grad_v, grad_mix, grad_rate_w, grad_w_out, grad_w_gate, grad_w_up, grad_w_down,
     grad_one, grad_b_one, grad_two, grad_b_two, grad_gain, grad_bias, rate_b, grad_pre, grad_post_gain, grad_post_bias,
     grad_ffn_gain) = finish(
        at_mix, ffn, down_cols, resid_cols, back_cols, grad_resid_cols, late, early_sum, ends, tiles, small,
        ((local_cols, rows), (local_cols, rows), square, square, square, square, (heads, full_width),
         (local_cols, held), (held, ffn), (held, ffn), (held, ffn),
         (heads, head_dim, hidden), (heads, hidden), (heads, head_dim, hidden), (heads, head_dim),
         (heads, head_dim), (heads, head_dim), (heads,), (local_cols,), (local_cols,), (local_cols,), (full_width,)))
    return (
        outputs.T,
        grad_inputs.T,
        grad_pre,
        grad_q,
        grad_k,
        grad_v,
        grad_mix,
        grad_rate_w.T,
        rate_b,
        grad_gain,
        grad_bias,
        grad_one,
        grad_b_one,
        grad_two.transpose(0, 2, 1),
        grad_b_two,
        grad_post_gain,
        grad_post_bias,
        grad_w_out,
        grad_ffn_gain,
        grad_w_gate,
        grad_w_up,
        grad_w_down.T,
    )


def solution(mesh):
    in_specs = (
        P("seq", "head"),
        P(),
        P(None, "head"),
        P(None, "head"),
        P(None, "head"),
        P(None, "head"),
        P(None, "head"),
        P("head"),
        P("head", None),
        P("head", None),
        P("head", None, None),
        P("head", None),
        P("head", None, None),
        P("head", None),
        P("head"),
        P("head"),
        P("head", None),
        P(),
        P(None, "head"),
        P(None, "head"),
        P("head", None),
        P("seq", "head"),
    )
    out_specs = (
        P("seq", "head"),
        P("seq", "head"),
        P("head"),
        P("seq", "head"),
        P("seq", "head"),
        P("seq", "head"),
        P("seq", "head"),
        P(None, "head"),
        P("head"),
        P("head", None),
        P("head", None),
        P("head", None, None),
        P("head", None),
        P("head", None, None),
        P("head", None),
        P("head"),
        P("head"),
        P("head", "seq"),
        P(),
        P("seq", "head"),
        P("seq", "head"),
        P("head", "seq"),
    )
    return jax.shard_map(local, mesh=mesh, in_specs=in_specs, out_specs=out_specs, check_vma=False)
```

```python
import functools

import jax
import jax.numpy as jnp
from jax import lax
from jax.experimental import pallas as pl
from jax.experimental.pallas import tpu as pltpu
from jax.sharding import PartitionSpec as P

MINI = 16
CHAIN = 8
FIRST = 2
AUG = 80
eps_norm = 1e-06
gelu_scale = 0.7978845608028654
f32 = jnp.float32
bf16 = jnp.bfloat16


def dot_nn(a, b):
    return lax.dot_general(a, b, (((1,), (0,)), ((), ())), preferred_element_type=f32)


def dot_nt(a, b):
    return lax.dot_general(a, b, (((1,), (1,)), ((), ())), preferred_element_type=f32)


def dot_tn(a, b):
    return lax.dot_general(a, b, (((0,), (0,)), ((), ())), preferred_element_type=f32)


def mean_row(x):
    return jnp.sum(x, axis=1, keepdims=True) * (1.0 / x.shape[1])


def gelu_first(z):
    sq = z * z
    th = jnp.tanh(gelu_scale * z * (1.0 + 0.044715 * sq))
    half = 0.5 * (1.0 + th)
    act = z * half
    der = half + (0.5 * gelu_scale) * z * (1.0 - th * th) * (1.0 + 0.134145 * sq)
    return act, der


def gelu_second(z):
    sq = z * z
    th = jnp.tanh(gelu_scale * z * (1.0 + 0.044715 * sq))
    half = 0.5 * (1.0 + th)
    act = z * half
    slope = gelu_scale * (1.0 + 0.134145 * sq)
    sech = 1.0 - th * th
    der = half + 0.5 * z * sech * slope
    curve = sech * (slope + z * (0.5 * gelu_scale * 0.26829 * z) - z * th * slope * slope)
    return act, der, curve


def tri_mask():
    rows = lax.broadcasted_iota(jnp.int32, (MINI, MINI), 0)
    cols = lax.broadcasted_iota(jnp.int32, (MINI, MINI), 1)
    return jnp.where(rows >= cols, 1.0, 0.0).astype(f32)


def forward_output(kept, gain, bias, tri, sink):
    z1b, act_h, w2_h, b2, s2_h = kept
    actb, _ = gelu_first(z1b)
    actb_h = actb.astype(bf16)
    yield
    att = dot_nt(actb_h, act_h)
    z2b = dot_nt(actb_h, w2_h) + b2
    yield
    z2b = z2b - dot_nn(((att + 1.0) * tri).astype(bf16), s2_h)
    yield
    z2b = z2b - mean_row(z2b)
    yield
    invb = lax.rsqrt(mean_row(z2b * z2b) + eps_norm)
    sink(z2b * invb * gain + bias, z2b)
    yield


def forward_chain(state, z1, post, key_aug, key_next, query_aug, base, rate, gain_sq, tri, save):
    w1, w2t, b2 = state
    width = gain_sq.shape[1]
    scale = 1.0 / width
    w2_h = w2t.astype(bf16)
    act, der = gelu_first(z1)
    act_h = act.astype(bf16)
    z = dot_nt(act_h, w2_h) + b2
    next(post, None)
    fixed = dot_nn(
        jnp.concatenate([base, jnp.broadcast_to(gain_sq, (8, width)), jnp.ones((8, width), f32)], axis=0).astype(bf16),
        w2_h)
    both = jnp.concatenate([key_next, query_aug], axis=0)
    coef = dot_nt(both, key_aug)
    coef = jnp.concatenate([coef[:MINI], coef[MINI:] * tri], axis=0).astype(bf16)
    m_b = mean_row(base)
    m_sq = mean_row(gain_sq)
    w1_h = w1.astype(bf16)
    next(post, None)
    zg = z * gain_sq
    prods = dot_nn(jnp.concatenate([zg, z], axis=0).astype(bf16), w2_h)
    mz = mean_row(z)
    m_zz = mean_row(z * z)
    m_zg = mean_row(zg)
    m_zzg = mean_row(zg * z)
    m_zb = mean_row(z * base)
    zz = dot_nn(both, w1_h)
    next(post, None)
    inv = lax.rsqrt(m_zz - mz * mz + eps_norm)
    c_zg = m_zg - mz * m_sq
    c_zzg = m_zzg - mz * (m_zg + c_zg)
    c_zb = m_zb - mz * m_b
    m_g = inv * c_zg + m_b
    m_gn = inv * (inv * c_zzg + c_zb)
    rinv = rate * inv
    rinv2 = rinv * inv
    skew = rinv2 * m_gn
    shift = skew * mz - rinv * m_g
    upd = (rinv2 * prods[:MINI] - skew * prods[MINI:]) + (
        (rinv * fixed[:MINI] + shift * fixed[MINI + 8 : MINI + 9]) - (rinv2 * mz) * fixed[MINI : MINI + 1])
    s1_h = (upd * der).astype(bf16)
    zz = zz - dot_nn(coef, s1_h)
    zc = z - mz
    s2 = rinv2 * zc * gain_sq - skew * zc + (rinv * base - rinv * m_g)
    s2_h = s2.astype(bf16)
    new_w2t = w2t - dot_tn(s2_h, act_h)
    new_w1 = w1 - dot_tn(key_aug, s1_h)
    new_b2 = b2 - jnp.sum(s2, axis=0, keepdims=True)
    next(post, None)
    next(post, None)
    z1b = zz[MINI:]
    save(w1_h, w2_h, z1, upd, zc, s2, z1b)
    return (new_w1, new_w2t, new_b2), zz[:MINI], (z1b, act_h, w2_h, b2, s2_h)


def prepare_back(store, saved, d_out, key_aug, query_aug, target, rate, gain, gain_sq, bias, tri):
    w1_h, w2_h, z1, upd, zc, s2, z1b, z2b = saved
    width = gain.shape[1]
    s2_h = s2.astype(bf16)
    actb, derb = gelu_first(z1b)
    actb_h = actb.astype(bf16)
    invb = lax.rsqrt(mean_row(z2b * z2b) + eps_norm)
    dn = d_out * gain
    m_dn = mean_row(dn)
    yield
    act, der, curve = gelu_second(z1)
    act_h = act.astype(bf16)
    s1_h = (upd * der).astype(bf16)
    store.update(act=act_h, der=der, bend=upd * curve, actb=actb_h, s1=s1_h, s2=s2_h)
    yield
    att2 = dot_nt(actb_h, act_h)
    att1 = dot_nt(query_aug, key_aug)
    nb = z2b * invb
    d_z2b = invb * (dn - m_dn - nb * mean_row(dn * nb))
    d_z2b_h = d_z2b.astype(bf16)
    yield
    inv = lax.rsqrt(mean_row(zc * zc) + eps_norm)
    d_att2 = dot_nt(d_z2b_h, s2_h)
    d_actb = dot_nn(d_z2b_h, w2_h)
    base = (bias - target) * gain
    m_sq = mean_row(gain_sq)
    yield
    att2 = ((att2 + 1.0) * tri).astype(bf16)
    att1 = (att1 * tri).astype(bf16)
    n = zc * inv
    ng = n * gain_sq
    big_g = ng + base
    m_g = mean_row(big_g)
    m_gn = mean_row(big_g * n)
    yield
    d_att2 = (-d_att2 * tri).astype(bf16)
    d_actb = d_actb + dot_nn(d_att2, act_h)
    c2 = dot_tn(att2, d_z2b_h)
    m_ng = mean_row(ng)
    m_nng = mean_row(n * ng)
    yield
    c3 = dot_tn(d_att2, actb_h)
    inv2 = inv * inv
    g = inv * (big_g - m_g - n * m_gn)
    fac = rate * inv2 * (gain_sq - m_gn)
    scale = rate * (1.0 / width)
    weights = (jnp.broadcast_to(scale, n.shape), scale * n, scale * gain_sq, scale * (ng * inv2 + g * inv))
    store.update(c2=c2, c3=c3, fac=fac, weights=weights, inv=inv, inv2=inv2, n=n)
    yield
    d_z1b_h = (d_actb * derb).astype(bf16)
    c1 = dot_tn(att1, d_z1b_h)
    row1 = inv2 * (gain_sq - (m_sq + m_gn) - n * m_ng)
    row2 = inv2 * (ng + big_g - (m_ng + m_g) - n * (m_nng + 2.0 * m_gn))
    store.update(dz2b=d_z2b_h, dz2bf=d_z2b, dz1b=d_z1b_h, c1=c1, row1=row1, row2=row2)
    yield
    fixed = dot_nn(jnp.concatenate([row1, row2, jnp.broadcast_to(inv2, n.shape), n], axis=0).astype(bf16), w2_h)
    d_att1 = dot_nt(d_z1b_h, s1_h)
    d_query = dot_nt(d_z1b_h, w1_h)
    yield
    prods = tuple(fixed[i * MINI : (i + 1) * MINI] for i in range(4))
    store.update(prods=prods)
    d_att1 = (-d_att1 * tri).astype(bf16)
    d_query = (d_query + dot_nn(d_att1, key_aug))[:, :width] + d_out
    d_key = dot_tn(d_att1, query_aug)[:, :width]
    yield
    d_gain = d_out * nb
    d_bias = d_out
    store.update(dq=d_query, dk=d_key, d_gain=d_gain, d_bias=d_bias, rate=rate, w1=w1_h, w2=w2_h, s2f=s2,
                 key=key_aug, query=query_aug, gslope=2.0 * n * gain + bias - target)
    yield


PIECES = 11


def settle(post, width):
    if post is None:
        return
    pre, d_s2, a1, a2, d_z1_h, p1_h, keep, gain, sink = post
    d_g = pre["inv"] * (pre["rate"] * d_s2 - a1 - pre["n"] * a2)
    d_gg = d_g * gain
    key_part = dot_nt(d_z1_h, pre["w1"])
    late_part = dot_nt(pre["s1"], p1_h)
    d_logit = keep * jnp.sum(d_s2 * pre["s2f"], axis=1, keepdims=True)
    yield
    d_gain = pre["d_gain"] + d_g * pre["gslope"]
    d_bias = pre["d_bias"] + d_gg
    d_key = pre["dk"] + d_gg + (key_part - late_part)[:, :width]
    sink(pre["dq"], d_key, -d_gg, d_logit, d_gain, d_bias)
    yield


def drain(maker):
    for _ in maker:
        pass


def backward_chain(carry, pre, post, fill, keep, gain, sink):
    p1, p2t, p2, dz, kq, left, right, dsum = carry
    width = gain.shape[1]
    key, act, der, w2_h = pre["key"], pre["act"], pre["der"], pre["w2"]
    after = settle(post, width)
    p1_h = p1.astype(bf16)
    coef1 = dot_nt(key, kq).astype(bf16)
    base1 = pre["c1"] + dot_nn(key, p1_h)
    d_s1 = -base1 - dot_nn(coef1, dz)
    p2_h = p2t.astype(bf16)
    coef2 = dot_nt(act, right).astype(bf16)
    p2 = p2 + dsum
    base2 = pre["c2"] + p2 + dot_nt(act, p2_h)
    fill(5)
    side = base2 + dot_nn(coef2, left)
    p1 = p1 + dot_tn(kq, dz)
    p2t = p2t + dot_tn(left, right)
    next(after, None)
    fill(1)
    d_upd = d_s1 * der
    d_upd_h = d_upd.astype(bf16)
    d_s2 = dot_nt(d_upd_h, w2_h) - side
    rest = pre["c3"] - dot_nn(pre["s2"], p2t.astype(bf16))
    p1_h = p1.astype(bf16)
    bend = d_s1 * pre["bend"]
    next(after, None)
    fill(3)
    d_fac = d_s2 * pre["fac"]
    main = dot_nn(d_fac.astype(bf16), w2_h)
    a1, a2, a3, a4 = (jnp.sum(d_s2 * w, axis=1, keepdims=True) for w in pre["weights"])
    fill(2)
    y1, y2, y3, y4 = pre["prods"]
    d_act = (main + rest) - ((a1 * y1 + a2 * y2) + (a3 * y3 + a4 * y4))
    d_z1_h = (d_act * der + bend).astype(bf16)
    d_zc = d_fac - ((a1 * pre["row1"] + a2 * pre["row2"]) + (a3 * pre["inv2"] + a4 * pre["n"]))
    d_zc_h = d_zc.astype(bf16)
    carry = (p1, p2t, p2, jnp.concatenate([d_z1_h, pre["dz1b"]], axis=0),
             jnp.concatenate([key, pre["query"]], axis=0),
             jnp.concatenate([pre["s2"], d_zc_h, pre["dz2b"]], axis=0),
             jnp.concatenate([d_upd_h, act, pre["actb"]], axis=0),
             jnp.sum(d_zc + pre["dz2bf"], axis=0, keepdims=True))
    return carry, (pre, d_s2, a1, a2, d_z1_h, p1_h, keep, gain, sink)


def backward_close(carry):
    p1, p2t, p2, dz, kq, left, right, dsum = carry
    return p1 + dot_tn(kq, dz), p2t + dot_tn(left, right), p2 + dsum


MESH = pl.DeviceIdType.MESH
PACK = 256
ENDS = 160


def seq_place():
    index = lax.axis_index("seq")
    pos = lax.rem(index, CHAIN)
    return pos, index - pos


def meet_group(pos, base):
    barrier = pltpu.get_barrier_semaphore()
    for d in range(1, CHAIN):
        pl.semaphore_signal(
            barrier, inc=1, device_id={"seq": base + lax.rem(pos + d, CHAIN)}, device_id_type=MESH)
    pl.semaphore_wait(barrier, CHAIN - 1)


def push(src, dst, send_sem, recv_sem, target):
    return pltpu.make_async_remote_copy(
        src_ref=src, dst_ref=dst, send_sem=send_sem, recv_sem=recv_sem,
        device_id={"seq": target}, device_id_type=MESH)


def await_bytes(ref, sem):
    pltpu.make_async_copy(ref, ref, sem).wait()


def swap_start(src, dst, send, recv, local_sem, pos, base):
    for d in range(1, CHAIN):
        peer = lax.rem(pos + d, CHAIN)
        push(src.at[peer], dst.at[pos], send.at[d - 1], recv.at[d - 1], base + peer).start()
    pltpu.make_async_copy(src.at[pos], dst.at[pos], local_sem).start()


def swap_wait(src, dst, send, recv, local_sem, pos, base):
    for d in range(1, CHAIN):
        peer = lax.rem(pos + d, CHAIN)
        origin = lax.rem(pos + CHAIN - d, CHAIN)
        push(src.at[peer], dst.at[pos], send.at[d - 1], recv.at[d - 1], base + peer).wait_send()
        await_bytes(dst.at[origin], recv.at[d - 1])
    await_bytes(dst.at[pos], local_sem)


def fwd_kernel(block, heads, count, pay_ref, ct_ref, w1_in, b1_in, w2_in, b2_in, gain_in, bias_in,
               mixed_ref, ct_out, k_out, q_out, aux_out, w1s_ref, w2s_ref, z1s_ref, upd_ref, zc_ref, s2_ref, z1b_ref, z2b_ref,
               got, k_all, q_all, base_all, aux_all, mixed_all, w1, w2t, b2, z1,
               pay_send, pay_recv, mix_send, mix_recv, ct_send, ct_recv, ct_loc):
    blk = pl.program_id(0)
    last = pl.num_programs(0) - 1
    pos, base = seq_place()
    width = gain_in.shape[1]
    hidden = w1.shape[1]
    rows_each = pay_ref.shape[0]
    per = rows_each // block
    piece = got.shape[1]
    parts = rows_each // piece
    owner = (pos >= FIRST) & (pos < FIRST + heads)
    mine = jnp.clip(pos - FIRST, 0, heads - 1)
    gain = gain_in[pl.ds(mine, 1), :]
    bias = bias_in[pl.ds(mine, 1), :]
    gain_sq = gain * gain
    tri = tri_mask()

    me, _ = head_place()

    @pl.when(blk == 0)
    def _():
        barrier = pltpu.get_barrier_semaphore()
        for d in range(1, count):
            pl.semaphore_signal(barrier, inc=1, device_id={"head": lax.rem(me + d, count)}, device_id_type=MESH)
        for d in range(1, CHAIN):
            pl.semaphore_signal(
                barrier, inc=1, device_id={"seq": base + lax.rem(pos + d, CHAIN)}, device_id_type=MESH)
        pl.semaphore_wait(barrier, CHAIN - 1 + count - 1)
        for s in range(parts):
            for j in range(heads):
                src = pay_ref.at[s * piece : (s + 1) * piece, j * PACK : (j + 1) * PACK]
                dst = got.at[pos * parts + s]

                @pl.when(pos != FIRST + j)
                def _():
                    push(src, dst, pay_send.at[j], pay_recv.at[pos * parts + s], base + FIRST + j).start()

                @pl.when(pos == FIRST + j)
                def _():
                    pltpu.make_async_copy(src, dst, pay_recv.at[pos * parts + s]).start()

    @pl.when(blk == 1)
    def _():
        for d in range(1, count):
            push_head(ct_ref, ct_out.at[me], ct_send.at[d - 1], ct_recv.at[d - 1], lax.rem(me + d, count)).start()
        pltpu.make_async_copy(ct_ref, ct_out.at[me], ct_loc).start()

    def take_in(p):
        await_bytes(got.at[p], pay_recv.at[p])
        part = got[p]
        rows = pl.ds(pl.multiple_of(p * piece, piece), piece)
        lane = lax.broadcasted_iota(jnp.int32, (piece, AUG), 1)
        one = jnp.ones((), bf16)
        zero = jnp.zeros((), bf16)
        tail = jnp.where(lane == width, one, zero)
        query = part[:, :AUG]
        key = part[:, width : width + AUG]
        q_all[rows, :] = jnp.where(lane < width, query, tail)
        k_all[rows, :] = jnp.where(lane < width, key, tail)
        key_f = part[:, width : 2 * width].astype(f32)
        target = part[:, 2 * width : 3 * width].astype(f32) - key_f
        logit = part[:, 3 * width : 3 * width + 1].astype(f32) + part[:, 3 * width + 1 : 3 * width + 2].astype(f32)
        sig = 1.0 / (1.0 + jnp.exp(-logit))
        base_all[rows, :] = (bias - target) * gain
        spot = lax.broadcasted_iota(jnp.int32, (piece, 2 * width), 1)
        wide = jnp.concatenate([target, target], axis=1)
        aux_all[rows, :] = jnp.where(
            spot < width, wide, jnp.where(spot == width, sig * (1.0 / width), 1.0 - sig))

    def send_mixed(b):
        p = lax.div(b, per)
        src = mixed_all.at[pl.ds(pl.multiple_of(b * block, block), block), :]
        dst = mixed_ref.at[mine, pl.ds(pl.multiple_of(lax.rem(b, per) * block, block), block), :]

        @pl.when(p != pos)
        def _():
            push(src, dst, mix_send, mix_recv.at[mine], base + p).start()

        @pl.when(p == pos)
        def _():
            pltpu.make_async_copy(src, dst, mix_recv.at[mine]).start()

    @pl.when(owner)
    def _():
        @pl.when(blk == 0)
        def _():
            row = lax.broadcasted_iota(jnp.int32, (AUG - width, hidden), 0)
            w1[pl.ds(0, width), :] = w1_in[mine]
            w1[pl.ds(width, AUG - width), :] = jnp.where(row == 0, b1_in[pl.ds(mine, 1), :], 0.0)
            turned = w2_in[mine]
            w2t[...] = turned - jnp.mean(turned, axis=0, keepdims=True)
            start = b2_in[pl.ds(mine, 1), :]
            b2[...] = start - mean_row(start)
            k_all[pl.ds(CHAIN * rows_each, MINI), :] = jnp.zeros((MINI, AUG), bf16)

        @pl.when(blk > 0)
        def _():
            send_mixed(blk - 1)

        def bring(p, _):
            take_in(p)
            return 0

        lax.fori_loop(jnp.where(blk == 0, 0, 2 * blk + 1), jnp.minimum(2 * blk + 3, 2 * last + 2), bring, 0)

        @pl.when(blk == 0)
        def _():
            z1[...] = dot_nn(k_all[0:MINI, :], w1[...].astype(bf16))

        state = (w1[...], w2t[...], b2[...])
        z1_now = z1[...]
        post = iter(())
        for loc in range(block // MINI):
            row = pl.multiple_of(blk * block + loc * MINI, MINI)
            rows = pl.ds(row, MINI)
            lr = pl.ds(loc * MINI, MINI)
            q_aug = q_all[rows, :]

            def save(w1_h, w2_h, z1_v, upd, zc, s2, z1b, loc=loc, lr=lr):
                w1s_ref[loc] = w1_h
                w2s_ref[loc] = w2_h
                z1s_ref[lr, :] = z1_v
                upd_ref[lr, :] = upd
                zc_ref[lr, :] = zc
                s2_ref[lr, :] = s2
                z1b_ref[lr, :] = z1b

            state, z1_now, kept = forward_chain(
                state, z1_now, post, k_all[rows, :], k_all[pl.ds(row + MINI, MINI), :], q_aug,
                base_all[rows, :], aux_all[rows, width : width + 1], gain_sq, tri, save)

            def sink(out, z2b, lr=lr, rows=rows, q_aug=q_aug):
                z2b_ref[lr, :] = z2b
                mixed_all[rows, :] = (out + q_aug[:, :width].astype(f32)).astype(bf16)

            post = forward_output(kept, gain, bias, tri, sink)
        drain(post)
        w1[...], w2t[...], b2[...] = state
        z1[...] = z1_now

        brows = pl.ds(pl.multiple_of(blk * block, block), block)
        k_out[...] = k_all[brows, :]
        q_out[...] = q_all[brows, :]
        aux_out[...] = aux_all[brows, :]

    @pl.when(blk == last)
    def _():
        @pl.when(owner)
        def _():
            send_mixed(last)
            others = mixed_all.at[pl.ds(0, (CHAIN - 1) * rows_each), :]
            await_bytes(others, mix_send)
        for j in range(heads):
            @pl.when(pos != FIRST + j)
            def _():
                await_bytes(got.at[pl.ds(0, parts)], pay_send.at[j])

            await_bytes(mixed_ref.at[j], mix_recv.at[j])

        for d in range(1, count):
            push_head(ct_ref, ct_out.at[me], ct_send.at[d - 1], ct_recv.at[d - 1],
                      lax.rem(me + d, count)).wait_send()
            await_bytes(ct_out.at[lax.rem(me + count - d, count)], ct_recv.at[d - 1])
        await_bytes(ct_out.at[me], ct_loc)


def chain_forward(payload, ct, w1, b1, w2, b2, gain, bias, block=256):
    rows = payload.shape[0]
    heads, width, hidden = w1.shape
    count = lax.axis_size("head")
    tokens = rows * CHAIN
    steps = tokens // MINI
    nb = block // MINI
    whole = lambda a: pl.BlockSpec(a.shape, lambda i: (0,) * a.ndim)
    rowblk = lambda w: pl.BlockSpec((block, w), lambda i: (i, 0))
    stepblk = lambda r: pl.BlockSpec((nb, r, hidden), lambda i: (i, 0, 0))
    anywhere = pl.BlockSpec(memory_space=pl.ANY)
    small = (w1, b1, w2, b2, gain, bias)
    dma = pltpu.SemaphoreType.DMA
    wide = jax.ShapeDtypeStruct((tokens, hidden), f32)
    narrow = jax.ShapeDtypeStruct((tokens, width), f32)
    return pl.pallas_call(
        functools.partial(fwd_kernel, block, heads, count),
        grid=(tokens // block,),
        in_specs=[anywhere, anywhere] + [whole(a) for a in small],
        out_specs=[anywhere, anywhere, rowblk(AUG), rowblk(AUG), rowblk(2 * width), stepblk(AUG), stepblk(width),
                   rowblk(hidden), rowblk(hidden), rowblk(width), rowblk(width), rowblk(hidden), rowblk(width)],
        out_shape=[jax.ShapeDtypeStruct((heads, rows, width), bf16),
                   jax.ShapeDtypeStruct((count,) + ct.shape, bf16),
                   jax.ShapeDtypeStruct((tokens, AUG), bf16),
                   jax.ShapeDtypeStruct((tokens, AUG), bf16),
                   jax.ShapeDtypeStruct((tokens, 2 * width), f32),
                   jax.ShapeDtypeStruct((steps, AUG, hidden), bf16),
                   jax.ShapeDtypeStruct((steps, width, hidden), bf16),
                   wide, wide, narrow, narrow, wide, narrow],
        scratch_shapes=[pltpu.VMEM((2 * tokens // block, block // 2, PACK), bf16),
                        pltpu.VMEM((tokens + MINI, AUG), bf16), pltpu.VMEM((tokens, AUG), bf16),
                        pltpu.VMEM((tokens, width), f32), pltpu.VMEM((tokens, 2 * width), f32),
                        pltpu.VMEM((tokens, width), bf16),
                        pltpu.VMEM((AUG, hidden), f32), pltpu.VMEM((width, hidden), f32),
                        pltpu.VMEM((1, width), f32), pltpu.VMEM((MINI, hidden), f32),
                        dma((heads,)), dma((2 * tokens // block,)), dma, dma((heads,)),
                        dma((count - 1,)), dma((count - 1,)), dma],
        compiler_params=pltpu.CompilerParams(collective_id=0, has_side_effects=True),
        name="inner_forward",
    )(payload, ct, *small)


def bwd_kernel(block, heads, turn, gm_ref, early_ref, small_ref, gain_in, bias_in, norm_ref, norm_last_ref,
               k_ref, q_ref, aux_ref, w1s_ref, w2s_ref, z1s_ref, upd_ref, zc_ref, s2_ref, z1b_ref, z2b_ref,
               grads_ref, ends_ref, late_ref, early_out, small_out,
               dout, half_got, half_mine, quarter, quarter_got, packed, ends, weights, late,
               p1, p2t, p2, dz, kq, left, right, dsum, dg, db, dl,
               gm_send, gm_recv, ha_send, ha_recv, ha_loc, qu_send, qu_recv, sm_send, sm_recv, sm_loc, bc_send, bc_recv, en_send, en_recv, la_send, la_recv):
    pid = pl.program_id(0)
    last = pl.num_programs(0) - 1
    blk = last - pid
    pos, base = seq_place()
    width = gain_in.shape[1]
    rows_each = gm_ref.shape[1]
    per = rows_each // block
    owner = (pos >= FIRST) & (pos < FIRST + heads)
    mine = jnp.clip(pos - FIRST, 0, heads - 1)
    gain = gain_in[pl.ds(mine, 1), :]
    bias = bias_in[pl.ds(mine, 1), :]
    gain_sq = gain * gain
    tri = tri_mask()
    count = block // MINI
    side = lax.rem(pos, 2)
    rank = lax.div(pos, 2)
    partner = pos + 1 - 2 * side
    state = (p1, p2t, p2, dz, kq, left, right, dsum)

    @pl.when(pid == 0)
    def _():
        meet_group(pos, base)
        for j in range(heads):
            @pl.when(pos != FIRST + j)
            def _():
                push(gm_ref.at[j], dout.at[pos], gm_send.at[j], gm_recv.at[pos], base + FIRST + j).start()

            @pl.when(pos == FIRST + j)
            def _():
                pltpu.make_async_copy(gm_ref.at[j], dout.at[pos], gm_recv.at[pos]).start()

        for d in range(1, CHAIN):
            push(small_ref, small_out.at[pos], sm_send.at[d - 1], sm_recv.at[d - 1],
                 base + lax.rem(pos + d, CHAIN)).start()
        pltpu.make_async_copy(small_ref, small_out.at[pos], sm_loc).start()
        push(early_ref.at[:, 1 - side], half_got, ha_send, ha_recv, base + partner).start()
        pltpu.make_async_copy(early_ref.at[:, side], half_mine, ha_loc).start()

    @pl.when(pid == turn)
    def _():
        push(early_ref.at[:, 1 - side], half_got, ha_send, ha_recv, base + partner).wait()
        await_bytes(half_mine, ha_loc)

        def pair_up(c, _):
            rows = pl.ds(pl.multiple_of(c * MINI, MINI), MINI)
            for r in range(CHAIN // 2):
                quarter[r, rows, :] = (half_mine[r, rows, :].astype(f32) + half_got[r, rows, :].astype(f32)).astype(bf16)
            return 0

        lax.fori_loop(0, half_mine.shape[1] // MINI, pair_up, 0)
        for d in range(1, CHAIN // 2):
            other = lax.rem(rank + d, CHAIN // 2)
            push(quarter.at[other], quarter_got.at[d - 1], qu_send.at[d - 1], qu_recv.at[d - 1],
                 base + 2 * other + side).start()

    def share_block(b):
        p = lax.div(b, per)
        src = packed.at[pl.ds(pl.multiple_of(b * block, block), block), :]
        dst = grads_ref.at[mine, pl.ds(pl.multiple_of(lax.rem(b, per) * block, block), block), :]

        @pl.when(p != pos)
        def _():
            push(src, dst, bc_send, bc_recv.at[mine], base + p).start()

        @pl.when(p == pos)
        def _():
            pltpu.make_async_copy(src, dst, bc_recv.at[mine]).start()

    share = late.shape[1]

    def weigh(norm, b, lo, hi):
        rows = pl.ds(pl.multiple_of(b * block, block), block)
        weights[lo:hi, :] += dot_tn(norm[:, lo:hi], packed[rows, :])

    slabs = [(i * 128, i * 128 + 128) for i in range(norm_ref.shape[1] // 128)]

    @pl.when(owner)
    def _():
        @pl.when(pid == 0)
        def _():
            for r in state + (dg, db, dl, weights):
                r[...] = jnp.zeros_like(r)
            packed[pl.ds(0, block), :] = jnp.zeros((block, PACK), bf16)

        @pl.when(lax.rem(pid, per) == 0)
        def _():
            p = lax.div(blk, per)
            await_bytes(dout.at[p], gm_recv.at[p])

        @pl.when(pid > 0)
        def _():
            share_block(blk + 1)

        carry = tuple(r[...] for r in state)
        totals = [dg[...], db[...], dl[...]]
        made = {}

        def start(loc):
            made[loc] = {}
            lr = pl.ds(loc * MINI, MINI)
            inner = pl.ds(pl.multiple_of(lax.rem(blk, per) * block + loc * MINI, MINI), MINI)
            saved = (w1s_ref[loc], w2s_ref[loc], z1s_ref[lr, :], upd_ref[lr, :], zc_ref[lr, :], s2_ref[lr, :],
                     z1b_ref[lr, :], z2b_ref[lr, :])
            return prepare_back(made[loc], saved, dout[lax.div(blk, per), inner, :].astype(f32), k_ref[lr, :],
                                q_ref[lr, :], aux_ref[lr, 0:width], aux_ref[lr, width : width + 1],
                                gain, gain_sq, bias, tri)

        drain(start(count - 1))
        post = None
        for loc in range(count - 1, -1, -1):
            ahead = start(loc - 1) if loc > 0 else iter(())

            def fill(pieces, ahead=ahead):
                for _ in range(pieces):
                    next(ahead, None)

            def sink(d_query, d_key, d_value, d_logit, d_gain, d_bias, loc=loc):
                totals[0] = totals[0] + d_gain
                totals[1] = totals[1] + d_bias
                totals[2] = totals[2] + d_logit
                high = d_logit.astype(bf16).astype(f32)
                lane = lax.broadcasted_iota(jnp.int32, (MINI, width), 1)
                extra = jnp.where(lane == 0, high, jnp.where(lane == 1, d_logit - high, 0.0))
                rows = pl.ds(pl.multiple_of(blk * block + loc * MINI, MINI), MINI)
                packed[rows, :] = jnp.concatenate([d_query, d_key, d_value, extra], axis=1).astype(bf16)

            if (count - 1 - loc) % 2 == 0 and (count - 1 - loc) // 2 < len(slabs):
                weigh(norm_ref, jnp.where(pid == 0, 0, blk + 1), *slabs[(count - 1 - loc) // 2])
            carry, post = backward_chain(
                carry, made.pop(loc), post, fill, aux_ref[pl.ds(loc * MINI, MINI), width + 1 : width + 2], gain, sink)
        drain(settle(post, width))
        for r, v in zip(state, carry):
            r[...] = v
        dg[...], db[...], dl[...] = totals

        @pl.when(pid == last)
        def _():
            end_one, end_two, end_b_two = backward_close(tuple(r[...] for r in state))
            ends[pl.ds(0, AUG), :] = end_one.astype(bf16)
            ends[pl.ds(AUG, width), :] = end_two.astype(bf16)
            rest = ENDS - AUG - width
            row = lax.broadcasted_iota(jnp.int32, (rest, width), 0)
            sums = [jnp.sum(r[...], axis=0, keepdims=True) for r in (dg, db, dl)]
            tailing = jnp.where(row == 0, end_b_two, jnp.where(row == 1, sums[0], jnp.where(row == 2, sums[1], 0.0)))
            high = sums[2].astype(bf16).astype(f32)
            tailing = tailing + jnp.where(row == 3, high, jnp.where(row == 4, sums[2] - high, 0.0))
            ends[pl.ds(AUG + width, rest), :] = jnp.concatenate([tailing] * 4, axis=1).astype(bf16)
            share_block(0)
            for slab in slabs:
                weigh(norm_last_ref, 0, *slab)
            for p in range(CHAIN):
                late[p] = weights[p * share : (p + 1) * share, :].astype(bf16)
            for d in range(1, CHAIN):
                peer = lax.rem(pos + d, CHAIN)
                push(late.at[peer], late_ref.at[mine], la_send.at[d - 1], la_recv.at[mine], base + peer).start()
            pltpu.make_async_copy(late.at[pos], late_ref.at[mine], la_recv.at[mine]).start()
            for d in range(1, CHAIN):
                push(ends, ends_ref.at[mine], en_send.at[d - 1], en_recv.at[mine],
                     base + lax.rem(pos + d, CHAIN)).start()
            pltpu.make_async_copy(ends, ends_ref.at[mine], en_recv.at[mine]).start()

    @pl.when(pid == last)
    def _():
        for d in range(1, CHAIN // 2):
            other = lax.rem(rank + d, CHAIN // 2)
            push(quarter.at[other], quarter_got.at[d - 1], qu_send.at[d - 1], qu_recv.at[d - 1],
                 base + 2 * other + side).wait()
        for d in range(1, CHAIN):
            push(small_ref, small_out.at[pos], sm_send.at[d - 1], sm_recv.at[d - 1],
                 base + lax.rem(pos + d, CHAIN)).wait_send()
            await_bytes(small_out.at[lax.rem(pos + CHAIN - d, CHAIN)], sm_recv.at[d - 1])
        await_bytes(small_out.at[pos], sm_loc)

        def add_up(c, _):
            rows = pl.ds(pl.multiple_of(c * MINI, MINI), MINI)
            acc = quarter[rank, rows, :].astype(f32)
            for d in range(1, CHAIN // 2):
                acc = acc + quarter_got[d - 1, rows, :].astype(f32)
            early_out[rows, :] = acc
            return 0

        lax.fori_loop(0, early_out.shape[0] // MINI, add_up, 0)
        for j in range(heads):
            @pl.when(pos != FIRST + j)
            def _():
                await_bytes(dout.at[pos], gm_send.at[j])

            await_bytes(grads_ref.at[j], bc_recv.at[j])
            await_bytes(ends_ref.at[j], en_recv.at[j])
            await_bytes(late_ref.at[j], la_recv.at[j])

        @pl.when(owner)
        def _():
            await_bytes(packed.at[pl.ds(0, (CHAIN - 1) * rows_each), :], bc_send)
            for d in range(1, CHAIN):
                await_bytes(ends, en_send.at[d - 1])
                await_bytes(late.at[0], la_send.at[d - 1])


def chain_backward(grad_mixed, early, small, gain, bias, normed, saved, block=256, turn=3):
    heads, rows, width = grad_mixed.shape
    tokens = rows * CHAIN
    hidden = saved[5].shape[1]
    nblk = tokens // block
    nb = block // MINI
    whole = lambda a: pl.BlockSpec(a.shape, lambda i: (0,) * a.ndim)
    rowblk = lambda w: pl.BlockSpec((block, w), lambda i: (nblk - 1 - i, 0))
    stepblk = lambda r: pl.BlockSpec((nb, r, hidden), lambda i: (nblk - 1 - i, 0, 0))
    behind = pl.BlockSpec((block, normed.shape[1]), lambda i: (jnp.minimum(nblk - i, nblk - 1), 0))
    first = pl.BlockSpec((block, normed.shape[1]), lambda i: (0, 0))
    anywhere = pl.BlockSpec(memory_space=pl.ANY)
    dma = pltpu.SemaphoreType.DMA
    seven = dma((CHAIN - 1,))
    share = early.shape[2:]
    three = dma((CHAIN // 2 - 1,))
    return pl.pallas_call(
        functools.partial(bwd_kernel, block, heads, turn),
        grid=(nblk,),
        in_specs=[anywhere] * 3 + [whole(gain), whole(bias), behind, first, rowblk(AUG), rowblk(AUG),
                                   rowblk(2 * width), stepblk(AUG), stepblk(width), rowblk(hidden), rowblk(hidden), rowblk(width),
                                   rowblk(width), rowblk(hidden), rowblk(width)],
        out_specs=[anywhere, anywhere, anywhere, pl.BlockSpec(share, lambda i: (0, 0)), anywhere],
        out_shape=[jax.ShapeDtypeStruct((heads, rows, PACK), bf16),
                   jax.ShapeDtypeStruct((heads, ENDS, hidden), bf16),
                   jax.ShapeDtypeStruct((heads, share[0], PACK), bf16),
                   jax.ShapeDtypeStruct(share, f32),
                   jax.ShapeDtypeStruct((CHAIN,) + small.shape, f32)],
        scratch_shapes=[pltpu.VMEM((CHAIN, rows, width), bf16), pltpu.VMEM((CHAIN // 2,) + share, bf16),
                        pltpu.VMEM((CHAIN // 2,) + share, bf16), pltpu.VMEM((CHAIN // 2,) + share, bf16),
                        pltpu.VMEM((CHAIN // 2 - 1,) + share, bf16),
                        pltpu.VMEM((tokens, PACK), bf16), pltpu.VMEM((ENDS, hidden), bf16),
                        pltpu.VMEM((CHAIN * share[0], PACK), f32), pltpu.VMEM((CHAIN, share[0], PACK), bf16),
                        pltpu.VMEM((AUG, hidden), f32), pltpu.VMEM((width, hidden), f32), pltpu.VMEM((1, width), f32),
                        pltpu.VMEM((2 * MINI, hidden), bf16), pltpu.VMEM((2 * MINI, AUG), bf16),
                        pltpu.VMEM((3 * MINI, width), bf16), pltpu.VMEM((3 * MINI, hidden), bf16),
                        pltpu.VMEM((1, width), f32), pltpu.VMEM((MINI, width), f32), pltpu.VMEM((MINI, width), f32),
                        pltpu.VMEM((MINI, 1), f32),
                        dma((heads,)), dma((CHAIN,)), dma, dma, dma, three, three, seven, seven, dma,
                        dma, dma((heads,)), seven, dma((heads,)), seven, dma((heads,))],
        compiler_params=pltpu.CompilerParams(collective_id=1, has_side_effects=True),
        name="inner_backward",
    )(grad_mixed, early, small, gain, bias, normed, normed, *saved)


def head_place():
    return lax.axis_index("head"), lax.axis_size("head")


def meet_heads(me, count):
    barrier = pltpu.get_barrier_semaphore()
    for d in range(1, count):
        pl.semaphore_signal(barrier, inc=1, device_id={"head": lax.rem(me + d, count)}, device_id_type=MESH)
    pl.semaphore_wait(barrier, count - 1)


def push_head(src, dst, send_sem, recv_sem, target):
    return pltpu.make_async_remote_copy(
        src_ref=src, dst_ref=dst, send_sem=send_sem, recv_sem=recv_sem,
        device_id={"head": target}, device_id_type=MESH)


def row_totals(first, second):
    ones = jnp.ones((8, first.shape[1]), f32)

    def total(x):
        return lax.dot_general(ones, x, (((1,), (1,)), ((), ())), precision=lax.Precision.HIGHEST,
                               preferred_element_type=f32)

    top, low = total(first), total(second)
    row = lax.broadcasted_iota(jnp.int32, top.shape, 0)
    return jnp.where(row == 0, top, low)


def mid_kernel(count, mixed_ref, x_ref, ctt_ref, mix_gate_ref, normed_ref, w_out_ref, w_gate_ref, w_up_ref, w_down_ref,
               post_gain_ref, post_bias_ref, ffn_gain_ref,
               gm_ref, early_ref, ggp_ref, out_ref, rco_ref, grc_ref, small_ref, norm_out,
               st_mine, st_got, pa_mine, pa_got, nt_all, rc_mine, rc_all, gn_mine, gn_got, dn_mine, dn_got, gov_all,
               gc_mine, gc_all, sb_mine, sb_got, gt_all, ct_ref, gh, gated, hidden, ggv, guv, resid,
               st_s, st_r, pa_s, pa_r, nt_s, nt_r, rc_s, rc_r, gn_s, gn_r, dn_s, dn_r, go_s, go_r, gc_s, gc_r, sb_s, sb_r,
               gt_s, gt_r, no_s, no_r):
    me, _ = head_place()
    heads, rows, width = mixed_ref.shape
    cols = heads * width
    full = cols * count
    part = rows // count
    peers = [(d, lax.rem(me + d, count)) for d in range(1, count)]
    pos, base = seq_place()
    owner = (pos >= FIRST) & (pos < FIRST + heads)
    barrier = pltpu.get_barrier_semaphore()
    for d in range(1, count):
        pl.semaphore_signal(barrier, inc=1, device_id={"head": lax.rem(me + d, count)}, device_id_type=MESH)
    for d in range(1, CHAIN):
        pl.semaphore_signal(
            barrier, inc=1, device_id={"seq": base + lax.rem(pos + d, CHAIN)}, device_id_type=MESH)
    pl.semaphore_wait(barrier, CHAIN - 1 + count - 1)
    ffn_gain = ffn_gain_ref[...][None, :]
    post_gain = post_gain_ref[...][None, :]
    post_bias = post_bias_ref[...][None, :]

    def rows_of(device):
        return pl.ds(pl.multiple_of(device * part, part), part)

    def send_all(src, dst, send, recv):
        for d, peer in peers:
            push_head(src, dst.at[d - 1], send.at[d - 1], recv.at[d - 1], peer).start()

    def wait_all(src, dst, send, recv):
        for d, peer in peers:
            push_head(src, dst.at[d - 1], send.at[d - 1], recv.at[d - 1], peer).wait()

    z = jnp.concatenate([mixed_ref[j] for j in range(heads)], axis=1).astype(f32)
    st_mine[...] = row_totals(z, z * z)
    send_all(st_mine, st_got, st_s, st_r)
    for j in range(heads):
        @pl.when(pos != FIRST + j)
        def _():
            push(normed_ref, norm_out.at[pos], no_s.at[j], no_r.at[pos], base + FIRST + j).start()

        @pl.when(pos == FIRST + j)
        def _():
            pltpu.make_async_copy(normed_ref, norm_out.at[pos], no_r.at[pos]).start()

    ct_ref[...] = ctt_ref[...].T
    gate_act, gate_der = gelu_first(dot_nt(normed_ref[...], mix_gate_ref[...]))
    gh[...] = dot_nt(ct_ref[...], w_down_ref[...])
    wait_all(st_mine, st_got, st_s, st_r)
    tot = st_mine[...]
    for d, _ in peers:
        tot = tot + st_got[d - 1]
    tot = tot.T * (1.0 / full)
    mean_z = tot[:, 0:1]
    inv_z = lax.rsqrt(tot[:, 1:2] - mean_z * mean_z + eps_norm)
    z_hat = (z - mean_z) * inv_z
    post_out = z_hat * post_gain + post_bias
    gated[...] = (post_out * gate_act).astype(bf16)

    def spread_rows(make, mine, got, send, recv):
        pending = None
        for d, peer in peers:
            mine[d - 1] = make(rows_of(peer)).astype(bf16)
            if pending is not None:
                pending.start()
            pending = push_head(mine.at[d - 1], got.at[d - 1], send.at[d - 1], recv.at[d - 1], peer)
        own = make(rows_of(me))
        pending.start()
        return own

    def add_rows(own, mine, got, send, recv):
        for d, peer in peers:
            push_head(mine.at[d - 1], got.at[d - 1], send.at[d - 1], recv.at[d - 1], peer).wait()
            own = own + got[d - 1].astype(f32)
        return own

    def gather_rows(all_ref, send, recv):
        for d, peer in peers:
            view = all_ref.at[rows_of(me), :]
            push_head(view, view, send.at[d - 1], recv.at[d - 1], peer).start()

    def gather_wait(all_ref, send, recv):
        for d, peer in peers:
            view = all_ref.at[rows_of(me), :]
            push_head(view, view, send.at[d - 1], recv.at[d - 1], peer).wait_send()
            await_bytes(all_ref.at[rows_of(lax.rem(me + count - d, count)), :], recv.at[d - 1])

    def turn_columns(value, mine, all_ref, send, recv):
        for b in range(count):
            mine[b] = value[:, b * cols : (b + 1) * cols]
        all_ref[rows_of(me), :] = mine[me]

    def turn_start(mine, all_ref, send, recv):
        for d, peer in peers:
            push_head(mine.at[peer], all_ref.at[rows_of(me), :], send.at[d - 1], recv.at[d - 1], peer).start()

    def turn_wait(mine, all_ref, send, recv):
        for d, peer in peers:
            push_head(mine.at[peer], all_ref.at[rows_of(me), :], send.at[d - 1], recv.at[d - 1], peer).wait_send()
            await_bytes(all_ref.at[rows_of(lax.rem(me + count - d, count)), :], recv.at[d - 1])

    w_out = w_out_ref[...]
    own = spread_rows(lambda r: dot_nn(gated[r, :], w_out), pa_mine, pa_got, pa_s, pa_r)
    res = x_ref[rows_of(me), :].astype(f32) + add_rows(own, pa_mine, pa_got, pa_s, pa_r)
    rms_two = lax.rsqrt(mean_row(res * res) + eps_norm)
    nt_all[rows_of(me), :] = (res * rms_two * ffn_gain).astype(bf16)
    turn_columns(res, rc_mine, rc_all, rc_s, rc_r)
    resid[...] = res
    gather_rows(nt_all, nt_s, nt_r)
    turn_start(rc_mine, rc_all, rc_s, rc_r)
    gather_wait(nt_all, nt_s, nt_r)
    def forward_rows(b, _):
        r = pl.ds(pl.multiple_of(b * part, part), part)
        nt = nt_all[r, :]
        gate_val = dot_nn(nt, w_gate_ref[...])
        up_val = dot_nn(nt, w_up_ref[...])
        sig = 1.0 / (1.0 + jnp.exp(-gate_val))
        silu = gate_val * sig
        hidden[r, :] = (silu * up_val).astype(bf16)
        g = gh[r, :]
        ggv[r, :] = (g * up_val * sig * (1.0 + gate_val * (1.0 - sig))).astype(bf16)
        guv[r, :] = (g * silu).astype(bf16)
        return 0

    lax.fori_loop(0, count, forward_rows, 0)
    own = spread_rows(lambda r: dot_nt(ggv[r, :], w_gate_ref[...]) + dot_nt(guv[r, :], w_up_ref[...]),
                      gn_mine, gn_got, gn_s, gn_r)
    for b in range(count):
        r = pl.ds(b * part, part)
        down = dot_nn(hidden[r, :], w_down_ref[...]).astype(bf16)
        for c in range(count):
            dn_mine[c, r, :] = down[:, c * cols : (c + 1) * cols]
    ffn = w_gate_ref.shape[1]
    half = full // 2
    for b in range(2):
        r = slice(b * half, (b + 1) * half)
        early_ref[r, 0:ffn] = dot_tn(nt_all[:, r], ggv[...]).astype(bf16)
    for d, peer in peers:
        push_head(dn_mine.at[peer], dn_got.at[d - 1], dn_s.at[d - 1], dn_r.at[d - 1], peer).start()
    gnt = add_rows(own, gn_mine, gn_got, gn_s, gn_r)
    res = resid[...]
    rms_two = lax.rsqrt(mean_row(res * res) + eps_norm)
    scaled = gnt * ffn_gain
    grad_res = ct_ref[rows_of(me), :].astype(f32) + rms_two * (
        scaled - res * rms_two * rms_two * mean_row(scaled * res))
    gov_all[rows_of(me), :] = grad_res.astype(bf16)
    gt_all[me] = jnp.broadcast_to(jnp.sum(gnt * res * rms_two, axis=0, keepdims=True), gt_all.shape[1:])
    turn_columns(grad_res, gc_mine, gc_all, gc_s, gc_r)
    gather_rows(gov_all, go_s, go_r)
    turn_start(gc_mine, gc_all, gc_s, gc_r)
    for d, peer in peers:
        push_head(gt_all.at[me], gt_all.at[me], gt_s.at[d - 1], gt_r.at[d - 1], peer).start()
    for b in range(2):
        r = slice(b * half, (b + 1) * half)
        early_ref[r, ffn : 2 * ffn] = dot_tn(nt_all[:, r], guv[...]).astype(bf16)
    gather_wait(gov_all, go_s, go_r)
    gov = gov_all[...]
    grad_gated = dot_nt(gov, w_out_ref[...])
    grad_post = grad_gated * gate_act
    grad_zhat = grad_post * post_gain
    sb_mine[...] = row_totals(grad_zhat, grad_zhat * z_hat)
    ggp = (grad_gated * post_out * gate_der).astype(bf16)
    ggp_ref[...] = ggp
    send_all(sb_mine, sb_got, sb_s, sb_r)
    early_ref[:, 3 * ffn : 3 * ffn + 2 * cols] = jnp.concatenate(
        [dot_tn(normed_ref[...], ggp).astype(bf16), dot_tn(gov, gated[...]).astype(bf16)], axis=1)
    row = lax.broadcasted_iota(jnp.int32, (8, cols), 0)
    wait_all(sb_mine, sb_got, sb_s, sb_r)
    tot = sb_mine[...]
    for d, _ in peers:
        tot = tot + sb_got[d - 1]
    tot = tot.T * (1.0 / full)
    grad_mixed = (inv_z * (grad_zhat - tot[:, 0:1] - z_hat * tot[:, 1:2])).astype(bf16)
    for j in range(heads):
        gm_ref[j] = grad_mixed[:, j * width : (j + 1) * width]
    for b in range(2):
        r = slice(b * half, (b + 1) * half)
        early_ref[r, 2 * ffn : 3 * ffn] = dot_nn(ctt_ref[r, :], hidden[...]).astype(bf16)
    turn_wait(rc_mine, rc_all, rc_s, rc_r)
    rco_ref[...] = rc_all[...]
    out = dn_mine[me].astype(f32)
    for d, peer in peers:
        push_head(dn_mine.at[peer], dn_got.at[d - 1], dn_s.at[d - 1], dn_r.at[d - 1], peer).wait()
        out = out + dn_got[d - 1].astype(f32)
    out_ref[...] = out
    turn_wait(gc_mine, gc_all, gc_s, gc_r)
    grc_ref[...] = gc_all[...]
    for d, peer in peers:
        push_head(gt_all.at[me], gt_all.at[me], gt_s.at[d - 1], gt_r.at[d - 1], peer).wait_send()
        await_bytes(gt_all.at[lax.rem(me + count - d, count)], gt_r.at[d - 1])
    gain_two = gt_all[0]
    for b in range(1, count):
        gain_two = gain_two + gt_all[b]
    post = jnp.where(row == 1, jnp.sum(grad_post * z_hat, axis=0, keepdims=True),
                     jnp.sum(grad_post, axis=0, keepdims=True))
    line = lax.broadcasted_iota(jnp.int32, (8, full), 0)
    small_ref[...] = jnp.where(
        line == 0, gain_two, jnp.concatenate([post] + [jnp.zeros_like(post)] * (count - 1), axis=1))
    for j in range(heads):
        @pl.when(pos != FIRST + j)
        def _():
            await_bytes(normed_ref, no_s.at[j])

    @pl.when(owner)
    def _():
        for p in range(CHAIN):
            await_bytes(norm_out.at[p], no_r.at[p])


def middle(mixed, x, ct, mix_gate, normed, w_out, w_gate, w_up, w_down, post_gain, post_bias, ffn_gain):
    count = lax.axis_size("head")
    heads, rows, width = mixed.shape
    cols = heads * width
    full = cols * count
    part = rows // count
    ffn = w_gate.shape[1]
    ins = (mixed, x, ct, mix_gate, normed, w_out, w_gate, w_up, w_down, post_gain, post_bias, ffn_gain)
    vmem = pl.BlockSpec(memory_space=pltpu.VMEM)
    V = pltpu.VMEM
    trio = count - 1
    sem = pltpu.SemaphoreType.DMA((trio,))
    return pl.pallas_call(
        functools.partial(mid_kernel, count),
        in_specs=[vmem] * len(ins),
        out_specs=[vmem] * 7 + [pl.BlockSpec(memory_space=pl.ANY)],
        out_shape=[jax.ShapeDtypeStruct((heads, rows, width), bf16),
                   jax.ShapeDtypeStruct((full, 3 * ffn + 2 * cols), bf16),
                   jax.ShapeDtypeStruct((rows, cols), bf16),
                   jax.ShapeDtypeStruct((rows, cols), f32),
                   jax.ShapeDtypeStruct((rows, cols), f32),
                   jax.ShapeDtypeStruct((rows, cols), f32),
                   jax.ShapeDtypeStruct((8, full), f32),
                   jax.ShapeDtypeStruct((CHAIN, rows, full), bf16)],
        scratch_shapes=[
            V((8, rows), f32), V((trio, 8, rows), f32),
            V((trio, part, full), bf16), V((trio, part, full), bf16),
            V((rows, full), bf16),
            V((count, part, cols), f32), V((rows, cols), f32),
            V((trio, part, full), bf16), V((trio, part, full), bf16),
            V((count, rows, cols), bf16), V((trio, rows, cols), bf16),
            V((rows, full), bf16),
            V((count, part, cols), f32), V((rows, cols), f32),
            V((8, rows), f32), V((trio, 8, rows), f32),
            V((count, 8, full), f32),
            V((rows, full), bf16), V((rows, ffn), f32), V((rows, cols), bf16),
            V((rows, ffn), bf16), V((rows, ffn), bf16), V((rows, ffn), bf16),
            V((part, full), f32)] + [sem] * 20 + [
            pltpu.SemaphoreType.DMA((heads,)), pltpu.SemaphoreType.DMA((CHAIN,))],
        compiler_params=pltpu.CompilerParams(
            collective_id=2, has_side_effects=True, vmem_limit_bytes=56 * 1024 * 1024),
        name="middle",
    )(*ins)


def front_kernel(count, in_ref, gain_ref, bias_ref, wq_ref, wk_ref, wv_ref, wr_ref, x_ref, normed_ref, pay_ref, gathered, send, recv):
    me, _ = head_place()
    cols, rows = in_ref.shape
    heads = wr_ref.shape[0]
    width = cols // heads
    part = rows // count
    meet_heads(me, count)
    here = pl.ds(pl.multiple_of(me * cols, cols), cols)
    for d in range(1, count):
        push_head(in_ref, gathered.at[here, :], send.at[d - 1], recv.at[d - 1], lax.rem(me + d, count)).start()
    gathered[here, :] = in_ref[...]
    for d in range(1, count):
        push_head(in_ref, gathered.at[here, :], send.at[d - 1], recv.at[d - 1], lax.rem(me + d, count)).wait_send()
        origin = lax.rem(me + count - d, count)
        await_bytes(gathered.at[pl.ds(pl.multiple_of(origin * cols, cols), cols), :], recv.at[d - 1])
    gain = gain_ref[...][None, :]
    rate_bias = bias_ref[...][None, :]
    x_ref[...] = gathered[...].T

    def project(b, _):
        r = pl.ds(pl.multiple_of(b * part, part), part)
        x = x_ref[r, :].astype(f32)
        nt = (x * lax.rsqrt(mean_row(x * x) + eps_norm) * gain).astype(bf16)
        normed_ref[r, :] = nt
        query = dot_nt(nt, wq_ref[...]).astype(bf16)
        key = dot_nt(nt, wk_ref[...]).astype(bf16)
        value = dot_nt(nt, wv_ref[...]).astype(bf16)
        logit = dot_nt(nt, wr_ref[...]) + rate_bias
        high = logit.astype(bf16)
        low = (logit - high.astype(f32)).astype(bf16)
        lane = lax.broadcasted_iota(jnp.int32, (part, width), 1)
        for j in range(heads):
            own = slice(j * width, (j + 1) * width)
            extra = jnp.where(lane == 0, high[:, j : j + 1].astype(f32),
                              jnp.where(lane == 1, low[:, j : j + 1].astype(f32), 0.0)).astype(bf16)
            pay_ref[r, j * PACK : (j + 1) * PACK] = jnp.concatenate(
                [query[:, own], key[:, own], value[:, own], extra], axis=1)
        return 0

    lax.fori_loop(0, count, project, 0)


def front(inputs_t, pre_gain, rate_bias, wq, wk, wv, wr):
    count = lax.axis_size("head")
    cols, rows = inputs_t.shape
    heads = wr.shape[0]
    vmem = pl.BlockSpec(memory_space=pltpu.VMEM)
    sem = pltpu.SemaphoreType.DMA((count - 1,))
    wide = jax.ShapeDtypeStruct((rows, cols * count), bf16)
    return pl.pallas_call(
        functools.partial(front_kernel, count),
        in_specs=[vmem] * 7,
        out_specs=[vmem] * 3,
        out_shape=[wide, wide, jax.ShapeDtypeStruct((rows, heads * PACK), bf16)],
        scratch_shapes=[pltpu.VMEM((cols * count, rows), bf16), sem, sem],
        compiler_params=pltpu.CompilerParams(collective_id=4, has_side_effects=True),
        name="front",
    )(inputs_t, pre_gain, rate_bias, wq, wk, wv, wr)


def tail_kernel(count, at_mix, grads_ref, wq_ref, wk_ref, wv_ref, wr_ref, mix_gate_ref, ggp_ref, x_ref, gain_ref,
                late_ref, early_ref,
                back_ref, tiles_ref,
                mine, got, tile, tile_got, wcols, ib_s, ib_r, th_s, th_r, ts_s, ts_r, ts_loc):
    me, _ = head_place()
    pos, base = seq_place()
    heads = grads_ref.shape[0]
    rows = x_ref.shape[0]
    cols = ggp_ref.shape[1]
    full = x_ref.shape[1]
    share = early_ref.shape[0]
    rate_lane = PACK - PACK // 4
    peers = [(d, lax.rem(me + d, count)) for d in range(1, count)]
    barrier = pltpu.get_barrier_semaphore()
    for d, peer in peers:
        pl.semaphore_signal(barrier, inc=1, device_id={"head": peer}, device_id_type=MESH)
    for d in range(1, CHAIN):
        pl.semaphore_signal(
            barrier, inc=1, device_id={"seq": base + lax.rem(pos + d, CHAIN)}, device_id_type=MESH)
    part = rows // count
    width = PACK // 4
    pre_gain = gain_ref[...][None, :]
    sides = (wq_ref, wk_ref, wv_ref)

    def back_rows(b, _):
        r = pl.ds(pl.multiple_of(b * part, part), part)
        grad = dot_nn(ggp_ref[r, :], mix_gate_ref[...])
        blocks = [grads_ref[j, r, :] for j in range(heads)]
        for i, side in enumerate(sides):
            joined = jnp.concatenate([b[:, i * width : (i + 1) * width] for b in blocks], axis=1)
            grad = grad + dot_nn(joined, side[...])
        for j in range(heads):
            rate = blocks[j][:, rate_lane : rate_lane + 1].astype(f32) + blocks[j][
                :, rate_lane + 1 : rate_lane + 2].astype(f32)
            grad = grad + rate.astype(bf16).astype(f32) * wr_ref[j : j + 1, :].astype(f32)
        x = x_ref[r, :].astype(f32)
        rms = lax.rsqrt(mean_row(x * x) + eps_norm)
        scaled = grad * pre_gain
        back = (rms * (scaled - x * rms * rms * mean_row(scaled * x))).astype(bf16)
        for c in range(count):
            mine[c, r, :] = back[:, c * cols : (c + 1) * cols]
        return 0

    lane = lax.broadcasted_iota(jnp.int32, (share, 128), 1)
    line = lax.broadcasted_iota(jnp.int32, (8, 128), 0)
    w_rows = pl.ds(pl.multiple_of(pos * share, share), share)
    slim = jnp.concatenate([wr_ref[j : j + 1, :].astype(f32) for j in range(heads)] + [pre_gain] * (8 - heads), axis=0)
    wcols[4, :, 0:8] = slim.T
    for i, side in enumerate(sides + (mix_gate_ref,)):
        wcols[i] = side[...].astype(f32).T
    gain = jnp.sum(early_ref[:, at_mix : at_mix + cols] * wcols[3, w_rows, :], axis=1, keepdims=True)
    table = jnp.zeros((share, 128), f32)
    blocks = [late_ref[j].astype(f32) for j in range(heads)]
    for i in range(3):
        joined = jnp.concatenate([b[:, i * width : (i + 1) * width] for b in blocks], axis=1)
        gain = gain + jnp.sum(joined * wcols[i, w_rows, :], axis=1, keepdims=True)
    for j in range(heads):
        rate = blocks[j][:, rate_lane : rate_lane + 1] + blocks[j][:, rate_lane + 1 : rate_lane + 2]
        gain = gain + rate * wcols[4, w_rows, j : j + 1]
        table = jnp.where(lane == j, rate, table)
    gain = gain / wcols[4, w_rows, heads : heads + 1]
    table = jnp.where(lane == heads, gain, table)
    flat = jnp.concatenate([table, jnp.zeros((128 - share, 128), f32)], axis=0).T[0:8]
    tile[...] = flat
    pl.semaphore_wait(barrier, count - 1 + CHAIN - 1)
    for d, peer in peers:
        push_head(tile, tile_got.at[d - 1], th_s.at[d - 1], th_r.at[d - 1], peer).start()
    lax.fori_loop(0, count, back_rows, 0)
    for d, peer in peers:
        push_head(mine.at[peer], got.at[d - 1], ib_s.at[d - 1], ib_r.at[d - 1], peer).start()
    back = mine[me].astype(f32)
    for d, peer in peers:
        push_head(tile, tile_got.at[d - 1], th_s.at[d - 1], th_r.at[d - 1], peer).wait()
    summed = flat
    for d, peer in peers:
        summed = summed + tile_got[d - 1]
    tile[...] = jnp.where(line == heads, summed, flat)
    for d in range(1, CHAIN):
        push(tile, tiles_ref.at[pos], ts_s.at[d - 1], ts_r.at[d - 1], base + lax.rem(pos + d, CHAIN)).start()
    pltpu.make_async_copy(tile, tiles_ref.at[pos], ts_loc).start()
    for d, peer in peers:
        push_head(mine.at[peer], got.at[d - 1], ib_s.at[d - 1], ib_r.at[d - 1], peer).wait()
        back = back + got[d - 1].astype(f32)
    back_ref[...] = back
    for d in range(1, CHAIN):
        push(tile, tiles_ref.at[pos], ts_s.at[d - 1], ts_r.at[d - 1], base + lax.rem(pos + d, CHAIN)).wait_send()
        await_bytes(tiles_ref.at[lax.rem(pos + CHAIN - d, CHAIN)], ts_r.at[d - 1])
    await_bytes(tiles_ref.at[pos], ts_loc)


def tail(at_mix, grads, wq, wk, wv, wr, mix_gate, ggp, x, pre_gain, late, early):
    count = lax.axis_size("head")
    rows, full = x.shape
    width = ggp.shape[1]
    vmem = pl.BlockSpec(memory_space=pltpu.VMEM)
    V = pltpu.VMEM
    dma = pltpu.SemaphoreType.DMA
    trio, seven = dma((count - 1,)), dma((CHAIN - 1,))
    return pl.pallas_call(
        functools.partial(tail_kernel, count, at_mix),
        in_specs=[vmem] * 11,
        out_specs=[vmem] * 2,
        out_shape=[jax.ShapeDtypeStruct((rows, width), f32),
                   jax.ShapeDtypeStruct((CHAIN, 8, 128), f32)],
        scratch_shapes=[V((count, rows, width), bf16), V((count - 1, rows, width), bf16),
                        V((8, 128), f32), V((count - 1, 8, 128), f32), V((5, full, width), f32),
                        trio, trio, trio, trio, seven, seven, dma],
        compiler_params=pltpu.CompilerParams(
            collective_id=3, has_side_effects=True, vmem_limit_bytes=56 * 1024 * 1024),
        name="tail",
    )(grads, wq, wk, wv, wr, mix_gate, ggp, x, pre_gain, late, early)


def final_kernel(at_mix, ffn, down_ref, resid_ref, back_ref, grc_ref, late_ref, early_ref, ends_ref, tiles_ref, small_ref,
                 out_ref, gin_ref, gq_ref, gk_ref, gv_ref, gmix_ref, rate_ref, gwout_ref, gwg_ref, gwu_ref, gwd_ref,
                 w1_ref, b1_ref, w2_ref, b2_ref, ig_ref, ib_ref, rb_ref, pre_ref, pg_ref, pb_ref, fg_ref):
    heads, width, hidden = w1_ref.shape
    cols = heads * width
    out_ref[...] = (down_ref[...] + resid_ref[...]).T
    gin_ref[...] = (back_ref[...] + grc_ref[...]).T
    for i, ref in enumerate((gq_ref, gk_ref, gv_ref)):
        ref[...] = jnp.concatenate([late_ref[j, :, i * width : (i + 1) * width].astype(f32) for j in range(heads)], axis=1)
    gwg_ref[...] = early_ref[:, 0:ffn]
    gwu_ref[...] = early_ref[:, ffn : 2 * ffn]
    rates = []
    gwd_ref[...] = early_ref[:, 2 * ffn : 3 * ffn]
    both = early_ref[:, at_mix : at_mix + 2 * cols]
    gmix_ref[...] = both[:, 0:cols]
    gwout_ref[...] = both[:, cols:].T
    for j in range(heads):
        w1_ref[j] = ends_ref[j, 0:width, :].astype(f32)
        b1_ref[pl.ds(j, 1), :] = ends_ref[j, width : AUG, :].astype(f32)[0:1]
        second = ends_ref[j, AUG : AUG + width, :].astype(f32)
        w2_ref[j] = second - jnp.mean(second, axis=0, keepdims=True)
        rest = ends_ref[j, AUG + width :, :].astype(f32)[0:8, 0:width]
        b2_ref[pl.ds(j, 1), :] = rest[0:1] - mean_row(rest[0:1])
        ig_ref[pl.ds(j, 1), :] = rest[1:2]
        ib_ref[pl.ds(j, 1), :] = rest[2:3]
        rates.append((rest[3:4] + rest[4:5])[:, 0:1])
    each = rate_ref.shape[1] // CHAIN
    strips = jnp.concatenate([tiles_ref[p, :, 0:each] for p in range(CHAIN)], axis=1)
    rate_ref[...] = strips[0:heads]
    me, count = head_place()
    pick = [tiles_ref[me * (CHAIN // count) + i, heads : heads + 1, 0:each] for i in range(CHAIN // count)]
    pre_ref[...] = jnp.concatenate(pick, axis=1)[0]
    rb_ref[...] = jnp.concatenate(rates, axis=1)[0]
    acc = small_ref[0]
    for p in range(1, CHAIN):
        acc = acc + small_ref[p]
    fg_ref[...] = acc[0]
    pg_ref[...] = acc[1:2, 0:cols][0]
    pb_ref[...] = acc[2:3, 0:cols][0]


def finish(at_mix, ffn, down, resid, back, grc, late, early, ends, tiles, small, shapes):
    ins = (down, resid, back, grc, late, early, ends, tiles, small)
    vmem = pl.BlockSpec(memory_space=pltpu.VMEM)
    return pl.pallas_call(
        functools.partial(final_kernel, at_mix, ffn),
        in_specs=[vmem] * len(ins),
        out_specs=[vmem] * len(shapes),
        out_shape=[jax.ShapeDtypeStruct(s, f32) for s in shapes],
        compiler_params=pltpu.CompilerParams(vmem_limit_bytes=48 * 1024 * 1024),
        name="final",
    )(*ins)


def stretch_groups(axis):
    count = lax.axis_size(axis)
    return [[start + step for step in range(0, count, CHAIN)] for start in range(CHAIN)]


def local(
    inputs,
    pre_gain,
    w_query,
    w_key,
    w_value,
    mix_gate,
    w_rate,
    rate_bias,
    inner_gain,
    inner_bias,
    init_w_one,
    init_b_one,
    init_w_two,
    init_b_two,
    post_gain,
    post_bias,
    w_out,
    ffn_gain,
    w_gate,
    w_up,
    w_down,
    cotangent,
):
    full_width = pre_gain.shape[0]
    rows, local_cols = inputs.shape
    heads, head_dim = inner_gain.shape
    stretches = lax.axis_size("seq") // CHAIN
    share = full_width // CHAIN

    sides = (w_query.T, w_key.T, w_value.T, w_rate.T)
    whole_low, normed_one, payload = front(inputs.T, pre_gain, rate_bias, *sides)
    mixed_h, ct_blocks, *saved = chain_forward(
        payload, cotangent.T, init_w_one, init_b_one, init_w_two.transpose(0, 2, 1), init_b_two,
        inner_gain, inner_bias)
    ffn = w_gate.shape[1]
    at_mix = 3 * ffn
    grad_mixed, early, grad_gate_pre, down_cols, resid_cols, grad_resid_cols, small, normed_all = middle(
        mixed_h, whole_low, ct_blocks.reshape(full_width, rows), mix_gate.T, normed_one, w_out, w_gate, w_up, w_down,
        post_gain, post_bias, ffn_gain)
    grads, ends, late, early_sum, small = chain_backward(
        grad_mixed, early.reshape(CHAIN // 2, 2, share, early.shape[1]), small, inner_gain, inner_bias,
        normed_all.reshape(CHAIN * rows, full_width), saved)
    back_cols, tiles = tail(
        at_mix, grads, *sides, mix_gate.T, grad_gate_pre, whole_low, pre_gain,
        late, early_sum)
    if stretches > 1:
        groups = stretch_groups("seq")
        ends, tiles, small = lax.psum((ends.astype(f32), tiles, small), "seq", axis_index_groups=groups)
        seq_index = lax.axis_index("seq")
        stretch_lists = [list(range(s, s + CHAIN)) for s in range(0, stretches * CHAIN, CHAIN)]

        def spread(mine_rows):
            summed = lax.psum(mine_rows, "seq", axis_index_groups=groups)
            total = lax.all_gather(
                summed, "seq", axis=summed.ndim - 2, tiled=True, axis_index_groups=stretch_lists)
            return lax.dynamic_slice_in_dim(
                total, seq_index * (share // stretches), share // stretches, summed.ndim - 2)

        late = spread(late.astype(f32))
        early_sum = spread(early_sum)
    held = share // stretches
    hidden = init_w_one.shape[2]
    square = (held, local_cols)
    (outputs, grad_inputs, grad_q, grad_k, grad_v, grad_mix, grad_rate_w, grad_w_out, grad_w_gate, grad_w_up, grad_w_down,
     grad_one, grad_b_one, grad_two, grad_b_two, grad_gain, grad_bias, rate_b, grad_pre, grad_post_gain, grad_post_bias,
     grad_ffn_gain) = finish(
        at_mix, ffn, down_cols, resid_cols, back_cols, grad_resid_cols, late, early_sum, ends, tiles, small,
        ((local_cols, rows), (local_cols, rows), square, square, square, square, (heads, full_width),
         (local_cols, held), (held, ffn), (held, ffn), (held, ffn),
         (heads, head_dim, hidden), (heads, hidden), (heads, head_dim, hidden), (heads, head_dim),
         (heads, head_dim), (heads, head_dim), (heads,), (local_cols,), (local_cols,), (local_cols,), (full_width,)))
    return (
        outputs.T,
        grad_inputs.T,
        grad_pre,
        grad_q,
        grad_k,
        grad_v,
        grad_mix,
        grad_rate_w.T,
        rate_b,
        grad_gain,
        grad_bias,
        grad_one,
        grad_b_one,
        grad_two.transpose(0, 2, 1),
        grad_b_two,
        grad_post_gain,
        grad_post_bias,
        grad_w_out,
        grad_ffn_gain,
        grad_w_gate,
        grad_w_up,
        grad_w_down.T,
    )


def solution(mesh):
    in_specs = (
        P("seq", "head"),
        P(),
        P(None, "head"),
        P(None, "head"),
        P(None, "head"),
        P(None, "head"),
        P(None, "head"),
        P("head"),
        P("head", None),
        P("head", None),
        P("head", None, None),
        P("head", None),
        P("head", None, None),
        P("head", None),
        P("head"),
        P("head"),
        P("head", None),
        P(),
        P(None, "head"),
        P(None, "head"),
        P("head", None),
        P("seq", "head"),
    )
    out_specs = (
        P("seq", "head"),
        P("seq", "head"),
        P("head"),
        P("seq", "head"),
        P("seq", "head"),
        P("seq", "head"),
        P("seq", "head"),
        P(None, "head"),
        P("head"),
        P("head", None),
        P("head", None),
        P("head", None, None),
        P("head", None),
        P("head", None, None),
        P("head", None),
        P("head"),
        P("head"),
        P("head", "seq"),
        P(),
        P("seq", "head"),
        P("seq", "head"),
        P("head", "seq"),
    )
    return jax.shard_map(local, mesh=mesh, in_specs=in_specs, out_specs=out_specs, check_vma=False)
```

```python
import functools

import jax
import jax.numpy as jnp
from jax import lax
from jax.experimental import pallas as pl
from jax.experimental.pallas import tpu as pltpu
from jax.sharding import PartitionSpec as P

MINI = 16
CHAIN = 8
FIRST = 2
AUG = 80
eps_norm = 1e-06
gelu_scale = 0.7978845608028654
f32 = jnp.float32
bf16 = jnp.bfloat16


def dot_nn(a, b):
    return lax.dot_general(a, b, (((1,), (0,)), ((), ())), preferred_element_type=f32)


def dot_nt(a, b):
    return lax.dot_general(a, b, (((1,), (1,)), ((), ())), preferred_element_type=f32)


def dot_tn(a, b):
    return lax.dot_general(a, b, (((0,), (0,)), ((), ())), preferred_element_type=f32)


def mean_row(x):
    return jnp.sum(x, axis=1, keepdims=True) * (1.0 / x.shape[1])


def gelu_first(z):
    sq = z * z
    th = jnp.tanh(gelu_scale * z * (1.0 + 0.044715 * sq))
    half = 0.5 * (1.0 + th)
    act = z * half
    der = half + (0.5 * gelu_scale) * z * (1.0 - th * th) * (1.0 + 0.134145 * sq)
    return act, der


def gelu_second(z):
    sq = z * z
    th = jnp.tanh(gelu_scale * z * (1.0 + 0.044715 * sq))
    half = 0.5 * (1.0 + th)
    act = z * half
    slope = gelu_scale * (1.0 + 0.134145 * sq)
    sech = 1.0 - th * th
    der = half + 0.5 * z * sech * slope
    curve = sech * (slope + z * (0.5 * gelu_scale * 0.26829 * z) - z * th * slope * slope)
    return act, der, curve


def tri_mask():
    rows = lax.broadcasted_iota(jnp.int32, (MINI, MINI), 0)
    cols = lax.broadcasted_iota(jnp.int32, (MINI, MINI), 1)
    return jnp.where(rows >= cols, 1.0, 0.0).astype(f32)


def forward_output(kept, gain, bias, tri, sink):
    z1b, act_h, w2_h, b2, s2_h = kept
    actb, _ = gelu_first(z1b)
    actb_h = actb.astype(bf16)
    yield
    att = dot_nt(actb_h, act_h)
    z2b = dot_nt(actb_h, w2_h) + b2
    yield
    z2b = z2b - dot_nn(((att + 1.0) * tri).astype(bf16), s2_h)
    yield
    z2b = z2b - mean_row(z2b)
    yield
    invb = lax.rsqrt(mean_row(z2b * z2b) + eps_norm)
    sink(z2b * invb * gain + bias, z2b)
    yield


def forward_chain(state, z1, post, key_aug, key_next, query_aug, base, rate, gain_sq, tri, save):
    w1, w2t, b2 = state
    width = gain_sq.shape[1]
    scale = 1.0 / width
    w2_h = w2t.astype(bf16)
    act, der = gelu_first(z1)
    act_h = act.astype(bf16)
    z = dot_nt(act_h, w2_h) + b2
    next(post, None)
    fixed = dot_nn(
        jnp.concatenate([base, jnp.broadcast_to(gain_sq, (8, width)), jnp.ones((8, width), f32)], axis=0).astype(bf16),
        w2_h)
    both = jnp.concatenate([key_next, query_aug], axis=0)
    coef = dot_nt(both, key_aug)
    coef = jnp.concatenate([coef[:MINI], coef[MINI:] * tri], axis=0).astype(bf16)
    m_b = mean_row(base)
    m_sq = mean_row(gain_sq)
    w1_h = w1.astype(bf16)
    next(post, None)
    zg = z * gain_sq
    prods = dot_nn(jnp.concatenate([zg, z], axis=0).astype(bf16), w2_h)
    mz = mean_row(z)
    m_zz = mean_row(z * z)
    m_zg = mean_row(zg)
    m_zzg = mean_row(zg * z)
    m_zb = mean_row(z * base)
    zz = dot_nn(both, w1_h)
    next(post, None)
    inv = lax.rsqrt(m_zz - mz * mz + eps_norm)
    c_zg = m_zg - mz * m_sq
    c_zzg = m_zzg - mz * (m_zg + c_zg)
    c_zb = m_zb - mz * m_b
    m_g = inv * c_zg + m_b
    m_gn = inv * (inv * c_zzg + c_zb)
    rinv = rate * inv
    rinv2 = rinv * inv
    skew = rinv2 * m_gn
    shift = skew * mz - rinv * m_g
    upd = (rinv2 * prods[:MINI] - skew * prods[MINI:]) + (
        (rinv * fixed[:MINI] + shift * fixed[MINI + 8 : MINI + 9]) - (rinv2 * mz) * fixed[MINI : MINI + 1])
    s1_h = (upd * der).astype(bf16)
    zz = zz - dot_nn(coef, s1_h)
    zc = z - mz
    s2 = rinv2 * zc * gain_sq - skew * zc + (rinv * base - rinv * m_g)
    s2_h = s2.astype(bf16)
    new_w2t = w2t - dot_tn(s2_h, act_h)
    new_w1 = w1 - dot_tn(key_aug, s1_h)
    new_b2 = b2 - jnp.sum(s2, axis=0, keepdims=True)
    next(post, None)
    next(post, None)
    z1b = zz[MINI:]
    save(w1_h, w2_h, z1, upd, zc, s2, z1b)
    return (new_w1, new_w2t, new_b2), zz[:MINI], (z1b, act_h, w2_h, b2, s2_h)


def prepare_back(store, saved, d_out, key_aug, query_aug, target, rate, gain, gain_sq, bias, tri):
    w1_h, w2_h, z1, upd, zc, s2, z1b, z2b = saved
    width = gain.shape[1]
    s2_h = s2.astype(bf16)
    actb, derb = gelu_first(z1b)
    actb_h = actb.astype(bf16)
    invb = lax.rsqrt(mean_row(z2b * z2b) + eps_norm)
    dn = d_out * gain
    m_dn = mean_row(dn)
    yield
    act, der, curve = gelu_second(z1)
    act_h = act.astype(bf16)
    s1_h = (upd * der).astype(bf16)
    store.update(act=act_h, der=der, bend=upd * curve, actb=actb_h, s1=s1_h, s2=s2_h)
    yield
    att2 = dot_nt(actb_h, act_h)
    att1 = dot_nt(query_aug, key_aug)
    nb = z2b * invb
    d_z2b = invb * (dn - m_dn - nb * mean_row(dn * nb))
    d_z2b_h = d_z2b.astype(bf16)
    yield
    inv = lax.rsqrt(mean_row(zc * zc) + eps_norm)
    d_att2 = dot_nt(d_z2b_h, s2_h)
    d_actb = dot_nn(d_z2b_h, w2_h)
    base = (bias - target) * gain
    m_sq = mean_row(gain_sq)
    yield
    att2 = ((att2 + 1.0) * tri).astype(bf16)
    att1 = (att1 * tri).astype(bf16)
    n = zc * inv
    ng = n * gain_sq
    big_g = ng + base
    m_g = mean_row(big_g)
    m_gn = mean_row(big_g * n)
    yield
    d_att2 = (-d_att2 * tri).astype(bf16)
    d_actb = d_actb + dot_nn(d_att2, act_h)
    c2 = dot_tn(att2, d_z2b_h)
    m_ng = mean_row(ng)
    m_nng = mean_row(n * ng)
    yield
    c3 = dot_tn(d_att2, actb_h)
    inv2 = inv * inv
    g = inv * (big_g - m_g - n * m_gn)
    fac = rate * inv2 * (gain_sq - m_gn)
    scale = rate * (1.0 / width)
    weights = (jnp.broadcast_to(scale, n.shape), scale * n, scale * gain_sq, scale * (ng * inv2 + g * inv))
    store.update(c2=c2, c3=c3, fac=fac, weights=weights, inv=inv, inv2=inv2, n=n)
    yield
    d_z1b_h = (d_actb * derb).astype(bf16)
    c1 = dot_tn(att1, d_z1b_h)
    row1 = inv2 * (gain_sq - (m_sq + m_gn) - n * m_ng)
    row2 = inv2 * (ng + big_g - (m_ng + m_g) - n * (m_nng + 2.0 * m_gn))
    store.update(dz2b=d_z2b_h, dz2bf=d_z2b, dz1b=d_z1b_h, c1=c1, row1=row1, row2=row2)
    yield
    fixed = dot_nn(jnp.concatenate([row1, row2, jnp.broadcast_to(inv2, n.shape), n], axis=0).astype(bf16), w2_h)
    d_att1 = dot_nt(d_z1b_h, s1_h)
    d_query = dot_nt(d_z1b_h, w1_h)
    yield
    prods = tuple(fixed[i * MINI : (i + 1) * MINI] for i in range(4))
    store.update(prods=prods)
    d_att1 = (-d_att1 * tri).astype(bf16)
    d_query = (d_query + dot_nn(d_att1, key_aug))[:, :width] + d_out
    d_key = dot_tn(d_att1, query_aug)[:, :width]
    yield
    d_gain = d_out * nb
    d_bias = d_out
    store.update(dq=d_query, dk=d_key, d_gain=d_gain, d_bias=d_bias, rate=rate, w1=w1_h, w2=w2_h, s2f=s2,
                 key=key_aug, query=query_aug, gslope=2.0 * n * gain + bias - target)
    yield


PIECES = 11


def settle(post, width):
    if post is None:
        return
    pre, d_s2, a1, a2, d_z1_h, p1_h, keep, gain, sink = post
    d_g = pre["inv"] * (pre["rate"] * d_s2 - a1 - pre["n"] * a2)
    d_gg = d_g * gain
    key_part = dot_nt(d_z1_h, pre["w1"])
    late_part = dot_nt(pre["s1"], p1_h)
    d_logit = keep * jnp.sum(d_s2 * pre["s2f"], axis=1, keepdims=True)
    yield
    d_gain = pre["d_gain"] + d_g * pre["gslope"]
    d_bias = pre["d_bias"] + d_gg
    d_key = pre["dk"] + d_gg + (key_part - late_part)[:, :width]
    sink(pre["dq"], d_key, -d_gg, d_logit, d_gain, d_bias)
    yield


def drain(maker):
    for _ in maker:
        pass


def backward_chain(carry, pre, post, fill, keep, gain, sink):
    p1, p2t, p2, dz, kq, left, right, dsum = carry
    width = gain.shape[1]
    key, act, der, w2_h = pre["key"], pre["act"], pre["der"], pre["w2"]
    after = settle(post, width)
    p1_h = p1.astype(bf16)
    coef1 = dot_nt(key, kq).astype(bf16)
    base1 = pre["c1"] + dot_nn(key, p1_h)
    d_s1 = -base1 - dot_nn(coef1, dz)
    p2_h = p2t.astype(bf16)
    coef2 = dot_nt(act, right).astype(bf16)
    p2 = p2 + dsum
    base2 = pre["c2"] + p2 + dot_nt(act, p2_h)
    fill(5)
    side = base2 + dot_nn(coef2, left)
    p1 = p1 + dot_tn(kq, dz)
    p2t = p2t + dot_tn(left, right)
    next(after, None)
    fill(2)
    d_upd = d_s1 * der
    d_upd_h = d_upd.astype(bf16)
    d_s2 = dot_nt(d_upd_h, w2_h) - side
    rest = pre["c3"] - dot_nn(pre["s2"], p2t.astype(bf16))
    p1_h = p1.astype(bf16)
    bend = d_s1 * pre["bend"]
    next(after, None)
    fill(2)
    d_fac = d_s2 * pre["fac"]
    main = dot_nn(d_fac.astype(bf16), w2_h)
    a1, a2, a3, a4 = (jnp.sum(d_s2 * w, axis=1, keepdims=True) for w in pre["weights"])
    fill(2)
    y1, y2, y3, y4 = pre["prods"]
    d_act = (main + rest) - ((a1 * y1 + a2 * y2) + (a3 * y3 + a4 * y4))
    d_z1_h = (d_act * der + bend).astype(bf16)
    d_zc = d_fac - ((a1 * pre["row1"] + a2 * pre["row2"]) + (a3 * pre["inv2"] + a4 * pre["n"]))
    d_zc_h = d_zc.astype(bf16)
    carry = (p1, p2t, p2, jnp.concatenate([d_z1_h, pre["dz1b"]], axis=0),
             jnp.concatenate([key, pre["query"]], axis=0),
             jnp.concatenate([pre["s2"], d_zc_h, pre["dz2b"]], axis=0),
             jnp.concatenate([d_upd_h, act, pre["actb"]], axis=0),
             jnp.sum(d_zc + pre["dz2bf"], axis=0, keepdims=True))
    return carry, (pre, d_s2, a1, a2, d_z1_h, p1_h, keep, gain, sink)


def backward_close(carry):
    p1, p2t, p2, dz, kq, left, right, dsum = carry
    return p1 + dot_tn(kq, dz), p2t + dot_tn(left, right), p2 + dsum


MESH = pl.DeviceIdType.MESH
PACK = 256
ENDS = 160


def seq_place():
    index = lax.axis_index("seq")
    pos = lax.rem(index, CHAIN)
    return pos, index - pos


def meet_group(pos, base):
    barrier = pltpu.get_barrier_semaphore()
    for d in range(1, CHAIN):
        pl.semaphore_signal(
            barrier, inc=1, device_id={"seq": base + lax.rem(pos + d, CHAIN)}, device_id_type=MESH)
    pl.semaphore_wait(barrier, CHAIN - 1)


def push(src, dst, send_sem, recv_sem, target):
    return pltpu.make_async_remote_copy(
        src_ref=src, dst_ref=dst, send_sem=send_sem, recv_sem=recv_sem,
        device_id={"seq": target}, device_id_type=MESH)


def await_bytes(ref, sem):
    pltpu.make_async_copy(ref, ref, sem).wait()


def swap_start(src, dst, send, recv, local_sem, pos, base):
    for d in range(1, CHAIN):
        peer = lax.rem(pos + d, CHAIN)
        push(src.at[peer], dst.at[pos], send.at[d - 1], recv.at[d - 1], base + peer).start()
    pltpu.make_async_copy(src.at[pos], dst.at[pos], local_sem).start()


def swap_wait(src, dst, send, recv, local_sem, pos, base):
    for d in range(1, CHAIN):
        peer = lax.rem(pos + d, CHAIN)
        origin = lax.rem(pos + CHAIN - d, CHAIN)
        push(src.at[peer], dst.at[pos], send.at[d - 1], recv.at[d - 1], base + peer).wait_send()
        await_bytes(dst.at[origin], recv.at[d - 1])
    await_bytes(dst.at[pos], local_sem)


def fwd_kernel(block, heads, count, pay_ref, ct_ref, w1_in, b1_in, w2_in, b2_in, gain_in, bias_in,
               mixed_ref, ct_out, k_out, q_out, aux_out, w1s_ref, w2s_ref, z1s_ref, upd_ref, zc_ref, s2_ref, z1b_ref, z2b_ref,
               got, k_all, q_all, base_all, aux_all, mixed_all, w1, w2t, b2, z1,
               pay_send, pay_recv, mix_send, mix_recv, ct_send, ct_recv, ct_loc):
    blk = pl.program_id(0)
    last = pl.num_programs(0) - 1
    pos, base = seq_place()
    width = gain_in.shape[1]
    hidden = w1.shape[1]
    rows_each = pay_ref.shape[0]
    per = rows_each // block
    piece = got.shape[1]
    parts = rows_each // piece
    owner = (pos >= FIRST) & (pos < FIRST + heads)
    mine = jnp.clip(pos - FIRST, 0, heads - 1)
    gain = gain_in[pl.ds(mine, 1), :]
    bias = bias_in[pl.ds(mine, 1), :]
    gain_sq = gain * gain
    tri = tri_mask()

    me, _ = head_place()

    @pl.when(blk == 0)
    def _():
        barrier = pltpu.get_barrier_semaphore()
        for d in range(1, count):
            pl.semaphore_signal(barrier, inc=1, device_id={"head": lax.rem(me + d, count)}, device_id_type=MESH)
        for d in range(1, CHAIN):
            pl.semaphore_signal(
                barrier, inc=1, device_id={"seq": base + lax.rem(pos + d, CHAIN)}, device_id_type=MESH)
        pl.semaphore_wait(barrier, CHAIN - 1 + count - 1)
        for s in range(parts):
            for j in range(heads):
                src = pay_ref.at[s * piece : (s + 1) * piece, j * PACK : (j + 1) * PACK]
                dst = got.at[pos * parts + s]

                @pl.when(pos != FIRST + j)
                def _():
                    push(src, dst, pay_send.at[j], pay_recv.at[pos * parts + s], base + FIRST + j).start()

                @pl.when(pos == FIRST + j)
                def _():
                    pltpu.make_async_copy(src, dst, pay_recv.at[pos * parts + s]).start()

    @pl.when(blk == 1)
    def _():
        for d in range(1, count):
            push_head(ct_ref, ct_out.at[me], ct_send.at[d - 1], ct_recv.at[d - 1], lax.rem(me + d, count)).start()
        pltpu.make_async_copy(ct_ref, ct_out.at[me], ct_loc).start()

    def take_in(p):
        await_bytes(got.at[p], pay_recv.at[p])
        part = got[p]
        rows = pl.ds(pl.multiple_of(p * piece, piece), piece)
        lane = lax.broadcasted_iota(jnp.int32, (piece, AUG), 1)
        one = jnp.ones((), bf16)
        zero = jnp.zeros((), bf16)
        tail = jnp.where(lane == width, one, zero)
        query = part[:, :AUG]
        key = part[:, width : width + AUG]
        q_all[rows, :] = jnp.where(lane < width, query, tail)
        k_all[rows, :] = jnp.where(lane < width, key, tail)
        key_f = part[:, width : 2 * width].astype(f32)
        target = part[:, 2 * width : 3 * width].astype(f32) - key_f
        logit = part[:, 3 * width : 3 * width + 1].astype(f32) + part[:, 3 * width + 1 : 3 * width + 2].astype(f32)
        sig = 1.0 / (1.0 + jnp.exp(-logit))
        base_all[rows, :] = (bias - target) * gain
        spot = lax.broadcasted_iota(jnp.int32, (piece, 2 * width), 1)
        wide = jnp.concatenate([target, target], axis=1)
        aux_all[rows, :] = jnp.where(
            spot < width, wide, jnp.where(spot == width, sig * (1.0 / width), 1.0 - sig))

    def send_mixed(b):
        p = lax.div(b, per)
        src = mixed_all.at[pl.ds(pl.multiple_of(b * block, block), block), :]
        dst = mixed_ref.at[mine, pl.ds(pl.multiple_of(lax.rem(b, per) * block, block), block), :]

        @pl.when(p != pos)
        def _():
            push(src, dst, mix_send, mix_recv.at[mine], base + p).start()

        @pl.when(p == pos)
        def _():
            pltpu.make_async_copy(src, dst, mix_recv.at[mine]).start()

    @pl.when(owner)
    def _():
        @pl.when(blk == 0)
        def _():
            row = lax.broadcasted_iota(jnp.int32, (AUG - width, hidden), 0)
            w1[pl.ds(0, width), :] = w1_in[mine]
            w1[pl.ds(width, AUG - width), :] = jnp.where(row == 0, b1_in[pl.ds(mine, 1), :], 0.0)
            turned = w2_in[mine]
            w2t[...] = turned - jnp.mean(turned, axis=0, keepdims=True)
            start = b2_in[pl.ds(mine, 1), :]
            b2[...] = start - mean_row(start)
            k_all[pl.ds(CHAIN * rows_each, MINI), :] = jnp.zeros((MINI, AUG), bf16)

        @pl.when(blk > 0)
        def _():
            send_mixed(blk - 1)

        def bring(p, _):
            take_in(p)
            return 0

        lax.fori_loop(jnp.where(blk == 0, 0, 2 * blk + 1), jnp.minimum(2 * blk + 3, 2 * last + 2), bring, 0)

        @pl.when(blk == 0)
        def _():
            z1[...] = dot_nn(k_all[0:MINI, :], w1[...].astype(bf16))

        state = (w1[...], w2t[...], b2[...])
        z1_now = z1[...]
        post = iter(())
        for loc in range(block // MINI):
            row = pl.multiple_of(blk * block + loc * MINI, MINI)
            rows = pl.ds(row, MINI)
            lr = pl.ds(loc * MINI, MINI)
            q_aug = q_all[rows, :]

            def save(w1_h, w2_h, z1_v, upd, zc, s2, z1b, loc=loc, lr=lr):
                w1s_ref[loc] = w1_h
                w2s_ref[loc] = w2_h
                z1s_ref[lr, :] = z1_v
                upd_ref[lr, :] = upd
                zc_ref[lr, :] = zc
                s2_ref[lr, :] = s2
                z1b_ref[lr, :] = z1b

            state, z1_now, kept = forward_chain(
                state, z1_now, post, k_all[rows, :], k_all[pl.ds(row + MINI, MINI), :], q_aug,
                base_all[rows, :], aux_all[rows, width : width + 1], gain_sq, tri, save)

            def sink(out, z2b, lr=lr, rows=rows, q_aug=q_aug):
                z2b_ref[lr, :] = z2b
                mixed_all[rows, :] = (out + q_aug[:, :width].astype(f32)).astype(bf16)

            post = forward_output(kept, gain, bias, tri, sink)
        drain(post)
        w1[...], w2t[...], b2[...] = state
        z1[...] = z1_now

        brows = pl.ds(pl.multiple_of(blk * block, block), block)
        k_out[...] = k_all[brows, :]
        q_out[...] = q_all[brows, :]
        aux_out[...] = aux_all[brows, :]

    @pl.when(blk == last)
    def _():
        @pl.when(owner)
        def _():
            send_mixed(last)
            others = mixed_all.at[pl.ds(0, (CHAIN - 1) * rows_each), :]
            await_bytes(others, mix_send)
        for j in range(heads):
            @pl.when(pos != FIRST + j)
            def _():
                await_bytes(got.at[pl.ds(0, parts)], pay_send.at[j])

            await_bytes(mixed_ref.at[j], mix_recv.at[j])

        for d in range(1, count):
            push_head(ct_ref, ct_out.at[me], ct_send.at[d - 1], ct_recv.at[d - 1],
                      lax.rem(me + d, count)).wait_send()
            await_bytes(ct_out.at[lax.rem(me + count - d, count)], ct_recv.at[d - 1])
        await_bytes(ct_out.at[me], ct_loc)


def chain_forward(payload, ct, w1, b1, w2, b2, gain, bias, block=256):
    rows = payload.shape[0]
    heads, width, hidden = w1.shape
    count = lax.axis_size("head")
    tokens = rows * CHAIN
    steps = tokens // MINI
    nb = block // MINI
    whole = lambda a: pl.BlockSpec(a.shape, lambda i: (0,) * a.ndim)
    rowblk = lambda w: pl.BlockSpec((block, w), lambda i: (i, 0))
    stepblk = lambda r: pl.BlockSpec((nb, r, hidden), lambda i: (i, 0, 0))
    anywhere = pl.BlockSpec(memory_space=pl.ANY)
    small = (w1, b1, w2, b2, gain, bias)
    dma = pltpu.SemaphoreType.DMA
    wide = jax.ShapeDtypeStruct((tokens, hidden), f32)
    narrow = jax.ShapeDtypeStruct((tokens, width), f32)
    return pl.pallas_call(
        functools.partial(fwd_kernel, block, heads, count),
        grid=(tokens // block,),
        in_specs=[anywhere, anywhere] + [whole(a) for a in small],
        out_specs=[anywhere, anywhere, rowblk(AUG), rowblk(AUG), rowblk(2 * width), stepblk(AUG), stepblk(width),
                   rowblk(hidden), rowblk(hidden), rowblk(width), rowblk(width), rowblk(hidden), rowblk(width)],
        out_shape=[jax.ShapeDtypeStruct((heads, rows, width), bf16),
                   jax.ShapeDtypeStruct((count,) + ct.shape, bf16),
                   jax.ShapeDtypeStruct((tokens, AUG), bf16),
                   jax.ShapeDtypeStruct((tokens, AUG), bf16),
                   jax.ShapeDtypeStruct((tokens, 2 * width), f32),
                   jax.ShapeDtypeStruct((steps, AUG, hidden), bf16),
                   jax.ShapeDtypeStruct((steps, width, hidden), bf16),
                   wide, wide, narrow, narrow, wide, narrow],
        scratch_shapes=[pltpu.VMEM((2 * tokens // block, block // 2, PACK), bf16),
                        pltpu.VMEM((tokens + MINI, AUG), bf16), pltpu.VMEM((tokens, AUG), bf16),
                        pltpu.VMEM((tokens, width), f32), pltpu.VMEM((tokens, 2 * width), f32),
                        pltpu.VMEM((tokens, width), bf16),
                        pltpu.VMEM((AUG, hidden), f32), pltpu.VMEM((width, hidden), f32),
                        pltpu.VMEM((1, width), f32), pltpu.VMEM((MINI, hidden), f32),
                        dma((heads,)), dma((2 * tokens // block,)), dma, dma((heads,)),
                        dma((count - 1,)), dma((count - 1,)), dma],
        compiler_params=pltpu.CompilerParams(collective_id=0, has_side_effects=True),
        name="inner_forward",
    )(payload, ct, *small)


def bwd_kernel(block, heads, turn, gm_ref, early_ref, small_ref, gain_in, bias_in, norm_ref, norm_last_ref,
               k_ref, q_ref, aux_ref, w1s_ref, w2s_ref, z1s_ref, upd_ref, zc_ref, s2_ref, z1b_ref, z2b_ref,
               grads_ref, ends_ref, late_ref, early_out, small_out,
               dout, half_got, half_mine, quarter, quarter_got, packed, ends, weights, late,
               p1, p2t, p2, dz, kq, left, right, dsum, dg, db, dl,
               gm_send, gm_recv, ha_send, ha_recv, ha_loc, qu_send, qu_recv, sm_send, sm_recv, sm_loc, bc_send, bc_recv, en_send, en_recv, la_send, la_recv):
    pid = pl.program_id(0)
    last = pl.num_programs(0) - 1
    blk = last - pid
    pos, base = seq_place()
    width = gain_in.shape[1]
    rows_each = gm_ref.shape[1]
    per = rows_each // block
    owner = (pos >= FIRST) & (pos < FIRST + heads)
    mine = jnp.clip(pos - FIRST, 0, heads - 1)
    gain = gain_in[pl.ds(mine, 1), :]
    bias = bias_in[pl.ds(mine, 1), :]
    gain_sq = gain * gain
    tri = tri_mask()
    count = block // MINI
    side = lax.rem(pos, 2)
    rank = lax.div(pos, 2)
    partner = pos + 1 - 2 * side
    state = (p1, p2t, p2, dz, kq, left, right, dsum)

    @pl.when(pid == 0)
    def _():
        meet_group(pos, base)
        for j in range(heads):
            @pl.when(pos != FIRST + j)
            def _():
                push(gm_ref.at[j], dout.at[pos], gm_send.at[j], gm_recv.at[pos], base + FIRST + j).start()

            @pl.when(pos == FIRST + j)
            def _():
                pltpu.make_async_copy(gm_ref.at[j], dout.at[pos], gm_recv.at[pos]).start()

        for d in range(1, CHAIN):
            push(small_ref, small_out.at[pos], sm_send.at[d - 1], sm_recv.at[d - 1],
                 base + lax.rem(pos + d, CHAIN)).start()
        pltpu.make_async_copy(small_ref, small_out.at[pos], sm_loc).start()
        push(early_ref.at[:, 1 - side], half_got, ha_send, ha_recv, base + partner).start()
        pltpu.make_async_copy(early_ref.at[:, side], half_mine, ha_loc).start()

    @pl.when(pid == turn)
    def _():
        push(early_ref.at[:, 1 - side], half_got, ha_send, ha_recv, base + partner).wait()
        await_bytes(half_mine, ha_loc)

        def pair_up(c, _):
            rows = pl.ds(pl.multiple_of(c * MINI, MINI), MINI)
            for r in range(CHAIN // 2):
                quarter[r, rows, :] = (half_mine[r, rows, :].astype(f32) + half_got[r, rows, :].astype(f32)).astype(bf16)
            return 0

        lax.fori_loop(0, half_mine.shape[1] // MINI, pair_up, 0)
        for d in range(1, CHAIN // 2):
            other = lax.rem(rank + d, CHAIN // 2)
            push(quarter.at[other], quarter_got.at[d - 1], qu_send.at[d - 1], qu_recv.at[d - 1],
                 base + 2 * other + side).start()

    def share_block(b):
        p = lax.div(b, per)
        src = packed.at[pl.ds(pl.multiple_of(b * block, block), block), :]
        dst = grads_ref.at[mine, pl.ds(pl.multiple_of(lax.rem(b, per) * block, block), block), :]

        @pl.when(p != pos)
        def _():
            push(src, dst, bc_send, bc_recv.at[mine], base + p).start()

        @pl.when(p == pos)
        def _():
            pltpu.make_async_copy(src, dst, bc_recv.at[mine]).start()

    share = late.shape[1]

    def weigh(norm, b, lo, hi):
        rows = pl.ds(pl.multiple_of(b * block, block), block)
        weights[lo:hi, :] += dot_tn(norm[:, lo:hi], packed[rows, :])

    slabs = [(i * 128, i * 128 + 128) for i in range(norm_ref.shape[1] // 128)]

    @pl.when(owner)
    def _():
        @pl.when(pid == 0)
        def _():
            for r in state + (dg, db, dl, weights):
                r[...] = jnp.zeros_like(r)
            packed[pl.ds(0, block), :] = jnp.zeros((block, PACK), bf16)

        @pl.when(lax.rem(pid, per) == 0)
        def _():
            p = lax.div(blk, per)
            await_bytes(dout.at[p], gm_recv.at[p])

        @pl.when(pid > 0)
        def _():
            share_block(blk + 1)

        carry = tuple(r[...] for r in state)
        totals = [dg[...], db[...], dl[...]]
        made = {}

        def start(loc):
            made[loc] = {}
            lr = pl.ds(loc * MINI, MINI)
            inner = pl.ds(pl.multiple_of(lax.rem(blk, per) * block + loc * MINI, MINI), MINI)
            saved = (w1s_ref[loc], w2s_ref[loc], z1s_ref[lr, :], upd_ref[lr, :], zc_ref[lr, :], s2_ref[lr, :],
                     z1b_ref[lr, :], z2b_ref[lr, :])
            return prepare_back(made[loc], saved, dout[lax.div(blk, per), inner, :].astype(f32), k_ref[lr, :],
                                q_ref[lr, :], aux_ref[lr, 0:width], aux_ref[lr, width : width + 1],
                                gain, gain_sq, bias, tri)

        drain(start(count - 1))
        post = None
        for loc in range(count - 1, -1, -1):
            ahead = start(loc - 1) if loc > 0 else iter(())

            def fill(pieces, ahead=ahead):
                for _ in range(pieces):
                    next(ahead, None)

            def sink(d_query, d_key, d_value, d_logit, d_gain, d_bias, loc=loc):
                totals[0] = totals[0] + d_gain
                totals[1] = totals[1] + d_bias
                totals[2] = totals[2] + d_logit
                high = d_logit.astype(bf16).astype(f32)
                lane = lax.broadcasted_iota(jnp.int32, (MINI, width), 1)
                extra = jnp.where(lane == 0, high, jnp.where(lane == 1, d_logit - high, 0.0))
                rows = pl.ds(pl.multiple_of(blk * block + loc * MINI, MINI), MINI)
                packed[rows, :] = jnp.concatenate([d_query, d_key, d_value, extra], axis=1).astype(bf16)

            if (count - 1 - loc) % 2 == 0 and (count - 1 - loc) // 2 < len(slabs):
                weigh(norm_ref, jnp.where(pid == 0, 0, blk + 1), *slabs[(count - 1 - loc) // 2])
            carry, post = backward_chain(
                carry, made.pop(loc), post, fill, aux_ref[pl.ds(loc * MINI, MINI), width + 1 : width + 2], gain, sink)
        drain(settle(post, width))
        for r, v in zip(state, carry):
            r[...] = v
        dg[...], db[...], dl[...] = totals

        @pl.when(pid == last)
        def _():
            end_one, end_two, end_b_two = backward_close(tuple(r[...] for r in state))
            ends[pl.ds(0, AUG), :] = end_one.astype(bf16)
            ends[pl.ds(AUG, width), :] = end_two.astype(bf16)
            rest = ENDS - AUG - width
            row = lax.broadcasted_iota(jnp.int32, (rest, width), 0)
            sums = [jnp.sum(r[...], axis=0, keepdims=True) for r in (dg, db, dl)]
            tailing = jnp.where(row == 0, end_b_two, jnp.where(row == 1, sums[0], jnp.where(row == 2, sums[1], 0.0)))
            high = sums[2].astype(bf16).astype(f32)
            tailing = tailing + jnp.where(row == 3, high, jnp.where(row == 4, sums[2] - high, 0.0))
            ends[pl.ds(AUG + width, rest), :] = jnp.concatenate([tailing] * 4, axis=1).astype(bf16)
            share_block(0)
            for slab in slabs:
                weigh(norm_last_ref, 0, *slab)
            for p in range(CHAIN):
                late[p] = weights[p * share : (p + 1) * share, :].astype(bf16)
            for d in range(1, CHAIN):
                peer = lax.rem(pos + d, CHAIN)
                push(late.at[peer], late_ref.at[mine], la_send.at[d - 1], la_recv.at[mine], base + peer).start()
            pltpu.make_async_copy(late.at[pos], late_ref.at[mine], la_recv.at[mine]).start()
            for d in range(1, CHAIN):
                push(ends, ends_ref.at[mine], en_send.at[d - 1], en_recv.at[mine],
                     base + lax.rem(pos + d, CHAIN)).start()
            pltpu.make_async_copy(ends, ends_ref.at[mine], en_recv.at[mine]).start()

    @pl.when(pid == last)
    def _():
        for d in range(1, CHAIN // 2):
            other = lax.rem(rank + d, CHAIN // 2)
            push(quarter.at[other], quarter_got.at[d - 1], qu_send.at[d - 1], qu_recv.at[d - 1],
                 base + 2 * other + side).wait()
        for d in range(1, CHAIN):
            push(small_ref, small_out.at[pos], sm_send.at[d - 1], sm_recv.at[d - 1],
                 base + lax.rem(pos + d, CHAIN)).wait_send()
            await_bytes(small_out.at[lax.rem(pos + CHAIN - d, CHAIN)], sm_recv.at[d - 1])
        await_bytes(small_out.at[pos], sm_loc)

        def add_up(c, _):
            rows = pl.ds(pl.multiple_of(c * MINI, MINI), MINI)
            acc = quarter[rank, rows, :].astype(f32)
            for d in range(1, CHAIN // 2):
                acc = acc + quarter_got[d - 1, rows, :].astype(f32)
            early_out[rows, :] = acc
            return 0

        lax.fori_loop(0, early_out.shape[0] // MINI, add_up, 0)
        for j in range(heads):
            @pl.when(pos != FIRST + j)
            def _():
                await_bytes(dout.at[pos], gm_send.at[j])

            await_bytes(grads_ref.at[j], bc_recv.at[j])
            await_bytes(ends_ref.at[j], en_recv.at[j])
            await_bytes(late_ref.at[j], la_recv.at[j])

        @pl.when(owner)
        def _():
            await_bytes(packed.at[pl.ds(0, (CHAIN - 1) * rows_each), :], bc_send)
            for d in range(1, CHAIN):
                await_bytes(ends, en_send.at[d - 1])
                await_bytes(late.at[0], la_send.at[d - 1])


def chain_backward(grad_mixed, early, small, gain, bias, normed, saved, block=256, turn=3):
    heads, rows, width = grad_mixed.shape
    tokens = rows * CHAIN
    hidden = saved[5].shape[1]
    nblk = tokens // block
    nb = block // MINI
    whole = lambda a: pl.BlockSpec(a.shape, lambda i: (0,) * a.ndim)
    rowblk = lambda w: pl.BlockSpec((block, w), lambda i: (nblk - 1 - i, 0))
    stepblk = lambda r: pl.BlockSpec((nb, r, hidden), lambda i: (nblk - 1 - i, 0, 0))
    behind = pl.BlockSpec((block, normed.shape[1]), lambda i: (jnp.minimum(nblk - i, nblk - 1), 0))
    first = pl.BlockSpec((block, normed.shape[1]), lambda i: (0, 0))
    anywhere = pl.BlockSpec(memory_space=pl.ANY)
    dma = pltpu.SemaphoreType.DMA
    seven = dma((CHAIN - 1,))
    share = early.shape[2:]
    three = dma((CHAIN // 2 - 1,))
    return pl.pallas_call(
        functools.partial(bwd_kernel, block, heads, turn),
        grid=(nblk,),
        in_specs=[anywhere] * 3 + [whole(gain), whole(bias), behind, first, rowblk(AUG), rowblk(AUG),
                                   rowblk(2 * width), stepblk(AUG), stepblk(width), rowblk(hidden), rowblk(hidden), rowblk(width),
                                   rowblk(width), rowblk(hidden), rowblk(width)],
        out_specs=[anywhere, anywhere, anywhere, pl.BlockSpec(share, lambda i: (0, 0)), anywhere],
        out_shape=[jax.ShapeDtypeStruct((heads, rows, PACK), bf16),
                   jax.ShapeDtypeStruct((heads, ENDS, hidden), bf16),
                   jax.ShapeDtypeStruct((heads, share[0], PACK), bf16),
                   jax.ShapeDtypeStruct(share, f32),
                   jax.ShapeDtypeStruct((CHAIN,) + small.shape, f32)],
        scratch_shapes=[pltpu.VMEM((CHAIN, rows, width), bf16), pltpu.VMEM((CHAIN // 2,) + share, bf16),
                        pltpu.VMEM((CHAIN // 2,) + share, bf16), pltpu.VMEM((CHAIN // 2,) + share, bf16),
                        pltpu.VMEM((CHAIN // 2 - 1,) + share, bf16),
                        pltpu.VMEM((tokens, PACK), bf16), pltpu.VMEM((ENDS, hidden), bf16),
                        pltpu.VMEM((CHAIN * share[0], PACK), f32), pltpu.VMEM((CHAIN, share[0], PACK), bf16),
                        pltpu.VMEM((AUG, hidden), f32), pltpu.VMEM((width, hidden), f32), pltpu.VMEM((1, width), f32),
                        pltpu.VMEM((2 * MINI, hidden), bf16), pltpu.VMEM((2 * MINI, AUG), bf16),
                        pltpu.VMEM((3 * MINI, width), bf16), pltpu.VMEM((3 * MINI, hidden), bf16),
                        pltpu.VMEM((1, width), f32), pltpu.VMEM((MINI, width), f32), pltpu.VMEM((MINI, width), f32),
                        pltpu.VMEM((MINI, 1), f32),
                        dma((heads,)), dma((CHAIN,)), dma, dma, dma, three, three, seven, seven, dma,
                        dma, dma((heads,)), seven, dma((heads,)), seven, dma((heads,))],
        compiler_params=pltpu.CompilerParams(collective_id=1, has_side_effects=True),
        name="inner_backward",
    )(grad_mixed, early, small, gain, bias, normed, normed, *saved)


def head_place():
    return lax.axis_index("head"), lax.axis_size("head")


def meet_heads(me, count):
    barrier = pltpu.get_barrier_semaphore()
    for d in range(1, count):
        pl.semaphore_signal(barrier, inc=1, device_id={"head": lax.rem(me + d, count)}, device_id_type=MESH)
    pl.semaphore_wait(barrier, count - 1)


def push_head(src, dst, send_sem, recv_sem, target):
    return pltpu.make_async_remote_copy(
        src_ref=src, dst_ref=dst, send_sem=send_sem, recv_sem=recv_sem,
        device_id={"head": target}, device_id_type=MESH)


def row_totals(first, second):
    ones = jnp.ones((8, first.shape[1]), f32)

    def total(x):
        return lax.dot_general(ones, x, (((1,), (1,)), ((), ())), precision=lax.Precision.HIGHEST,
                               preferred_element_type=f32)

    top, low = total(first), total(second)
    row = lax.broadcasted_iota(jnp.int32, top.shape, 0)
    return jnp.where(row == 0, top, low)


def mid_kernel(count, mixed_ref, x_ref, ctt_ref, mix_gate_ref, normed_ref, w_out_ref, w_gate_ref, w_up_ref, w_down_ref,
               post_gain_ref, post_bias_ref, ffn_gain_ref,
               gm_ref, early_ref, ggp_ref, out_ref, rco_ref, grc_ref, small_ref, norm_out,
               st_mine, st_got, pa_mine, pa_got, nt_all, rc_mine, rc_all, gn_mine, gn_got, dn_mine, dn_got, gov_all,
               gc_mine, gc_all, sb_mine, sb_got, gt_all, ct_ref, gh, gated, hidden, ggv, guv, resid,
               st_s, st_r, pa_s, pa_r, nt_s, nt_r, rc_s, rc_r, gn_s, gn_r, dn_s, dn_r, go_s, go_r, gc_s, gc_r, sb_s, sb_r,
               gt_s, gt_r, no_s, no_r):
    me, _ = head_place()
    heads, rows, width = mixed_ref.shape
    cols = heads * width
    full = cols * count
    part = rows // count
    peers = [(d, lax.rem(me + d, count)) for d in range(1, count)]
    pos, base = seq_place()
    owner = (pos >= FIRST) & (pos < FIRST + heads)
    barrier = pltpu.get_barrier_semaphore()
    for d in range(1, count):
        pl.semaphore_signal(barrier, inc=1, device_id={"head": lax.rem(me + d, count)}, device_id_type=MESH)
    for d in range(1, CHAIN):
        pl.semaphore_signal(
            barrier, inc=1, device_id={"seq": base + lax.rem(pos + d, CHAIN)}, device_id_type=MESH)
    pl.semaphore_wait(barrier, CHAIN - 1 + count - 1)
    ffn_gain = ffn_gain_ref[...][None, :]
    post_gain = post_gain_ref[...][None, :]
    post_bias = post_bias_ref[...][None, :]

    def rows_of(device):
        return pl.ds(pl.multiple_of(device * part, part), part)

    def send_all(src, dst, send, recv):
        for d, peer in peers:
            push_head(src, dst.at[d - 1], send.at[d - 1], recv.at[d - 1], peer).start()

    def wait_all(src, dst, send, recv):
        for d, peer in peers:
            push_head(src, dst.at[d - 1], send.at[d - 1], recv.at[d - 1], peer).wait()

    z = jnp.concatenate([mixed_ref[j] for j in range(heads)], axis=1).astype(f32)
    st_mine[...] = row_totals(z, z * z)
    send_all(st_mine, st_got, st_s, st_r)
    for j in range(heads):
        @pl.when(pos != FIRST + j)
        def _():
            push(normed_ref, norm_out.at[pos], no_s.at[j], no_r.at[pos], base + FIRST + j).start()

        @pl.when(pos == FIRST + j)
        def _():
            pltpu.make_async_copy(normed_ref, norm_out.at[pos], no_r.at[pos]).start()

    ct_ref[...] = ctt_ref[...].T
    gate_act, gate_der = gelu_first(dot_nt(normed_ref[...], mix_gate_ref[...]))
    gh[...] = dot_nt(ct_ref[...], w_down_ref[...])
    wait_all(st_mine, st_got, st_s, st_r)
    tot = st_mine[...]
    for d, _ in peers:
        tot = tot + st_got[d - 1]
    tot = tot.T * (1.0 / full)
    mean_z = tot[:, 0:1]
    inv_z = lax.rsqrt(tot[:, 1:2] - mean_z * mean_z + eps_norm)
    z_hat = (z - mean_z) * inv_z
    post_out = z_hat * post_gain + post_bias
    gated[...] = (post_out * gate_act).astype(bf16)

    def spread_rows(make, mine, got, send, recv):
        pending = None
        for d, peer in peers:
            mine[d - 1] = make(rows_of(peer)).astype(bf16)
            if pending is not None:
                pending.start()
            pending = push_head(mine.at[d - 1], got.at[d - 1], send.at[d - 1], recv.at[d - 1], peer)
        own = make(rows_of(me))
        pending.start()
        return own

    def add_rows(own, mine, got, send, recv):
        for d, peer in peers:
            push_head(mine.at[d - 1], got.at[d - 1], send.at[d - 1], recv.at[d - 1], peer).wait()
            own = own + got[d - 1].astype(f32)
        return own

    def gather_rows(all_ref, send, recv):
        for d, peer in peers:
            view = all_ref.at[rows_of(me), :]
            push_head(view, view, send.at[d - 1], recv.at[d - 1], peer).start()

    def gather_wait(all_ref, send, recv):
        for d, peer in peers:
            view = all_ref.at[rows_of(me), :]
            push_head(view, view, send.at[d - 1], recv.at[d - 1], peer).wait_send()
            await_bytes(all_ref.at[rows_of(lax.rem(me + count - d, count)), :], recv.at[d - 1])

    def turn_columns(value, mine, all_ref, send, recv):
        for b in range(count):
            mine[b] = value[:, b * cols : (b + 1) * cols]
        all_ref[rows_of(me), :] = mine[me]

    def turn_start(mine, all_ref, send, recv):
        for d, peer in peers:
            push_head(mine.at[peer], all_ref.at[rows_of(me), :], send.at[d - 1], recv.at[d - 1], peer).start()

    def turn_wait(mine, all_ref, send, recv):
        for d, peer in peers:
            push_head(mine.at[peer], all_ref.at[rows_of(me), :], send.at[d - 1], recv.at[d - 1], peer).wait_send()
            await_bytes(all_ref.at[rows_of(lax.rem(me + count - d, count)), :], recv.at[d - 1])

    w_out = w_out_ref[...]
    own = spread_rows(lambda r: dot_nn(gated[r, :], w_out), pa_mine, pa_got, pa_s, pa_r)
    res = x_ref[rows_of(me), :].astype(f32) + add_rows(own, pa_mine, pa_got, pa_s, pa_r)
    rms_two = lax.rsqrt(mean_row(res * res) + eps_norm)
    nt_all[rows_of(me), :] = (res * rms_two * ffn_gain).astype(bf16)
    turn_columns(res, rc_mine, rc_all, rc_s, rc_r)
    resid[...] = res
    gather_rows(nt_all, nt_s, nt_r)
    turn_start(rc_mine, rc_all, rc_s, rc_r)
    gather_wait(nt_all, nt_s, nt_r)
    def forward_rows(b, _):
        r = pl.ds(pl.multiple_of(b * part, part), part)
        nt = nt_all[r, :]
        gate_val = dot_nn(nt, w_gate_ref[...])
        up_val = dot_nn(nt, w_up_ref[...])
        sig = 1.0 / (1.0 + jnp.exp(-gate_val))
        silu = gate_val * sig
        hidden[r, :] = (silu * up_val).astype(bf16)
        g = gh[r, :]
        ggv[r, :] = (g * up_val * sig * (1.0 + gate_val * (1.0 - sig))).astype(bf16)
        guv[r, :] = (g * silu).astype(bf16)
        return 0

    lax.fori_loop(0, count, forward_rows, 0)
    own = spread_rows(lambda r: dot_nt(ggv[r, :], w_gate_ref[...]) + dot_nt(guv[r, :], w_up_ref[...]),
                      gn_mine, gn_got, gn_s, gn_r)
    for b in range(count):
        r = pl.ds(b * part, part)
        down = dot_nn(hidden[r, :], w_down_ref[...]).astype(bf16)
        for c in range(count):
            dn_mine[c, r, :] = down[:, c * cols : (c + 1) * cols]
    ffn = w_gate_ref.shape[1]
    half = full // 2
    for b in range(2):
        r = slice(b * half, (b + 1) * half)
        early_ref[r, 0:ffn] = dot_tn(nt_all[:, r], ggv[...]).astype(bf16)
    for d, peer in peers:
        push_head(dn_mine.at[peer], dn_got.at[d - 1], dn_s.at[d - 1], dn_r.at[d - 1], peer).start()
    gnt = add_rows(own, gn_mine, gn_got, gn_s, gn_r)
    res = resid[...]
    rms_two = lax.rsqrt(mean_row(res * res) + eps_norm)
    scaled = gnt * ffn_gain
    grad_res = ct_ref[rows_of(me), :].astype(f32) + rms_two * (
        scaled - res * rms_two * rms_two * mean_row(scaled * res))
    gov_all[rows_of(me), :] = grad_res.astype(bf16)
    gt_all[me] = jnp.broadcast_to(jnp.sum(gnt * res * rms_two, axis=0, keepdims=True), gt_all.shape[1:])
    turn_columns(grad_res, gc_mine, gc_all, gc_s, gc_r)
    gather_rows(gov_all, go_s, go_r)
    turn_start(gc_mine, gc_all, gc_s, gc_r)
    for d, peer in peers:
        push_head(gt_all.at[me], gt_all.at[me], gt_s.at[d - 1], gt_r.at[d - 1], peer).start()
    for b in range(2):
        r = slice(b * half, (b + 1) * half)
        early_ref[r, ffn : 2 * ffn] = dot_tn(nt_all[:, r], guv[...]).astype(bf16)
    gather_wait(gov_all, go_s, go_r)
    gov = gov_all[...]
    grad_gated = dot_nt(gov, w_out_ref[...])
    grad_post = grad_gated * gate_act
    grad_zhat = grad_post * post_gain
    sb_mine[...] = row_totals(grad_zhat, grad_zhat * z_hat)
    ggp = (grad_gated * post_out * gate_der).astype(bf16)
    ggp_ref[...] = ggp
    send_all(sb_mine, sb_got, sb_s, sb_r)
    early_ref[:, 3 * ffn : 3 * ffn + 2 * cols] = jnp.concatenate(
        [dot_tn(normed_ref[...], ggp).astype(bf16), dot_tn(gov, gated[...]).astype(bf16)], axis=1)
    row = lax.broadcasted_iota(jnp.int32, (8, cols), 0)
    wait_all(sb_mine, sb_got, sb_s, sb_r)
    tot = sb_mine[...]
    for d, _ in peers:
        tot = tot + sb_got[d - 1]
    tot = tot.T * (1.0 / full)
    grad_mixed = (inv_z * (grad_zhat - tot[:, 0:1] - z_hat * tot[:, 1:2])).astype(bf16)
    for j in range(heads):
        gm_ref[j] = grad_mixed[:, j * width : (j + 1) * width]
    for b in range(2):
        r = slice(b * half, (b + 1) * half)
        early_ref[r, 2 * ffn : 3 * ffn] = dot_nn(ctt_ref[r, :], hidden[...]).astype(bf16)
    turn_wait(rc_mine, rc_all, rc_s, rc_r)
    rco_ref[...] = rc_all[...]
    out = dn_mine[me].astype(f32)
    for d, peer in peers:
        push_head(dn_mine.at[peer], dn_got.at[d - 1], dn_s.at[d - 1], dn_r.at[d - 1], peer).wait()
        out = out + dn_got[d - 1].astype(f32)
    out_ref[...] = out
    turn_wait(gc_mine, gc_all, gc_s, gc_r)
    grc_ref[...] = gc_all[...]
    for d, peer in peers:
        push_head(gt_all.at[me], gt_all.at[me], gt_s.at[d - 1], gt_r.at[d - 1], peer).wait_send()
        await_bytes(gt_all.at[lax.rem(me + count - d, count)], gt_r.at[d - 1])
    gain_two = gt_all[0]
    for b in range(1, count):
        gain_two = gain_two + gt_all[b]
    post = jnp.where(row == 1, jnp.sum(grad_post * z_hat, axis=0, keepdims=True),
                     jnp.sum(grad_post, axis=0, keepdims=True))
    line = lax.broadcasted_iota(jnp.int32, (8, full), 0)
    small_ref[...] = jnp.where(
        line == 0, gain_two, jnp.concatenate([post] + [jnp.zeros_like(post)] * (count - 1), axis=1))
    for j in range(heads):
        @pl.when(pos != FIRST + j)
        def _():
            await_bytes(normed_ref, no_s.at[j])

    @pl.when(owner)
    def _():
        for p in range(CHAIN):
            await_bytes(norm_out.at[p], no_r.at[p])


def middle(mixed, x, ct, mix_gate, normed, w_out, w_gate, w_up, w_down, post_gain, post_bias, ffn_gain):
    count = lax.axis_size("head")
    heads, rows, width = mixed.shape
    cols = heads * width
    full = cols * count
    part = rows // count
    ffn = w_gate.shape[1]
    ins = (mixed, x, ct, mix_gate, normed, w_out, w_gate, w_up, w_down, post_gain, post_bias, ffn_gain)
    vmem = pl.BlockSpec(memory_space=pltpu.VMEM)
    V = pltpu.VMEM
    trio = count - 1
    sem = pltpu.SemaphoreType.DMA((trio,))
    return pl.pallas_call(
        functools.partial(mid_kernel, count),
        in_specs=[vmem] * len(ins),
        out_specs=[vmem] * 7 + [pl.BlockSpec(memory_space=pl.ANY)],
        out_shape=[jax.ShapeDtypeStruct((heads, rows, width), bf16),
                   jax.ShapeDtypeStruct((full, 3 * ffn + 2 * cols), bf16),
                   jax.ShapeDtypeStruct((rows, cols), bf16),
                   jax.ShapeDtypeStruct((rows, cols), f32),
                   jax.ShapeDtypeStruct((rows, cols), f32),
                   jax.ShapeDtypeStruct((rows, cols), f32),
                   jax.ShapeDtypeStruct((8, full), f32),
                   jax.ShapeDtypeStruct((CHAIN, rows, full), bf16)],
        scratch_shapes=[
            V((8, rows), f32), V((trio, 8, rows), f32),
            V((trio, part, full), bf16), V((trio, part, full), bf16),
            V((rows, full), bf16),
            V((count, part, cols), f32), V((rows, cols), f32),
            V((trio, part, full), bf16), V((trio, part, full), bf16),
            V((count, rows, cols), bf16), V((trio, rows, cols), bf16),
            V((rows, full), bf16),
            V((count, part, cols), f32), V((rows, cols), f32),
            V((8, rows), f32), V((trio, 8, rows), f32),
            V((count, 8, full), f32),
            V((rows, full), bf16), V((rows, ffn), f32), V((rows, cols), bf16),
            V((rows, ffn), bf16), V((rows, ffn), bf16), V((rows, ffn), bf16),
            V((part, full), f32)] + [sem] * 20 + [
            pltpu.SemaphoreType.DMA((heads,)), pltpu.SemaphoreType.DMA((CHAIN,))],
        compiler_params=pltpu.CompilerParams(
            collective_id=2, has_side_effects=True, vmem_limit_bytes=56 * 1024 * 1024),
        name="middle",
    )(*ins)


def front_kernel(count, in_ref, gain_ref, bias_ref, wq_ref, wk_ref, wv_ref, wr_ref, x_ref, normed_ref, pay_ref, gathered, send, recv):
    me, _ = head_place()
    cols, rows = in_ref.shape
    heads = wr_ref.shape[0]
    width = cols // heads
    part = rows // count
    meet_heads(me, count)
    here = pl.ds(pl.multiple_of(me * cols, cols), cols)
    for d in range(1, count):
        push_head(in_ref, gathered.at[here, :], send.at[d - 1], recv.at[d - 1], lax.rem(me + d, count)).start()
    gathered[here, :] = in_ref[...]
    for d in range(1, count):
        push_head(in_ref, gathered.at[here, :], send.at[d - 1], recv.at[d - 1], lax.rem(me + d, count)).wait_send()
        origin = lax.rem(me + count - d, count)
        await_bytes(gathered.at[pl.ds(pl.multiple_of(origin * cols, cols), cols), :], recv.at[d - 1])
    gain = gain_ref[...][None, :]
    rate_bias = bias_ref[...][None, :]
    x_ref[...] = gathered[...].T

    def project(b, _):
        r = pl.ds(pl.multiple_of(b * part, part), part)
        x = x_ref[r, :].astype(f32)
        nt = (x * lax.rsqrt(mean_row(x * x) + eps_norm) * gain).astype(bf16)
        normed_ref[r, :] = nt
        query = dot_nt(nt, wq_ref[...]).astype(bf16)
        key = dot_nt(nt, wk_ref[...]).astype(bf16)
        value = dot_nt(nt, wv_ref[...]).astype(bf16)
        logit = dot_nt(nt, wr_ref[...]) + rate_bias
        high = logit.astype(bf16)
        low = (logit - high.astype(f32)).astype(bf16)
        lane = lax.broadcasted_iota(jnp.int32, (part, width), 1)
        for j in range(heads):
            own = slice(j * width, (j + 1) * width)
            extra = jnp.where(lane == 0, high[:, j : j + 1].astype(f32),
                              jnp.where(lane == 1, low[:, j : j + 1].astype(f32), 0.0)).astype(bf16)
            pay_ref[r, j * PACK : (j + 1) * PACK] = jnp.concatenate(
                [query[:, own], key[:, own], value[:, own], extra], axis=1)
        return 0

    lax.fori_loop(0, count, project, 0)


def front(inputs_t, pre_gain, rate_bias, wq, wk, wv, wr):
    count = lax.axis_size("head")
    cols, rows = inputs_t.shape
    heads = wr.shape[0]
    vmem = pl.BlockSpec(memory_space=pltpu.VMEM)
    sem = pltpu.SemaphoreType.DMA((count - 1,))
    wide = jax.ShapeDtypeStruct((rows, cols * count), bf16)
    return pl.pallas_call(
        functools.partial(front_kernel, count),
        in_specs=[vmem] * 7,
        out_specs=[vmem] * 3,
        out_shape=[wide, wide, jax.ShapeDtypeStruct((rows, heads * PACK), bf16)],
        scratch_shapes=[pltpu.VMEM((cols * count, rows), bf16), sem, sem],
        compiler_params=pltpu.CompilerParams(collective_id=4, has_side_effects=True),
        name="front",
    )(inputs_t, pre_gain, rate_bias, wq, wk, wv, wr)


def tail_kernel(count, at_mix, grads_ref, wq_ref, wk_ref, wv_ref, wr_ref, mix_gate_ref, ggp_ref, x_ref, gain_ref,
                late_ref, early_ref,
                back_ref, tiles_ref,
                mine, got, tile, tile_got, wcols, ib_s, ib_r, th_s, th_r, ts_s, ts_r, ts_loc):
    me, _ = head_place()
    pos, base = seq_place()
    heads = grads_ref.shape[0]
    rows = x_ref.shape[0]
    cols = ggp_ref.shape[1]
    full = x_ref.shape[1]
    share = early_ref.shape[0]
    rate_lane = PACK - PACK // 4
    peers = [(d, lax.rem(me + d, count)) for d in range(1, count)]
    barrier = pltpu.get_barrier_semaphore()
    for d, peer in peers:
        pl.semaphore_signal(barrier, inc=1, device_id={"head": peer}, device_id_type=MESH)
    for d in range(1, CHAIN):
        pl.semaphore_signal(
            barrier, inc=1, device_id={"seq": base + lax.rem(pos + d, CHAIN)}, device_id_type=MESH)
    part = rows // count
    width = PACK // 4
    pre_gain = gain_ref[...][None, :]
    sides = (wq_ref, wk_ref, wv_ref)

    def back_rows(b, _):
        r = pl.ds(pl.multiple_of(b * part, part), part)
        grad = dot_nn(ggp_ref[r, :], mix_gate_ref[...])
        blocks = [grads_ref[j, r, :] for j in range(heads)]
        for i, side in enumerate(sides):
            joined = jnp.concatenate([b[:, i * width : (i + 1) * width] for b in blocks], axis=1)
            grad = grad + dot_nn(joined, side[...])
        for j in range(heads):
            rate = blocks[j][:, rate_lane : rate_lane + 1].astype(f32) + blocks[j][
                :, rate_lane + 1 : rate_lane + 2].astype(f32)
            grad = grad + rate.astype(bf16).astype(f32) * wr_ref[j : j + 1, :].astype(f32)
        x = x_ref[r, :].astype(f32)
        rms = lax.rsqrt(mean_row(x * x) + eps_norm)
        scaled = grad * pre_gain
        back = (rms * (scaled - x * rms * rms * mean_row(scaled * x))).astype(bf16)
        for c in range(count):
            mine[c, r, :] = back[:, c * cols : (c + 1) * cols]
        return 0

    lane = lax.broadcasted_iota(jnp.int32, (share, 128), 1)
    line = lax.broadcasted_iota(jnp.int32, (8, 128), 0)
    w_rows = pl.ds(pl.multiple_of(pos * share, share), share)
    slim = jnp.concatenate([wr_ref[j : j + 1, :].astype(f32) for j in range(heads)] + [pre_gain] * (8 - heads), axis=0)
    wcols[4, :, 0:8] = slim.T
    for i, side in enumerate(sides + (mix_gate_ref,)):
        wcols[i] = side[...].astype(f32).T
    gain = jnp.sum(early_ref[:, at_mix : at_mix + cols] * wcols[3, w_rows, :], axis=1, keepdims=True)
    table = jnp.zeros((share, 128), f32)
    blocks = [late_ref[j].astype(f32) for j in range(heads)]
    for i in range(3):
        joined = jnp.concatenate([b[:, i * width : (i + 1) * width] for b in blocks], axis=1)
        gain = gain + jnp.sum(joined * wcols[i, w_rows, :], axis=1, keepdims=True)
    for j in range(heads):
        rate = blocks[j][:, rate_lane : rate_lane + 1] + blocks[j][:, rate_lane + 1 : rate_lane + 2]
        gain = gain + rate * wcols[4, w_rows, j : j + 1]
        table = jnp.where(lane == j, rate, table)
    gain = gain / wcols[4, w_rows, heads : heads + 1]
    table = jnp.where(lane == heads, gain, table)
    flat = jnp.concatenate([table, jnp.zeros((128 - share, 128), f32)], axis=0).T[0:8]
    tile[...] = flat
    pl.semaphore_wait(barrier, count - 1 + CHAIN - 1)
    for d, peer in peers:
        push_head(tile, tile_got.at[d - 1], th_s.at[d - 1], th_r.at[d - 1], peer).start()
    lax.fori_loop(0, count, back_rows, 0)
    for d, peer in peers:
        push_head(mine.at[peer], got.at[d - 1], ib_s.at[d - 1], ib_r.at[d - 1], peer).start()
    back = mine[me].astype(f32)
    for d, peer in peers:
        push_head(tile, tile_got.at[d - 1], th_s.at[d - 1], th_r.at[d - 1], peer).wait()
    summed = flat
    for d, peer in peers:
        summed = summed + tile_got[d - 1]
    tile[...] = jnp.where(line == heads, summed, flat)
    for d in range(1, CHAIN):
        push(tile, tiles_ref.at[pos], ts_s.at[d - 1], ts_r.at[d - 1], base + lax.rem(pos + d, CHAIN)).start()
    pltpu.make_async_copy(tile, tiles_ref.at[pos], ts_loc).start()
    for d, peer in peers:
        push_head(mine.at[peer], got.at[d - 1], ib_s.at[d - 1], ib_r.at[d - 1], peer).wait()
        back = back + got[d - 1].astype(f32)
    back_ref[...] = back
    for d in range(1, CHAIN):
        push(tile, tiles_ref.at[pos], ts_s.at[d - 1], ts_r.at[d - 1], base + lax.rem(pos + d, CHAIN)).wait_send()
        await_bytes(tiles_ref.at[lax.rem(pos + CHAIN - d, CHAIN)], ts_r.at[d - 1])
    await_bytes(tiles_ref.at[pos], ts_loc)


def tail(at_mix, grads, wq, wk, wv, wr, mix_gate, ggp, x, pre_gain, late, early):
    count = lax.axis_size("head")
    rows, full = x.shape
    width = ggp.shape[1]
    vmem = pl.BlockSpec(memory_space=pltpu.VMEM)
    V = pltpu.VMEM
    dma = pltpu.SemaphoreType.DMA
    trio, seven = dma((count - 1,)), dma((CHAIN - 1,))
    return pl.pallas_call(
        functools.partial(tail_kernel, count, at_mix),
        in_specs=[vmem] * 11,
        out_specs=[vmem] * 2,
        out_shape=[jax.ShapeDtypeStruct((rows, width), f32),
                   jax.ShapeDtypeStruct((CHAIN, 8, 128), f32)],
        scratch_shapes=[V((count, rows, width), bf16), V((count - 1, rows, width), bf16),
                        V((8, 128), f32), V((count - 1, 8, 128), f32), V((5, full, width), f32),
                        trio, trio, trio, trio, seven, seven, dma],
        compiler_params=pltpu.CompilerParams(
            collective_id=3, has_side_effects=True, vmem_limit_bytes=56 * 1024 * 1024),
        name="tail",
    )(grads, wq, wk, wv, wr, mix_gate, ggp, x, pre_gain, late, early)


def final_kernel(at_mix, ffn, down_ref, resid_ref, back_ref, grc_ref, late_ref, early_ref, ends_ref, tiles_ref, small_ref,
                 out_ref, gin_ref, gq_ref, gk_ref, gv_ref, gmix_ref, rate_ref, gwout_ref, gwg_ref, gwu_ref, gwd_ref,
                 w1_ref, b1_ref, w2_ref, b2_ref, ig_ref, ib_ref, rb_ref, pre_ref, pg_ref, pb_ref, fg_ref):
    heads, width, hidden = w1_ref.shape
    cols = heads * width
    out_ref[...] = (down_ref[...] + resid_ref[...]).T
    gin_ref[...] = (back_ref[...] + grc_ref[...]).T
    for i, ref in enumerate((gq_ref, gk_ref, gv_ref)):
        ref[...] = jnp.concatenate([late_ref[j, :, i * width : (i + 1) * width].astype(f32) for j in range(heads)], axis=1)
    gwg_ref[...] = early_ref[:, 0:ffn]
    gwu_ref[...] = early_ref[:, ffn : 2 * ffn]
    rates = []
    gwd_ref[...] = early_ref[:, 2 * ffn : 3 * ffn]
    both = early_ref[:, at_mix : at_mix + 2 * cols]
    gmix_ref[...] = both[:, 0:cols]
    gwout_ref[...] = both[:, cols:].T
    for j in range(heads):
        w1_ref[j] = ends_ref[j, 0:width, :].astype(f32)
        b1_ref[pl.ds(j, 1), :] = ends_ref[j, width : AUG, :].astype(f32)[0:1]
        second = ends_ref[j, AUG : AUG + width, :].astype(f32)
        w2_ref[j] = second - jnp.mean(second, axis=0, keepdims=True)
        rest = ends_ref[j, AUG + width :, :].astype(f32)[0:8, 0:width]
        b2_ref[pl.ds(j, 1), :] = rest[0:1] - mean_row(rest[0:1])
        ig_ref[pl.ds(j, 1), :] = rest[1:2]
        ib_ref[pl.ds(j, 1), :] = rest[2:3]
        rates.append((rest[3:4] + rest[4:5])[:, 0:1])
    each = rate_ref.shape[1] // CHAIN
    strips = jnp.concatenate([tiles_ref[p, :, 0:each] for p in range(CHAIN)], axis=1)
    rate_ref[...] = strips[0:heads]
    me, count = head_place()
    pick = [tiles_ref[me * (CHAIN // count) + i, heads : heads + 1, 0:each] for i in range(CHAIN // count)]
    pre_ref[...] = jnp.concatenate(pick, axis=1)[0]
    rb_ref[...] = jnp.concatenate(rates, axis=1)[0]
    acc = small_ref[0]
    for p in range(1, CHAIN):
        acc = acc + small_ref[p]
    fg_ref[...] = acc[0]
    pg_ref[...] = acc[1:2, 0:cols][0]
    pb_ref[...] = acc[2:3, 0:cols][0]


def finish(at_mix, ffn, down, resid, back, grc, late, early, ends, tiles, small, shapes):
    ins = (down, resid, back, grc, late, early, ends, tiles, small)
    vmem = pl.BlockSpec(memory_space=pltpu.VMEM)
    return pl.pallas_call(
        functools.partial(final_kernel, at_mix, ffn),
        in_specs=[vmem] * len(ins),
        out_specs=[vmem] * len(shapes),
        out_shape=[jax.ShapeDtypeStruct(s, f32) for s in shapes],
        compiler_params=pltpu.CompilerParams(vmem_limit_bytes=48 * 1024 * 1024),
        name="final",
    )(*ins)


def stretch_groups(axis):
    count = lax.axis_size(axis)
    return [[start + step for step in range(0, count, CHAIN)] for start in range(CHAIN)]


def local(
    inputs,
    pre_gain,
    w_query,
    w_key,
    w_value,
    mix_gate,
    w_rate,
    rate_bias,
    inner_gain,
    inner_bias,
    init_w_one,
    init_b_one,
    init_w_two,
    init_b_two,
    post_gain,
    post_bias,
    w_out,
    ffn_gain,
    w_gate,
    w_up,
    w_down,
    cotangent,
):
    full_width = pre_gain.shape[0]
    rows, local_cols = inputs.shape
    heads, head_dim = inner_gain.shape
    stretches = lax.axis_size("seq") // CHAIN
    share = full_width // CHAIN

    sides = (w_query.T, w_key.T, w_value.T, w_rate.T)
    whole_low, normed_one, payload = front(inputs.T, pre_gain, rate_bias, *sides)
    mixed_h, ct_blocks, *saved = chain_forward(
        payload, cotangent.T, init_w_one, init_b_one, init_w_two.transpose(0, 2, 1), init_b_two,
        inner_gain, inner_bias)
    ffn = w_gate.shape[1]
    at_mix = 3 * ffn
    grad_mixed, early, grad_gate_pre, down_cols, resid_cols, grad_resid_cols, small, normed_all = middle(
        mixed_h, whole_low, ct_blocks.reshape(full_width, rows), mix_gate.T, normed_one, w_out, w_gate, w_up, w_down,
        post_gain, post_bias, ffn_gain)
    grads, ends, late, early_sum, small = chain_backward(
        grad_mixed, early.reshape(CHAIN // 2, 2, share, early.shape[1]), small, inner_gain, inner_bias,
        normed_all.reshape(CHAIN * rows, full_width), saved)
    back_cols, tiles = tail(
        at_mix, grads, *sides, mix_gate.T, grad_gate_pre, whole_low, pre_gain,
        late, early_sum)
    if stretches > 1:
        groups = stretch_groups("seq")
        ends, tiles, small = lax.psum((ends.astype(f32), tiles, small), "seq", axis_index_groups=groups)
        seq_index = lax.axis_index("seq")
        stretch_lists = [list(range(s, s + CHAIN)) for s in range(0, stretches * CHAIN, CHAIN)]

        def spread(mine_rows):
            summed = lax.psum(mine_rows, "seq", axis_index_groups=groups)
            total = lax.all_gather(
                summed, "seq", axis=summed.ndim - 2, tiled=True, axis_index_groups=stretch_lists)
            return lax.dynamic_slice_in_dim(
                total, seq_index * (share // stretches), share // stretches, summed.ndim - 2)

        late = spread(late.astype(f32))
        early_sum = spread(early_sum)
    held = share // stretches
    hidden = init_w_one.shape[2]
    square = (held, local_cols)
    (outputs, grad_inputs, grad_q, grad_k, grad_v, grad_mix, grad_rate_w, grad_w_out, grad_w_gate, grad_w_up, grad_w_down,
     grad_one, grad_b_one, grad_two, grad_b_two, grad_gain, grad_bias, rate_b, grad_pre, grad_post_gain, grad_post_bias,
     grad_ffn_gain) = finish(
        at_mix, ffn, down_cols, resid_cols, back_cols, grad_resid_cols, late, early_sum, ends, tiles, small,
        ((local_cols, rows), (local_cols, rows), square, square, square, square, (heads, full_width),
         (local_cols, held), (held, ffn), (held, ffn), (held, ffn),
         (heads, head_dim, hidden), (heads, hidden), (heads, head_dim, hidden), (heads, head_dim),
         (heads, head_dim), (heads, head_dim), (heads,), (local_cols,), (local_cols,), (local_cols,), (full_width,)))
    return (
        outputs.T,
        grad_inputs.T,
        grad_pre,
        grad_q,
        grad_k,
        grad_v,
        grad_mix,
        grad_rate_w.T,
        rate_b,
        grad_gain,
        grad_bias,
        grad_one,
        grad_b_one,
        grad_two.transpose(0, 2, 1),
        grad_b_two,
        grad_post_gain,
        grad_post_bias,
        grad_w_out,
        grad_ffn_gain,
        grad_w_gate,
        grad_w_up,
        grad_w_down.T,
    )


def solution(mesh):
    in_specs = (
        P("seq", "head"),
        P(),
        P(None, "head"),
        P(None, "head"),
        P(None, "head"),
        P(None, "head"),
        P(None, "head"),
        P("head"),
        P("head", None),
        P("head", None),
        P("head", None, None),
        P("head", None),
        P("head", None, None),
        P("head", None),
        P("head"),
        P("head"),
        P("head", None),
        P(),
        P(None, "head"),
        P(None, "head"),
        P("head", None),
        P("seq", "head"),
    )
    out_specs = (
        P("seq", "head"),
        P("seq", "head"),
        P("head"),
        P("seq", "head"),
        P("seq", "head"),
        P("seq", "head"),
        P("seq", "head"),
        P(None, "head"),
        P("head"),
        P("head", None),
        P("head", None),
        P("head", None, None),
        P("head", None),
        P("head", None, None),
        P("head", None),
        P("head"),
        P("head"),
        P("head", "seq"),
        P(),
        P("seq", "head"),
        P("seq", "head"),
        P("head", "seq"),
    )
    return jax.shard_map(local, mesh=mesh, in_specs=in_specs, out_specs=out_specs, check_vma=False)
```
